32 devices in a mesh: seq: 4 (over z), row: 2 (over x), col: 4 (over y, core).
Axes of the slice: x: 2, y: 2, z: 4, core: 2. Of those that a mesh axis runs over, the one named last changes fastest.
Arguments:
- stream_in: float32 [2, 4096, 1536], P(None, 'seq', ('col', 'row')), may hold values from -6 to 6
- cotangent: float32 [2, 4096, 1536], P(None, 'seq', ('col', 'row')), may hold values from -6 to 6
- doc_lengths: int32 [2, 8], replicated, may hold values from 1 to 2048, 4096 in all within a row
- mixer_gain: float32 [1536], P(('col', 'row')), may hold values from 0.5 to 1.5
- input_weight: bfloat16 [1536, 2048], P('col', 'row'), may hold values from -0.15625 to 0.15625
- branch_weight: bfloat16 [1536, 2048], P('col', 'row'), may hold values from -0.15625 to 0.15625
- filter_taps: float32 [4, 2048], P(None, ('row', 'col')), may hold values from -3 to 3
- recall_gate: float32 [16, 128, 128], P('row'), may hold values from -0.5 to 0.5
- admit_gate: float32 [16, 128, 128], P('row'), may hold values from -0.5 to 0.5
- decay_param: float32 [2048], P(('row', 'col')), may hold values from 1 to 14
- output_weight: bfloat16 [2048, 1536], P('row', 'col'), may hold values from -0.25 to 0.25
- feed_gain: float32 [1536], P(('col', 'row')), may hold values from 0.5 to 1.5
- gate_weight: bfloat16 [1536, 4608], P('col', 'row'), may hold values from -0.15625 to 0.15625
- up_weight: bfloat16 [1536, 4608], P('col', 'row'), may hold values from -0.15625 to 0.15625
- down_weight: bfloat16 [4608, 1536], P('row', 'col'), may hold values from -0.1875 to 0.1875
Outputs:
- block_out: float32 [2, 4096, 1536], P(None, 'seq', ('col', 'row'))
- grad_stream: float32 [2, 4096, 1536], P(None, 'seq', ('col', 'row'))
- grad_mixer_gain: float32 [1536], P(('col', 'row'))
- grad_input_weight: float32 [1536, 2048], P('col', 'row')
- grad_branch_weight: float32 [1536, 2048], P('col', 'row')
- grad_filter_taps: float32 [4, 2048], P(None, ('row', 'col'))
- grad_recall_gate: float32 [16, 128, 128], P('row')
- grad_admit_gate: float32 [16, 128, 128], P('row')
- grad_decay_param: float32 [2048], P(('row', 'col'))
- grad_output_weight: float32 [2048, 1536], P('row', 'col')
- grad_feed_gain: float32 [1536], P(('col', 'row'))
- grad_gate_weight: float32 [1536, 4608], P('col', 'row')
- grad_up_weight: float32 [1536, 4608], P('col', 'row')
- grad_down_weight: float32 [4608, 1536], P('row', 'col')
The draws below stay inside these ranges and needn't reach their ends.
All inputs are finite; a program needn't handle non-finite values.
Results may differ from the reference program's by a relative error of at most 0.014.
Values may be sent and summed in bfloat16 or wider, within the bound.
A program may use at most 256 MiB of HBM per device.

```python
import math
import jax
import jax.numpy as jnp
import numpy as np
from jax import lax

D = 1536
F = 2048
FF = 4608
HEAD = 128
KW = 4
MB = 2
NDOCS = 8
HEADS = 16
SEQ_LEN = 4096
MOST_LEN = 2048


def draw_decay_param(key, part):
    floor_log = math.log(1.0 / (4.0 * SEQ_LEN))
    ceiling_log = math.log(0.25)
    rates = jnp.exp(jax.random.uniform(key, (F,), jnp.float32, floor_log, ceiling_log))
    return (-jnp.log(jnp.expm1(rates))).astype(jnp.float32)


def block_levels(key, shape, pieces, least, top_value):
    level, own = 1.0, jax.random.fold_in(key, 6)
    for position, shards_of in pieces:
        draws = jnp.exp(jax.random.uniform(jax.random.fold_in(own, position), (shards_of,), jnp.float32, least / len(pieces), top_value / len(pieces)))
        level = level * jnp.repeat(draws, shape[position] // shards_of).reshape([-1 if axis == position else 1 for axis in range(len(shape))])
    return level


def split_up(number_of, total, reach, slope):
    weights = [(1 << 20) // math.isqrt(grade ** slope) + 1 for grade in range(2, number_of + 1)]
    surplus, holding = total - reach - (number_of - 1), [1] * (number_of - 1)
    while surplus > 0:
        free = [i for i in range(number_of - 1) if holding[i] < reach]
        whole, budget = sum([weights[i] for i in free]), surplus
        for i in free:
            more = min(reach - holding[i], max(1, budget * weights[i] // whole), surplus)
            holding[i] = holding[i] + more
            surplus = surplus - more
    return np.array([reach] + holding)


def ragged_sizes(rng, number_of, total, bound, slope):
    if number_of == 2:
        one = jax.random.randint(rng, (), max(1, total - bound), min(bound, total - 1) + 1)
        return jnp.stack([one, total - one])
    sizes = jnp.asarray(split_up(number_of, total, bound, slope), jnp.int32)
    couples = (number_of - 1) // 2
    donor, sink = sizes[1:1 + 2 * couples:2], sizes[2:2 + 2 * couples:2]
    margin = jnp.minimum(donor - 1, bound - sink)
    shifted = jax.random.randint(jax.random.fold_in(rng, 1), (couples,), 0, 1 << 20) % (margin + 1)
    sizes = sizes.at[1:1 + 2 * couples:2].set(donor - shifted).at[2:2 + 2 * couples:2].set(sink + shifted)
    return sizes[jax.random.permutation(jax.random.fold_in(rng, 2), number_of)]


def normal_values(key, dims, spread, bound, pieces=(), held_as=jnp.bfloat16):
    drawn = jax.random.normal(key, dims, jnp.float32) * spread
    if len(pieces) > 0:
        drawn = block_levels(key, dims, pieces, -0.22, 0.18) * drawn
    return jnp.clip(drawn, min=-bound, max=bound).astype(held_as)


def setup_inputs(seed: int = 0) -> dict:
    keys = jax.random.split(jax.random.key(seed), 16)
    stream_in = normal_values(keys[0], (MB, SEQ_LEN, D), 1.0, 6.0, ((1, 4), (2, 8)), jnp.float32)
    cotangent = normal_values(keys[1], (MB, SEQ_LEN, D), 1.0, 6.0, ((1, 4), (2, 8)), jnp.float32)
    doc_lengths = jax.vmap(lambda own: ragged_sizes(own, NDOCS, SEQ_LEN, MOST_LEN, 2))(jax.random.split(keys[2], MB)).reshape((MB, NDOCS)).astype(jnp.int32)
    mixer_gain = jnp.clip(1.0 + 0.1 * jax.random.normal(keys[3], (D,), jnp.float32), 0.5, 1.5)
    input_weight = normal_values(keys[4], (D, F), D ** -0.5, 0.15625, ((0, 4), (1, 2)))
    branch_weight = normal_values(keys[5], (D, F), D ** -0.5, 0.15625, ((0, 4), (1, 2)))
    filter_taps = normal_values(keys[6], (KW, F), 0.5, 3.0, ((1, 8),), jnp.float32)
    recall_gate = normal_values(keys[7], (HEADS, HEAD, HEAD), HEAD ** -0.5, 0.5, ((0, 2),), jnp.float32)
    admit_gate = normal_values(keys[8], (HEADS, HEAD, HEAD), HEAD ** -0.5, 0.5, ((0, 2),), jnp.float32)
    decay_param = draw_decay_param(jax.random.fold_in(keys[15], 71), 0)
    output_weight = normal_values(keys[10], (F, D), (F // 4) ** -0.5, 0.25, ((0, 2), (1, 4)))
    feed_gain = jnp.clip(1.0 + 0.1 * jax.random.normal(keys[11], (D,), jnp.float32), 0.5, 1.5)
    gate_weight = normal_values(keys[12], (D, FF), D ** -0.5, 0.15625, ((0, 4), (1, 2)))
    up_weight = normal_values(keys[13], (D, FF), D ** -0.5, 0.15625, ((0, 4), (1, 2)))
    down_weight = normal_values(keys[14], (FF, D), (FF // 4) ** -0.5, 0.1875, ((0, 2), (1, 4)))
    return {"stream_in": stream_in, "cotangent": cotangent, "doc_lengths": doc_lengths, "mixer_gain": mixer_gain, "input_weight": input_weight, "branch_weight": branch_weight, "filter_taps": filter_taps, "recall_gate": recall_gate, "admit_gate": admit_gate, "decay_param": decay_param, "output_weight": output_weight, "feed_gain": feed_gain, "gate_weight": gate_weight, "up_weight": up_weight, "down_weight": down_weight}


EPSILON = 1e-06
PRECISE = lax.Precision.HIGHEST

@jax.custom_vjp
def low(v):
    return lax.optimization_barrier(v.astype(jnp.bfloat16)).astype(jnp.float32)

@jax.custom_vjp
def low_back(v):
    return v

def low_keep(v):
    return (low(v), None)

def low_pass(kept, grad):
    return (grad,)

def back_keep(v):
    return (v, None)

def back_low(kept, grad):
    return (low(grad),)
low.defvjp(low_keep, low_pass)
low_back.defvjp(back_keep, back_low)

def matmul(left, right):
    return jnp.dot(left, right, precision=PRECISE, preferred_element_type=jnp.float32)

def rms_scale(source, scales):
    return source * lax.rsqrt(lax.optimization_barrier(jnp.mean(source * source, axis=-1, keepdims=True)) + EPSILON) * scales

def compose(first, second):
    return (first[0] * second[0], second[0] * first[1] + second[1])

def doc_offset(lengths):
    starts = jnp.cumsum(lengths, dtype=jnp.int32) - lengths
    places = jnp.arange(SEQ_LEN, dtype=jnp.int32)
    begins = lax.optimization_barrier(jnp.max(jnp.where(starts[None, :] <= places[:, None], starts[None, :], 0), axis=1))
    return (places - begins).astype(jnp.int32)

def convolve(source, taps, offset, border):
    tokens = source.shape[0]
    extended = jnp.concatenate([border, source], axis=0)
    result = jnp.zeros_like(source)
    for lag_index in range(KW):
        anchor = KW - 1 - lag_index
        valid = (offset >= lag_index).astype(jnp.float32)[:, None]
        result = result + taps[lag_index] * extended[anchor:anchor + tokens] * valid
    return result

def gate_terms(conv_out, recall_gate, admit_gate, decay_param, resume):
    tokens = conv_out.shape[0]
    blocks = conv_out.reshape(tokens, recall_gate.shape[0], recall_gate.shape[1])
    recall_pre = jnp.einsum('thi,hij->thj', blocks, recall_gate, precision=PRECISE).reshape(tokens, -1)
    admit_pre = jnp.einsum('thi,hij->thj', blocks, admit_gate, precision=PRECISE).reshape(tokens, -1)
    recall = jax.nn.sigmoid(recall_pre)
    admit = jax.nn.sigmoid(admit_pre)
    log_decay = -8.0 * recall * jax.nn.softplus(-decay_param)
    decays = jnp.exp(log_decay) * resume[:, None]
    drives = jnp.sqrt(-jnp.expm1(2.0 * log_decay)) * admit * conv_out
    return (decays, drives)

def block(source, weights, offset):
    mixer_gain, input_weight, branch_weight, filter_taps, recall_gate, admit_gate, decay_param, output_weight, feed_gain, gate_weight, up_weight, down_weight = weights
    normed = low(rms_scale(source, mixer_gain))
    rec_in = low_back(matmul(normed, input_weight))
    branch = low_back(matmul(normed, branch_weight))
    conv_out = convolve(rec_in, filter_taps, offset, jnp.zeros((KW - 1, F), jnp.float32))
    resume = (offset > 0).astype(jnp.float32)
    decays, drives = gate_terms(conv_out, recall_gate, admit_gate, decay_param, resume)
    states = lax.associative_scan(compose, (decays, drives), axis=0)[1]
    mixed = low(states * jax.nn.gelu(branch))
    middle = source + low_back(matmul(mixed, output_weight))
    normed_two = low(rms_scale(middle, feed_gain))
    gate_pre = low_back(matmul(normed_two, gate_weight))
    up_pre = low_back(matmul(normed_two, up_weight))
    hidden = low(jax.nn.gelu(gate_pre) * up_pre)
    return middle + low_back(matmul(hidden, down_weight))

def reference(stream_in, cotangent, doc_lengths, mixer_gain, input_weight, branch_weight, filter_taps, recall_gate, admit_gate, decay_param, output_weight, feed_gain, gate_weight, up_weight, down_weight):
    weights = tuple((w.astype(jnp.float32) for w in (mixer_gain, input_weight, branch_weight, filter_taps, recall_gate, admit_gate, decay_param, output_weight, feed_gain, gate_weight, up_weight, down_weight)))
    totals = tuple((jnp.zeros_like(w) for w in weights))
    outputs = []
    grads_in = []
    for micro in range(MB):
        offset = doc_offset(doc_lengths[micro])

        def forward(source, params):
            return block(source, params, offset)
        result, pullback = jax.vjp(forward, stream_in[micro], weights)
        grad_source, grad_params = pullback(cotangent[micro])
        outputs.append(result)
        grads_in.append(grad_source)
        totals = tuple((acc + new for acc, new in zip(totals, grad_params)))
    return (jnp.stack(outputs), jnp.stack(grads_in), totals[0], totals[1], totals[2], totals[3], totals[4], totals[5], totals[6], totals[7], totals[8], totals[9], totals[10], totals[11])
```

```python
import functools

import jax
import jax.numpy as jnp
from jax import lax
from jax.experimental import pallas as pl
from jax.experimental.pallas import tpu as pltpu
from jax.sharding import PartitionSpec as P

D = 1536
KW = 4


EPSILON = 1e-06
PRECISE = lax.Precision.HIGHEST
SUM_ROWS = (((0,), (0,)), ((), ()))
SUM_COLS = (((1,), (1,)), ((), ()))


def as_sent(value):
    return jax.tree.map(lambda a: a.astype(jnp.bfloat16) if a.dtype == jnp.float32 else a, value)


def passed_along(block, axis, distance):
    devices = range(lax.axis_size(axis))
    route = [(i - distance, i) for i in devices if i - distance in devices]
    return lax.ppermute(block, axis, route)


def entering_2(part, axis, combine, identity, reverse):
    count = lax.axis_size(axis)
    place = lax.axis_index(axis)
    ahead = count - 1 - place if reverse else place
    gathered = jax.tree.map(lambda a: lax.all_gather(a, axis), part)
    state = jax.tree.map(lambda a, e: jnp.zeros_like(a) + jnp.asarray(e, a.dtype), part, identity)

    def one(hop, state):
        source = count - 1 - hop if reverse else hop
        return combine(
            state, jax.tree.map(lambda a: lax.dynamic_index_in_dim(a, source, 0, False), gathered)
        )

    return lax.fori_loop(0, ahead, one, state)


def compose(first, second):
    return (first[0] * second[0], second[0] * first[1] + second[1])


def convolve(source, taps, offset, border):
    tokens = source.shape[0]
    extended = jnp.concatenate([border, source], axis=0)
    result = jnp.zeros_like(source)
    for lag_index in range(KW):
        anchor = KW - 1 - lag_index
        valid = (offset >= lag_index).astype(jnp.float32)[:, None]
        result = result + taps[lag_index] * extended[anchor : anchor + tokens] * valid
    return result


def slab_pre(conv_value, recall_value, admit_value):
    tokens = conv_value.shape[0]
    blocks = conv_value.reshape(tokens, recall_value.shape[0], recall_value.shape[1])
    recall_pre = jnp.einsum("thi,hij->thj", blocks, recall_value, precision=PRECISE).reshape(
        tokens, -1
    )
    admit_pre = jnp.einsum("thi,hij->thj", blocks, admit_value, precision=PRECISE).reshape(
        tokens, -1
    )
    return (recall_pre, admit_pre)


def own_terms(conv_value, recall_pre, admit_pre, decay_value, resume):
    recall = jax.nn.sigmoid(recall_pre)
    admit = jax.nn.sigmoid(admit_pre)
    log_decay = -8.0 * recall * jax.nn.softplus(-decay_value)
    decays = jnp.exp(log_decay) * resume[:, None]
    drives = jnp.sqrt(-jnp.expm1(2.0 * log_decay)) * admit * conv_value
    return (decays, drives)


def width_total(partial_value):
    return lax.psum(partial_value, ("row", "col"))


def gather_row(source):
    return lax.all_gather(source, "row", axis=1, tiled=True)


def gather_col(source):
    return jax.tree.map(
        lambda part, own: part.astype(own.dtype),
        lax.all_gather(as_sent(source), "col", axis=1, tiled=True),
        source,
    )


def scatter_col(source):
    return (
        lax.psum_scatter(source[0], "col", scatter_dimension=1, tiled=True),
        lax.psum_scatter(source[1], "col", scatter_dimension=1, tiled=True),
    )


def scatter_col_back(source):
    return lax.psum_scatter(source, "col", scatter_dimension=1, tiled=True)


def scatter_row(source):
    return lax.psum_scatter(source, "row", scatter_dimension=1, tiled=True)


def over_seq(grads):
    return (
        lax.psum(grads[0].astype(jnp.bfloat16), "seq").astype(jnp.float32),
        lax.psum(grads[1].astype(jnp.bfloat16), "seq").astype(jnp.float32),
        lax.psum(grads[2].astype(jnp.bfloat16), "seq").astype(jnp.float32),
        lax.psum(grads[3].astype(jnp.bfloat16), "seq").astype(jnp.float32),
        lax.psum(grads[4].astype(jnp.bfloat16), "seq").astype(jnp.float32),
        lax.psum(grads[5].astype(jnp.bfloat16), "seq").astype(jnp.float32),
        lax.psum(grads[6].astype(jnp.bfloat16), "seq").astype(jnp.float32),
        lax.psum(grads[7].astype(jnp.bfloat16), "seq").astype(jnp.float32),
        lax.psum(grads[8].astype(jnp.bfloat16), "seq").astype(jnp.float32),
        lax.psum(grads[9].astype(jnp.bfloat16), "seq").astype(jnp.float32),
        lax.psum(grads[10].astype(jnp.bfloat16), "seq").astype(jnp.float32),
        lax.psum(grads[11].astype(jnp.bfloat16), "seq").astype(jnp.float32),
    )


def normalize(source, scales):
    factor = lax.rsqrt(width_total(jnp.sum(source * source, axis=1)) / D + EPSILON)
    return (source * factor[:, None] * scales, factor)


def norm_back(source, scales, factor, grad_norm):
    weighted = scales * grad_norm
    summed = width_total(jnp.sum(weighted * source, axis=1))
    grad_source = (
        factor[:, None] * weighted - source * (factor * factor * factor * summed / D)[:, None]
    )
    grad_scales = jnp.sum(grad_norm * source * factor[:, None], axis=0)
    return (grad_source, grad_scales)


def doc_offset(lengths, anchor, tokens):
    starts = jnp.cumsum(lengths, dtype=jnp.int32) - lengths
    places = anchor + jnp.arange(tokens, dtype=jnp.int32)
    begins = jnp.max(jnp.where(starts[None, :] <= places[:, None], starts[None, :], 0), axis=1)
    return places - begins


def matmul_rows(left, right):
    return lax.dot_general(left, right, SUM_ROWS, preferred_element_type=jnp.float32)


def matmul_cols(left, right):
    return lax.dot_general(left, right, SUM_COLS, preferred_element_type=jnp.float32)


def local(
    stream_in,
    cotangent,
    doc_lengths,
    mixer_gain,
    input_weight,
    branch_weight,
    filter_taps,
    recall_gate,
    admit_gate,
    decay_param,
    output_weight,
    feed_gain,
    gate_weight,
    up_weight,
    down_weight,
):
    tokens = stream_in.shape[1]
    anchor = lax.axis_index("seq") * tokens
    channels = decay_param.shape[0]
    col_start = lax.axis_index("col") * channels
    params = (
        mixer_gain,
        input_weight,
        branch_weight,
        filter_taps,
        recall_gate,
        admit_gate,
        decay_param,
        output_weight,
        feed_gain,
        gate_weight,
        up_weight,
        down_weight,
    )
    totals = tuple((jnp.zeros(w.shape, jnp.float32) for w in params))
    identity = (jnp.ones_like(decay_param), jnp.zeros_like(decay_param))
    outputs = []
    grads_in = []
    for micro in range(stream_in.shape[0]):
        offset = doc_offset(doc_lengths[micro], anchor, tokens)
        resume = (offset > 0).astype(jnp.float32)
        source = stream_in[micro]
        normed, factor_one = normalize(source, mixer_gain)
        normed_low = normed.astype(jnp.bfloat16)
        normed_all = gather_row(normed_low)
        rec_in, branch = scatter_col(
            (
                jnp.dot(normed_all, input_weight, preferred_element_type=jnp.float32),
                jnp.dot(normed_all, branch_weight, preferred_element_type=jnp.float32),
            )
        )
        border = passed_along(rec_in[tokens - (KW - 1) :], "seq", 1)
        conv_out = convolve(rec_in, filter_taps, offset, border)
        conv_slab = lax.all_gather(conv_out, "col", axis=1, tiled=True)
        slab_values, slab_pull = jax.vjp(slab_pre, conv_slab, recall_gate, admit_gate)
        recall_pre = lax.dynamic_slice_in_dim(slab_values[0], col_start, channels, 1)
        admit_pre = lax.dynamic_slice_in_dim(slab_values[1], col_start, channels, 1)

        def local_gates(conv_value, recall_value, admit_value, decay_value):
            return own_terms(conv_value, recall_value, admit_value, decay_value, resume)

        (decays, drives), gates_pull = jax.vjp(
            local_gates, conv_out, recall_pre, admit_pre, decay_param
        )
        cum_decay, local_state = lax.associative_scan(compose, (decays, drives), axis=0)
        entering = entering_2((cum_decay[-1], local_state[-1]), "seq", compose, identity, False)[1]
        states = local_state + cum_decay * entering
        branch_act = jax.nn.gelu(branch)
        mixed_all = gather_col((states * branch_act).astype(jnp.bfloat16))
        middle = source + scatter_row(
            jnp.dot(mixed_all, output_weight, preferred_element_type=jnp.float32)
        )
        normed_two, factor_two = normalize(middle, feed_gain)
        normed_two_low = normed_two.astype(jnp.bfloat16)
        normed_two_all = gather_row(normed_two_low)
        gate_pre, up_pre = scatter_col(
            (
                jnp.dot(normed_two_all, gate_weight, preferred_element_type=jnp.float32),
                jnp.dot(normed_two_all, up_weight, preferred_element_type=jnp.float32),
            )
        )
        gate_act = jax.nn.gelu(gate_pre)
        hidden_all = gather_col((gate_act * up_pre).astype(jnp.bfloat16))
        outputs.append(
            middle
            + scatter_row(jnp.dot(hidden_all, down_weight, preferred_element_type=jnp.float32))
        )
        upstream = cotangent[micro]
        upstream_all = gather_row(upstream.astype(jnp.bfloat16))
        grad_down = matmul_rows(hidden_all, upstream_all)
        grad_hidden = scatter_col_back(matmul_cols(upstream_all, down_weight))
        gate_value, gelu_pull = jax.vjp(jax.nn.gelu, gate_pre)
        error_gate = gelu_pull(grad_hidden * up_pre)[0].astype(jnp.bfloat16)
        error_up = (grad_hidden * gate_act).astype(jnp.bfloat16)
        gate_err_all, up_err_all = gather_col((error_gate, error_up))
        grad_gate = matmul_rows(normed_two_all, gate_err_all)
        grad_up = matmul_rows(normed_two_all, up_err_all)
        grad_normed_two = scatter_row(
            matmul_cols(gate_err_all, gate_weight) + matmul_cols(up_err_all, up_weight)
        )
        back_middle, grad_feed = norm_back(middle, feed_gain, factor_two, grad_normed_two)
        grad_middle = upstream + back_middle
        rec_err_all = gather_row(grad_middle.astype(jnp.bfloat16))
        grad_output = matmul_rows(mixed_all, rec_err_all)
        grad_mixed = scatter_col_back(matmul_cols(rec_err_all, output_weight))
        branch_value, branch_pull = jax.vjp(jax.nn.gelu, branch)
        error_branch = branch_pull(grad_mixed * states)[0].astype(jnp.bfloat16)
        direct = grad_mixed * branch_act
        ahead = jnp.concatenate([decays[1:], jnp.ones_like(decays[:1])], axis=0)
        reach, partial_adj = lax.associative_scan(compose, (ahead, direct), axis=0, reverse=True)
        incoming = entering_2(
            (decays[0] * reach[0], decays[0] * partial_adj[0]), "seq", compose, identity, True
        )[1]
        adjoint = partial_adj + reach * incoming
        previous = jnp.concatenate([entering[None, :], states[:-1]], axis=0)
        conv_direct, grad_recall_pre, grad_admit_pre, grad_decay = gates_pull(
            (adjoint * previous, adjoint)
        )
        recall_all, admit_all = (
            lax.all_gather(grad_recall_pre.astype(jnp.bfloat16), "col", axis=1, tiled=True).astype(
                grad_recall_pre.dtype
            ),
            lax.all_gather(grad_admit_pre.astype(jnp.bfloat16), "col", axis=1, tiled=True).astype(
                grad_admit_pre.dtype
            ),
        )
        grad_slab, grad_recall, grad_admit = slab_pull((recall_all, admit_all))
        grad_conv_out = conv_direct + lax.dynamic_slice_in_dim(grad_slab, col_start, channels, 1)

        def local_conv(input_value, taps_value, border_value):
            return convolve(input_value, taps_value, offset, border_value)

        conv_value, conv_pull = jax.vjp(local_conv, rec_in, filter_taps, border)
        grad_rec_in, grad_taps, grad_border = conv_pull(grad_conv_out)
        from_next = passed_along(grad_border, "seq", -1)
        grad_rec_in = grad_rec_in + jnp.pad(from_next, ((tokens - (KW - 1), 0), (0, 0)))
        error_input = grad_rec_in.astype(jnp.bfloat16)
        in_err_all, branch_err_all = gather_col((error_input, error_branch))
        grad_input = matmul_rows(normed_all, in_err_all)
        grad_branch = matmul_rows(normed_all, branch_err_all)
        grad_normed = scatter_row(
            matmul_cols(in_err_all, input_weight) + matmul_cols(branch_err_all, branch_weight)
        )
        back_source, grad_mixer = norm_back(source, mixer_gain, factor_one, grad_normed)
        grads_in.append(grad_middle + back_source)
        local_grads = (
            grad_mixer,
            grad_input,
            grad_branch,
            grad_taps,
            grad_recall,
            grad_admit,
            grad_decay,
            grad_output,
            grad_feed,
            grad_gate,
            grad_up,
            grad_down,
        )
        local_grads = over_seq(local_grads)
        totals = tuple((acc + new for acc, new in zip(totals, local_grads)))
    return (jnp.stack(outputs), jnp.stack(grads_in)) + tuple(totals)


BF = jnp.bfloat16
F32 = jnp.float32
VMEM_LIMIT = 56 * 1024 * 1024
ROW_BLOCK = 256
GELU_A = 0.7978845608028654
GELU_B = 0.044715


def flip_row(a):
    return lax.ppermute(a, "row", [(0, 1), (1, 0)])


def flip_y(a):
    return lax.ppermute(a, "col", [(i, i ^ 2) for i in range(4)])


def flip_core(a):
    return lax.ppermute(a, "col", [(i, i ^ 1) for i in range(4)])


def shifted(a, distance):
    return passed_along(a, "seq", distance)


def cost(flops, moved, trans=0):
    return pl.CostEstimate(flops=int(flops), bytes_accessed=int(moved), transcendentals=int(trans))


def params():
    return pltpu.CompilerParams(vmem_limit_bytes=VMEM_LIMIT, dimension_semantics=("arbitrary",))


def nbytes(*arrays):
    return sum(a.size * a.dtype.itemsize for a in arrays)


def spread(halves):
    first, second = halves
    ax, ay = flip_row(first), flip_y(first)
    bx, by = flip_row(second), flip_y(second)
    return ((first, ax, ay, flip_y(ax)), (second, bx, by, flip_row(by)))


def collect(halves):
    (a0, a1, a2, a3), (b0, b1, b2, b3) = halves
    a2 = (a2.astype(F32) + flip_row(a3).astype(F32)).astype(BF)
    b1 = (b1.astype(F32) + flip_y(b3).astype(F32)).astype(BF)
    return (
        a0 + flip_row(a1).astype(F32) + flip_y(a2).astype(F32),
        b0 + flip_row(b1).astype(F32) + flip_y(b2).astype(F32),
    )


def gelu_pair(v):
    t = jnp.tanh(GELU_A * (v + GELU_B * v * v * v))
    value = 0.5 * v * (1.0 + t)
    slope = 0.5 * (1.0 + t) + 0.5 * v * (1.0 - t * t) * GELU_A * (1.0 + 3.0 * GELU_B * v * v)
    return value, slope


def minus_expm1(x):
    series = 1.0 + x * (1.0 / 7.0)
    for n in (6, 5, 4, 3, 2):
        series = 1.0 + x * (1.0 / n) * series
    return jnp.where(x > -0.3, -x * series, 1.0 - jnp.exp(x))


def pair_up(left, right):
    width = left.shape[1]
    lane = lax.broadcasted_iota(jnp.int32, left.shape, 1)
    low = lane < width // 2
    return (
        jnp.where(low, left, pltpu.roll(right, width // 2, 1)),
        jnp.where(low, pltpu.roll(left, width // 2, 1), right),
    )


def dot_nn(a, b, precision=None):
    return lax.dot_general(
        a, b, (((1,), (0,)), ((), ())), precision=precision, preferred_element_type=F32
    )


def dot_nt(a, b, precision=None):
    return lax.dot_general(
        a, b, (((1,), (1,)), ((), ())), precision=precision, preferred_element_type=F32
    )


def dot_tn(a, b, precision=None):
    return lax.dot_general(
        a, b, (((0,), (0,)), ((), ())), precision=precision, preferred_element_type=F32
    )


def rows_spec(block, width, start=0):
    return pl.BlockSpec((block, width), lambda i: (i + start, 0))


def whole_spec(shape):
    rank = len(shape)
    return pl.BlockSpec(shape, lambda i: (0,) * rank, pipeline_mode=pl.Buffered(1))


def head_spec(rows, width=128):
    return pl.BlockSpec((rows, width), lambda h: (0, h))


def sds(shape, dtype):
    return jax.ShapeDtypeStruct(shape, dtype)


def norm_uv_body(x0, x1, x2, x3, gain, w, keep, pass_on, u, v, scale):
    parts = [r[...].astype(F32) for r in (x0, x1, x2, x3)]
    width = parts[0].shape[1]
    total = sum(jnp.sum(p * p, axis=1, keepdims=True) for p in parts)
    s = lax.rsqrt(total / D + EPSILON)
    scale[...] = s
    normed = [p * s * gain[0:1, j * width : (j + 1) * width] for j, p in enumerate(parts)]
    acc = None
    for j, n in enumerate(normed):
        term = dot_nn(n.astype(BF), w[j * width : (j + 1) * width, :])
        acc = term if acc is None else acc + term
    channels = u.shape[1]
    u[...] = acc[:, :channels]
    v[...] = acc[:, channels:]
    for j in (0, 1):
        k, p = pair_up(normed[2 * j], normed[2 * j + 1])
        keep[:, j * width : (j + 1) * width] = k.astype(BF)
        pass_on[:, j * width : (j + 1) * width] = p.astype(BF)


def norm_uv(chunks, gain, w):
    rows, width = chunks[0].shape
    channels = w.shape[1] // 2
    block = ROW_BLOCK
    return pl.pallas_call(
        norm_uv_body,
        grid=(rows // block,),
        in_specs=[rows_spec(block, width)] * 4 + [whole_spec(gain.shape), whole_spec(w.shape)],
        out_specs=[rows_spec(block, 2 * width)] * 2
        + [rows_spec(block, channels)] * 2
        + [rows_spec(block, 1)],
        out_shape=[sds((rows, 2 * width), BF)] * 2
        + [sds((rows, channels), F32)] * 2
        + [sds((rows, 1), F32)],
        compiler_params=params(),
        cost_estimate=cost(2 * rows * w.size, nbytes(w, *chunks) * 2),
        name="norm_uv",
    )(*chunks, gain, w)


def chain(entries, count):
    state = entries[(count - 1) * 8 + 1 : (count - 1) * 8 + 2, :]
    for n in range(count - 2, -1, -1):
        state = entries[n * 8 + 1 : n * 8 + 2, :] + entries[n * 8 : n * 8 + 1, :] * state
    return state


def recur_body(
    ua, ub, border, off, taps, recall_w, admit_w, soft, conv, recall, admit, state, cum, ends, ext
):
    half = ua.shape[0]
    rows = 2 * half
    ext[0:8, :] = border[...]
    ext[8 : 8 + half, :] = ua[...]
    ext[8 + half : 8 + rows, :] = ub[...]
    step = ROW_BLOCK
    for r in range(0, rows, step):
        o = off[8 + r : 8 + r + step, :]
        total = taps[0:1, :] * ext[8 + r : 8 + r + step, :]
        for k in range(1, KW):
            term = taps[k : k + 1, :] * ext[8 + r - k : 8 + r - k + step, :]
            total = total + jnp.where(o >= k, term, 0.0)
        conv[r : r + step, :] = total
        rec = jax.nn.sigmoid(dot_nn(total, recall_w[0], PRECISE))
        adm = jax.nn.sigmoid(dot_nn(total, admit_w[0], PRECISE))
        recall[r : r + step, :] = rec
        admit[r : r + step, :] = adm
        ell = -8.0 * rec * soft[0:1, :]
        cum[r : r + step, :] = jnp.where(o > 0, jnp.exp(ell), 0.0)
        state[r : r + step, :] = jnp.sqrt(minus_expm1(2.0 * ell)) * adm * total
    seg = rows // 8

    def one(i, carry):
        h, p = carry
        at = pl.ds(i, 8, stride=seg)
        d = cum[at, :]
        h = d * h + state[at, :]
        p = d * p
        state[at, :] = h
        cum[at, :] = p
        return h, p

    zero = jnp.zeros((8, 128), F32)
    h, p = lax.fori_loop(0, seg, one, (zero, zero + 1.0), unroll=8)
    carry_h, carry_p = h[0:1, :], p[0:1, :]
    for s in range(1, 8):
        at = slice(s * seg, (s + 1) * seg)
        c = cum[at, :]
        state[at, :] = state[at, :] + c * carry_h
        cum[at, :] = c * carry_p
        carry_h = h[s : s + 1, :] + p[s : s + 1, :] * carry_h
        carry_p = p[s : s + 1, :] * carry_p
    ends[0:1, :] = carry_p
    ends[1:2, :] = carry_h
    ends[2:8, :] = jnp.zeros((6, 128), F32)


def recur(ua, ub, border, off, taps, recall_w, admit_w, soft):
    half, channels = ua.shape
    rows = 2 * half
    heads = channels // 128
    gate = pl.BlockSpec((1, 128, 128), lambda h: (h, 0, 0))
    full = sds((rows, channels), F32)
    return pl.pallas_call(
        recur_body,
        grid=(heads,),
        in_specs=[
            head_spec(half),
            head_spec(half),
            head_spec(8),
            whole_spec(off.shape),
            head_spec(KW),
            gate,
            gate,
            head_spec(1),
        ],
        out_specs=[head_spec(rows)] * 5 + [head_spec(8)],
        out_shape=[full] * 5 + [sds((8, channels), F32)],
        scratch_shapes=[pltpu.VMEM((rows + 8, 128), F32)],
        compiler_params=params(),
        cost_estimate=cost(rows * channels * 128 * 24, rows * channels * 4 * 6, rows * channels * 6),
        name="recur",
    )(ua, ub, border, off, taps, recall_w, admit_w, soft)


def mix_body(count, local, cum, v, entries, w, states, mixed, q0, q1, q2, q3):
    entering = chain(entries, count)
    st = local[...] + cum[...] * entering
    states[...] = st
    act = gelu_pair(v[...])[0]
    m = (st * act).astype(BF)
    mixed[...] = m
    width = q0.shape[1]
    for j, q in enumerate((q0, q1, q2, q3)):
        q[...] = dot_nn(m, w[:, j * width : (j + 1) * width]).astype(q.dtype)


def mix(half_index, local, cum, v, entries, w):
    rows, channels = v.shape
    width = w.shape[1] // 4
    block = ROW_BLOCK
    start = half_index * (rows // block)
    return pl.pallas_call(
        functools.partial(mix_body, entries.shape[0] // 8),
        grid=(rows // block,),
        in_specs=[rows_spec(block, channels, start)] * 2
        + [rows_spec(block, channels), whole_spec(entries.shape), whole_spec(w.shape)],
        out_specs=[rows_spec(block, channels)] * 2 + [rows_spec(block, width)] * 4,
        out_shape=[sds((rows, channels), F32), sds((rows, channels), BF), sds((rows, width), F32)]
        + [sds((rows, width), BF)] * 3,
        compiler_params=params(),
        cost_estimate=cost(2 * rows * w.size, rows * channels * 18 + nbytes(w)),
        name="mix",
    )(local, cum, v, entries, w)


def feed_body(*refs):
    (x0, x1, x2, x3, e0, e1, e2, e3, gain, wgu, wd) = refs[:11]
    (keep, pass_on, hid, eg, eu, ekeep, epass, scale, dots) = refs[11:20]
    outs, backs = refs[20:24], refs[24:28]
    parts = [r[...].astype(F32) for r in (x0, x1, x2, x3)]
    width = parts[0].shape[1]
    total = sum(jnp.sum(p * p, axis=1, keepdims=True) for p in parts)
    s = lax.rsqrt(total / D + EPSILON)
    scale[...] = s
    normed = [p * s * gain[1:2, j * width : (j + 1) * width] for j, p in enumerate(parts)]
    acc = None
    for j, n in enumerate(normed):
        term = dot_nn(n.astype(BF), wgu[j * width : (j + 1) * width, :])
        acc = term if acc is None else acc + term
    for j in (0, 1):
        k, p = pair_up(normed[2 * j], normed[2 * j + 1])
        keep[:, j * width : (j + 1) * width] = k.astype(BF)
        pass_on[:, j * width : (j + 1) * width] = p.astype(BF)
    errs = [r[...] for r in (e0, e1, e2, e3)]
    wide = [e.astype(F32) for e in errs]
    for j in (0, 1):
        k, p = pair_up(wide[2 * j], wide[2 * j + 1])
        ekeep[:, j * width : (j + 1) * width] = k.astype(BF)
        epass[:, j * width : (j + 1) * width] = p.astype(BF)
    units = hid.shape[1]
    pre, up = acc[:, :units], acc[:, units:]
    act, slope = gelu_pair(pre)
    h = (act * up).astype(BF)
    hid[...] = h
    dh = None
    for j, e in enumerate(errs):
        term = dot_nt(e, wd[:, j * width : (j + 1) * width])
        dh = term if dh is None else dh + term
    g = (dh * up * slope).astype(BF)
    b = (dh * act).astype(BF)
    eg[...] = g
    eu[...] = b
    dots[...] = jnp.sum(g.astype(F32) * pre + b.astype(F32) * up, axis=1, keepdims=True)
    for j, q in enumerate(backs):
        q[...] = (
            dot_nt(g, wgu[j * width : (j + 1) * width, :units])
            + dot_nt(b, wgu[j * width : (j + 1) * width, units:])
        ).astype(q.dtype)
    for j, q in enumerate(outs):
        q[...] = dot_nn(h, wd[:, j * width : (j + 1) * width]).astype(q.dtype)


def feed(chunks, errs, gain, wgu, wd):
    rows, width = chunks[0].shape
    units = wd.shape[0]
    block = ROW_BLOCK
    quarters = [sds((rows, width), F32)] + [sds((rows, width), BF)] * 3
    return pl.pallas_call(
        feed_body,
        grid=(rows // block,),
        in_specs=[rows_spec(block, width)] * 8
        + [whole_spec(gain.shape), whole_spec(wgu.shape), whole_spec(wd.shape)],
        out_specs=[rows_spec(block, 2 * width)] * 2
        + [rows_spec(block, units)] * 3
        + [rows_spec(block, 2 * width)] * 2
        + [rows_spec(block, 1)] * 2
        + [rows_spec(block, width)] * 8,
        out_shape=[sds((rows, 2 * width), BF)] * 2
        + [sds((rows, units), BF)] * 3
        + [sds((rows, 2 * width), BF)] * 2
        + [sds((rows, 1), F32)] * 2
        + quarters
        + quarters,
        compiler_params=params(),
        cost_estimate=cost(
            4 * rows * (wgu.size + wd.size), nbytes(wgu, wd) + rows * 30000, rows * units
        ),
        name="feed",
    )(*chunks, *errs, gain, wgu, wd)


def adjoint_body(*refs):
    ea, eb = refs[0:4], refs[4:8]
    (w, sa, sb, va, vb, recall, off, soft) = refs[8:16]
    (part, reach, eva, evb, ends, keep, pass_on, ext) = refs[16:]
    half = sa.shape[0]
    rows = 2 * half
    width = ea[0].shape[1]
    step = ROW_BLOCK

    @pl.when(pl.program_id(0) == 0)
    def _():
        for group, base in ((ea, 0), (eb, half)):
            for j in (0, 1):
                k, p = pair_up(group[2 * j][...].astype(F32), group[2 * j + 1][...].astype(F32))
                at = (slice(base, base + half), slice(j * width, (j + 1) * width))
                keep[at] = k.astype(BF)
                pass_on[at] = p.astype(BF)

    for r in range(0, rows, step):
        o = off[8 + r : 8 + r + step, :]
        ell = -8.0 * recall[r : r + step, :] * soft[0:1, :]
        ext[r : r + step, :] = jnp.where(o > 0, jnp.exp(ell), 0.0)
        group, states, branch, ev, base = (
            (ea, sa, va, eva, r) if r < half else (eb, sb, vb, evb, r - half)
        )
        at = slice(base, base + step)
        dm = None
        for j in range(4):
            term = dot_nt(group[j][at, :], w[:, j * width : (j + 1) * width])
            dm = term if dm is None else dm + term
        act, slope = gelu_pair(branch[at, :])
        ev[at, :] = (dm * states[at, :] * slope).astype(BF)
        part[r : r + step, :] = dm * act
    ext[rows : rows + 8, :] = jnp.ones((8, 128), F32)
    for r in range(0, rows, step):
        reach[r : r + step, :] = ext[r + 1 : r + 1 + step, :]
    seg = rows // 8

    def one(n, carry):
        h, p = carry
        at = pl.ds(seg - 1 - n, 8, stride=seg)
        d = reach[at, :]
        h = d * h + part[at, :]
        p = d * p
        part[at, :] = h
        reach[at, :] = p
        return h, p

    zero = jnp.zeros((8, 128), F32)
    h, p = lax.fori_loop(0, seg, one, (zero, zero + 1.0), unroll=8)
    carry_h, carry_p = h[7:8, :], p[7:8, :]
    for s in range(6, -1, -1):
        at = slice(s * seg, (s + 1) * seg)
        c = reach[at, :]
        part[at, :] = part[at, :] + c * carry_h
        reach[at, :] = c * carry_p
        carry_h = h[s : s + 1, :] + p[s : s + 1, :] * carry_h
        carry_p = p[s : s + 1, :] * carry_p
    first = ext[0:1, :]
    ends[0:1, :] = first * carry_p
    ends[1:2, :] = first * carry_h
    ends[2:8, :] = jnp.zeros((6, 128), F32)


def adjoint(errs, w, states, branch, recall, off, soft):
    half, channels = states[0].shape
    rows = 2 * half
    width = errs[0][0].shape[1]
    return pl.pallas_call(
        adjoint_body,
        grid=(channels // 128,),
        in_specs=[whole_spec((half, width))] * 8
        + [pl.BlockSpec((128, w.shape[1]), lambda h: (h, 0))]
        + [head_spec(half)] * 4
        + [head_spec(rows), whole_spec(off.shape), head_spec(1)],
        out_specs=[head_spec(rows)] * 2
        + [head_spec(half)] * 2
        + [head_spec(8)]
        + [whole_spec((rows, 2 * width))] * 2,
        out_shape=[sds((rows, channels), F32)] * 2
        + [sds((half, channels), BF)] * 2
        + [sds((8, channels), F32)]
        + [sds((rows, 2 * width), BF)] * 2,
        scratch_shapes=[pltpu.VMEM((rows + 8, 128), F32)],
        compiler_params=params(),
        cost_estimate=cost(2 * rows * w.size, rows * channels * 20 + rows * D * 6, rows * channels * 3),
        name="adjoint",
    )(*errs[0], *errs[1], w, *states, *branch, recall, off, soft)


def recur_back_body(count, *refs):
    (part, reach, later, earlier, sa, sb, conv, recall, admit, off) = refs[:10]
    (ua, ub, border, taps, recall_w, admit_w, soft) = refs[10:17]
    (du, out_border, grad_recall, grad_admit, grad_small, st, uext, dc) = refs[17:]
    half = sa.shape[0]
    rows = 2 * half
    step = ROW_BLOCK
    st[0:8, :] = jnp.broadcast_to(chain(earlier, count), (8, 128))
    st[8 : 8 + half, :] = sa[...]
    st[8 + half : 8 + rows, :] = sb[...]
    uext[0:8, :] = border[...]
    uext[8 : 8 + half, :] = ua[...]
    uext[8 + half : 8 + rows, :] = ub[...]
    incoming = chain(later, count)
    sp = soft[0:1, :]
    dc[0:8, :] = jnp.zeros((8, 128), F32)
    dc[8 + rows : 16 + rows, :] = jnp.zeros((8, 128), F32)
    gr = ga = None
    sums = [None] * (KW + 1)

    def plus(total, term):
        return term if total is None else total + term

    for r in range(0, rows, step):
        at = slice(r, r + step)
        o = off[8 + r : 8 + r + step, :]
        adj = part[at, :] + reach[at, :] * incoming
        rec, adm, cv = recall[at, :], admit[at, :], conv[at, :]
        ell = -8.0 * rec * sp
        e = jnp.exp(ell)
        m = jnp.sqrt(minus_expm1(2.0 * ell))
        previous = jnp.where(o > 0, e * st[7 + r : 7 + r + step, :], 0.0)
        ac = adj * cv
        d_ell = adj * previous - ac * adm * (e * e) / m
        d_rp = -8.0 * sp * d_ell * rec * (1.0 - rec)
        d_ip = ac * m * adm * (1.0 - adm)
        d_conv = (
            adj * m * adm + dot_nt(d_rp, recall_w[0], PRECISE) + dot_nt(d_ip, admit_w[0], PRECISE)
        )
        dc[8 + r : 8 + r + step, :] = d_conv
        gr = plus(gr, dot_tn(cv, d_rp, PRECISE))
        ga = plus(ga, dot_tn(cv, d_ip, PRECISE))
        for k in range(KW):
            term = d_conv * uext[8 + r - k : 8 + r - k + step, :]
            if k:
                term = jnp.where(o >= k, term, 0.0)
            sums[k] = plus(sums[k], jnp.sum(term, axis=0, keepdims=True))
        sums[KW] = plus(sums[KW], jnp.sum(rec * d_ell, axis=0, keepdims=True))
    grad_recall[0] = gr
    grad_admit[0] = ga
    for k in range(KW + 1):
        grad_small[k : k + 1, :] = sums[k]
    grad_small[KW + 1 : 8, :] = jnp.zeros((7 - KW, 128), F32)
    for r in range(0, rows, step):
        total = taps[0:1, :] * dc[8 + r : 8 + r + step, :]
        for k in range(1, KW):
            o = off[8 + r + k : 8 + r + k + step, :]
            term = taps[k : k + 1, :] * dc[8 + r + k : 8 + r + k + step, :]
            total = total + jnp.where(o >= k, term, 0.0)
        du[r : r + step, :] = total
    total = jnp.zeros((8, 128), F32)
    for k in range(1, KW):
        term = taps[k : k + 1, :] * dc[k : k + 8, :]
        total = total + jnp.where(off[k : k + 8, :] >= k, term, 0.0)
    out_border[...] = total


def recur_back(part, reach, later, earlier, states, conv, recall, admit, off, u, border, taps, rw, aw, soft):
    rows, channels = part.shape
    half = rows // 2
    heads = channels // 128
    gate = pl.BlockSpec((1, 128, 128), lambda h: (h, 0, 0))
    return pl.pallas_call(
        functools.partial(recur_back_body, later.shape[0] // 8),
        grid=(heads,),
        in_specs=[
            head_spec(rows),
            head_spec(rows),
            head_spec(later.shape[0]),
            head_spec(earlier.shape[0]),
            head_spec(half),
            head_spec(half),
            head_spec(rows),
            head_spec(rows),
            head_spec(rows),
            whole_spec(off.shape),
            head_spec(half),
            head_spec(half),
            head_spec(8),
            head_spec(KW),
            gate,
            gate,
            head_spec(1),
        ],
        out_specs=[head_spec(rows), head_spec(8), gate, gate, head_spec(8)],
        out_shape=[
            sds((rows, channels), F32),
            sds((8, channels), F32),
            sds((heads, 128, 128), F32),
            sds((heads, 128, 128), F32),
            sds((8, channels), F32),
        ],
        scratch_shapes=[
            pltpu.VMEM((rows + 8, 128), F32),
            pltpu.VMEM((rows + 8, 128), F32),
            pltpu.VMEM((rows + 16, 128), F32),
        ],
        compiler_params=params(),
        cost_estimate=cost(rows * channels * 128 * 48, rows * channels * 36, rows * channels * 4),
        name="recur_back",
    )(part, reach, later, earlier, *states, conv, recall, admit, off, *u, border, taps, rw, aw, soft)


def enter_back_body(last, du, tail, ev, u, v, w, eu, dots, q0, q1, q2, q3):
    d = du[...]
    if last:
        rows = d.shape[0]
        extra = jnp.concatenate([jnp.zeros((rows - 8, d.shape[1]), F32), tail[...]], axis=0)
        at_end = pl.program_id(0) == pl.num_programs(0) - 1
        d = d + jnp.where(at_end, extra, 0.0)
    e = d.astype(BF)
    eu[...] = e
    b = ev[...]
    dots[...] = jnp.sum(e.astype(F32) * u[...] + b.astype(F32) * v[...], axis=1, keepdims=True)
    channels = e.shape[1]
    width = q0.shape[1]
    for j, q in enumerate((q0, q1, q2, q3)):
        q[...] = (
            dot_nt(e, w[j * width : (j + 1) * width, :channels])
            + dot_nt(b, w[j * width : (j + 1) * width, channels:])
        ).astype(q.dtype)


def enter_back(half_index, du, tail, ev, u, v, w):
    rows, channels = u.shape
    width = w.shape[0] // 4
    block = ROW_BLOCK
    start = half_index * (rows // block)
    return pl.pallas_call(
        functools.partial(enter_back_body, half_index == 1),
        grid=(rows // block,),
        in_specs=[rows_spec(block, channels, start), whole_spec(tail.shape)]
        + [rows_spec(block, channels)] * 3
        + [whole_spec(w.shape)],
        out_specs=[rows_spec(block, channels), rows_spec(block, 1)] + [rows_spec(block, width)] * 4,
        out_shape=[sds((rows, channels), BF), sds((rows, 1), F32), sds((rows, width), F32)]
        + [sds((rows, width), BF)] * 3,
        compiler_params=params(),
        cost_estimate=cost(2 * rows * w.size, rows * channels * 16 + nbytes(w)),
        name="enter_back",
    )(du, tail, ev, u, v, w)


def outer_body(la, lb, ra, rb, out):
    out[...] = (dot_tn(la[...], ra[...]) + dot_tn(lb[...], rb[...])).astype(out.dtype)


def outer(left, right):
    rows, m = left[0].shape
    n = right[0].shape[1]
    block = 256 if m % 256 == 0 else 128
    lhs = pl.BlockSpec((rows, block), lambda i: (0, i))
    return pl.pallas_call(
        outer_body,
        grid=(m // block,),
        in_specs=[lhs, lhs, whole_spec((rows, n)), whole_spec((rows, n))],
        out_specs=rows_spec(block, n),
        out_shape=sds((m, n), BF),
        compiler_params=params(),
        cost_estimate=cost(4 * rows * m * n, rows * (m + n) * 4 + m * n * 2),
        name="outer",
    )(*left, *right)


def add_low(a, b):
    return (a.astype(F32) + b.astype(F32)).astype(BF)


def total_seq(g):
    count = lax.axis_size("seq")
    if count != 4:
        return lax.psum(g, "seq")
    place = lax.axis_index("seq")
    g = add_low(g, lax.ppermute(g, "seq", [(0, 1), (3, 2)]))
    g = add_low(g, lax.ppermute(g, "seq", [(1, 2), (2, 1)]))
    back = lax.ppermute(g, "seq", [(1, 0), (2, 3)])
    return jnp.where((place == 0) | (place == 3), back, g)


def local_fast(
    stream_in,
    cotangent,
    doc_lengths,
    mixer_gain,
    input_weight,
    branch_weight,
    filter_taps,
    recall_gate,
    admit_gate,
    decay_param,
    output_weight,
    feed_gain,
    gate_weight,
    up_weight,
    down_weight,
):
    tokens = stream_in.shape[1]
    half = tokens // 2
    count = lax.axis_size("seq")
    part = stream_in.shape[2]
    seq = lax.axis_index("seq")
    row = lax.axis_index("row")
    col = lax.axis_index("col")
    y, core = col // 2, col % 2
    lower = row == 0

    def own_and_other(a, pick, axis):
        size = a.shape[axis] // 2
        return (
            lax.dynamic_slice_in_dim(a, pick * size, size, axis),
            lax.dynamic_slice_in_dim(a, (1 - pick) * size, size, axis),
        )

    def by_core(a):
        own, other = own_and_other(a, core, 0)
        return jnp.concatenate([own[0], flip_core(other)[0]], axis=1)

    def in_halves(a):
        return (a[:half], a[half:])

    gains = jnp.stack([mixer_gain, feed_gain])
    gains = jnp.concatenate([gains, flip_core(gains)], axis=1)
    gains_x = flip_row(gains)
    gains_y = flip_y(gains)
    gains_all = jnp.concatenate([gains, gains_x, gains_y, flip_y(gains_x)], axis=1)

    x = by_core(stream_in)
    g = by_core(cotangent)

    def four_blocks(w, axis):
        own, other = own_and_other(w, y, axis)
        far = flip_y(other)
        return ((own, flip_core(own)), (far, flip_core(far)))

    def rows_in_order(ws):
        blocks = [four_blocks(w, 1) for w in ws]
        pieces = []
        for dy in (0, 1):
            for dx in (0, 1):
                for dc in (0, 1):
                    start = part * (row ^ dx)
                    pieces.append(
                        jnp.concatenate(
                            [lax.dynamic_slice_in_dim(b[dy][dc], start, part, 0) for b in blocks], axis=1
                        )
                    )
        return jnp.concatenate(pieces, axis=0)

    def cols_in_order(w):
        blocks = four_blocks(w, 0)
        chunks = []
        for dy in (0, 1):
            near, far = blocks[dy]
            first = jnp.concatenate([near[:, :part], far[:, :part]], axis=1)
            second = jnp.concatenate([near[:, part:], far[:, part:]], axis=1)
            chunks += [jnp.where(lower, first, second), jnp.where(lower, second, first)]
        return jnp.concatenate(chunks, axis=1)

    w_in = rows_in_order((input_weight, branch_weight))
    w_out = cols_in_order(output_weight)
    w_gu = rows_in_order((gate_weight, up_weight))
    w_down = cols_in_order(down_weight)

    heads = recall_gate.shape[0] // 2
    rw = lax.dynamic_slice_in_dim(recall_gate, y * heads, heads, 0)
    aw = lax.dynamic_slice_in_dim(admit_gate, y * heads, heads, 0)
    small = jnp.concatenate([filter_taps, decay_param[None], jnp.zeros((3,) + decay_param.shape, F32)])
    sibling = flip_core(small)
    small = jnp.where(
        core == 0,
        jnp.concatenate([small, sibling], axis=1),
        jnp.concatenate([sibling, small], axis=1),
    )
    taps, decay = small[:KW], small[KW : KW + 1]
    soft = jax.nn.softplus(-decay)

    lengths = lax.dynamic_index_in_dim(doc_lengths, core, 0, False)
    offset = doc_offset(lengths, seq * tokens, tokens)
    edge = jnp.full((8,), -1, jnp.int32)
    off = jnp.concatenate([edge, offset, edge])[:, None]

    def neighbours(ends, sign):
        return jnp.concatenate([shifted(ends, sign * n) for n in range(1, count)], axis=0)

    ca, cb = spread(in_halves(x.astype(BF)))
    nka, nsa, ua, va, s1a = norm_uv(ca, gains_all, w_in)
    nkb, nsb, ub, vb, s1b = norm_uv(cb, gains_all, w_in)
    border = shifted(ub[half - 8 :], 1)
    conv, recall, admit, local_state, cum, ends = recur(ua, ub, border, off, taps, rw, aw, soft)
    earlier = neighbours(ends, 1)
    sa, ma, *qa = mix(0, local_state, cum, va, earlier, w_out)
    sb, mb, *qb = mix(1, local_state, cum, vb, earlier, w_out)
    mid = [r + h for r, h in zip(collect((qa, qb)), in_halves(x))]
    da, db = spread([m.astype(BF) for m in mid])
    fa, fb = spread(in_halves(g.astype(BF)))
    feed_a = feed(da, fa, gains_all, w_gu, w_down)
    feed_b = feed(db, fb, gains_all, w_gu, w_down)
    out_chunk = jnp.concatenate(
        [r + m for r, m in zip(collect((feed_a[9:13], feed_b[9:13])), mid)], axis=0
    )

    def summed(dots):
        d = jnp.concatenate([a[:, 0] for a in dots])
        d = d + flip_row(d)
        d = d + flip_y(d)
        return in_halves(d)

    def norm_back_local(dn, dots, scales, source, gain):
        grads, gain_grad = [], 0.0
        for d, t, s, x_half in zip(dn, dots, scales, source):
            grads.append(s * gain * d - x_half * (s * s * t[:, None] / D))
            gain_grad = gain_grad + jnp.sum(d * x_half * s, axis=0)
        return grads, gain_grad

    dots2 = summed((feed_a[8], feed_b[8]))
    dn2 = collect((feed_a[13:17], feed_b[13:17]))
    back2, grad_feed = norm_back_local(dn2, dots2, (feed_a[7], feed_b[7]), mid, gains[1:2])
    dx2 = [b + h for b, h in zip(back2, in_halves(g))]
    ra, rb = spread([d.astype(BF) for d in dx2])

    part_adj, reach, eva, evb, back_ends, erk, ers = adjoint(
        (ra, rb), w_out, (sa, sb), (va, vb), recall, off, soft
    )
    later = neighbours(back_ends, -1)
    du, out_border, grad_recall, grad_admit, grad_small = recur_back(
        part_adj, reach, later, earlier, (sa, sb), conv, recall, admit, off, (ua, ub), border, taps, rw, aw, soft
    )
    tail = shifted(out_border, -1)
    eua, dots_a, *ba = enter_back(0, du, tail, eva, ua, va, w_in)
    eub, dots_b, *bb = enter_back(1, du, tail, evb, ub, vb, w_in)
    dots1 = summed((dots_a, dots_b))
    dn1 = collect((ba, bb))
    back1, grad_mixer = norm_back_local(dn1, dots1, (s1a, s1b), in_halves(x), gains[0:1])
    grad_chunk = jnp.concatenate([b + d for b, d in zip(back1, dx2)], axis=0)

    def reduced(keep, send, axis):
        both = add_low(keep, flip_core(send))
        n = both.shape[axis] // 2
        mine = lax.slice_in_dim(both, 0, n, axis=axis)
        theirs = flip_y(lax.slice_in_dim(both, n, 2 * n, axis=axis))
        return total_seq(mine), total_seq(theirs)

    def rows_out(keep, send):
        mine, theirs = reduced(keep, send, 0)
        wide = jnp.where(
            y == 0, jnp.concatenate([mine, theirs], axis=1), jnp.concatenate([theirs, mine], axis=1)
        )
        swapped = jnp.concatenate([wide[part:], wide[:part]], axis=0)
        return jnp.where(lower, wide, swapped).astype(F32)

    def cols_out(keep, send):
        mine, theirs = reduced(keep, send, 1)
        tall = jnp.where(
            y == 0, jnp.concatenate([mine, theirs], axis=0), jnp.concatenate([theirs, mine], axis=0)
        )
        swapped = jnp.concatenate([tall[:, part:], tall[:, :part]], axis=1)
        return jnp.where(lower, tall, swapped).astype(F32)

    n2k, n2s = (feed_a[0], feed_b[0]), (feed_a[1], feed_b[1])
    hid = (feed_a[2], feed_b[2])
    eg, eu2 = (feed_a[3], feed_b[3]), (feed_a[4], feed_b[4])
    eok, eos = (feed_a[5], feed_b[5]), (feed_a[6], feed_b[6])
    grad_down = cols_out(outer(hid, eok), outer(hid, eos))
    grad_gate = rows_out(outer(n2k, eg), outer(n2s, eg))
    grad_up = rows_out(outer(n2k, eu2), outer(n2s, eu2))
    grad_output = cols_out(
        outer((ma, mb), in_halves(erk)), outer((ma, mb), in_halves(ers))
    )
    grad_input = rows_out(outer((nka, nkb), (eua, eub)), outer((nsa, nsb), (eua, eub)))
    grad_branch = rows_out(outer((nka, nkb), (eva, evb)), outer((nsa, nsb), (eva, evb)))

    width = recall_gate.shape[2] * heads
    gain_rows = jnp.concatenate(
        [grad_mixer[:part], grad_feed[:part], grad_mixer[part:], grad_feed[part:]]
    )
    channels = taps.shape[1]
    lane = 128
    pieces = [
        grad_small[:KW].reshape(-1),
        (grad_small[KW] * 8.0 * jax.nn.sigmoid(-decay[0])),
        grad_recall.reshape(-1),
        grad_admit.reshape(-1),
    ]
    flat = jnp.concatenate(pieces)
    flat = flat + flip_core(flat)
    mine_gain = gain_rows[: 2 * part] + flip_core(gain_rows[2 * part :])
    flat = jnp.concatenate([flat, mine_gain])
    flat = lax.psum(flat, "seq")
    sizes = [KW * channels, channels, grad_recall.size, grad_admit.size, part, part]
    cuts, at = [], 0
    for s in sizes:
        cuts.append(flat[at : at + s])
        at += s
    own = channels // 2
    g_taps = lax.dynamic_slice_in_dim(cuts[0].reshape(KW, channels), core * own, own, 1)
    g_decay = lax.dynamic_slice_in_dim(cuts[1], core * own, own, 0)
    gates = jnp.stack([cuts[2].reshape(grad_recall.shape), cuts[3].reshape(grad_admit.shape)])
    far = flip_y(gates)
    gates = jnp.where(
        y == 0, jnp.concatenate([gates, far], axis=1), jnp.concatenate([far, gates], axis=1)
    )

    def stacked(chunk):
        own, other = chunk[:, :part], flip_core(chunk[:, part:])
        return jnp.where(core == 0, jnp.stack([own, other]), jnp.stack([other, own]))

    return (
        stacked(out_chunk),
        stacked(grad_chunk),
        cuts[4],
        grad_input,
        grad_branch,
        g_taps,
        gates[0],
        gates[1],
        g_decay,
        grad_output,
        cuts[5],
        grad_gate,
        grad_up,
        grad_down,
    )


def solution(mesh):
    in_specs = (
        P(None, "seq", ("col", "row")),
        P(None, "seq", ("col", "row")),
        P(),
        P(("col", "row")),
        P("col", "row"),
        P("col", "row"),
        P(None, ("row", "col")),
        P("row", None, None),
        P("row", None, None),
        P(("row", "col")),
        P("row", "col"),
        P(("col", "row")),
        P("col", "row"),
        P("col", "row"),
        P("row", "col"),
    )
    out_specs = (
        P(None, "seq", ("col", "row")),
        P(None, "seq", ("col", "row")),
        P(("col", "row")),
        P("col", "row"),
        P("col", "row"),
        P(None, ("row", "col")),
        P("row", None, None),
        P("row", None, None),
        P(("row", "col")),
        P("row", "col"),
        P(("col", "row")),
        P("col", "row"),
        P("col", "row"),
        P("row", "col"),
    )
    plan = local_fast if mesh.shape["row"] == 2 and mesh.shape["col"] == 4 else local
    return jax.shard_map(plan, mesh=mesh, in_specs=in_specs, out_specs=out_specs, check_vma=False)
```

```python
import functools

import jax
import jax.numpy as jnp
from jax import lax
from jax.experimental import pallas as pl
from jax.experimental.pallas import tpu as pltpu
from jax.sharding import PartitionSpec as P

D = 1536
KW = 4


EPSILON = 1e-06
PRECISE = lax.Precision.HIGHEST
SUM_ROWS = (((0,), (0,)), ((), ()))
SUM_COLS = (((1,), (1,)), ((), ()))


def as_sent(value):
    return jax.tree.map(lambda a: a.astype(jnp.bfloat16) if a.dtype == jnp.float32 else a, value)


def passed_along(block, axis, distance):
    devices = range(lax.axis_size(axis))
    route = [(i - distance, i) for i in devices if i - distance in devices]
    return lax.ppermute(block, axis, route)


def entering_2(part, axis, combine, identity, reverse):
    count = lax.axis_size(axis)
    place = lax.axis_index(axis)
    ahead = count - 1 - place if reverse else place
    gathered = jax.tree.map(lambda a: lax.all_gather(a, axis), part)
    state = jax.tree.map(lambda a, e: jnp.zeros_like(a) + jnp.asarray(e, a.dtype), part, identity)

    def one(hop, state):
        source = count - 1 - hop if reverse else hop
        return combine(
            state, jax.tree.map(lambda a: lax.dynamic_index_in_dim(a, source, 0, False), gathered)
        )

    return lax.fori_loop(0, ahead, one, state)


def compose(first, second):
    return (first[0] * second[0], second[0] * first[1] + second[1])


def convolve(source, taps, offset, border):
    tokens = source.shape[0]
    extended = jnp.concatenate([border, source], axis=0)
    result = jnp.zeros_like(source)
    for lag_index in range(KW):
        anchor = KW - 1 - lag_index
        valid = (offset >= lag_index).astype(jnp.float32)[:, None]
        result = result + taps[lag_index] * extended[anchor : anchor + tokens] * valid
    return result


def slab_pre(conv_value, recall_value, admit_value):
    tokens = conv_value.shape[0]
    blocks = conv_value.reshape(tokens, recall_value.shape[0], recall_value.shape[1])
    recall_pre = jnp.einsum("thi,hij->thj", blocks, recall_value, precision=PRECISE).reshape(
        tokens, -1
    )
    admit_pre = jnp.einsum("thi,hij->thj", blocks, admit_value, precision=PRECISE).reshape(
        tokens, -1
    )
    return (recall_pre, admit_pre)


def own_terms(conv_value, recall_pre, admit_pre, decay_value, resume):
    recall = jax.nn.sigmoid(recall_pre)
    admit = jax.nn.sigmoid(admit_pre)
    log_decay = -8.0 * recall * jax.nn.softplus(-decay_value)
    decays = jnp.exp(log_decay) * resume[:, None]
    drives = jnp.sqrt(-jnp.expm1(2.0 * log_decay)) * admit * conv_value
    return (decays, drives)


def width_total(partial_value):
    return lax.psum(partial_value, ("row", "col"))


def gather_row(source):
    return lax.all_gather(source, "row", axis=1, tiled=True)


def gather_col(source):
    return jax.tree.map(
        lambda part, own: part.astype(own.dtype),
        lax.all_gather(as_sent(source), "col", axis=1, tiled=True),
        source,
    )


def scatter_col(source):
    return (
        lax.psum_scatter(source[0], "col", scatter_dimension=1, tiled=True),
        lax.psum_scatter(source[1], "col", scatter_dimension=1, tiled=True),
    )


def scatter_col_back(source):
    return lax.psum_scatter(source, "col", scatter_dimension=1, tiled=True)


def scatter_row(source):
    return lax.psum_scatter(source, "row", scatter_dimension=1, tiled=True)


def over_seq(grads):
    return (
        lax.psum(grads[0].astype(jnp.bfloat16), "seq").astype(jnp.float32),
        lax.psum(grads[1].astype(jnp.bfloat16), "seq").astype(jnp.float32),
        lax.psum(grads[2].astype(jnp.bfloat16), "seq").astype(jnp.float32),
        lax.psum(grads[3].astype(jnp.bfloat16), "seq").astype(jnp.float32),
        lax.psum(grads[4].astype(jnp.bfloat16), "seq").astype(jnp.float32),
        lax.psum(grads[5].astype(jnp.bfloat16), "seq").astype(jnp.float32),
        lax.psum(grads[6].astype(jnp.bfloat16), "seq").astype(jnp.float32),
        lax.psum(grads[7].astype(jnp.bfloat16), "seq").astype(jnp.float32),
        lax.psum(grads[8].astype(jnp.bfloat16), "seq").astype(jnp.float32),
        lax.psum(grads[9].astype(jnp.bfloat16), "seq").astype(jnp.float32),
        lax.psum(grads[10].astype(jnp.bfloat16), "seq").astype(jnp.float32),
        lax.psum(grads[11].astype(jnp.bfloat16), "seq").astype(jnp.float32),
    )


def normalize(source, scales):
    factor = lax.rsqrt(width_total(jnp.sum(source * source, axis=1)) / D + EPSILON)
    return (source * factor[:, None] * scales, factor)


def norm_back(source, scales, factor, grad_norm):
    weighted = scales * grad_norm
    summed = width_total(jnp.sum(weighted * source, axis=1))
    grad_source = (
        factor[:, None] * weighted - source * (factor * factor * factor * summed / D)[:, None]
    )
    grad_scales = jnp.sum(grad_norm * source * factor[:, None], axis=0)
    return (grad_source, grad_scales)


def doc_offset(lengths, anchor, tokens):
    starts = jnp.cumsum(lengths, dtype=jnp.int32) - lengths
    places = anchor + jnp.arange(tokens, dtype=jnp.int32)
    begins = jnp.max(jnp.where(starts[None, :] <= places[:, None], starts[None, :], 0), axis=1)
    return places - begins


def matmul_rows(left, right):
    return lax.dot_general(left, right, SUM_ROWS, preferred_element_type=jnp.float32)


def matmul_cols(left, right):
    return lax.dot_general(left, right, SUM_COLS, preferred_element_type=jnp.float32)


def local(
    stream_in,
    cotangent,
    doc_lengths,
    mixer_gain,
    input_weight,
    branch_weight,
    filter_taps,
    recall_gate,
    admit_gate,
    decay_param,
    output_weight,
    feed_gain,
    gate_weight,
    up_weight,
    down_weight,
):
    tokens = stream_in.shape[1]
    anchor = lax.axis_index("seq") * tokens
    channels = decay_param.shape[0]
    col_start = lax.axis_index("col") * channels
    params = (
        mixer_gain,
        input_weight,
        branch_weight,
        filter_taps,
        recall_gate,
        admit_gate,
        decay_param,
        output_weight,
        feed_gain,
        gate_weight,
        up_weight,
        down_weight,
    )
    totals = tuple((jnp.zeros(w.shape, jnp.float32) for w in params))
    identity = (jnp.ones_like(decay_param), jnp.zeros_like(decay_param))
    outputs = []
    grads_in = []
    for micro in range(stream_in.shape[0]):
        offset = doc_offset(doc_lengths[micro], anchor, tokens)
        resume = (offset > 0).astype(jnp.float32)
        source = stream_in[micro]
        normed, factor_one = normalize(source, mixer_gain)
        normed_low = normed.astype(jnp.bfloat16)
        normed_all = gather_row(normed_low)
        rec_in, branch = scatter_col(
            (
                jnp.dot(normed_all, input_weight, preferred_element_type=jnp.float32),
                jnp.dot(normed_all, branch_weight, preferred_element_type=jnp.float32),
            )
        )
        border = passed_along(rec_in[tokens - (KW - 1) :], "seq", 1)
        conv_out = convolve(rec_in, filter_taps, offset, border)
        conv_slab = lax.all_gather(conv_out, "col", axis=1, tiled=True)
        slab_values, slab_pull = jax.vjp(slab_pre, conv_slab, recall_gate, admit_gate)
        recall_pre = lax.dynamic_slice_in_dim(slab_values[0], col_start, channels, 1)
        admit_pre = lax.dynamic_slice_in_dim(slab_values[1], col_start, channels, 1)

        def local_gates(conv_value, recall_value, admit_value, decay_value):
            return own_terms(conv_value, recall_value, admit_value, decay_value, resume)

        (decays, drives), gates_pull = jax.vjp(
            local_gates, conv_out, recall_pre, admit_pre, decay_param
        )
        cum_decay, local_state = lax.associative_scan(compose, (decays, drives), axis=0)
        entering = entering_2((cum_decay[-1], local_state[-1]), "seq", compose, identity, False)[1]
        states = local_state + cum_decay * entering
        branch_act = jax.nn.gelu(branch)
        mixed_all = gather_col((states * branch_act).astype(jnp.bfloat16))
        middle = source + scatter_row(
            jnp.dot(mixed_all, output_weight, preferred_element_type=jnp.float32)
        )
        normed_two, factor_two = normalize(middle, feed_gain)
        normed_two_low = normed_two.astype(jnp.bfloat16)
        normed_two_all = gather_row(normed_two_low)
        gate_pre, up_pre = scatter_col(
            (
                jnp.dot(normed_two_all, gate_weight, preferred_element_type=jnp.float32),
                jnp.dot(normed_two_all, up_weight, preferred_element_type=jnp.float32),
            )
        )
        gate_act = jax.nn.gelu(gate_pre)
        hidden_all = gather_col((gate_act * up_pre).astype(jnp.bfloat16))
        outputs.append(
            middle
            + scatter_row(jnp.dot(hidden_all, down_weight, preferred_element_type=jnp.float32))
        )
        upstream = cotangent[micro]
        upstream_all = gather_row(upstream.astype(jnp.bfloat16))
        grad_down = matmul_rows(hidden_all, upstream_all)
        grad_hidden = scatter_col_back(matmul_cols(upstream_all, down_weight))
        gate_value, gelu_pull = jax.vjp(jax.nn.gelu, gate_pre)
        error_gate = gelu_pull(grad_hidden * up_pre)[0].astype(jnp.bfloat16)
        error_up = (grad_hidden * gate_act).astype(jnp.bfloat16)
        gate_err_all, up_err_all = gather_col((error_gate, error_up))
        grad_gate = matmul_rows(normed_two_all, gate_err_all)
        grad_up = matmul_rows(normed_two_all, up_err_all)
        grad_normed_two = scatter_row(
            matmul_cols(gate_err_all, gate_weight) + matmul_cols(up_err_all, up_weight)
        )
        back_middle, grad_feed = norm_back(middle, feed_gain, factor_two, grad_normed_two)
        grad_middle = upstream + back_middle
        rec_err_all = gather_row(grad_middle.astype(jnp.bfloat16))
        grad_output = matmul_rows(mixed_all, rec_err_all)
        grad_mixed = scatter_col_back(matmul_cols(rec_err_all, output_weight))
        branch_value, branch_pull = jax.vjp(jax.nn.gelu, branch)
        error_branch = branch_pull(grad_mixed * states)[0].astype(jnp.bfloat16)
        direct = grad_mixed * branch_act
        ahead = jnp.concatenate([decays[1:], jnp.ones_like(decays[:1])], axis=0)
        reach, partial_adj = lax.associative_scan(compose, (ahead, direct), axis=0, reverse=True)
        incoming = entering_2(
            (decays[0] * reach[0], decays[0] * partial_adj[0]), "seq", compose, identity, True
        )[1]
        adjoint = partial_adj + reach * incoming
        previous = jnp.concatenate([entering[None, :], states[:-1]], axis=0)
        conv_direct, grad_recall_pre, grad_admit_pre, grad_decay = gates_pull(
            (adjoint * previous, adjoint)
        )
        recall_all, admit_all = (
            lax.all_gather(grad_recall_pre.astype(jnp.bfloat16), "col", axis=1, tiled=True).astype(
                grad_recall_pre.dtype
            ),
            lax.all_gather(grad_admit_pre.astype(jnp.bfloat16), "col", axis=1, tiled=True).astype(
                grad_admit_pre.dtype
            ),
        )
        grad_slab, grad_recall, grad_admit = slab_pull((recall_all, admit_all))
        grad_conv_out = conv_direct + lax.dynamic_slice_in_dim(grad_slab, col_start, channels, 1)

        def local_conv(input_value, taps_value, border_value):
            return convolve(input_value, taps_value, offset, border_value)

        conv_value, conv_pull = jax.vjp(local_conv, rec_in, filter_taps, border)
        grad_rec_in, grad_taps, grad_border = conv_pull(grad_conv_out)
        from_next = passed_along(grad_border, "seq", -1)
        grad_rec_in = grad_rec_in + jnp.pad(from_next, ((tokens - (KW - 1), 0), (0, 0)))
        error_input = grad_rec_in.astype(jnp.bfloat16)
        in_err_all, branch_err_all = gather_col((error_input, error_branch))
        grad_input = matmul_rows(normed_all, in_err_all)
        grad_branch = matmul_rows(normed_all, branch_err_all)
        grad_normed = scatter_row(
            matmul_cols(in_err_all, input_weight) + matmul_cols(branch_err_all, branch_weight)
        )
        back_source, grad_mixer = norm_back(source, mixer_gain, factor_one, grad_normed)
        grads_in.append(grad_middle + back_source)
        local_grads = (
            grad_mixer,
            grad_input,
            grad_branch,
            grad_taps,
            grad_recall,
            grad_admit,
            grad_decay,
            grad_output,
            grad_feed,
            grad_gate,
            grad_up,
            grad_down,
        )
        local_grads = over_seq(local_grads)
        totals = tuple((acc + new for acc, new in zip(totals, local_grads)))
    return (jnp.stack(outputs), jnp.stack(grads_in)) + tuple(totals)


BF = jnp.bfloat16
F32 = jnp.float32
VMEM_LIMIT = 56 * 1024 * 1024
ROW_BLOCK = 256
GELU_A = 0.7978845608028654
GELU_B = 0.044715


def flip_row(a):
    return lax.ppermute(a, "row", [(0, 1), (1, 0)])


def flip_y(a):
    return lax.ppermute(a, "col", [(i, i ^ 2) for i in range(4)])


def flip_core(a):
    return lax.ppermute(a, "col", [(i, i ^ 1) for i in range(4)])


def shifted(a, distance):
    return passed_along(a, "seq", distance)


def cost(flops, moved, trans=0):
    return pl.CostEstimate(flops=int(flops), bytes_accessed=int(moved), transcendentals=int(trans))


def params():
    return pltpu.CompilerParams(vmem_limit_bytes=VMEM_LIMIT, dimension_semantics=("arbitrary",))


def nbytes(*arrays):
    return sum(a.size * a.dtype.itemsize for a in arrays)


def spread(halves):
    first, second = halves
    ax, ay = flip_row(first), flip_y(first)
    bx, by = flip_row(second), flip_y(second)
    return ((first, ax, ay, flip_y(ax)), (second, bx, by, flip_row(by)))


def collect(halves):
    (a0, a1, a2, a3), (b0, b1, b2, b3) = halves
    a2 = (a2.astype(F32) + flip_row(a3).astype(F32)).astype(BF)
    b1 = (b1.astype(F32) + flip_y(b3).astype(F32)).astype(BF)
    return (
        a0 + flip_row(a1).astype(F32) + flip_y(a2).astype(F32),
        b0 + flip_row(b1).astype(F32) + flip_y(b2).astype(F32),
    )


def gelu_pair(v):
    t = jnp.tanh(GELU_A * (v + GELU_B * v * v * v))
    value = 0.5 * v * (1.0 + t)
    slope = 0.5 * (1.0 + t) + 0.5 * v * (1.0 - t * t) * GELU_A * (1.0 + 3.0 * GELU_B * v * v)
    return value, slope


def minus_expm1(x):
    series = 1.0 + x * (1.0 / 7.0)
    for n in (6, 5, 4, 3, 2):
        series = 1.0 + x * (1.0 / n) * series
    return jnp.where(x > -0.3, -x * series, 1.0 - jnp.exp(x))


def pair_up(left, right):
    width = left.shape[1]
    lane = lax.broadcasted_iota(jnp.int32, left.shape, 1)
    low = lane < width // 2
    return (
        jnp.where(low, left, pltpu.roll(right, width // 2, 1)),
        jnp.where(low, pltpu.roll(left, width // 2, 1), right),
    )


def dot_nn(a, b, precision=None):
    return lax.dot_general(
        a, b, (((1,), (0,)), ((), ())), precision=precision, preferred_element_type=F32
    )


def dot_nt(a, b, precision=None):
    return lax.dot_general(
        a, b, (((1,), (1,)), ((), ())), precision=precision, preferred_element_type=F32
    )


def dot_tn(a, b, precision=None):
    return lax.dot_general(
        a, b, (((0,), (0,)), ((), ())), precision=precision, preferred_element_type=F32
    )


def rows_spec(block, width, start=0):
    return pl.BlockSpec((block, width), lambda i: (i + start, 0))


def whole_spec(shape):
    rank = len(shape)
    return pl.BlockSpec(shape, lambda i: (0,) * rank, pipeline_mode=pl.Buffered(1))


def head_spec(rows, width=128):
    return pl.BlockSpec((rows, width), lambda h: (0, h))


def sds(shape, dtype):
    return jax.ShapeDtypeStruct(shape, dtype)


MESH_ID = pl.DeviceIdType.MESH


def neighbour_x():
    return {"row": 1 - lax.axis_index("row")}


def neighbour_y():
    return {"col": lax.rem(lax.axis_index("col") + 2, 4)}


def greet():
    barrier = pltpu.get_barrier_semaphore()
    for device in (neighbour_x(), neighbour_y()):
        pl.semaphore_signal(barrier, inc=1, device_id=device, device_id_type=MESH_ID)
    pl.semaphore_wait(barrier, 2)


def message(src, dst, device, sems, n):
    send, recv = sems
    return pltpu.make_async_remote_copy(
        src_ref=src,
        dst_ref=dst,
        send_sem=send.at[n],
        recv_sem=recv.at[n],
        device_id=device,
        device_id_type=MESH_ID,
    )


def scatter_messages(q1, q2, q3, r3, rx, ry, sems, base):
    half = q1.shape[0] // 2
    a, b = pl.ds(0, half), pl.ds(half, half)
    x, y = neighbour_x(), neighbour_y()
    plan = ((q3, r3, a, x), (q3, r3, b, y), (q1, rx, a, x), (q2, ry, a, y), (q2, ry, b, y), (q1, rx, b, x))
    return [
        message(src.at[at, :], dst.at[at, :], dev, sems, base + n)
        for n, (src, dst, at, dev) in enumerate(plan)
    ]


def gather_messages(own, gx, gy, gd, sems, base):
    half = own.shape[0] // 2
    a, b = pl.ds(0, half), pl.ds(half, half)
    x, y = neighbour_x(), neighbour_y()
    plan = ((own, gx, a, x), (own, gy, a, y), (own, gx, b, x), (own, gy, b, y), (gx, gd, a, y), (gy, gd, b, x))
    return [
        message(src.at[at, :], dst.at[at, :], dev, sems, base + n)
        for n, (src, dst, at, dev) in enumerate(plan)
    ]


def add_into(dst, src, start, rows):
    step = 128
    for r in range(start, start + rows, step):
        at = slice(r, r + step)
        dst[at, :] = (dst[at, :].astype(F32) + src[at, :].astype(F32)).astype(dst.dtype)


def load_rows(near, far, dst, sem):
    part = near.shape[1] // 2
    row = lax.axis_index("row")
    copies = []
    for dy in (0, 1):
        for dx in (0, 1):
            start = pl.multiple_of(part * (row + dx - 2 * row * dx), part)
            for dc, src in enumerate((near, far)):
                at = ((dy * 2 + dx) * 2 + dc) * part
                copies.append(
                    pltpu.make_async_copy(
                        src.at[dy, pl.ds(start, part), :], dst.at[pl.ds(at, part), :], sem.at[len(copies)]
                    )
                )
    for c in copies:
        c.start()
    return copies


def comm_params(n):
    return pltpu.CompilerParams(
        vmem_limit_bytes=VMEM_LIMIT,
        dimension_semantics=("arbitrary",),
        collective_id=n,
        has_side_effects=True,
    )


def any_spec():
    return pl.BlockSpec(memory_space=pl.ANY)


def held_spec(block, width, last):
    return pl.BlockSpec((block, width), lambda i: (jnp.minimum(i, last), 0))


def full_spec(shape):
    rank = len(shape)
    return pl.BlockSpec(shape, lambda i: (0,) * rank)


def row_sums(values):
    return dot_nt(jnp.ones((8, values.shape[1]), F32), values, PRECISE)


def as_column(lanes, width):
    first = (lax.broadcasted_iota(jnp.int32, (8, width), 0) == 0).astype(F32)
    return dot_tn(lanes, first, PRECISE)


def norm_uv_body(blocks, own, gain, near, far, n1, u, v, scale, w, gx, gy, gd, load, send, recv):
    i = pl.program_id(0)
    gather = gather_messages(own, gx, gy, gd, (send, recv), 0)

    @pl.when(i == 0)
    def _():
        greet()
        for n in range(4):
            gather[n].start()
        copies = load_rows(near, far, w, load)
        gather[0].wait_recv()
        gather[4].start()
        gather[3].wait_recv()
        gather[5].start()
        for c in copies:
            c.wait()
        gather[1].wait_recv()
        gather[4].wait_recv()

    @pl.when(i == blocks // 2)
    def _():
        gather[2].wait_recv()
        gather[5].wait_recv()
        for m in gather:
            m.wait_send()

    block = u.shape[0]
    at = pl.ds(pl.multiple_of(i * block, block), block)
    parts = [r[at, :].astype(F32) for r in (own, gx, gy, gd)]
    width = parts[0].shape[1]
    total = sum(jnp.sum(p * p, axis=1, keepdims=True) for p in parts)
    s = lax.rsqrt(total / D + EPSILON)
    scale[...] = s
    normed = [p * s * gain[0:1, j * width : (j + 1) * width] for j, p in enumerate(parts)]
    acc = None
    for j, n in enumerate(normed):
        term = dot_nn(n.astype(BF), w[j * width : (j + 1) * width, :])
        acc = term if acc is None else acc + term
    channels = u.shape[1]
    u[...] = acc[:, :channels]
    v[...] = acc[:, channels:]
    for j in (0, 1):
        k, p = pair_up(normed[2 * j], normed[2 * j + 1])
        n1[:, j * width : (j + 1) * width] = k.astype(BF)
        n1[:, (j + 2) * width : (j + 3) * width] = p.astype(BF)


def norm_uv(own, gain, near, far):
    rows, width = own.shape
    w = pltpu.VMEM((4 * width, near.shape[2]), BF)
    channels = near.shape[2] // 2
    block = ROW_BLOCK
    blocks = rows // block
    return pl.pallas_call(
        functools.partial(norm_uv_body, blocks),
        grid=(blocks,),
        in_specs=[whole_spec(own.shape), whole_spec(gain.shape), any_spec(), any_spec()],
        out_specs=[rows_spec(block, 4 * width)] + [rows_spec(block, channels)] * 2 + [rows_spec(block, 1)],
        out_shape=[sds((rows, 4 * width), BF)] + [sds((rows, channels), F32)] * 2 + [sds((rows, 1), F32)],
        scratch_shapes=[w]
        + [pltpu.VMEM((rows, width), BF)] * 3
        + [pltpu.SemaphoreType.DMA((8,))]
        + [pltpu.SemaphoreType.DMA((6,))] * 2,
        compiler_params=comm_params(1),
        cost_estimate=cost(60 * rows * near.size, nbytes(near, far)),
        name="norm_uv",
    )(own, gain, near, far)


def chain(entries, count):
    state = entries[(count - 1) * 8 + 1 : (count - 1) * 8 + 2, :]
    for n in range(count - 2, -1, -1):
        state = entries[n * 8 + 1 : n * 8 + 2, :] + entries[n * 8 : n * 8 + 1, :] * state
    return state


def recur_body(
    heads, u, border, off, taps, recall_w, admit_w, soft, own, conv, recall, admit, state, cum, ends, gx, gy, gd, ext, send, recv
):
    rows = u.shape[0]
    gather = gather_messages(own, gx, gy, gd, (send, recv), 0)
    h = pl.program_id(0)

    @pl.when(h == 0)
    def _():
        greet()
        for n in range(4):
            gather[n].start()

    @pl.when(h == heads - 1)
    def _():
        gather[0].wait_recv()
        gather[4].start()
        gather[3].wait_recv()
        gather[5].start()

    ext[0:8, :] = border[...]
    ext[8 : 8 + rows, :] = u[...]
    step = ROW_BLOCK
    for r in range(0, rows, step):
        o = off[8 + r : 8 + r + step, :]
        total = taps[0:1, :] * ext[8 + r : 8 + r + step, :]
        for k in range(1, KW):
            term = taps[k : k + 1, :] * ext[8 + r - k : 8 + r - k + step, :]
            total = total + jnp.where(o >= k, term, 0.0)
        conv[r : r + step, :] = total
        rec = jax.nn.sigmoid(dot_nn(total, recall_w[0], PRECISE))
        adm = jax.nn.sigmoid(dot_nn(total, admit_w[0], PRECISE))
        recall[r : r + step, :] = rec
        admit[r : r + step, :] = adm
        ell = -8.0 * rec * soft[0:1, :]
        cum[r : r + step, :] = jnp.where(o > 0, jnp.exp(ell), 0.0)
        state[r : r + step, :] = jnp.sqrt(minus_expm1(2.0 * ell)) * adm * total
    seg = rows // 8

    def one(i, carry):
        h, p = carry
        at = pl.ds(i, 8, stride=seg)
        d = cum[at, :]
        h = d * h + state[at, :]
        p = d * p
        state[at, :] = h
        cum[at, :] = p
        return h, p

    zero = jnp.zeros((8, 128), F32)
    h, p = lax.fori_loop(0, seg, one, (zero, zero + 1.0), unroll=8)
    carry_h, carry_p = h[0:1, :], p[0:1, :]
    for s in range(1, 8):
        at = slice(s * seg, (s + 1) * seg)
        c = cum[at, :]
        state[at, :] = state[at, :] + c * carry_h
        cum[at, :] = c * carry_p
        carry_h = h[s : s + 1, :] + p[s : s + 1, :] * carry_h
        carry_p = p[s : s + 1, :] * carry_p
    ends[0:1, :] = carry_p
    ends[1:2, :] = carry_h
    ends[2:8, :] = jnp.zeros((6, 128), F32)

    @pl.when(pl.program_id(0) == heads - 1)
    def _():
        for n in (1, 2, 4, 5):
            gather[n].wait_recv()
        for m in gather:
            m.wait_send()


def recur(u, border, off, taps, recall_w, admit_w, soft, own):
    rows, channels = u.shape
    heads = channels // 128
    gate = pl.BlockSpec((1, 128, 128), lambda h: (h, 0, 0))
    full = sds((rows, channels), F32)
    return pl.pallas_call(
        functools.partial(recur_body, heads),
        grid=(heads,),
        in_specs=[
            head_spec(rows),
            head_spec(8),
            whole_spec(off.shape),
            head_spec(KW),
            gate,
            gate,
            head_spec(1),
            whole_spec(own.shape),
        ],
        out_specs=[head_spec(rows)] * 5 + [head_spec(8)] + [any_spec()] * 3,
        out_shape=[full] * 5 + [sds((8, channels), F32)] + [sds(own.shape, BF)] * 3,
        scratch_shapes=[pltpu.VMEM((rows + 8, 128), F32)] + [pltpu.SemaphoreType.DMA((6,))] * 2,
        compiler_params=comm_params(5),
        cost_estimate=cost(rows * channels * 128 * 24, rows * channels * 4 * 6, rows * channels * 6),
        name="recur",
    )(u, border, off, taps, recall_w, admit_w, soft, own)


def mix_body(
    count, blocks, local, cum, v, x, entries, w, states, mixed, x2, own, gx, gy, gd, q0, q1, q2, q3, r3, rx, ry, send, recv
):
    i = pl.program_id(0)
    sems = (send, recv)
    scatter = scatter_messages(q1, q2, q3, r3, rx, ry, sems, 0)
    gather = gather_messages(own, gx, gy, gd, sems, 6)
    block = local.shape[0]
    width = x.shape[1]
    rows = x.shape[0]
    half = rows // 2

    @pl.when(i == 0)
    def _():
        greet()

    @pl.when(i < blocks)
    def _():
        entering = chain(entries, count)
        st = local[...] + cum[...] * entering
        states[...] = st
        m = (st * gelu_pair(v[...])[0]).astype(BF)
        mixed[...] = m
        at = pl.ds(pl.multiple_of(i * block, block), block)
        for j, q in ((3, q3), (1, q1), (2, q2), (0, q0)):
            q[at, :] = dot_nn(m, w[:, j * width : (j + 1) * width]).astype(q.dtype)

    @pl.when(i == blocks // 2 - 1)
    def _():
        scatter[0].start()
        scatter[2].start()

    @pl.when(i == blocks - 1)
    def _():
        scatter[1].start()

    @pl.when(i == blocks)
    def _():
        scatter[0].wait_recv()
        add_into(q2, r3, 0, half)
        scatter[3].start()
        scatter[4].start()
        scatter[1].wait_recv()
        add_into(q1, r3, half, half)
        scatter[5].start()
        for base, first in ((0, 2), (half, 4)):
            scatter[first].wait_recv()
            scatter[first + 1].wait_recv()
            for r in range(base, base + half, 128):
                at = slice(r, r + 128)
                total = x[at, :] + q0[at, :] + rx[at, :].astype(F32) + ry[at, :].astype(F32)
                x2[at, :] = total
                own[at, :] = total.astype(BF)
            start = 0 if base == 0 else 2
            gather[start].start()
            gather[start + 1].start()
        gather[0].wait_recv()
        gather[4].start()
        gather[3].wait_recv()
        gather[5].start()
        for n in (1, 2, 4, 5):
            gather[n].wait_recv()
        for m in scatter + gather:
            m.wait_send()


def mix(local, cum, v, x, entries, w):
    rows, channels = v.shape
    width = w.shape[1] // 4
    block = ROW_BLOCK
    blocks = rows // block
    held = functools.partial(held_spec, block, last=blocks - 1)
    chunk = pltpu.VMEM((rows, width), BF)
    return pl.pallas_call(
        functools.partial(mix_body, entries.shape[0] // 8, blocks),
        grid=(blocks + 1,),
        in_specs=[held(channels)] * 3
        + [whole_spec(x.shape), whole_spec(entries.shape), whole_spec(w.shape)],
        out_specs=[held(channels)] * 2 + [full_spec((rows, width))] * 2 + [any_spec()] * 3,
        out_shape=[sds((rows, channels), F32), sds((rows, channels), BF), sds((rows, width), F32)]
        + [sds((rows, width), BF)] * 4,
        scratch_shapes=[pltpu.VMEM((rows, width), F32)]
        + [chunk] * 6
        + [pltpu.SemaphoreType.DMA((12,))] * 2,
        compiler_params=comm_params(2),
        cost_estimate=cost(40 * rows * w.size, rows * channels * 18 + nbytes(w)),
        name="mix",
    )(local, cum, v, x, entries, w)


def feed_body(blocks, *refs):
    (x0, x1, x2, x3, e0, e1, e2, e3, mid, cot, gain, near, far, wd) = refs[:14]
    outs = refs[14:18]
    (dx, own, gx, gy, gd, gain_grad, g_down, g_gu) = refs[18:26]
    (wgu, load, n2, hid, ee, err, scale) = refs[26:33]
    (q0, q1, q2, q3, r3, rx, ry, dots, dots_x, dots_y, send, recv) = refs[33:]
    i = pl.program_id(0)
    sems = (send, recv)
    scatter = scatter_messages(q1, q2, q3, r3, rx, ry, sems, 0)
    gather = gather_messages(own, gx, gy, gd, sems, 6)
    small_x = message(dots, dots_x, neighbour_x(), sems, 12)
    small_y = message(dots_x, dots_y, neighbour_y(), sems, 13)
    block, width = x0.shape
    rows = mid.shape[0]
    half = rows // 2
    units = hid.shape[1]

    @pl.when(i == 0)
    def _():
        copies = load_rows(near, far, wgu, load)
        greet()
        for c in copies:
            c.wait()

    @pl.when(i < blocks)
    def _():
        at = pl.ds(pl.multiple_of(i * block, block), block)
        parts = [r[...].astype(F32) for r in (x0, x1, x2, x3)]
        total = sum(jnp.sum(p * p, axis=1, keepdims=True) for p in parts)
        s = lax.rsqrt(total / D + EPSILON)
        scale[at, :] = s
        normed = [p * s * gain[1:2, j * width : (j + 1) * width] for j, p in enumerate(parts)]
        acc = None
        for j, n in enumerate(normed):
            term = dot_nn(n.astype(BF), wgu[j * width : (j + 1) * width, :])
            acc = term if acc is None else acc + term
        errs = [r[...] for r in (e0, e1, e2, e3)]
        wide = [e.astype(F32) for e in errs]
        for source, target in ((normed, n2), (wide, ee)):
            for j in (0, 1):
                k, p = pair_up(source[2 * j], source[2 * j + 1])
                target[at, j * width : (j + 1) * width] = k.astype(BF)
                target[at, (j + 2) * width : (j + 3) * width] = p.astype(BF)
        pre, up = acc[:, :units], acc[:, units:]
        act, slope = gelu_pair(pre)
        h = (act * up).astype(BF)
        hid[at, :] = h
        dh = None
        for j, e in enumerate(errs):
            term = dot_nt(e, wd[:, j * width : (j + 1) * width])
            dh = term if dh is None else dh + term
        g = (dh * up * slope).astype(BF)
        b = (dh * act).astype(BF)
        err[at, :units] = g
        err[at, units:] = b
        dots[:, at] = row_sums(g.astype(F32) * pre + b.astype(F32) * up)
        for j, q in ((3, q3), (1, q1), (2, q2), (0, q0)):
            rows_w = slice(j * width, (j + 1) * width)
            q[at, :] = (dot_nt(g, wgu[rows_w, :units]) + dot_nt(b, wgu[rows_w, units:])).astype(q.dtype)
        for j, q in enumerate(outs):
            q[...] = dot_nn(h, wd[:, j * width : (j + 1) * width]).astype(q.dtype)

    @pl.when(i == blocks // 2 - 1)
    def _():
        scatter[0].start()
        scatter[2].start()

    @pl.when(i == blocks - 1)
    def _():
        scatter[1].start()
        small_x.start()

    @pl.when(i == blocks)
    def _():
        scatter[0].wait_recv()
        add_into(q2, r3, 0, half)
        scatter[3].start()
        scatter[4].start()
        small_x.wait_recv()
        dots_x[...] = dots_x[...] + dots[...]
        small_y.start()

    @pl.when(i == blocks + 1)
    def _():
        scatter[1].wait_recv()
        add_into(q1, r3, half, half)
        scatter[5].start()

    def finish(base, first, start):
        scatter[first].wait_recv()
        scatter[first + 1].wait_recv()
        sum_grad = None
        for r in range(base, base + half, 128):
            at = slice(r, r + 128)
            d = q0[at, :] + rx[at, :].astype(F32) + ry[at, :].astype(F32)
            s, m = scale[at, :], mid[at, :]
            t = as_column(dots_x[:, at] + dots_y[:, at], width)
            new = cot[at, :] + s * own_gain * d - m * (s * s) * t * (1.0 / D)
            dx[at, :] = new
            own[at, :] = new.astype(BF)
            term = jnp.sum(d * m * s, axis=0, keepdims=True)
            sum_grad = term if sum_grad is None else sum_grad + term
        gather[start].start()
        gather[start + 1].start()
        return sum_grad

    own_gain = gain[1:2, :width]

    @pl.when(i == blocks + 2)
    def _():
        small_y.wait_recv()
        gain_grad[0:1, :] = finish(0, 2, 0)

    @pl.when(i == blocks + 4)
    def _():
        gain_grad[0:1, :] = gain_grad[0:1, :] + finish(half, 4, 2)

    @pl.when(i == blocks + 5)
    def _():
        gather[0].wait_recv()
        gather[4].start()

    @pl.when(i == blocks + 6)
    def _():
        gather[3].wait_recv()
        gather[5].start()

    tiles = units // width

    @pl.when((i >= blocks) & (i < blocks + tiles))
    def _():
        at = pl.ds(pl.multiple_of((i - blocks) * width, width), width)
        g_down[...] = dot_tn(hid[:, at], ee[...]).astype(BF)

    @pl.when((i >= blocks + tiles) & (i < blocks + tiles + 4))
    def _():
        at = pl.ds(pl.multiple_of((i - blocks - tiles) * width, width), width)
        g_gu[...] = dot_tn(n2[:, at], err[...]).astype(BF)

    @pl.when(i == blocks + tiles + 4)
    def _():
        for n in (1, 2, 4, 5):
            gather[n].wait_recv()
        for m in scatter + gather + [small_x, small_y]:
            m.wait_send()


def feed(chunks, errs, mid, cot, gain, near, far, wd):
    rows, width = chunks[0].shape
    units = wd.shape[0]
    block = ROW_BLOCK
    blocks = rows // block
    tiles = units // width
    held = functools.partial(held_spec, block, last=blocks - 1)
    chunk = pltpu.VMEM((rows, width), BF)
    lanes = pltpu.VMEM((8, rows), F32)
    down_spec = pl.BlockSpec((width, 4 * width), lambda i: (jnp.clip(i - blocks, 0, tiles - 1), 0))
    gu_spec = pl.BlockSpec((width, 2 * units), lambda i: (jnp.clip(i - blocks - tiles, 0, 3), 0))
    return pl.pallas_call(
        functools.partial(feed_body, blocks),
        grid=(blocks + tiles + 5,),
        in_specs=[held(width)] * 8
        + [whole_spec(mid.shape), whole_spec(cot.shape), whole_spec(gain.shape)]
        + [any_spec(), any_spec(), whole_spec(wd.shape)],
        out_specs=[held(width)] * 4
        + [whole_spec((rows, width))] * 2
        + [any_spec()] * 3
        + [whole_spec((8, width)), down_spec, gu_spec],
        out_shape=[sds((rows, width), F32)]
        + [sds((rows, width), BF)] * 3
        + [sds((rows, width), F32)]
        + [sds((rows, width), BF)] * 4
        + [sds((8, width), F32), sds((units, 4 * width), BF), sds((4 * width, 2 * units), BF)],
        scratch_shapes=[
            pltpu.VMEM((4 * width, 2 * units), BF),
            pltpu.SemaphoreType.DMA((8,)),
            pltpu.VMEM((rows, 4 * width), BF),
            pltpu.VMEM((rows, units), BF),
            pltpu.VMEM((rows, 4 * width), BF),
            pltpu.VMEM((rows, 2 * units), BF),
            pltpu.VMEM((rows, 1), F32),
            pltpu.VMEM((rows, width), F32),
        ]
        + [chunk] * 6
        + [lanes] * 3
        + [pltpu.SemaphoreType.DMA((14,))] * 2,
        compiler_params=comm_params(3),
        cost_estimate=cost(48 * rows * wd.size, 3 * nbytes(wd) + rows * 30000, rows * units),
        name="feed",
    )(*chunks, *errs, mid, cot, gain, near, far, wd)


def adjoint_body(*refs):
    errs = refs[0:4]
    (w, states, branch, recall, off, soft) = refs[4:10]
    (part, reach, ev, ends, paired, ext) = refs[10:]
    rows = states.shape[0]
    width = errs[0].shape[1]
    step = ROW_BLOCK

    @pl.when(pl.program_id(0) == 0)
    def _():
        for r in range(0, rows, step):
            at = slice(r, r + step)
            for j in (0, 1):
                k, p = pair_up(errs[2 * j][at, :].astype(F32), errs[2 * j + 1][at, :].astype(F32))
                paired[at, j * width : (j + 1) * width] = k.astype(BF)
                paired[at, (j + 2) * width : (j + 3) * width] = p.astype(BF)

    for r in range(0, rows, step):
        o = off[8 + r : 8 + r + step, :]
        ell = -8.0 * recall[r : r + step, :] * soft[0:1, :]
        ext[r : r + step, :] = jnp.where(o > 0, jnp.exp(ell), 0.0)
        at = slice(r, r + step)
        dm = None
        for j in range(4):
            term = dot_nt(errs[j][at, :], w[:, j * width : (j + 1) * width])
            dm = term if dm is None else dm + term
        act, slope = gelu_pair(branch[at, :])
        ev[at, :] = (dm * states[at, :] * slope).astype(BF)
        part[r : r + step, :] = dm * act
    ext[rows : rows + 8, :] = jnp.ones((8, 128), F32)
    for r in range(0, rows, step):
        reach[r : r + step, :] = ext[r + 1 : r + 1 + step, :]
    seg = rows // 8

    def one(n, carry):
        h, p = carry
        at = pl.ds(seg - 1 - n, 8, stride=seg)
        d = reach[at, :]
        h = d * h + part[at, :]
        p = d * p
        part[at, :] = h
        reach[at, :] = p
        return h, p

    zero = jnp.zeros((8, 128), F32)
    h, p = lax.fori_loop(0, seg, one, (zero, zero + 1.0), unroll=8)
    carry_h, carry_p = h[7:8, :], p[7:8, :]
    for s in range(6, -1, -1):
        at = slice(s * seg, (s + 1) * seg)
        c = reach[at, :]
        part[at, :] = part[at, :] + c * carry_h
        reach[at, :] = c * carry_p
        carry_h = h[s : s + 1, :] + p[s : s + 1, :] * carry_h
        carry_p = p[s : s + 1, :] * carry_p
    first = ext[0:1, :]
    ends[0:1, :] = first * carry_p
    ends[1:2, :] = first * carry_h
    ends[2:8, :] = jnp.zeros((6, 128), F32)


def adjoint(errs, w, states, branch, recall, off, soft):
    rows, channels = states.shape
    width = errs[0].shape[1]
    return pl.pallas_call(
        adjoint_body,
        grid=(channels // 128,),
        in_specs=[whole_spec((rows, width))] * 4
        + [pl.BlockSpec((128, w.shape[1]), lambda h: (h, 0))]
        + [head_spec(rows)] * 3
        + [whole_spec(off.shape), head_spec(1)],
        out_specs=[head_spec(rows)] * 3 + [head_spec(8), whole_spec((rows, 4 * width))],
        out_shape=[sds((rows, channels), F32)] * 2
        + [sds((rows, channels), BF), sds((8, channels), F32), sds((rows, 4 * width), BF)],
        scratch_shapes=[pltpu.VMEM((rows + 8, 128), F32)],
        compiler_params=params(),
        cost_estimate=cost(2 * rows * w.size, rows * channels * 20 + rows * D * 6, rows * channels * 3),
        name="adjoint",
    )(*errs, w, states, branch, recall, off, soft)


def recur_back_body(count, *refs):
    (part, reach, later, earlier, states, conv, recall, admit, off) = refs[:9]
    (u, border, taps, recall_w, admit_w, soft) = refs[9:15]
    (du, out_border, grad_recall, grad_admit, grad_small, st, uext, dc) = refs[15:]
    rows = states.shape[0]
    step = ROW_BLOCK
    st[0:8, :] = jnp.broadcast_to(chain(earlier, count), (8, 128))
    st[8 : 8 + rows, :] = states[...]
    uext[0:8, :] = border[...]
    uext[8 : 8 + rows, :] = u[...]
    incoming = chain(later, count)
    sp = soft[0:1, :]
    dc[0:8, :] = jnp.zeros((8, 128), F32)
    dc[8 + rows : 16 + rows, :] = jnp.zeros((8, 128), F32)
    gr = ga = None
    sums = [None] * (KW + 1)

    def plus(total, term):
        return term if total is None else total + term

    for r in range(0, rows, step):
        at = slice(r, r + step)
        o = off[8 + r : 8 + r + step, :]
        adj = part[at, :] + reach[at, :] * incoming
        rec, adm, cv = recall[at, :], admit[at, :], conv[at, :]
        ell = -8.0 * rec * sp
        e = jnp.exp(ell)
        m = jnp.sqrt(minus_expm1(2.0 * ell))
        previous = jnp.where(o > 0, e * st[7 + r : 7 + r + step, :], 0.0)
        ac = adj * cv
        d_ell = adj * previous - ac * adm * (e * e) / m
        d_rp = -8.0 * sp * d_ell * rec * (1.0 - rec)
        d_ip = ac * m * adm * (1.0 - adm)
        d_conv = (
            adj * m * adm + dot_nt(d_rp, recall_w[0], PRECISE) + dot_nt(d_ip, admit_w[0], PRECISE)
        )
        dc[8 + r : 8 + r + step, :] = d_conv
        gr = plus(gr, dot_tn(cv, d_rp, PRECISE))
        ga = plus(ga, dot_tn(cv, d_ip, PRECISE))
        for k in range(KW):
            term = d_conv * uext[8 + r - k : 8 + r - k + step, :]
            if k:
                term = jnp.where(o >= k, term, 0.0)
            sums[k] = plus(sums[k], jnp.sum(term, axis=0, keepdims=True))
        sums[KW] = plus(sums[KW], jnp.sum(rec * d_ell, axis=0, keepdims=True))
    grad_recall[0] = gr
    grad_admit[0] = ga
    for k in range(KW + 1):
        grad_small[k : k + 1, :] = sums[k]
    grad_small[KW + 1 : 8, :] = jnp.zeros((7 - KW, 128), F32)
    for r in range(0, rows, step):
        total = taps[0:1, :] * dc[8 + r : 8 + r + step, :]
        for k in range(1, KW):
            o = off[8 + r + k : 8 + r + k + step, :]
            term = taps[k : k + 1, :] * dc[8 + r + k : 8 + r + k + step, :]
            total = total + jnp.where(o >= k, term, 0.0)
        du[r : r + step, :] = total
    total = jnp.zeros((8, 128), F32)
    for k in range(1, KW):
        term = taps[k : k + 1, :] * dc[k : k + 8, :]
        total = total + jnp.where(off[k : k + 8, :] >= k, term, 0.0)
    out_border[...] = total


def recur_back(part, reach, later, earlier, states, conv, recall, admit, off, u, border, taps, rw, aw, soft):
    rows, channels = part.shape
    heads = channels // 128
    gate = pl.BlockSpec((1, 128, 128), lambda h: (h, 0, 0))
    return pl.pallas_call(
        functools.partial(recur_back_body, later.shape[0] // 8),
        grid=(heads,),
        in_specs=[
            head_spec(rows),
            head_spec(rows),
            head_spec(later.shape[0]),
            head_spec(earlier.shape[0]),
            head_spec(rows),
            head_spec(rows),
            head_spec(rows),
            head_spec(rows),
            whole_spec(off.shape),
            head_spec(rows),
            head_spec(8),
            head_spec(KW),
            gate,
            gate,
            head_spec(1),
        ],
        out_specs=[head_spec(rows), head_spec(8), gate, gate, head_spec(8)],
        out_shape=[
            sds((rows, channels), F32),
            sds((8, channels), F32),
            sds((heads, 128, 128), F32),
            sds((heads, 128, 128), F32),
            sds((8, channels), F32),
        ],
        scratch_shapes=[
            pltpu.VMEM((rows + 8, 128), F32),
            pltpu.VMEM((rows + 8, 128), F32),
            pltpu.VMEM((rows + 16, 128), F32),
        ],
        compiler_params=params(),
        cost_estimate=cost(rows * channels * 128 * 48, rows * channels * 36, rows * channels * 4),
        name="recur_back",
    )(part, reach, later, earlier, states, conv, recall, admit, off, u, border, taps, rw, aw, soft)


def enter_back_body(blocks, *refs):
    (du, tail, ev, u, v, near, far, scale, x, dx, gain) = refs[:11]
    (eu, grad, gain_grad) = refs[11:14]
    (w, load, q0, q1, q2, q3, r3, rx, ry, dots, dots_x, dots_y, send, recv) = refs[14:]
    i = pl.program_id(0)
    sems = (send, recv)
    scatter = scatter_messages(q1, q2, q3, r3, rx, ry, sems, 0)
    small_x = message(dots, dots_x, neighbour_x(), sems, 6)
    small_y = message(dots_x, dots_y, neighbour_y(), sems, 7)
    block, channels = du.shape
    rows, width = x.shape
    half = rows // 2

    @pl.when(i == 0)
    def _():
        copies = load_rows(near, far, w, load)
        greet()
        for c in copies:
            c.wait()

    @pl.when(i < blocks)
    def _():
        at = pl.ds(pl.multiple_of(i * block, block), block)
        d = du[...]
        extra = jnp.concatenate([jnp.zeros((block - 8, channels), F32), tail[...]], axis=0)
        d = d + jnp.where(i == blocks - 1, extra, 0.0)
        e = d.astype(BF)
        eu[...] = e
        b = ev[...]
        dots[:, at] = row_sums(e.astype(F32) * u[...] + b.astype(F32) * v[...])
        for j, q in ((3, q3), (1, q1), (2, q2), (0, q0)):
            rows_w = slice(j * width, (j + 1) * width)
            q[at, :] = (dot_nt(e, w[rows_w, :channels]) + dot_nt(b, w[rows_w, channels:])).astype(q.dtype)

    @pl.when(i == blocks // 2 - 1)
    def _():
        scatter[0].start()
        scatter[2].start()

    @pl.when(i == blocks - 1)
    def _():
        scatter[1].start()
        small_x.start()

    @pl.when(i == blocks)
    def _():
        scatter[0].wait_recv()
        add_into(q2, r3, 0, half)
        scatter[3].start()
        scatter[4].start()
        small_x.wait_recv()
        dots_x[...] = dots_x[...] + dots[...]
        small_y.start()
        scatter[1].wait_recv()
        add_into(q1, r3, half, half)
        scatter[5].start()
        small_y.wait_recv()
        sum_grad = None
        for base, first in ((0, 2), (half, 4)):
            scatter[first].wait_recv()
            scatter[first + 1].wait_recv()
            for r in range(base, base + half, 128):
                at = slice(r, r + 128)
                d = q0[at, :] + rx[at, :].astype(F32) + ry[at, :].astype(F32)
                s, m = scale[at, :], x[at, :]
                t = as_column(dots_x[:, at] + dots_y[:, at], width)
                grad[at, :] = dx[at, :] + s * gain[0:1, :width] * d - m * (s * s) * t * (1.0 / D)
                term = jnp.sum(d * m * s, axis=0, keepdims=True)
                sum_grad = term if sum_grad is None else sum_grad + term
        gain_grad[0:1, :] = sum_grad
        for m in scatter + [small_x, small_y]:
            m.wait_send()


def enter_back(du, tail, ev, u, v, near, far, scale, x, dx, gain):
    rows, channels = u.shape
    width = x.shape[1]
    block = ROW_BLOCK
    blocks = rows // block
    held = functools.partial(held_spec, block, last=blocks - 1)
    chunk = pltpu.VMEM((rows, width), BF)
    lanes = pltpu.VMEM((8, rows), F32)
    return pl.pallas_call(
        functools.partial(enter_back_body, blocks),
        grid=(blocks + 1,),
        in_specs=[held(channels), whole_spec(tail.shape)]
        + [held(channels)] * 3
        + [any_spec(), any_spec(), whole_spec(scale.shape), whole_spec(x.shape), whole_spec(dx.shape)]
        + [whole_spec(gain.shape)],
        out_specs=[held(channels), whole_spec((rows, width)), whole_spec((8, width))],
        out_shape=[sds((rows, channels), BF), sds((rows, width), F32), sds((8, width), F32)],
        scratch_shapes=[pltpu.VMEM((4 * width, 2 * channels), BF), pltpu.SemaphoreType.DMA((8,))]
        + [pltpu.VMEM((rows, width), F32)]
        + [chunk] * 6
        + [lanes] * 3
        + [pltpu.SemaphoreType.DMA((8,))] * 2,
        compiler_params=comm_params(4),
        cost_estimate=cost(40 * rows * near.size, rows * channels * 16 + nbytes(near, far)),
        name="enter_back",
    )(du, tail, ev, u, v, near, far, scale, x, dx, gain)


def neighbour_core():
    col = lax.axis_index("col")
    return {"col": col + 1 - 2 * lax.rem(col, 2)}


def neighbour_end():
    seq = lax.axis_index("seq")
    return {"seq": seq + 1 - 2 * lax.rem(seq, 2)}


def neighbour_middle():
    return {"seq": 3 - lax.axis_index("seq")}


def plus_in(dst, src, rows, start=0):
    step = 64
    for r in range(start, start + rows, step):
        at = slice(r, min(r + step, start + rows))
        dst[at, :] = (dst[at, :].astype(F32) + src[at, :].astype(F32)).astype(dst.dtype)


def tail_body(n1, eu, ev, mixed, er, small, mine_in, far_in, mine_out, far_out, small_out, *scratch):
    (s_in, p_in, c_in, a_in, b_in, y_in, s_out, p_out, c_out, a_out, b_out, y_out) = scratch[:12]
    (s_sm, c_sm, a_sm, b_sm, send, recv) = scratch[12:]
    sems = (send, recv)
    width = er.shape[1] // 4
    half = width // 2
    channels = eu.shape[1]
    seq = lax.axis_index("seq")
    middle = (seq == 1) | (seq == 2)
    end = (seq == 0) | (seq == 3)
    barrier = pltpu.get_barrier_semaphore()
    for device in (neighbour_core(), neighbour_y(), neighbour_end(), neighbour_middle()):
        pl.semaphore_signal(barrier, inc=1, device_id=device, device_id_type=MESH_ID)
    pl.semaphore_wait(barrier, 4)

    a, b = pl.ds(0, half), pl.ds(half, half)
    c, d = pl.ds(2 * half, half), pl.ds(3 * half, half)
    everything = pl.ds(0, s_sm.shape[0])
    lanes_far, lanes_own = pl.ds(width, width), pl.ds(0, width)
    group_in, group_out, group_sm = (s_in, a_in, b_in), (s_out, a_out, b_out), (s_sm, a_sm, b_sm)
    views = [
        [r.at[everything, :] for r in group_sm],
        [r.at[:, lanes_far] for r in group_out],
        [r.at[:, lanes_own] for r in group_out],
        [r.at[c, :] for r in group_in],
        [r.at[d, :] for r in group_in],
        [r.at[a, :] for r in group_in],
        [r.at[b, :] for r in group_in],
    ]
    count = len(views)
    to_end = [message(s, z1, neighbour_end(), sems, n) for n, (s, z1, z2) in enumerate(views)]
    to_middle = [message(s, z2, neighbour_middle(), sems, count + n) for n, (s, z1, z2) in enumerate(views)]
    base = 2 * count
    core_sm = message(small, c_sm, neighbour_core(), sems, base)
    core_out = message(p_out, c_out, neighbour_core(), sems, base + 1)
    core_in = [
        message(p_in.at[at, :], c_in.at[at, :], neighbour_core(), sems, base + 2 + n)
        for n, at in enumerate((c, d, a, b))
    ]
    y_out_m = message(s_out.at[:, lanes_far], y_out, neighbour_y(), sems, base + 6)
    y_in_m = [
        message(s_in.at[at, :], y_in.at[to, :], neighbour_y(), sems, base + 7 + n)
        for n, (at, to) in enumerate(((c, a), (d, b)))
    ]

    core_sm.start()
    g = dot_tn(mixed[...], er[...])
    p_out[...] = g[:, 2 * width :].astype(BF)
    core_out.start()
    s_out[...] = g[:, : 2 * width].astype(BF)
    s_sm[...] = small[...]

    def tile(n, target, row):
        at = slice(n * width, (n + 1) * width)
        where = slice(row, row + width)
        target[where, :channels] = dot_tn(n1[:, at], eu[...]).astype(BF)
        target[where, channels:] = dot_tn(n1[:, at], ev[...]).astype(BF)

    def begin(n):
        @pl.when(end)
        def _():
            to_end[n].start()

    def relay(n):
        s, z1, z2 = views[n]

        @pl.when(middle)
        def _():
            to_end[n].wait_recv()
            plus_in(s, z1, s.shape[0])
            to_middle[n].start()

    def settle(n):
        s, z1, z2 = views[n]

        @pl.when(middle)
        def _():
            to_middle[n].wait_recv()
            to_middle[n].wait_send()
            plus_in(s, z2, s.shape[0])
            to_end[n].start()

    def finish(n):
        s, z1, z2 = views[n]

        @pl.when(end)
        def _():
            to_end[n].wait_recv()
            to_end[n].wait_send()
            step = 64
            for r in range(0, s.shape[0], step):
                at = slice(r, min(r + step, s.shape[0]))
                s[at, :] = z1[at, :]

        @pl.when(middle)
        def _():
            to_end[n].wait_send()

    core_sm.wait_recv()
    plus_in(s_sm, c_sm, s_sm.shape[0])
    begin(0)
    tile(3, p_in, width)
    core_in[0].start()
    core_in[1].start()
    core_out.wait_recv()
    plus_in(s_out, c_out, s_out.shape[0])
    begin(1)
    begin(2)
    tile(1, s_in, width)
    tile(2, p_in, 0)
    core_in[2].start()
    core_in[3].start()
    core_in[0].wait_recv()
    core_in[1].wait_recv()
    plus_in(s_in, c_in, width, width)
    begin(3)
    begin(4)
    tile(0, s_in, 0)
    core_in[2].wait_recv()
    core_in[3].wait_recv()
    plus_in(s_in, c_in, width, 0)
    begin(5)
    begin(6)
    relay(0)
    relay(1)
    settle(0)
    relay(2)
    settle(1)
    finish(0)
    finish(1)
    y_out_m.start()
    for n in range(3, count):
        relay(n)
        settle(n - 1)
        if n < 5:
            finish(n - 1)
            if n == 4:
                y_in_m[0].start()
    settle(count - 1)
    finish(4)
    y_in_m[1].start()
    finish(5)
    finish(6)
    small_out[...] = s_sm[...]
    mine_in[...] = s_in[0:width, :]
    mine_out[...] = s_out[:, 0:width]
    y_out_m.wait_recv()
    far_out[...] = y_out[...]
    for m in y_in_m:
        m.wait_recv()
    far_in[...] = y_in[...]
    for m in [core_sm, core_out, y_out_m] + core_in + y_in_m:
        m.wait_send()


def tail(n1, eu, ev, mixed, er, small):
    rows, channels = eu.shape
    width = er.shape[1] // 4
    inner = mixed.shape[1]
    big = pltpu.VMEM((2 * width, 2 * channels), BF)
    tall = pltpu.VMEM((inner, 2 * width), BF)
    tiny = pltpu.VMEM(small.shape, F32)
    quarter_in, quarter_out = (width, 2 * channels), (inner, width)
    return pl.pallas_call(
        tail_body,
        out_shape=[sds(quarter_in, BF)] * 2 + [sds(quarter_out, BF)] * 2 + [sds(small.shape, F32)],
        scratch_shapes=[big] * 5
        + [pltpu.VMEM(quarter_in, BF)]
        + [tall] * 5
        + [pltpu.VMEM(quarter_out, BF)]
        + [tiny] * 4
        + [pltpu.SemaphoreType.DMA((23,))] * 2,
        compiler_params=pltpu.CompilerParams(
            vmem_limit_bytes=VMEM_LIMIT, collective_id=6, has_side_effects=True
        ),
        cost_estimate=cost(20 * rows * n1.shape[1] * channels * 3, nbytes(n1, eu, ev, mixed, er)),
        name="tail",
    )(n1, eu, ev, mixed, er, small)


def add_low(a, b):
    return (a.astype(F32) + b.astype(F32)).astype(BF)


def total_seq(g):
    count = lax.axis_size("seq")
    if count != 4:
        return lax.psum(g, "seq")
    place = lax.axis_index("seq")
    g = add_low(g, lax.ppermute(g, "seq", [(0, 1), (3, 2)]))
    g = add_low(g, lax.ppermute(g, "seq", [(1, 2), (2, 1)]))
    back = lax.ppermute(g, "seq", [(1, 0), (2, 3)])
    return jnp.where((place == 0) | (place == 3), back, g)


def local_fast(
    stream_in,
    cotangent,
    doc_lengths,
    mixer_gain,
    input_weight,
    branch_weight,
    filter_taps,
    recall_gate,
    admit_gate,
    decay_param,
    output_weight,
    feed_gain,
    gate_weight,
    up_weight,
    down_weight,
):
    tokens = stream_in.shape[1]
    half = tokens // 2
    count = lax.axis_size("seq")
    part = stream_in.shape[2]
    seq = lax.axis_index("seq")
    row = lax.axis_index("row")
    col = lax.axis_index("col")
    y, core = col // 2, col % 2
    lower = row == 0

    def own_and_other(a, pick, axis):
        size = a.shape[axis] // 2
        return (
            lax.dynamic_slice_in_dim(a, pick * size, size, axis),
            lax.dynamic_slice_in_dim(a, (1 - pick) * size, size, axis),
        )

    def by_core(a):
        own, other = own_and_other(a, core, 0)
        return jnp.concatenate([own[0], flip_core(other)[0]], axis=1)

    def in_halves(a):
        return (a[:half], a[half:])

    gains = jnp.stack([mixer_gain, feed_gain])
    gains = jnp.concatenate([gains, flip_core(gains)], axis=1)
    gains_x = flip_row(gains)
    gains_y = flip_y(gains)
    gains_all = jnp.concatenate([gains, gains_x, gains_y, flip_y(gains_x)], axis=1)

    x = by_core(stream_in)
    g = by_core(cotangent)

    def with_core(own, far):
        near = jnp.stack([own, far])
        return near, flip_core(near)

    own_in, other_in = own_and_other(jnp.stack([input_weight, branch_weight]), y, 2)
    far_in = flip_y(other_in)
    near_in, sib_in = with_core(
        jnp.concatenate([own_in[0], own_in[1]], axis=1), jnp.concatenate([far_in[0], far_in[1]], axis=1)
    )

    lanes = 2 * part
    share = gate_weight.shape[0] // count
    units = gate_weight.shape[1] // 2

    def other_share(w, axis):
        rows = w.shape[0] // (2 if axis == 0 else 1)
        take = rows // count
        start = seq * take + ((1 - y) * rows if axis == 0 else 0)
        if axis == 0:
            return lax.dynamic_slice(w, (start, 0), (take, w.shape[1]))
        cols = w.shape[1] // 2
        piece = lax.dynamic_slice(w, (start, (1 - y) * cols), (take, cols))
        return jnp.concatenate([piece[:, n : n + lanes] for n in range(0, cols, lanes)], axis=0)

    packed = jnp.concatenate(
        [
            other_share(gate_weight, 1),
            other_share(up_weight, 1),
            other_share(down_weight, 0),
            other_share(output_weight, 0),
        ],
        axis=0,
    )
    packed = lax.all_gather(flip_y(packed), "seq", axis=0)

    def late_weights(packed, gate_weight, up_weight, down_weight, output_weight):
        def wide(at):
            blocks = packed[:, at : at + share * (units // lanes)].reshape(count, units // lanes, share, lanes)
            return blocks.transpose(0, 2, 1, 3).reshape(count * share, units)

        step = share * (units // lanes)
        far_gu = jnp.concatenate([wide(0), wide(step)], axis=1)
        own_gu = jnp.concatenate(
            [own_and_other(gate_weight, y, 1)[0], own_and_other(up_weight, y, 1)[0]], axis=1
        )
        near_gu, sib_gu = with_core(own_gu, far_gu)
        d_rows = down_weight.shape[0] // 2
        o_rows = output_weight.shape[0] // 2
        at = 2 * step
        far_d = packed[:, at : at + d_rows // count].reshape(d_rows, lanes)
        at += d_rows // count
        far_o = packed[:, at : at + o_rows // count].reshape(o_rows, lanes)
        own_do = jnp.concatenate(
            [own_and_other(output_weight, y, 0)[0], own_and_other(down_weight, y, 0)[0]], axis=0
        )
        near, sib = with_core(own_do, jnp.concatenate([far_o, far_d], axis=0))
        chunks = []
        for dy in (0, 1):
            first = jnp.concatenate([near[dy][:, :part], sib[dy][:, :part]], axis=1)
            second = jnp.concatenate([near[dy][:, part:], sib[dy][:, part:]], axis=1)
            chunks += [jnp.where(lower, first, second), jnp.where(lower, second, first)]
        both = jnp.concatenate(chunks, axis=1)
        return near_gu, sib_gu, both[:o_rows], both[o_rows:]

    heads = recall_gate.shape[0] // 2
    rw = lax.dynamic_slice_in_dim(recall_gate, y * heads, heads, 0)
    aw = lax.dynamic_slice_in_dim(admit_gate, y * heads, heads, 0)
    small = jnp.concatenate([filter_taps, decay_param[None], jnp.zeros((3,) + decay_param.shape, F32)])
    sibling = flip_core(small)
    small = jnp.where(
        core == 0,
        jnp.concatenate([small, sibling], axis=1),
        jnp.concatenate([sibling, small], axis=1),
    )
    taps, decay = small[:KW], small[KW : KW + 1]
    soft = jax.nn.softplus(-decay)

    lengths = lax.dynamic_index_in_dim(doc_lengths, core, 0, False)
    offset = doc_offset(lengths, seq * tokens, tokens)
    edge = jnp.full((8,), -1, jnp.int32)
    off = jnp.concatenate([edge, offset, edge])[:, None]

    def neighbours(ends, sign):
        return jnp.concatenate([shifted(ends, sign * n) for n in range(1, count)], axis=0)

    n1, u, v, s1 = norm_uv(x.astype(BF), gains_all, near_in, sib_in)
    border = shifted(u[tokens - 8 :], 1)
    g_low = g.astype(BF)
    conv, recall, admit, local_state, cum, ends, *errs = recur(
        u, border, off, taps, rw, aw, soft, g_low
    )
    late = lax.optimization_barrier(
        (ends, packed, gate_weight, up_weight, down_weight, output_weight)
    )
    near_gu, sib_gu, w_out, w_down = late_weights(*late[1:])
    earlier = neighbours(ends, 1)
    states, mixed, mid, *mid_all = mix(local_state, cum, v, x, earlier, w_out)
    p0, p1, p2, p3, dx2, *dx_all, grad_feed, g_down, g_gu = feed(
        mid_all, [g_low] + errs, mid, g, gains_all, near_gu, sib_gu, w_down
    )
    outs = collect(tuple(zip(*(in_halves(p) for p in (p0, p1, p2, p3)))))
    out_chunk = jnp.concatenate(outs, axis=0) + mid

    part_adj, reach, ev, back_ends, er = adjoint(dx_all, w_out, states, v, recall, off, soft)
    later = neighbours(back_ends, -1)
    du, out_border, grad_recall, grad_admit, grad_small = recur_back(
        part_adj, reach, later, earlier, states, conv, recall, admit, off, u, border, taps, rw, aw, soft
    )
    from_later = shifted(out_border, -1)
    eu, grad_chunk, grad_mixer = enter_back(du, from_later, ev, u, v, near_in, sib_in, s1, x, dx2, gains_all)

    def rows_out(mine, theirs):
        wide = jnp.where(
            y == 0, jnp.concatenate([mine, theirs], axis=1), jnp.concatenate([theirs, mine], axis=1)
        )
        swapped = jnp.concatenate([wide[part:], wide[:part]], axis=0)
        return jnp.where(lower, wide, swapped).astype(F32)

    def cols_out(mine, theirs):
        tall = jnp.where(
            y == 0, jnp.concatenate([mine, theirs], axis=0), jnp.concatenate([theirs, mine], axis=0)
        )
        swapped = jnp.concatenate([tall[:, part:], tall[:, :part]], axis=1)
        return jnp.where(lower, tall, swapped).astype(F32)

    kept = 4 * part
    channels = taps.shape[1]
    sum_down = add_low(g_down[:, :kept], flip_core(g_down[:, kept:]))
    sum_gu = add_low(g_gu[:kept], flip_core(g_gu[kept:]))
    mine_down, far_down = sum_down[:, :lanes], flip_y(sum_down[:, lanes:])
    mine_gu, far_gu = sum_gu[:lanes], flip_y(sum_gu[lanes:])
    mine_down, mine_gu = lax.psum((mine_down, mine_gu), "seq")
    far_down, far_gu, _, _ = lax.optimization_barrier((far_down, far_gu, mine_down, mine_gu))
    far_down, far_gu = lax.psum((far_down, far_gu), "seq")

    own = channels // 2
    pieces = [
        grad_small[:KW].reshape(-1),
        grad_small[KW] * 8.0 * jax.nn.sigmoid(-decay[0]),
        grad_recall.reshape(-1),
        grad_admit.reshape(-1),
    ]
    gain_rows = jnp.stack([grad_mixer[0], grad_feed[0]])
    gain_rows = jnp.where(
        core == 0, gain_rows, jnp.concatenate([gain_rows[:, part:], gain_rows[:, :part]], axis=1)
    )
    pieces.append(gain_rows.reshape(-1))
    sizes = [p.size for p in pieces]
    flat = jnp.concatenate(pieces)
    flat = jnp.pad(flat, (0, -flat.size % 8192)).reshape(-1, 128)
    mine_in, far_in, mine_out, far_out, flat = tail(n1, eu, ev, mixed, er, flat)
    flat = flat.reshape(-1)
    cuts, at = [], 0
    for s in sizes:
        cuts.append(flat[at : at + s])
        at += s
    grad_down = cols_out(mine_down, far_down)
    grad_gate = rows_out(mine_gu[:, :units], far_gu[:, :units])
    grad_up = rows_out(mine_gu[:, units:], far_gu[:, units:])
    grad_output = cols_out(mine_out, far_out)
    grad_input = rows_out(mine_in[:, :channels], far_in[:, :channels])
    grad_branch = rows_out(mine_in[:, channels:], far_in[:, channels:])
    g_taps = lax.dynamic_slice_in_dim(cuts[0].reshape(KW, channels), core * own, own, 1)
    g_decay = lax.dynamic_slice_in_dim(cuts[1], core * own, own, 0)
    gates = jnp.stack([cuts[2].reshape(grad_recall.shape), cuts[3].reshape(grad_admit.shape)])
    far = flip_y(gates)
    gates = jnp.where(
        y == 0, jnp.concatenate([gates, far], axis=1), jnp.concatenate([far, gates], axis=1)
    )
    gain_grads = lax.dynamic_slice_in_dim(cuts[4].reshape(2, 2 * part), core * part, part, 1)

    def stacked(chunk):
        own, other = chunk[:, :part], flip_core(chunk[:, part:])
        return jnp.where(core == 0, jnp.stack([own, other]), jnp.stack([other, own]))

    return (
        stacked(out_chunk),
        stacked(grad_chunk),
        gain_grads[0],
        grad_input,
        grad_branch,
        g_taps,
        gates[0],
        gates[1],
        g_decay,
        grad_output,
        gain_grads[1],
        grad_gate,
        grad_up,
        grad_down,
    )


def solution(mesh):
    in_specs = (
        P(None, "seq", ("col", "row")),
        P(None, "seq", ("col", "row")),
        P(),
        P(("col", "row")),
        P("col", "row"),
        P("col", "row"),
        P(None, ("row", "col")),
        P("row", None, None),
        P("row", None, None),
        P(("row", "col")),
        P("row", "col"),
        P(("col", "row")),
        P("col", "row"),
        P("col", "row"),
        P("row", "col"),
    )
    out_specs = (
        P(None, "seq", ("col", "row")),
        P(None, "seq", ("col", "row")),
        P(("col", "row")),
        P("col", "row"),
        P("col", "row"),
        P(None, ("row", "col")),
        P("row", None, None),
        P("row", None, None),
        P(("row", "col")),
        P("row", "col"),
        P(("col", "row")),
        P("col", "row"),
        P("col", "row"),
        P("row", "col"),
    )
    plan = local_fast if dict(mesh.shape) == {"seq": 4, "row": 2, "col": 4} else local
    return jax.shard_map(plan, mesh=mesh, in_specs=in_specs, out_specs=out_specs, check_vma=False)
```

```python
import functools

import jax
import jax.numpy as jnp
from jax import lax
from jax.experimental import pallas as pl
from jax.experimental.pallas import tpu as pltpu
from jax.sharding import PartitionSpec as P

D = 1536
KW = 4


EPSILON = 1e-06
PRECISE = lax.Precision.HIGHEST
SUM_ROWS = (((0,), (0,)), ((), ()))
SUM_COLS = (((1,), (1,)), ((), ()))


def as_sent(value):
    return jax.tree.map(lambda a: a.astype(jnp.bfloat16) if a.dtype == jnp.float32 else a, value)


def passed_along(block, axis, distance):
    devices = range(lax.axis_size(axis))
    route = [(i - distance, i) for i in devices if i - distance in devices]
    return lax.ppermute(block, axis, route)


def entering_2(part, axis, combine, identity, reverse):
    count = lax.axis_size(axis)
    place = lax.axis_index(axis)
    ahead = count - 1 - place if reverse else place
    gathered = jax.tree.map(lambda a: lax.all_gather(a, axis), part)
    state = jax.tree.map(lambda a, e: jnp.zeros_like(a) + jnp.asarray(e, a.dtype), part, identity)

    def one(hop, state):
        source = count - 1 - hop if reverse else hop
        return combine(
            state, jax.tree.map(lambda a: lax.dynamic_index_in_dim(a, source, 0, False), gathered)
        )

    return lax.fori_loop(0, ahead, one, state)


def compose(first, second):
    return (first[0] * second[0], second[0] * first[1] + second[1])


def convolve(source, taps, offset, border):
    tokens = source.shape[0]
    extended = jnp.concatenate([border, source], axis=0)
    result = jnp.zeros_like(source)
    for lag_index in range(KW):
        anchor = KW - 1 - lag_index
        valid = (offset >= lag_index).astype(jnp.float32)[:, None]
        result = result + taps[lag_index] * extended[anchor : anchor + tokens] * valid
    return result


def slab_pre(conv_value, recall_value, admit_value):
    tokens = conv_value.shape[0]
    blocks = conv_value.reshape(tokens, recall_value.shape[0], recall_value.shape[1])
    recall_pre = jnp.einsum("thi,hij->thj", blocks, recall_value, precision=PRECISE).reshape(
        tokens, -1
    )
    admit_pre = jnp.einsum("thi,hij->thj", blocks, admit_value, precision=PRECISE).reshape(
        tokens, -1
    )
    return (recall_pre, admit_pre)


def own_terms(conv_value, recall_pre, admit_pre, decay_value, resume):
    recall = jax.nn.sigmoid(recall_pre)
    admit = jax.nn.sigmoid(admit_pre)
    log_decay = -8.0 * recall * jax.nn.softplus(-decay_value)
    decays = jnp.exp(log_decay) * resume[:, None]
    drives = jnp.sqrt(-jnp.expm1(2.0 * log_decay)) * admit * conv_value
    return (decays, drives)


def width_total(partial_value):
    return lax.psum(partial_value, ("row", "col"))


def gather_row(source):
    return lax.all_gather(source, "row", axis=1, tiled=True)


def gather_col(source):
    return jax.tree.map(
        lambda part, own: part.astype(own.dtype),
        lax.all_gather(as_sent(source), "col", axis=1, tiled=True),
        source,
    )


def scatter_col(source):
    return (
        lax.psum_scatter(source[0], "col", scatter_dimension=1, tiled=True),
        lax.psum_scatter(source[1], "col", scatter_dimension=1, tiled=True),
    )


def scatter_col_back(source):
    return lax.psum_scatter(source, "col", scatter_dimension=1, tiled=True)


def scatter_row(source):
    return lax.psum_scatter(source, "row", scatter_dimension=1, tiled=True)


def over_seq(grads):
    return (
        lax.psum(grads[0].astype(jnp.bfloat16), "seq").astype(jnp.float32),
        lax.psum(grads[1].astype(jnp.bfloat16), "seq").astype(jnp.float32),
        lax.psum(grads[2].astype(jnp.bfloat16), "seq").astype(jnp.float32),
        lax.psum(grads[3].astype(jnp.bfloat16), "seq").astype(jnp.float32),
        lax.psum(grads[4].astype(jnp.bfloat16), "seq").astype(jnp.float32),
        lax.psum(grads[5].astype(jnp.bfloat16), "seq").astype(jnp.float32),
        lax.psum(grads[6].astype(jnp.bfloat16), "seq").astype(jnp.float32),
        lax.psum(grads[7].astype(jnp.bfloat16), "seq").astype(jnp.float32),
        lax.psum(grads[8].astype(jnp.bfloat16), "seq").astype(jnp.float32),
        lax.psum(grads[9].astype(jnp.bfloat16), "seq").astype(jnp.float32),
        lax.psum(grads[10].astype(jnp.bfloat16), "seq").astype(jnp.float32),
        lax.psum(grads[11].astype(jnp.bfloat16), "seq").astype(jnp.float32),
    )


def normalize(source, scales):
    factor = lax.rsqrt(width_total(jnp.sum(source * source, axis=1)) / D + EPSILON)
    return (source * factor[:, None] * scales, factor)


def norm_back(source, scales, factor, grad_norm):
    weighted = scales * grad_norm
    summed = width_total(jnp.sum(weighted * source, axis=1))
    grad_source = (
        factor[:, None] * weighted - source * (factor * factor * factor * summed / D)[:, None]
    )
    grad_scales = jnp.sum(grad_norm * source * factor[:, None], axis=0)
    return (grad_source, grad_scales)


def doc_offset(lengths, anchor, tokens):
    starts = jnp.cumsum(lengths, dtype=jnp.int32) - lengths
    places = anchor + jnp.arange(tokens, dtype=jnp.int32)
    begins = jnp.max(jnp.where(starts[None, :] <= places[:, None], starts[None, :], 0), axis=1)
    return places - begins


def matmul_rows(left, right):
    return lax.dot_general(left, right, SUM_ROWS, preferred_element_type=jnp.float32)


def matmul_cols(left, right):
    return lax.dot_general(left, right, SUM_COLS, preferred_element_type=jnp.float32)


def local(
    stream_in,
    cotangent,
    doc_lengths,
    mixer_gain,
    input_weight,
    branch_weight,
    filter_taps,
    recall_gate,
    admit_gate,
    decay_param,
    output_weight,
    feed_gain,
    gate_weight,
    up_weight,
    down_weight,
):
    tokens = stream_in.shape[1]
    anchor = lax.axis_index("seq") * tokens
    channels = decay_param.shape[0]
    col_start = lax.axis_index("col") * channels
    params = (
        mixer_gain,
        input_weight,
        branch_weight,
        filter_taps,
        recall_gate,
        admit_gate,
        decay_param,
        output_weight,
        feed_gain,
        gate_weight,
        up_weight,
        down_weight,
    )
    totals = tuple((jnp.zeros(w.shape, jnp.float32) for w in params))
    identity = (jnp.ones_like(decay_param), jnp.zeros_like(decay_param))
    outputs = []
    grads_in = []
    for micro in range(stream_in.shape[0]):
        offset = doc_offset(doc_lengths[micro], anchor, tokens)
        resume = (offset > 0).astype(jnp.float32)
        source = stream_in[micro]
        normed, factor_one = normalize(source, mixer_gain)
        normed_low = normed.astype(jnp.bfloat16)
        normed_all = gather_row(normed_low)
        rec_in, branch = scatter_col(
            (
                jnp.dot(normed_all, input_weight, preferred_element_type=jnp.float32),
                jnp.dot(normed_all, branch_weight, preferred_element_type=jnp.float32),
            )
        )
        border = passed_along(rec_in[tokens - (KW - 1) :], "seq", 1)
        conv_out = convolve(rec_in, filter_taps, offset, border)
        conv_slab = lax.all_gather(conv_out, "col", axis=1, tiled=True)
        slab_values, slab_pull = jax.vjp(slab_pre, conv_slab, recall_gate, admit_gate)
        recall_pre = lax.dynamic_slice_in_dim(slab_values[0], col_start, channels, 1)
        admit_pre = lax.dynamic_slice_in_dim(slab_values[1], col_start, channels, 1)

        def local_gates(conv_value, recall_value, admit_value, decay_value):
            return own_terms(conv_value, recall_value, admit_value, decay_value, resume)

        (decays, drives), gates_pull = jax.vjp(
            local_gates, conv_out, recall_pre, admit_pre, decay_param
        )
        cum_decay, local_state = lax.associative_scan(compose, (decays, drives), axis=0)
        entering = entering_2((cum_decay[-1], local_state[-1]), "seq", compose, identity, False)[1]
        states = local_state + cum_decay * entering
        branch_act = jax.nn.gelu(branch)
        mixed_all = gather_col((states * branch_act).astype(jnp.bfloat16))
        middle = source + scatter_row(
            jnp.dot(mixed_all, output_weight, preferred_element_type=jnp.float32)
        )
        normed_two, factor_two = normalize(middle, feed_gain)
        normed_two_low = normed_two.astype(jnp.bfloat16)
        normed_two_all = gather_row(normed_two_low)
        gate_pre, up_pre = scatter_col(
            (
                jnp.dot(normed_two_all, gate_weight, preferred_element_type=jnp.float32),
                jnp.dot(normed_two_all, up_weight, preferred_element_type=jnp.float32),
            )
        )
        gate_act = jax.nn.gelu(gate_pre)
        hidden_all = gather_col((gate_act * up_pre).astype(jnp.bfloat16))
        outputs.append(
            middle
            + scatter_row(jnp.dot(hidden_all, down_weight, preferred_element_type=jnp.float32))
        )
        upstream = cotangent[micro]
        upstream_all = gather_row(upstream.astype(jnp.bfloat16))
        grad_down = matmul_rows(hidden_all, upstream_all)
        grad_hidden = scatter_col_back(matmul_cols(upstream_all, down_weight))
        gate_value, gelu_pull = jax.vjp(jax.nn.gelu, gate_pre)
        error_gate = gelu_pull(grad_hidden * up_pre)[0].astype(jnp.bfloat16)
        error_up = (grad_hidden * gate_act).astype(jnp.bfloat16)
        gate_err_all, up_err_all = gather_col((error_gate, error_up))
        grad_gate = matmul_rows(normed_two_all, gate_err_all)
        grad_up = matmul_rows(normed_two_all, up_err_all)
        grad_normed_two = scatter_row(
            matmul_cols(gate_err_all, gate_weight) + matmul_cols(up_err_all, up_weight)
        )
        back_middle, grad_feed = norm_back(middle, feed_gain, factor_two, grad_normed_two)
        grad_middle = upstream + back_middle
        rec_err_all = gather_row(grad_middle.astype(jnp.bfloat16))
        grad_output = matmul_rows(mixed_all, rec_err_all)
        grad_mixed = scatter_col_back(matmul_cols(rec_err_all, output_weight))
        branch_value, branch_pull = jax.vjp(jax.nn.gelu, branch)
        error_branch = branch_pull(grad_mixed * states)[0].astype(jnp.bfloat16)
        direct = grad_mixed * branch_act
        ahead = jnp.concatenate([decays[1:], jnp.ones_like(decays[:1])], axis=0)
        reach, partial_adj = lax.associative_scan(compose, (ahead, direct), axis=0, reverse=True)
        incoming = entering_2(
            (decays[0] * reach[0], decays[0] * partial_adj[0]), "seq", compose, identity, True
        )[1]
        adjoint = partial_adj + reach * incoming
        previous = jnp.concatenate([entering[None, :], states[:-1]], axis=0)
        conv_direct, grad_recall_pre, grad_admit_pre, grad_decay = gates_pull(
            (adjoint * previous, adjoint)
        )
        recall_all, admit_all = (
            lax.all_gather(grad_recall_pre.astype(jnp.bfloat16), "col", axis=1, tiled=True).astype(
                grad_recall_pre.dtype
            ),
            lax.all_gather(grad_admit_pre.astype(jnp.bfloat16), "col", axis=1, tiled=True).astype(
                grad_admit_pre.dtype
            ),
        )
        grad_slab, grad_recall, grad_admit = slab_pull((recall_all, admit_all))
        grad_conv_out = conv_direct + lax.dynamic_slice_in_dim(grad_slab, col_start, channels, 1)

        def local_conv(input_value, taps_value, border_value):
            return convolve(input_value, taps_value, offset, border_value)

        conv_value, conv_pull = jax.vjp(local_conv, rec_in, filter_taps, border)
        grad_rec_in, grad_taps, grad_border = conv_pull(grad_conv_out)
        from_next = passed_along(grad_border, "seq", -1)
        grad_rec_in = grad_rec_in + jnp.pad(from_next, ((tokens - (KW - 1), 0), (0, 0)))
        error_input = grad_rec_in.astype(jnp.bfloat16)
        in_err_all, branch_err_all = gather_col((error_input, error_branch))
        grad_input = matmul_rows(normed_all, in_err_all)
        grad_branch = matmul_rows(normed_all, branch_err_all)
        grad_normed = scatter_row(
            matmul_cols(in_err_all, input_weight) + matmul_cols(branch_err_all, branch_weight)
        )
        back_source, grad_mixer = norm_back(source, mixer_gain, factor_one, grad_normed)
        grads_in.append(grad_middle + back_source)
        local_grads = (
            grad_mixer,
            grad_input,
            grad_branch,
            grad_taps,
            grad_recall,
            grad_admit,
            grad_decay,
            grad_output,
            grad_feed,
            grad_gate,
            grad_up,
            grad_down,
        )
        local_grads = over_seq(local_grads)
        totals = tuple((acc + new for acc, new in zip(totals, local_grads)))
    return (jnp.stack(outputs), jnp.stack(grads_in)) + tuple(totals)


BF = jnp.bfloat16
F32 = jnp.float32
VMEM_LIMIT = 60 * 1024 * 1024
ROW_BLOCK = 256
GELU_A = 0.7978845608028654
GELU_B = 0.044715


def flip_row(a):
    return lax.ppermute(a, "row", [(0, 1), (1, 0)])


def flip_y(a):
    return lax.ppermute(a, "col", [(i, i ^ 2) for i in range(4)])


def flip_core(a):
    return lax.ppermute(a, "col", [(i, i ^ 1) for i in range(4)])


def shifted(a, distance):
    return passed_along(a, "seq", distance)


def cost(flops, moved, trans=0):
    return pl.CostEstimate(flops=int(flops), bytes_accessed=int(moved), transcendentals=int(trans))


def params():
    return pltpu.CompilerParams(vmem_limit_bytes=VMEM_LIMIT, dimension_semantics=("arbitrary",))


def nbytes(*arrays):
    return sum(a.size * a.dtype.itemsize for a in arrays)


def spread(halves):
    first, second = halves
    ax, ay = flip_row(first), flip_y(first)
    bx, by = flip_row(second), flip_y(second)
    return ((first, ax, ay, flip_y(ax)), (second, bx, by, flip_row(by)))


def collect(halves):
    (a0, a1, a2, a3), (b0, b1, b2, b3) = halves
    a2 = (a2.astype(F32) + flip_row(a3).astype(F32)).astype(BF)
    b1 = (b1.astype(F32) + flip_y(b3).astype(F32)).astype(BF)
    return (
        a0 + flip_row(a1).astype(F32) + flip_y(a2).astype(F32),
        b0 + flip_row(b1).astype(F32) + flip_y(b2).astype(F32),
    )


def gelu_pair(v):
    t = jnp.tanh(GELU_A * (v + GELU_B * v * v * v))
    value = 0.5 * v * (1.0 + t)
    slope = 0.5 * (1.0 + t) + 0.5 * v * (1.0 - t * t) * GELU_A * (1.0 + 3.0 * GELU_B * v * v)
    return value, slope


def minus_expm1(x):
    series = 1.0 + x * (1.0 / 7.0)
    for n in (6, 5, 4, 3, 2):
        series = 1.0 + x * (1.0 / n) * series
    return jnp.where(x > -0.3, -x * series, 1.0 - jnp.exp(x))


def pair_up(left, right):
    width = left.shape[1]
    lane = lax.broadcasted_iota(jnp.int32, left.shape, 1)
    low = lane < width // 2
    return (
        jnp.where(low, left, pltpu.roll(right, width // 2, 1)),
        jnp.where(low, pltpu.roll(left, width // 2, 1), right),
    )


def dot_nn(a, b, precision=None):
    return lax.dot_general(
        a, b, (((1,), (0,)), ((), ())), precision=precision, preferred_element_type=F32
    )


def dot_nt(a, b, precision=None):
    return lax.dot_general(
        a, b, (((1,), (1,)), ((), ())), precision=precision, preferred_element_type=F32
    )


def dot_tn(a, b, precision=None):
    return lax.dot_general(
        a, b, (((0,), (0,)), ((), ())), precision=precision, preferred_element_type=F32
    )


def rows_spec(block, width, start=0):
    return pl.BlockSpec((block, width), lambda i: (i + start, 0))


def whole_spec(shape):
    rank = len(shape)
    return pl.BlockSpec(shape, lambda i: (0,) * rank, pipeline_mode=pl.Buffered(1))


def head_spec(rows, width=128):
    return pl.BlockSpec((rows, width), lambda h: (0, h))


def sds(shape, dtype):
    return jax.ShapeDtypeStruct(shape, dtype)


MESH_ID = pl.DeviceIdType.MESH


def neighbour_x():
    return {"row": 1 - lax.axis_index("row")}


def neighbour_y():
    return {"col": lax.rem(lax.axis_index("col") + 2, 4)}


def greet():
    barrier = pltpu.get_barrier_semaphore()
    for device in (neighbour_x(), neighbour_y()):
        pl.semaphore_signal(barrier, inc=1, device_id=device, device_id_type=MESH_ID)
    pl.semaphore_wait(barrier, 2)


def message(src, dst, device, sems, n):
    send, recv = sems
    return pltpu.make_async_remote_copy(
        src_ref=src,
        dst_ref=dst,
        send_sem=send.at[n],
        recv_sem=recv.at[n],
        device_id=device,
        device_id_type=MESH_ID,
    )


def neighbour_core():
    col = lax.axis_index("col")
    return {"col": col + 1 - 2 * lax.rem(col, 2)}


def neighbour_end():
    seq = lax.axis_index("seq")
    return {"seq": seq + 1 - 2 * lax.rem(seq, 2)}


def neighbour_middle():
    return {"seq": 3 - lax.axis_index("seq")}


def greet_all(devices):
    barrier = pltpu.get_barrier_semaphore()
    for device in devices:
        pl.semaphore_signal(barrier, inc=1, device_id=device, device_id_type=MESH_ID)
    pl.semaphore_wait(barrier, len(devices))


def row_step(ref):
    rows, lanes = ref.shape
    step = 16
    while step * 2 * lanes <= 32768 and rows % (step * 2) == 0:
        step *= 2
    return step


def plus_in(dst, src):
    step = row_step(dst)

    def one(n, carry):
        at = pl.ds(pl.multiple_of(n * step, step), step)
        dst[at, :] = (dst[at, :].astype(F32) + src[at, :].astype(F32)).astype(dst.dtype)
        return carry

    lax.fori_loop(0, dst.shape[0] // step, one, 0)


def put_in(dst, src):
    step = row_step(dst)

    def one(n, carry):
        at = pl.ds(pl.multiple_of(n * step, step), step)
        dst[at, :] = src[at, :].astype(dst.dtype)
        return carry

    lax.fori_loop(0, dst.shape[0] // step, one, 0)


class SeqSum:
    def __init__(self, pieces, sems, base):
        self.pieces = pieces
        count = len(pieces)
        self.to_end = [message(s, a, neighbour_end(), sems, base + n) for n, (s, a, b) in enumerate(pieces)]
        self.across = [
            message(s, b, neighbour_middle(), sems, base + count + n) for n, (s, a, b) in enumerate(pieces)
        ]
        seq = lax.axis_index("seq")
        self.middle = (seq == 1) | (seq == 2)
        self.end = (seq == 0) | (seq == 3)

    def begin(self, n):
        @pl.when(self.end)
        def _():
            self.to_end[n].start()

    def relay(self, n):
        s, a, b = self.pieces[n]

        @pl.when(self.middle)
        def _():
            self.to_end[n].wait_recv()
            plus_in(s, a)
            self.across[n].start()

    def settle(self, n):
        s, a, b = self.pieces[n]

        @pl.when(self.middle)
        def _():
            self.across[n].wait_recv()
            self.across[n].wait_send()
            plus_in(s, b)
            self.to_end[n].start()

    def finish(self, n):
        s, a, b = self.pieces[n]

        @pl.when(self.end)
        def _():
            self.to_end[n].wait_recv()
            self.to_end[n].wait_send()
            put_in(s, a)

        @pl.when(self.middle)
        def _():
            self.to_end[n].wait_send()


def scatter_messages(q1, q2, q3, r3, rx, ry, sems, base):
    half = q1.shape[0] // 2
    a, b = pl.ds(0, half), pl.ds(half, half)
    x, y = neighbour_x(), neighbour_y()
    plan = ((q3, r3, a, x), (q3, r3, b, y), (q1, rx, a, x), (q2, ry, a, y), (q2, ry, b, y), (q1, rx, b, x))
    return [
        message(src.at[at, :], dst.at[at, :], dev, sems, base + n)
        for n, (src, dst, at, dev) in enumerate(plan)
    ]


def gather_messages(own, gx, gy, gd, sems, base):
    half = own.shape[0] // 2
    a, b = pl.ds(0, half), pl.ds(half, half)
    x, y = neighbour_x(), neighbour_y()
    plan = ((own, gx, a, x), (own, gy, a, y), (own, gx, b, x), (own, gy, b, y), (gx, gd, a, y), (gy, gd, b, x))
    return [
        message(src.at[at, :], dst.at[at, :], dev, sems, base + n)
        for n, (src, dst, at, dev) in enumerate(plan)
    ]


def add_into(dst, src, start, rows):
    step = 128
    for r in range(start, start + rows, step):
        at = slice(r, r + step)
        dst[at, :] = (dst[at, :].astype(F32) + src[at, :].astype(F32)).astype(dst.dtype)


def load_rows(near, far, dst, sem):
    part = near.shape[1] // 2
    row = lax.axis_index("row")
    copies = []
    for dy in (0, 1):
        for dx in (0, 1):
            start = pl.multiple_of(part * (row + dx - 2 * row * dx), part)
            for dc, src in enumerate((near, far)):
                at = ((dy * 2 + dx) * 2 + dc) * part
                copies.append(
                    pltpu.make_async_copy(
                        src.at[dy, pl.ds(start, part), :], dst.at[pl.ds(at, part), :], sem.at[len(copies)]
                    )
                )
    for c in copies:
        c.start()
    return copies


def comm_params(n):
    return pltpu.CompilerParams(
        vmem_limit_bytes=VMEM_LIMIT,
        dimension_semantics=("arbitrary",),
        collective_id=n,
        has_side_effects=True,
    )


def any_spec():
    return pl.BlockSpec(memory_space=pl.ANY)


def held_spec(block, width, last):
    return pl.BlockSpec((block, width), lambda i: (jnp.minimum(i, last), 0))


def full_spec(shape):
    rank = len(shape)
    return pl.BlockSpec(shape, lambda i: (0,) * rank)


def row_sums(values):
    return dot_nt(jnp.ones((8, values.shape[1]), F32), values, PRECISE)


def as_column(lanes, width):
    first = (lax.broadcasted_iota(jnp.int32, (8, width), 0) == 0).astype(F32)
    return dot_tn(lanes, first, PRECISE)


def norm_uv_body(blocks, own, gain, near, far, n1, u, v, scale, w, gx, gy, gd, load, send, recv):
    i = pl.program_id(0)
    gather = gather_messages(own, gx, gy, gd, (send, recv), 0)

    @pl.when(i == 0)
    def _():
        greet()
        for n in range(4):
            gather[n].start()
        copies = load_rows(near, far, w, load)
        gather[0].wait_recv()
        gather[4].start()
        gather[3].wait_recv()
        gather[5].start()
        for c in copies:
            c.wait()
        gather[1].wait_recv()
        gather[4].wait_recv()

    @pl.when(i == blocks // 2)
    def _():
        gather[2].wait_recv()
        gather[5].wait_recv()
        for m in gather:
            m.wait_send()

    block = u.shape[0]
    at = pl.ds(pl.multiple_of(i * block, block), block)
    parts = [r[at, :].astype(F32) for r in (own, gx, gy, gd)]
    width = parts[0].shape[1]
    total = sum(jnp.sum(p * p, axis=1, keepdims=True) for p in parts)
    s = lax.rsqrt(total / D + EPSILON)
    scale[...] = s
    normed = [p * s * gain[0:1, j * width : (j + 1) * width] for j, p in enumerate(parts)]
    acc = None
    for j, n in enumerate(normed):
        term = dot_nn(n.astype(BF), w[j * width : (j + 1) * width, :])
        acc = term if acc is None else acc + term
    channels = u.shape[1]
    u[...] = acc[:, :channels]
    v[...] = acc[:, channels:]
    for j in (0, 1):
        k, p = pair_up(normed[2 * j], normed[2 * j + 1])
        n1[:, j * width : (j + 1) * width] = k.astype(BF)
        n1[:, (j + 2) * width : (j + 3) * width] = p.astype(BF)


def norm_uv(own, gain, near, far):
    rows, width = own.shape
    w = pltpu.VMEM((4 * width, near.shape[2]), BF)
    channels = near.shape[2] // 2
    block = ROW_BLOCK
    blocks = rows // block
    return pl.pallas_call(
        functools.partial(norm_uv_body, blocks),
        grid=(blocks,),
        in_specs=[whole_spec(own.shape), whole_spec(gain.shape), any_spec(), any_spec()],
        out_specs=[rows_spec(block, 4 * width)] + [rows_spec(block, channels)] * 2 + [rows_spec(block, 1)],
        out_shape=[sds((rows, 4 * width), BF)] + [sds((rows, channels), F32)] * 2 + [sds((rows, 1), F32)],
        scratch_shapes=[w]
        + [pltpu.VMEM((rows, width), BF)] * 3
        + [pltpu.SemaphoreType.DMA((8,))]
        + [pltpu.SemaphoreType.DMA((6,))] * 2,
        compiler_params=comm_params(1),
        cost_estimate=cost(60 * rows * near.size, nbytes(near, far)),
        name="norm_uv",
    )(own, gain, near, far)


def chain(entries, count):
    state = entries[(count - 1) * 8 + 1 : (count - 1) * 8 + 2, :]
    for n in range(count - 2, -1, -1):
        state = entries[n * 8 + 1 : n * 8 + 2, :] + entries[n * 8 : n * 8 + 1, :] * state
    return state


def recur_body(
    heads, u, border, off, taps, recall_w, admit_w, soft, own, conv, recall, admit, state, cum, ends, gx, gy, gd, ext, send, recv
):
    rows = u.shape[0]
    gather = gather_messages(own, gx, gy, gd, (send, recv), 0)
    h = pl.program_id(0)

    @pl.when(h == 0)
    def _():
        greet()
        for n in range(4):
            gather[n].start()

    @pl.when(h == heads - 1)
    def _():
        gather[0].wait_recv()
        gather[4].start()
        gather[3].wait_recv()
        gather[5].start()

    ext[0:8, :] = border[...]
    ext[8 : 8 + rows, :] = u[...]
    step = ROW_BLOCK
    for r in range(0, rows, step):
        o = off[8 + r : 8 + r + step, :]
        total = taps[0:1, :] * ext[8 + r : 8 + r + step, :]
        for k in range(1, KW):
            term = taps[k : k + 1, :] * ext[8 + r - k : 8 + r - k + step, :]
            total = total + jnp.where(o >= k, term, 0.0)
        conv[r : r + step, :] = total
        rec = jax.nn.sigmoid(dot_nn(total, recall_w[0], PRECISE))
        adm = jax.nn.sigmoid(dot_nn(total, admit_w[0], PRECISE))
        recall[r : r + step, :] = rec
        admit[r : r + step, :] = adm
        ell = -8.0 * rec * soft[0:1, :]
        cum[r : r + step, :] = jnp.where(o > 0, jnp.exp(ell), 0.0)
        state[r : r + step, :] = jnp.sqrt(minus_expm1(2.0 * ell)) * adm * total
    seg = rows // 8

    def one(i, carry):
        h, p = carry
        at = pl.ds(i, 8, stride=seg)
        d = cum[at, :]
        h = d * h + state[at, :]
        p = d * p
        state[at, :] = h
        cum[at, :] = p
        return h, p

    zero = jnp.zeros((8, 128), F32)
    h, p = lax.fori_loop(0, seg, one, (zero, zero + 1.0), unroll=8)
    carry_h, carry_p = h[0:1, :], p[0:1, :]
    for s in range(1, 8):
        at = slice(s * seg, (s + 1) * seg)
        c = cum[at, :]
        state[at, :] = state[at, :] + c * carry_h
        cum[at, :] = c * carry_p
        carry_h = h[s : s + 1, :] + p[s : s + 1, :] * carry_h
        carry_p = p[s : s + 1, :] * carry_p
    ends[0:1, :] = carry_p
    ends[1:2, :] = carry_h
    ends[2:8, :] = jnp.zeros((6, 128), F32)

    @pl.when(pl.program_id(0) == heads - 1)
    def _():
        for n in (1, 2, 4, 5):
            gather[n].wait_recv()
        for m in gather:
            m.wait_send()


def recur(u, border, off, taps, recall_w, admit_w, soft, own):
    rows, channels = u.shape
    heads = channels // 128
    gate = pl.BlockSpec((1, 128, 128), lambda h: (h, 0, 0))
    full = sds((rows, channels), F32)
    return pl.pallas_call(
        functools.partial(recur_body, heads),
        grid=(heads,),
        in_specs=[
            head_spec(rows),
            head_spec(8),
            whole_spec(off.shape),
            head_spec(KW),
            gate,
            gate,
            head_spec(1),
            whole_spec(own.shape),
        ],
        out_specs=[head_spec(rows)] * 5 + [head_spec(8)] + [any_spec()] * 3,
        out_shape=[full] * 5 + [sds((8, channels), F32)] + [sds(own.shape, BF)] * 3,
        scratch_shapes=[pltpu.VMEM((rows + 8, 128), F32)] + [pltpu.SemaphoreType.DMA((6,))] * 2,
        compiler_params=comm_params(5),
        cost_estimate=cost(rows * channels * 128 * 24, rows * channels * 4 * 6, rows * channels * 6),
        name="recur",
    )(u, border, off, taps, recall_w, admit_w, soft, own)


def mix_body(
    count, blocks, local, cum, v, x, entries, w, states, mixed, x2, own, gx, gy, gd, q0, q1, q2, q3, r3, rx, ry, send, recv
):
    i = pl.program_id(0)
    sems = (send, recv)
    scatter = scatter_messages(q1, q2, q3, r3, rx, ry, sems, 0)
    gather = gather_messages(own, gx, gy, gd, sems, 6)
    block = local.shape[0]
    width = x.shape[1]
    rows = x.shape[0]
    half = rows // 2

    @pl.when(i == 0)
    def _():
        greet()

    @pl.when(i < blocks)
    def _():
        entering = chain(entries, count)
        st = local[...] + cum[...] * entering
        states[...] = st
        m = (st * gelu_pair(v[...])[0]).astype(BF)
        mixed[...] = m
        at = pl.ds(pl.multiple_of(i * block, block), block)
        for j, q in ((3, q3), (1, q1), (2, q2), (0, q0)):
            q[at, :] = dot_nn(m, w[:, j * width : (j + 1) * width]).astype(q.dtype)

    @pl.when(i == blocks // 2 - 1)
    def _():
        scatter[0].start()
        scatter[2].start()

    @pl.when(i == blocks - 1)
    def _():
        scatter[1].start()

    @pl.when(i == blocks)
    def _():
        scatter[0].wait_recv()
        add_into(q2, r3, 0, half)
        scatter[3].start()
        scatter[4].start()
        scatter[1].wait_recv()
        add_into(q1, r3, half, half)
        scatter[5].start()
        for base, first in ((0, 2), (half, 4)):
            scatter[first].wait_recv()
            scatter[first + 1].wait_recv()
            for r in range(base, base + half, 128):
                at = slice(r, r + 128)
                total = x[at, :] + q0[at, :] + rx[at, :].astype(F32) + ry[at, :].astype(F32)
                x2[at, :] = total
                own[at, :] = total.astype(BF)
            start = 0 if base == 0 else 2
            gather[start].start()
            gather[start + 1].start()
        gather[0].wait_recv()
        gather[4].start()
        gather[3].wait_recv()
        gather[5].start()
        for n in (1, 2, 4, 5):
            gather[n].wait_recv()
        for m in scatter + gather:
            m.wait_send()


def mix(local, cum, v, x, entries, w):
    rows, channels = v.shape
    width = w.shape[1] // 4
    block = ROW_BLOCK
    blocks = rows // block
    held = functools.partial(held_spec, block, last=blocks - 1)
    chunk = pltpu.VMEM((rows, width), BF)
    return pl.pallas_call(
        functools.partial(mix_body, entries.shape[0] // 8, blocks),
        grid=(blocks + 1,),
        in_specs=[held(channels)] * 3
        + [whole_spec(x.shape), whole_spec(entries.shape), whole_spec(w.shape)],
        out_specs=[held(channels)] * 2 + [full_spec((rows, width))] * 2 + [any_spec()] * 3,
        out_shape=[sds((rows, channels), F32), sds((rows, channels), BF), sds((rows, width), F32)]
        + [sds((rows, width), BF)] * 4,
        scratch_shapes=[pltpu.VMEM((rows, width), F32)]
        + [chunk] * 6
        + [pltpu.SemaphoreType.DMA((12,))] * 2,
        compiler_params=comm_params(2),
        cost_estimate=cost(40 * rows * w.size, rows * channels * 18 + nbytes(w)),
        name="mix",
    )(local, cum, v, x, entries, w)


def feed_body(blocks, *refs):
    (x0, x1, x2, x3, e0, e1, e2, e3, mid, cot, gain, near, far, wd) = refs[:14]
    outs = refs[14:18]
    (dx, own, gx, gy, gd, gain_grad, s_down, s_gu) = refs[18:26]
    (wgu, load, n2, hid, ee, err, scale, stage, c_down, c_gu) = refs[26:36]
    (q0, q1, q2, q3, r3, rx, ry, dots, dots_x, dots_y, send, recv) = refs[36:]
    i = pl.program_id(0)
    sems = (send, recv)
    scatter = scatter_messages(q1, q2, q3, r3, rx, ry, sems, 0)
    gather = gather_messages(own, gx, gy, gd, sems, 6)
    small_x = message(dots, dots_x, neighbour_x(), sems, 12)
    small_y = message(dots_x, dots_y, neighbour_y(), sems, 13)
    block, width = x0.shape
    rows = mid.shape[0]
    half = rows // 2
    units = hid.shape[1]

    @pl.when(i == 0)
    def _():
        copies = load_rows(near, far, wgu, load)
        greet_all((neighbour_x(), neighbour_y(), neighbour_core()))
        for c in copies:
            c.wait()

    @pl.when(i < blocks)
    def _():
        at = pl.ds(pl.multiple_of(i * block, block), block)
        parts = [r[...].astype(F32) for r in (x0, x1, x2, x3)]
        total = sum(jnp.sum(p * p, axis=1, keepdims=True) for p in parts)
        s = lax.rsqrt(total / D + EPSILON)
        scale[at, :] = s
        normed = [p * s * gain[1:2, j * width : (j + 1) * width] for j, p in enumerate(parts)]
        acc = None
        for j, n in enumerate(normed):
            term = dot_nn(n.astype(BF), wgu[j * width : (j + 1) * width, :])
            acc = term if acc is None else acc + term
        errs = [r[...] for r in (e0, e1, e2, e3)]
        wide = [e.astype(F32) for e in errs]
        for source, target in ((normed, n2), (wide, ee)):
            for j in (0, 1):
                k, p = pair_up(source[2 * j], source[2 * j + 1])
                target[at, j * width : (j + 1) * width] = k.astype(BF)
                target[at, (j + 2) * width : (j + 3) * width] = p.astype(BF)
        pre, up = acc[:, :units], acc[:, units:]
        act, slope = gelu_pair(pre)
        h = (act * up).astype(BF)
        hid[at, :] = h
        dh = None
        for j, e in enumerate(errs):
            term = dot_nt(e, wd[:, j * width : (j + 1) * width])
            dh = term if dh is None else dh + term
        g = (dh * up * slope).astype(BF)
        b = (dh * act).astype(BF)
        err[at, :units] = g
        err[at, units:] = b
        dots[:, at] = row_sums(g.astype(F32) * pre + b.astype(F32) * up)
        for j, q in ((3, q3), (1, q1), (2, q2), (0, q0)):
            rows_w = slice(j * width, (j + 1) * width)
            q[at, :] = (dot_nt(g, wgu[rows_w, :units]) + dot_nt(b, wgu[rows_w, units:])).astype(q.dtype)
        for j, q in enumerate(outs):
            q[...] = dot_nn(h, wd[:, j * width : (j + 1) * width]).astype(q.dtype)

    @pl.when(i == blocks // 2 - 1)
    def _():
        scatter[0].start()
        scatter[2].start()

    @pl.when(i == blocks - 1)
    def _():
        scatter[1].start()
        small_x.start()

    @pl.when(i == blocks)
    def _():
        scatter[0].wait_recv()
        add_into(q2, r3, 0, half)
        scatter[3].start()
        scatter[4].start()
        small_x.wait_recv()
        dots_x[...] = dots_x[...] + dots[...]
        small_y.start()

    @pl.when(i == blocks + 1)
    def _():
        scatter[1].wait_recv()
        add_into(q1, r3, half, half)
        scatter[5].start()

    def finish(base, first, start):
        scatter[first].wait_recv()
        scatter[first + 1].wait_recv()
        sum_grad = None
        for r in range(base, base + half, 128):
            at = slice(r, r + 128)
            d = q0[at, :] + rx[at, :].astype(F32) + ry[at, :].astype(F32)
            s, m = scale[at, :], mid[at, :]
            t = as_column(dots_x[:, at] + dots_y[:, at], width)
            new = cot[at, :] + s * own_gain * d - m * (s * s) * t * (1.0 / D)
            dx[at, :] = new
            own[at, :] = new.astype(BF)
            term = jnp.sum(d * m * s, axis=0, keepdims=True)
            sum_grad = term if sum_grad is None else sum_grad + term
        gather[start].start()
        gather[start + 1].start()
        return sum_grad

    own_gain = gain[1:2, :width]

    @pl.when(i == blocks + 2)
    def _():
        small_y.wait_recv()
        gain_grad[0:1, :] = finish(0, 2, 0)

    @pl.when(i == blocks + 4)
    def _():
        gain_grad[0:1, :] = gain_grad[0:1, :] + finish(half, 4, 2)

    @pl.when(i == blocks + 5)
    def _():
        gather[0].wait_recv()
        gather[4].start()

    @pl.when(i == blocks + 6)
    def _():
        gather[3].wait_recv()
        gather[5].start()

    tiles = units // width
    to_core = [
        message(stage, c_gu.at[pl.ds(n * width, width), :], neighbour_core(), sems, 14 + n) for n in (0, 1)
    ] + [
        message(
            stage.at[:, pl.ds(n * 2 * width, 2 * width)],
            c_down.at[pl.ds(n * width, width), :],
            neighbour_core(),
            sems,
            16 + n,
        )
        for n in range(tiles)
    ]

    def gu_tile(n):
        return dot_tn(n2[:, n * width : (n + 1) * width], err[...])

    for n in (0, 1):

        @pl.when(i == blocks + n)
        def _():
            g = gu_tile(2 + n).astype(BF)
            if n:
                to_core[0].wait_send()
            stage[...] = g
            to_core[n].start()

    for n in range(tiles):

        @pl.when(i == blocks + 2 + n)
        def _():
            at = slice(n * width, (n + 1) * width)
            g = dot_tn(hid[:, at], ee[...])
            if n == 0:
                to_core[1].wait_send()
            stage[:, n * 2 * width : (n + 1) * 2 * width] = g[:, 2 * width :].astype(BF)
            to_core[2 + n].start()
            s_down[at, :] = g[:, : 2 * width].astype(BF)

    for n in (1, 0):

        @pl.when(i == blocks + tiles + 3 - n)
        def _():
            to_core[n].wait_recv()
            at = slice(n * width, (n + 1) * width)
            s_gu[...] = (gu_tile(n) + c_gu[at, :].astype(F32)).astype(BF)

    @pl.when(i == blocks + tiles + 4)
    def _():
        for n in range(tiles):
            to_core[2 + n].wait_recv()
            to_core[2 + n].wait_send()
        plus_in(s_down, c_down)
        for n in (1, 2, 4, 5):
            gather[n].wait_recv()
        for m in scatter + gather + [small_x, small_y]:
            m.wait_send()


def feed(chunks, errs, mid, cot, gain, near, far, wd):
    rows, width = chunks[0].shape
    units = wd.shape[0]
    block = ROW_BLOCK
    blocks = rows // block
    tiles = units // width
    held = functools.partial(held_spec, block, last=blocks - 1)
    chunk = pltpu.VMEM((rows, width), BF)
    lanes = pltpu.VMEM((8, rows), F32)
    gu_spec = pl.BlockSpec((width, 2 * units), lambda i: (jnp.where(i >= blocks + tiles + 3, 0, 1), 0))
    return pl.pallas_call(
        functools.partial(feed_body, blocks),
        grid=(blocks + tiles + 5,),
        in_specs=[held(width)] * 8
        + [whole_spec(mid.shape), whole_spec(cot.shape), whole_spec(gain.shape)]
        + [any_spec(), any_spec(), whole_spec(wd.shape)],
        out_specs=[held(width)] * 4
        + [whole_spec((rows, width))] * 2
        + [any_spec()] * 3
        + [whole_spec((8, width)), whole_spec((units, 2 * width)), gu_spec],
        out_shape=[sds((rows, width), F32)]
        + [sds((rows, width), BF)] * 3
        + [sds((rows, width), F32)]
        + [sds((rows, width), BF)] * 4
        + [sds((8, width), F32), sds((units, 2 * width), BF), sds((2 * width, 2 * units), BF)],
        scratch_shapes=[
            pltpu.VMEM((4 * width, 2 * units), BF),
            pltpu.SemaphoreType.DMA((8,)),
            pltpu.VMEM((rows, 4 * width), BF),
            pltpu.VMEM((rows, units), BF),
            pltpu.VMEM((rows, 4 * width), BF),
            pltpu.VMEM((rows, 2 * units), BF),
            pltpu.VMEM((rows, 1), F32),
            pltpu.VMEM((width, 2 * units), BF),
            pltpu.VMEM((units, 2 * width), BF),
            pltpu.VMEM((2 * width, 2 * units), BF),
            pltpu.VMEM((rows, width), F32),
        ]
        + [chunk] * 6
        + [lanes] * 3
        + [pltpu.SemaphoreType.DMA((16 + tiles,))] * 2,
        compiler_params=comm_params(3),
        cost_estimate=cost(48 * rows * wd.size, 3 * nbytes(wd) + rows * 30000, rows * units),
        name="feed",
    )(*chunks, *errs, mid, cot, gain, near, far, wd)


def carried(entries, h, count):
    state = entries[count - 1, h, 1:2, :]
    for n in range(count - 2, -1, -1):
        state = entries[n, h, 1:2, :] + entries[n, h, 0:1, :] * state
    return state


def back_body(heads, blocks, count, *refs):
    errs = refs[0:4]
    (w_out, states, branch, recall, conv, admit, u_head, off, soft) = refs[4:13]
    (taps, recall_w, admit_w, border, earlier, u, v, near, far, scale, x, dx, gain) = refs[13:26]
    (sum_gu, sum_down) = refs[26:28]
    (ev, paired, eu, grad, gain_grad, grad_recall, grad_admit, grad_small) = refs[28:36]
    (mine_gu, far_gu, mine_down, far_down) = refs[36:40]
    (part, reach, ext, st, uext, dc, ends, later, edge, from_later, w, load) = refs[40:52]
    (q0, q1, q2, q3, r3, rx, ry, dots, dots_x, dots_y) = refs[52:62]
    (s_gu, a_gu, b_gu, s_dn, a_dn, b_dn, store, send, recv) = refs[62:]
    i = pl.program_id(0)
    sems = (send, recv)
    seq = lax.axis_index("seq")
    rows, width = x.shape
    half = rows // 2
    step = ROW_BLOCK
    seg = rows // 8
    channels = heads * 128
    block = step

    scatter = scatter_messages(q1, q2, q3, r3, rx, ry, sems, 0)
    small_x = message(dots, dots_x, neighbour_x(), sems, 6)
    small_y = message(dots_x, dots_y, neighbour_y(), sems, 7)
    hand_on = [message(ends, later.at[n - 1], {"seq": seq - n}, sems, 7 + n) for n in range(1, count + 1)]
    base = 8 + count
    hand_edge = message(edge, from_later, {"seq": seq - 1}, sems, base)
    base += 1

    rows_gu, rows_dn = width // 4, sum_down.shape[0] // 2
    group_gu, group_dn = (s_gu, a_gu, b_gu), (s_dn, a_dn, b_dn)

    def gu_at(n):
        return pl.ds(n * rows_gu, rows_gu)

    def dn_at(n):
        return pl.ds(n * rows_dn, rows_dn)

    places = [("gu", n) for n in (4, 5, 6, 7)] + [("far", n) for n in (0, 1)]
    places += [("own", n) for n in (0, 1)] + [("gu", n) for n in (0, 1, 2, 3)]

    def view(kind, n, ref):
        if kind == "gu":
            return ref.at[gu_at(n), :]
        return ref.at[dn_at(n), pl.ds(width if kind == "far" else 0, width)]

    pieces = [
        [view(kind, n, r) for r in (group_gu if kind == "gu" else group_dn)] for kind, n in places
    ]
    total = SeqSum(pieces, sems, base)
    base += 2 * len(pieces)
    to_y, to_out = {}, {}
    for p, (kind, n) in enumerate(places):
        source = pieces[p][0]
        if kind == "far":
            to_y[p] = message(source, far_down.at[dn_at(n), :], neighbour_y(), sems, base + len(to_y))
        elif kind == "own":
            to_out[p] = pltpu.make_async_copy(source, mine_down.at[dn_at(n), :], store.at[len(to_out)])
        elif n >= 4:
            to_y[p] = message(source, far_gu.at[gu_at(n - 4), :], neighbour_y(), sems, base + len(to_y))
        else:
            to_out[p] = pltpu.make_async_copy(source, mine_gu.at[gu_at(n), :], store.at[len(to_out)])
    loads = [
        pltpu.make_async_copy(sum_gu, s_gu, load.at[8]),
        pltpu.make_async_copy(sum_down, s_dn, load.at[9]),
    ]

    def tick(t):
        if t + 2 < len(pieces):
            total.begin(t + 2)
        if t < len(pieces):
            total.relay(t)
        if 0 <= t - 1 < len(pieces):
            total.settle(t - 1)
        if 0 <= t - 2 < len(pieces):
            total.finish(t - 2)
            if t - 2 in to_y:
                to_y[t - 2].start()
            else:
                to_out[t - 2].start()

    @pl.when(i == 0)
    def _():
        for c in loads:
            c.start()
        copies = load_rows(near, far, w, load)
        later[...] = jnp.zeros_like(later)
        from_later[...] = jnp.zeros_like(from_later)
        greet_all(
            [neighbour_x(), neighbour_y()]
            + [{"seq": lax.rem(seq + n, count + 1)} for n in range(1, count + 1)]
        )
        for c in loads + copies:
            c.wait()
        total.begin(0)
        total.begin(1)
        for r in range(0, rows, step):
            at = slice(r, r + step)
            for j in (0, 1):
                k, p = pair_up(errs[2 * j][at, :].astype(F32), errs[2 * j + 1][at, :].astype(F32))
                paired[at, j * width : (j + 1) * width] = k.astype(BF)
                paired[at, (j + 2) * width : (j + 3) * width] = p.astype(BF)

    @pl.when(i < heads)
    def _():
        sp = soft[0:1, :]
        part_h, reach_h = part.at[i], reach.at[i]
        lane = pl.ds(pl.multiple_of(i * 128, 128), 128)
        for r in range(0, rows, step):
            at = slice(r, r + step)
            o = off[8 + r : 8 + r + step, :]
            ext[at, :] = jnp.where(o > 0, jnp.exp(-8.0 * recall[at, :] * sp), 0.0)
            dm = None
            for j in range(4):
                term = dot_nt(errs[j][at, :], w_out[:, j * width : (j + 1) * width])
                dm = term if dm is None else dm + term
            act, slope = gelu_pair(branch[at, :])
            ev[at, lane] = (dm * states[at, :] * slope).astype(BF)
            part_h[at, :] = dm * act
        ext[rows : rows + 8, :] = jnp.ones((8, 128), F32)
        for r in range(0, rows, step):
            reach_h[r : r + step, :] = ext[r + 1 : r + 1 + step, :]

        def one(n, carry):
            h, p = carry
            at = pl.ds(seg - 1 - n, 8, stride=seg)
            d = reach_h[at, :]
            h = d * h + part_h[at, :]
            p = d * p
            part_h[at, :] = h
            reach_h[at, :] = p
            return h, p

        zero = jnp.zeros((8, 128), F32)
        h, p = lax.fori_loop(0, seg, one, (zero, zero + 1.0), unroll=8)
        carry_h, carry_p = h[7:8, :], p[7:8, :]
        for s in range(6, -1, -1):
            at = slice(s * seg, (s + 1) * seg)
            c = reach_h[at, :]
            part_h[at, :] = part_h[at, :] + c * carry_h
            reach_h[at, :] = c * carry_p
            carry_h = h[s : s + 1, :] + p[s : s + 1, :] * carry_h
            carry_p = p[s : s + 1, :] * carry_p
        first = ext[0:1, :]
        ends[i, 0:1, :] = first * carry_p
        ends[i, 1:2, :] = first * carry_h
        ends[i, 2:8, :] = jnp.zeros((6, 128), F32)

    for n in range(1, count + 1):

        @pl.when((i == heads - 1) & (seq >= n))
        def _():
            hand_on[n - 1].start()

        @pl.when((i == heads) & (seq <= count - n))
        def _():
            hand_on[n - 1].wait_recv()

    @pl.when((i >= heads) & (i < 2 * heads))
    def _():
        h = i - heads
        part_h, reach_h = part.at[h], reach.at[h]
        st[0:8, :] = jnp.broadcast_to(chain(earlier, count), (8, 128))
        st[8 : 8 + rows, :] = states[...]
        uext[0:8, :] = border[...]
        uext[8 : 8 + rows, :] = u_head[...]
        incoming = carried(later, h, count)
        sp = soft[0:1, :]
        dc[0:8, :] = jnp.zeros((8, 128), F32)
        dc[8 + rows : 16 + rows, :] = jnp.zeros((8, 128), F32)
        gr = ga = None
        sums = [None] * (KW + 1)

        def plus(total, term):
            return term if total is None else total + term

        for r in range(0, rows, step):
            at = slice(r, r + step)
            o = off[8 + r : 8 + r + step, :]
            adj = part_h[at, :] + reach_h[at, :] * incoming
            rec, adm, cv = recall[at, :], admit[at, :], conv[at, :]
            ell = -8.0 * rec * sp
            e = jnp.exp(ell)
            m = jnp.sqrt(minus_expm1(2.0 * ell))
            previous = jnp.where(o > 0, e * st[7 + r : 7 + r + step, :], 0.0)
            ac = adj * cv
            d_ell = adj * previous - ac * adm * (e * e) / m
            d_rp = -8.0 * sp * d_ell * rec * (1.0 - rec)
            d_ip = ac * m * adm * (1.0 - adm)
            d_conv = (
                adj * m * adm
                + dot_nt(d_rp, recall_w[0], PRECISE)
                + dot_nt(d_ip, admit_w[0], PRECISE)
            )
            dc[8 + r : 8 + r + step, :] = d_conv
            gr = plus(gr, dot_tn(cv, d_rp, PRECISE))
            ga = plus(ga, dot_tn(cv, d_ip, PRECISE))
            for k in range(KW):
                term = d_conv * uext[8 + r - k : 8 + r - k + step, :]
                if k:
                    term = jnp.where(o >= k, term, 0.0)
                sums[k] = plus(sums[k], jnp.sum(term, axis=0, keepdims=True))
            sums[KW] = plus(sums[KW], jnp.sum(rec * d_ell, axis=0, keepdims=True))
        grad_recall[0] = gr
        grad_admit[0] = ga
        for k in range(KW + 1):
            grad_small[k : k + 1, :] = sums[k]
        grad_small[KW + 1 : 8, :] = jnp.zeros((7 - KW, 128), F32)
        for r in range(0, rows, step):
            du = taps[0:1, :] * dc[8 + r : 8 + r + step, :]
            for k in range(1, KW):
                o = off[8 + r + k : 8 + r + k + step, :]
                term = taps[k : k + 1, :] * dc[8 + r + k : 8 + r + k + step, :]
                du = du + jnp.where(o >= k, term, 0.0)
            part_h[r : r + step, :] = du
        over = jnp.zeros((8, 128), F32)
        for k in range(1, KW):
            term = taps[k : k + 1, :] * dc[k : k + 8, :]
            over = over + jnp.where(off[k : k + 8, :] >= k, term, 0.0)
        edge[h] = over

    @pl.when((i == 2 * heads - 1) & (seq >= 1))
    def _():
        hand_edge.start()

    @pl.when((i == 2 * heads) & (seq < count))
    def _():
        hand_edge.wait_recv()

    third = 2 * heads

    @pl.when((i >= third) & (i < third + blocks))
    def _():
        at = pl.ds(pl.multiple_of((i - third) * block, block), block)
        d = jnp.concatenate([part[h, at, :] for h in range(heads)], axis=1)
        late = jnp.concatenate([from_later[h] for h in range(heads)], axis=1)
        extra = jnp.concatenate([jnp.zeros((block - 8, channels), F32), late], axis=0)
        d = d + jnp.where(i == third + blocks - 1, extra, 0.0)
        e = d.astype(BF)
        eu[...] = e
        b = ev[at, :]
        dots[:, at] = row_sums(e.astype(F32) * u[...] + b.astype(F32) * v[...])
        for j, q in ((3, q3), (1, q1), (2, q2), (0, q0)):
            rows_w = slice(j * width, (j + 1) * width)
            q[at, :] = (dot_nt(e, w[rows_w, :channels]) + dot_nt(b, w[rows_w, channels:])).astype(q.dtype)

    @pl.when(i == third + blocks // 2 - 1)
    def _():
        scatter[0].start()
        scatter[2].start()

    @pl.when(i == third + blocks - 1)
    def _():
        scatter[1].start()
        small_x.start()
        scatter[0].wait_recv()
        add_into(q2, r3, 0, half)
        scatter[3].start()
        scatter[4].start()

    last = third + blocks

    @pl.when(i == last)
    def _():
        small_x.wait_recv()
        dots_x[...] = dots_x[...] + dots[...]
        small_y.start()
        scatter[1].wait_recv()
        add_into(q1, r3, half, half)
        scatter[5].start()

    def finish(start, first):
        scatter[first].wait_recv()
        scatter[first + 1].wait_recv()
        sum_grad = None
        for r in range(start, start + half, 128):
            at = slice(r, r + 128)
            d = q0[at, :] + rx[at, :].astype(F32) + ry[at, :].astype(F32)
            s, m = scale[at, :], x[at, :]
            t = as_column(dots_x[:, at] + dots_y[:, at], width)
            grad[at, :] = dx[at, :] + s * gain[0:1, :width] * d - m * (s * s) * t * (1.0 / D)
            term = jnp.sum(d * m * s, axis=0, keepdims=True)
            sum_grad = term if sum_grad is None else sum_grad + term
        return sum_grad

    for t in range(len(pieces) + 2):

        @pl.when(i == t + 1)
        def _():
            tick(t)

    @pl.when(i == last + 1)
    def _():
        small_y.wait_recv()
        gain_grad[0:1, :] = finish(0, 2)

    @pl.when(i == last + 2)
    def _():
        gain_grad[0:1, :] = gain_grad[0:1, :] + finish(half, 4)
        for n in range(1, count + 1):

            @pl.when(seq >= n)
            def _():
                hand_on[n - 1].wait_send()

        @pl.when(seq >= 1)
        def _():
            hand_edge.wait_send()

        for m in to_y.values():
            m.wait_recv()
        for m in scatter + [small_x, small_y] + list(to_y.values()):
            m.wait_send()
        for c in to_out.values():
            c.wait()


def back(errs, w_out, states, v, recall, conv, admit, u, off, soft, taps, rw, aw, border, earlier, near, far, scale, x, dx, gain, sum_gu, sum_down):
    rows, channels = states.shape
    width = x.shape[1]
    heads = channels // 128
    block = ROW_BLOCK
    blocks = rows // block
    count = earlier.shape[0] // 8
    steps = 2 * heads + blocks + 3
    assert steps >= 15

    def both(i):
        return jnp.where(i < heads, i, jnp.clip(i - heads, 0, heads - 1))

    def second(i):
        return jnp.clip(i - heads, 0, heads - 1)

    def on(shape, pick, axis):
        if axis == 0:
            return pl.BlockSpec(shape, lambda i: (pick(i),) + (0,) * (len(shape) - 1))
        return pl.BlockSpec(shape, lambda i: (0, pick(i)))

    def third(i):
        return jnp.clip(i - 2 * heads, 0, blocks - 1)

    def first(i):
        return jnp.minimum(i, heads - 1)

    tall = (rows, 128)
    gate = (1, 128, 128)
    chunk = pltpu.VMEM((rows, width), BF)
    lanes = pltpu.VMEM((8, rows), F32)
    gu, dn = pltpu.VMEM(sum_gu.shape, BF), pltpu.VMEM(sum_down.shape, BF)
    piece = pltpu.VMEM((heads, 8, 128), F32)
    half_gu, half_dn = (sum_gu.shape[0] // 2, sum_gu.shape[1]), (sum_down.shape[0], width)
    count_sems = 8 + count + 1 + 24 + 6
    return pl.pallas_call(
        functools.partial(back_body, heads, blocks, count),
        grid=(steps,),
        in_specs=[whole_spec((rows, width))] * 4
        + [
            on((128, 4 * width), first, 0),
            on(tall, both, 1),
            on(tall, first, 1),
            on(tall, both, 1),
            on(tall, second, 1),
            on(tall, second, 1),
            on(tall, second, 1),
            whole_spec(off.shape),
            on((1, 128), both, 1),
            on((KW, 128), second, 1),
            on(gate, second, 0),
            on(gate, second, 0),
            on((8, 128), second, 1),
            on((8 * count, 128), second, 1),
            on((block, channels), third, 0),
            on((block, channels), third, 0),
            any_spec(),
            any_spec(),
            whole_spec(scale.shape),
            whole_spec(x.shape),
            whole_spec(dx.shape),
            whole_spec(gain.shape),
            any_spec(),
            any_spec(),
        ],
        out_specs=[
            whole_spec((rows, channels)),
            whole_spec((rows, 4 * width)),
            on((block, channels), third, 0),
            whole_spec((rows, width)),
            whole_spec((8, width)),
            on(gate, second, 0),
            on(gate, second, 0),
            on((8, 128), second, 1),
        ]
        + [any_spec()] * 4,
        out_shape=[
            sds((rows, channels), BF),
            sds((rows, 4 * width), BF),
            sds((rows, channels), BF),
            sds((rows, width), F32),
            sds((8, width), F32),
            sds((heads, 128, 128), F32),
            sds((heads, 128, 128), F32),
            sds((8, channels), F32),
            sds(half_gu, BF),
            sds(half_gu, BF),
            sds(half_dn, BF),
            sds(half_dn, BF),
        ],
        scratch_shapes=[pltpu.VMEM((heads, rows, 128), F32)] * 2
        + [
            pltpu.VMEM((rows + 8, 128), F32),
            pltpu.VMEM((rows + 8, 128), F32),
            pltpu.VMEM((rows + 8, 128), F32),
            pltpu.VMEM((rows + 16, 128), F32),
            piece,
            pltpu.VMEM((count, heads, 8, 128), F32),
            piece,
            piece,
            pltpu.VMEM((4 * width, 2 * channels), BF),
            pltpu.SemaphoreType.DMA((10,)),
            pltpu.VMEM((rows, width), F32),
        ]
        + [chunk] * 6
        + [lanes] * 3
        + [gu] * 3
        + [dn] * 3
        + [pltpu.SemaphoreType.DMA((6,))]
        + [pltpu.SemaphoreType.DMA((count_sems,))] * 2,
        compiler_params=comm_params(4),
        cost_estimate=cost(4 * rows * near.size * 16, rows * channels * 60, rows * channels * 8),
        name="back",
    )(
        *errs, w_out, states, v, recall, conv, admit, u, off, soft, taps, rw, aw, border, earlier,
        u, v, near, far, scale, x, dx, gain, sum_gu, sum_down,
    )


def tail_body(n1, eu, ev, mixed, er, small, mine_in, far_in, mine_out, far_out, small_out, *scratch):
    (s_in, p_in, c_in, a_in, b_in, y_in, s_out, p_out, c_out, a_out, b_out, y_out) = scratch[:12]
    (s_sm, c_sm, a_sm, b_sm, send, recv) = scratch[12:]
    sems = (send, recv)
    width = er.shape[1] // 4
    half = width // 2
    channels = eu.shape[1]
    greet_all((neighbour_core(), neighbour_y(), neighbour_end(), neighbour_middle()))
    half_rows = pl.ds(0, half)
    a, b = half_rows, pl.ds(half, half)
    c, d = pl.ds(2 * half, half), pl.ds(3 * half, half)
    inner = s_out.shape[0] // 2
    up, low = pl.ds(0, inner), pl.ds(inner, inner)
    lanes_far, lanes_own = pl.ds(width, width), pl.ds(0, width)
    group_in, group_out = (s_in, a_in, b_in), (s_out, a_out, b_out)
    pieces = [[s_sm, a_sm, b_sm]]
    pieces += [[r.at[at, lanes_far] for r in group_out] for at in (up, low)]
    pieces += [[r.at[at, lanes_own] for r in group_out] for at in (up, low)]
    pieces += [[r.at[at, :] for r in group_in] for at in (c, d, a, b)]
    count = len(pieces)
    total = SeqSum(pieces, sems, 0)
    base = 2 * count
    core_sm = message(small, c_sm, neighbour_core(), sems, base)
    core_out = message(p_out, c_out, neighbour_core(), sems, base + 1)
    core_in = [
        message(p_in.at[at, :], c_in.at[at, :], neighbour_core(), sems, base + 2 + n)
        for n, at in enumerate((c, d, a, b))
    ]
    to_y = {
        1: message(s_out.at[up, lanes_far], y_out.at[up, :], neighbour_y(), sems, base + 6),
        2: message(s_out.at[low, lanes_far], y_out.at[low, :], neighbour_y(), sems, base + 7),
        5: message(s_in.at[c, :], y_in.at[a, :], neighbour_y(), sems, base + 8),
        6: message(s_in.at[d, :], y_in.at[b, :], neighbour_y(), sems, base + 9),
    }

    core_sm.start()
    g = dot_tn(mixed[...], er[...])
    p_out[...] = g[:, 2 * width :].astype(BF)
    core_out.start()
    s_out[...] = g[:, : 2 * width].astype(BF)
    s_sm[...] = small[...]

    def tile(n, target, row):
        at = slice(n * width, (n + 1) * width)
        where = slice(row, row + width)
        target[where, :channels] = dot_tn(n1[:, at], eu[...]).astype(BF)
        target[where, channels:] = dot_tn(n1[:, at], ev[...]).astype(BF)

    core_sm.wait_recv()
    plus_in(s_sm, c_sm)
    total.begin(0)
    tile(3, p_in, width)
    core_in[0].start()
    core_in[1].start()
    core_out.wait_recv()
    plus_in(s_out, c_out)
    for n in range(1, 5):
        total.begin(n)
    tile(1, s_in, width)
    tile(2, p_in, 0)
    core_in[2].start()
    core_in[3].start()
    core_in[0].wait_recv()
    core_in[1].wait_recv()
    plus_in(s_in.at[pl.ds(width, width), :], c_in.at[pl.ds(width, width), :])
    total.begin(5)
    total.begin(6)
    total.relay(0)
    total.relay(1)
    total.settle(0)
    tile(0, s_in, 0)
    core_in[2].wait_recv()
    core_in[3].wait_recv()
    plus_in(s_in.at[pl.ds(0, width), :], c_in.at[pl.ds(0, width), :])
    total.begin(7)
    total.begin(8)
    for n in range(2, count + 2):
        if n < count:
            total.relay(n)
        if n - 1 < count:
            total.settle(n - 1)
        total.finish(n - 2)
        if n - 2 in to_y:
            to_y[n - 2].start()
    put_in(small_out, s_sm)
    put_in(mine_in, s_in.at[pl.ds(0, width), :])
    put_in(mine_out, s_out.at[:, lanes_own])
    for m in to_y.values():
        m.wait_recv()
    put_in(far_out, y_out)
    put_in(far_in, y_in)
    for m in [core_sm, core_out] + core_in + list(to_y.values()):
        m.wait_send()


def tail(n1, eu, ev, mixed, er, small):
    rows, channels = eu.shape
    width = er.shape[1] // 4
    inner = mixed.shape[1]
    big = pltpu.VMEM((2 * width, 2 * channels), BF)
    tall = pltpu.VMEM((inner, 2 * width), BF)
    tiny = pltpu.VMEM(small.shape, F32)
    quarter_in, quarter_out = (width, 2 * channels), (inner, width)
    return pl.pallas_call(
        tail_body,
        out_shape=[sds(quarter_in, BF)] * 2 + [sds(quarter_out, BF)] * 2 + [sds(small.shape, F32)],
        scratch_shapes=[big] * 5
        + [pltpu.VMEM(quarter_in, BF)]
        + [tall] * 5
        + [pltpu.VMEM(quarter_out, BF)]
        + [tiny] * 4
        + [pltpu.SemaphoreType.DMA((28,))] * 2,
        compiler_params=pltpu.CompilerParams(
            vmem_limit_bytes=VMEM_LIMIT, collective_id=6, has_side_effects=True
        ),
        cost_estimate=cost(20 * rows * n1.shape[1] * channels * 3, nbytes(n1, eu, ev, mixed, er)),
        name="tail",
    )(n1, eu, ev, mixed, er, small)


def local_fast(
    stream_in,
    cotangent,
    doc_lengths,
    mixer_gain,
    input_weight,
    branch_weight,
    filter_taps,
    recall_gate,
    admit_gate,
    decay_param,
    output_weight,
    feed_gain,
    gate_weight,
    up_weight,
    down_weight,
):
    tokens = stream_in.shape[1]
    half = tokens // 2
    count = lax.axis_size("seq")
    part = stream_in.shape[2]
    seq = lax.axis_index("seq")
    row = lax.axis_index("row")
    col = lax.axis_index("col")
    y, core = col // 2, col % 2
    lower = row == 0

    def own_and_other(a, pick, axis):
        size = a.shape[axis] // 2
        return (
            lax.dynamic_slice_in_dim(a, pick * size, size, axis),
            lax.dynamic_slice_in_dim(a, (1 - pick) * size, size, axis),
        )

    def by_core(a):
        own, other = own_and_other(a, core, 0)
        return jnp.concatenate([own[0], flip_core(other)[0]], axis=1)

    def in_halves(a):
        return (a[:half], a[half:])

    gains = jnp.stack([mixer_gain, feed_gain])
    gains = jnp.concatenate([gains, flip_core(gains)], axis=1)
    gains_x = flip_row(gains)
    gains_y = flip_y(gains)
    gains_all = jnp.concatenate([gains, gains_x, gains_y, flip_y(gains_x)], axis=1)

    x = by_core(stream_in)
    g = by_core(cotangent)

    def with_core(own, far):
        near = jnp.stack([own, far])
        return near, flip_core(near)

    own_in, other_in = own_and_other(jnp.stack([input_weight, branch_weight]), y, 2)
    far_in = flip_y(other_in)
    near_in, sib_in = with_core(
        jnp.concatenate([own_in[0], own_in[1]], axis=1), jnp.concatenate([far_in[0], far_in[1]], axis=1)
    )

    lanes = 2 * part
    share = gate_weight.shape[0] // count
    units = gate_weight.shape[1] // 2

    def other_share(w, axis):
        rows = w.shape[0] // (2 if axis == 0 else 1)
        take = rows // count
        start = seq * take + ((1 - y) * rows if axis == 0 else 0)
        if axis == 0:
            return lax.dynamic_slice(w, (start, 0), (take, w.shape[1]))
        cols = w.shape[1] // 2
        piece = lax.dynamic_slice(w, (start, (1 - y) * cols), (take, cols))
        return jnp.concatenate([piece[:, n : n + lanes] for n in range(0, cols, lanes)], axis=0)

    packed = jnp.concatenate(
        [
            other_share(gate_weight, 1),
            other_share(up_weight, 1),
            other_share(down_weight, 0),
            other_share(output_weight, 0),
        ],
        axis=0,
    )
    packed = lax.all_gather(flip_y(packed), "seq", axis=0)

    def late_weights(packed, gate_weight, up_weight, down_weight, output_weight):
        def wide(at):
            blocks = packed[:, at : at + share * (units // lanes)].reshape(count, units // lanes, share, lanes)
            return blocks.transpose(0, 2, 1, 3).reshape(count * share, units)

        step = share * (units // lanes)
        far_gu = jnp.concatenate([wide(0), wide(step)], axis=1)
        own_gu = jnp.concatenate(
            [own_and_other(gate_weight, y, 1)[0], own_and_other(up_weight, y, 1)[0]], axis=1
        )
        near_gu, sib_gu = with_core(own_gu, far_gu)
        d_rows = down_weight.shape[0] // 2
        o_rows = output_weight.shape[0] // 2
        at = 2 * step
        far_d = packed[:, at : at + d_rows // count].reshape(d_rows, lanes)
        at += d_rows // count
        far_o = packed[:, at : at + o_rows // count].reshape(o_rows, lanes)
        own_do = jnp.concatenate(
            [own_and_other(output_weight, y, 0)[0], own_and_other(down_weight, y, 0)[0]], axis=0
        )
        near, sib = with_core(own_do, jnp.concatenate([far_o, far_d], axis=0))
        chunks = []
        for dy in (0, 1):
            first = jnp.concatenate([near[dy][:, :part], sib[dy][:, :part]], axis=1)
            second = jnp.concatenate([near[dy][:, part:], sib[dy][:, part:]], axis=1)
            chunks += [jnp.where(lower, first, second), jnp.where(lower, second, first)]
        both = jnp.concatenate(chunks, axis=1)
        return near_gu, sib_gu, both[:o_rows], both[o_rows:]

    heads = recall_gate.shape[0] // 2
    rw = lax.dynamic_slice_in_dim(recall_gate, y * heads, heads, 0)
    aw = lax.dynamic_slice_in_dim(admit_gate, y * heads, heads, 0)
    small = jnp.concatenate([filter_taps, decay_param[None], jnp.zeros((3,) + decay_param.shape, F32)])
    sibling = flip_core(small)
    small = jnp.where(
        core == 0,
        jnp.concatenate([small, sibling], axis=1),
        jnp.concatenate([sibling, small], axis=1),
    )
    taps, decay = small[:KW], small[KW : KW + 1]
    soft = jax.nn.softplus(-decay)

    lengths = lax.dynamic_index_in_dim(doc_lengths, core, 0, False)
    offset = doc_offset(lengths, seq * tokens, tokens)
    edge = jnp.full((8,), -1, jnp.int32)
    off = jnp.concatenate([edge, offset, edge])[:, None]

    def neighbours(ends, sign):
        return jnp.concatenate([shifted(ends, sign * n) for n in range(1, count)], axis=0)

    n1, u, v, s1 = norm_uv(x.astype(BF), gains_all, near_in, sib_in)
    border = shifted(u[tokens - 8 :], 1)
    g_low = g.astype(BF)
    conv, recall, admit, local_state, cum, ends, *errs = recur(
        u, border, off, taps, rw, aw, soft, g_low
    )
    late = lax.optimization_barrier(
        (ends, packed, gate_weight, up_weight, down_weight, output_weight)
    )
    near_gu, sib_gu, w_out, w_down = late_weights(*late[1:])
    earlier = neighbours(ends, 1)
    states, mixed, mid, *mid_all = mix(local_state, cum, v, x, earlier, w_out)
    p0, p1, p2, p3, dx2, *dx_all, grad_feed, sum_down, sum_gu = feed(
        mid_all, [g_low] + errs, mid, g, gains_all, near_gu, sib_gu, w_down
    )
    outs = collect(tuple(zip(*(in_halves(p) for p in (p0, p1, p2, p3)))))
    out_chunk = jnp.concatenate(outs, axis=0) + mid

    (
        ev, er, eu, grad_chunk, grad_mixer, grad_recall, grad_admit, grad_small, mine_gu, far_gu, mine_down, far_down
    ) = back(
        dx_all, w_out, states, v, recall, conv, admit, u, off, soft, taps, rw, aw, border, earlier,
        near_in, sib_in, s1, x, dx2, gains_all, sum_gu, sum_down,
    )

    def rows_out(mine, theirs):
        wide = jnp.where(
            y == 0, jnp.concatenate([mine, theirs], axis=1), jnp.concatenate([theirs, mine], axis=1)
        )
        swapped = jnp.concatenate([wide[part:], wide[:part]], axis=0)
        return jnp.where(lower, wide, swapped).astype(F32)

    def cols_out(mine, theirs):
        tall = jnp.where(
            y == 0, jnp.concatenate([mine, theirs], axis=0), jnp.concatenate([theirs, mine], axis=0)
        )
        swapped = jnp.concatenate([tall[:, part:], tall[:, :part]], axis=1)
        return jnp.where(lower, tall, swapped).astype(F32)

    channels = taps.shape[1]
    own = channels // 2
    pieces = [
        grad_small[:KW].reshape(-1),
        grad_small[KW] * 8.0 * jax.nn.sigmoid(-decay[0]),
        grad_recall.reshape(-1),
        grad_admit.reshape(-1),
    ]
    gain_rows = jnp.stack([grad_mixer[0], grad_feed[0]])
    gain_rows = jnp.where(
        core == 0, gain_rows, jnp.concatenate([gain_rows[:, part:], gain_rows[:, :part]], axis=1)
    )
    pieces.append(gain_rows.reshape(-1))
    sizes = [p.size for p in pieces]
    flat = jnp.concatenate(pieces)
    flat = jnp.pad(flat, (0, -flat.size % 8192)).reshape(-1, 128)
    mine_in, far_in, mine_out, far_out, flat = tail(n1, eu, ev, mixed, er, flat)
    flat = flat.reshape(-1)
    cuts, at = [], 0
    for s in sizes:
        cuts.append(flat[at : at + s])
        at += s
    grad_down = cols_out(mine_down, far_down)
    grad_gate = rows_out(mine_gu[:, :units], far_gu[:, :units])
    grad_up = rows_out(mine_gu[:, units:], far_gu[:, units:])
    grad_output = cols_out(mine_out, far_out)
    grad_input = rows_out(mine_in[:, :channels], far_in[:, :channels])
    grad_branch = rows_out(mine_in[:, channels:], far_in[:, channels:])
    g_taps = lax.dynamic_slice_in_dim(cuts[0].reshape(KW, channels), core * own, own, 1)
    g_decay = lax.dynamic_slice_in_dim(cuts[1], core * own, own, 0)
    gates = jnp.stack([cuts[2].reshape(grad_recall.shape), cuts[3].reshape(grad_admit.shape)])
    far = flip_y(gates)
    gates = jnp.where(
        y == 0, jnp.concatenate([gates, far], axis=1), jnp.concatenate([far, gates], axis=1)
    )
    gain_grads = lax.dynamic_slice_in_dim(cuts[4].reshape(2, 2 * part), core * part, part, 1)

    def stacked(chunk):
        own, other = chunk[:, :part], flip_core(chunk[:, part:])
        return jnp.where(core == 0, jnp.stack([own, other]), jnp.stack([other, own]))

    return (
        stacked(out_chunk),
        stacked(grad_chunk),
        gain_grads[0],
        grad_input,
        grad_branch,
        g_taps,
        gates[0],
        gates[1],
        g_decay,
        grad_output,
        gain_grads[1],
        grad_gate,
        grad_up,
        grad_down,
    )


def solution(mesh):
    in_specs = (
        P(None, "seq", ("col", "row")),
        P(None, "seq", ("col", "row")),
        P(),
        P(("col", "row")),
        P("col", "row"),
        P("col", "row"),
        P(None, ("row", "col")),
        P("row", None, None),
        P("row", None, None),
        P(("row", "col")),
        P("row", "col"),
        P(("col", "row")),
        P("col", "row"),
        P("col", "row"),
        P("row", "col"),
    )
    out_specs = (
        P(None, "seq", ("col", "row")),
        P(None, "seq", ("col", "row")),
        P(("col", "row")),
        P("col", "row"),
        P("col", "row"),
        P(None, ("row", "col")),
        P("row", None, None),
        P("row", None, None),
        P(("row", "col")),
        P("row", "col"),
        P(("col", "row")),
        P("col", "row"),
        P("col", "row"),
        P("row", "col"),
    )
    plan = local_fast if dict(mesh.shape) == {"seq": 4, "row": 2, "col": 4} else local
    return jax.shard_map(plan, mesh=mesh, in_specs=in_specs, out_specs=out_specs, check_vma=False)
```

```python
import functools

import jax
import jax.numpy as jnp
from jax import lax
from jax.experimental import pallas as pl
from jax.experimental.pallas import tpu as pltpu
from jax.sharding import PartitionSpec as P

D = 1536
KW = 4


EPSILON = 1e-06
PRECISE = lax.Precision.HIGHEST
SUM_ROWS = (((0,), (0,)), ((), ()))
SUM_COLS = (((1,), (1,)), ((), ()))


def as_sent(value):
    return jax.tree.map(lambda a: a.astype(jnp.bfloat16) if a.dtype == jnp.float32 else a, value)


def passed_along(block, axis, distance):
    devices = range(lax.axis_size(axis))
    route = [(i - distance, i) for i in devices if i - distance in devices]
    return lax.ppermute(block, axis, route)


def entering_2(part, axis, combine, identity, reverse):
    count = lax.axis_size(axis)
    place = lax.axis_index(axis)
    ahead = count - 1 - place if reverse else place
    gathered = jax.tree.map(lambda a: lax.all_gather(a, axis), part)
    state = jax.tree.map(lambda a, e: jnp.zeros_like(a) + jnp.asarray(e, a.dtype), part, identity)

    def one(hop, state):
        source = count - 1 - hop if reverse else hop
        return combine(
            state, jax.tree.map(lambda a: lax.dynamic_index_in_dim(a, source, 0, False), gathered)
        )

    return lax.fori_loop(0, ahead, one, state)


def compose(first, second):
    return (first[0] * second[0], second[0] * first[1] + second[1])


def convolve(source, taps, offset, border):
    tokens = source.shape[0]
    extended = jnp.concatenate([border, source], axis=0)
    result = jnp.zeros_like(source)
    for lag_index in range(KW):
        anchor = KW - 1 - lag_index
        valid = (offset >= lag_index).astype(jnp.float32)[:, None]
        result = result + taps[lag_index] * extended[anchor : anchor + tokens] * valid
    return result


def slab_pre(conv_value, recall_value, admit_value):
    tokens = conv_value.shape[0]
    blocks = conv_value.reshape(tokens, recall_value.shape[0], recall_value.shape[1])
    recall_pre = jnp.einsum("thi,hij->thj", blocks, recall_value, precision=PRECISE).reshape(
        tokens, -1
    )
    admit_pre = jnp.einsum("thi,hij->thj", blocks, admit_value, precision=PRECISE).reshape(
        tokens, -1
    )
    return (recall_pre, admit_pre)


def own_terms(conv_value, recall_pre, admit_pre, decay_value, resume):
    recall = jax.nn.sigmoid(recall_pre)
    admit = jax.nn.sigmoid(admit_pre)
    log_decay = -8.0 * recall * jax.nn.softplus(-decay_value)
    decays = jnp.exp(log_decay) * resume[:, None]
    drives = jnp.sqrt(-jnp.expm1(2.0 * log_decay)) * admit * conv_value
    return (decays, drives)


def width_total(partial_value):
    return lax.psum(partial_value, ("row", "col"))


def gather_row(source):
    return lax.all_gather(source, "row", axis=1, tiled=True)


def gather_col(source):
    return jax.tree.map(
        lambda part, own: part.astype(own.dtype),
        lax.all_gather(as_sent(source), "col", axis=1, tiled=True),
        source,
    )


def scatter_col(source):
    return (
        lax.psum_scatter(source[0], "col", scatter_dimension=1, tiled=True),
        lax.psum_scatter(source[1], "col", scatter_dimension=1, tiled=True),
    )


def scatter_col_back(source):
    return lax.psum_scatter(source, "col", scatter_dimension=1, tiled=True)


def scatter_row(source):
    return lax.psum_scatter(source, "row", scatter_dimension=1, tiled=True)


def over_seq(grads):
    return (
        lax.psum(grads[0].astype(jnp.bfloat16), "seq").astype(jnp.float32),
        lax.psum(grads[1].astype(jnp.bfloat16), "seq").astype(jnp.float32),
        lax.psum(grads[2].astype(jnp.bfloat16), "seq").astype(jnp.float32),
        lax.psum(grads[3].astype(jnp.bfloat16), "seq").astype(jnp.float32),
        lax.psum(grads[4].astype(jnp.bfloat16), "seq").astype(jnp.float32),
        lax.psum(grads[5].astype(jnp.bfloat16), "seq").astype(jnp.float32),
        lax.psum(grads[6].astype(jnp.bfloat16), "seq").astype(jnp.float32),
        lax.psum(grads[7].astype(jnp.bfloat16), "seq").astype(jnp.float32),
        lax.psum(grads[8].astype(jnp.bfloat16), "seq").astype(jnp.float32),
        lax.psum(grads[9].astype(jnp.bfloat16), "seq").astype(jnp.float32),
        lax.psum(grads[10].astype(jnp.bfloat16), "seq").astype(jnp.float32),
        lax.psum(grads[11].astype(jnp.bfloat16), "seq").astype(jnp.float32),
    )


def normalize(source, scales):
    factor = lax.rsqrt(width_total(jnp.sum(source * source, axis=1)) / D + EPSILON)
    return (source * factor[:, None] * scales, factor)


def norm_back(source, scales, factor, grad_norm):
    weighted = scales * grad_norm
    summed = width_total(jnp.sum(weighted * source, axis=1))
    grad_source = (
        factor[:, None] * weighted - source * (factor * factor * factor * summed / D)[:, None]
    )
    grad_scales = jnp.sum(grad_norm * source * factor[:, None], axis=0)
    return (grad_source, grad_scales)


def doc_offset(lengths, anchor, tokens):
    starts = jnp.cumsum(lengths, dtype=jnp.int32) - lengths
    places = anchor + jnp.arange(tokens, dtype=jnp.int32)
    begins = jnp.max(jnp.where(starts[None, :] <= places[:, None], starts[None, :], 0), axis=1)
    return places - begins


def matmul_rows(left, right):
    return lax.dot_general(left, right, SUM_ROWS, preferred_element_type=jnp.float32)


def matmul_cols(left, right):
    return lax.dot_general(left, right, SUM_COLS, preferred_element_type=jnp.float32)


def local(
    stream_in,
    cotangent,
    doc_lengths,
    mixer_gain,
    input_weight,
    branch_weight,
    filter_taps,
    recall_gate,
    admit_gate,
    decay_param,
    output_weight,
    feed_gain,
    gate_weight,
    up_weight,
    down_weight,
):
    tokens = stream_in.shape[1]
    anchor = lax.axis_index("seq") * tokens
    channels = decay_param.shape[0]
    col_start = lax.axis_index("col") * channels
    params = (
        mixer_gain,
        input_weight,
        branch_weight,
        filter_taps,
        recall_gate,
        admit_gate,
        decay_param,
        output_weight,
        feed_gain,
        gate_weight,
        up_weight,
        down_weight,
    )
    totals = tuple((jnp.zeros(w.shape, jnp.float32) for w in params))
    identity = (jnp.ones_like(decay_param), jnp.zeros_like(decay_param))
    outputs = []
    grads_in = []
    for micro in range(stream_in.shape[0]):
        offset = doc_offset(doc_lengths[micro], anchor, tokens)
        resume = (offset > 0).astype(jnp.float32)
        source = stream_in[micro]
        normed, factor_one = normalize(source, mixer_gain)
        normed_low = normed.astype(jnp.bfloat16)
        normed_all = gather_row(normed_low)
        rec_in, branch = scatter_col(
            (
                jnp.dot(normed_all, input_weight, preferred_element_type=jnp.float32),
                jnp.dot(normed_all, branch_weight, preferred_element_type=jnp.float32),
            )
        )
        border = passed_along(rec_in[tokens - (KW - 1) :], "seq", 1)
        conv_out = convolve(rec_in, filter_taps, offset, border)
        conv_slab = lax.all_gather(conv_out, "col", axis=1, tiled=True)
        slab_values, slab_pull = jax.vjp(slab_pre, conv_slab, recall_gate, admit_gate)
        recall_pre = lax.dynamic_slice_in_dim(slab_values[0], col_start, channels, 1)
        admit_pre = lax.dynamic_slice_in_dim(slab_values[1], col_start, channels, 1)

        def local_gates(conv_value, recall_value, admit_value, decay_value):
            return own_terms(conv_value, recall_value, admit_value, decay_value, resume)

        (decays, drives), gates_pull = jax.vjp(
            local_gates, conv_out, recall_pre, admit_pre, decay_param
        )
        cum_decay, local_state = lax.associative_scan(compose, (decays, drives), axis=0)
        entering = entering_2((cum_decay[-1], local_state[-1]), "seq", compose, identity, False)[1]
        states = local_state + cum_decay * entering
        branch_act = jax.nn.gelu(branch)
        mixed_all = gather_col((states * branch_act).astype(jnp.bfloat16))
        middle = source + scatter_row(
            jnp.dot(mixed_all, output_weight, preferred_element_type=jnp.float32)
        )
        normed_two, factor_two = normalize(middle, feed_gain)
        normed_two_low = normed_two.astype(jnp.bfloat16)
        normed_two_all = gather_row(normed_two_low)
        gate_pre, up_pre = scatter_col(
            (
                jnp.dot(normed_two_all, gate_weight, preferred_element_type=jnp.float32),
                jnp.dot(normed_two_all, up_weight, preferred_element_type=jnp.float32),
            )
        )
        gate_act = jax.nn.gelu(gate_pre)
        hidden_all = gather_col((gate_act * up_pre).astype(jnp.bfloat16))
        outputs.append(
            middle
            + scatter_row(jnp.dot(hidden_all, down_weight, preferred_element_type=jnp.float32))
        )
        upstream = cotangent[micro]
        upstream_all = gather_row(upstream.astype(jnp.bfloat16))
        grad_down = matmul_rows(hidden_all, upstream_all)
        grad_hidden = scatter_col_back(matmul_cols(upstream_all, down_weight))
        gate_value, gelu_pull = jax.vjp(jax.nn.gelu, gate_pre)
        error_gate = gelu_pull(grad_hidden * up_pre)[0].astype(jnp.bfloat16)
        error_up = (grad_hidden * gate_act).astype(jnp.bfloat16)
        gate_err_all, up_err_all = gather_col((error_gate, error_up))
        grad_gate = matmul_rows(normed_two_all, gate_err_all)
        grad_up = matmul_rows(normed_two_all, up_err_all)
        grad_normed_two = scatter_row(
            matmul_cols(gate_err_all, gate_weight) + matmul_cols(up_err_all, up_weight)
        )
        back_middle, grad_feed = norm_back(middle, feed_gain, factor_two, grad_normed_two)
        grad_middle = upstream + back_middle
        rec_err_all = gather_row(grad_middle.astype(jnp.bfloat16))
        grad_output = matmul_rows(mixed_all, rec_err_all)
        grad_mixed = scatter_col_back(matmul_cols(rec_err_all, output_weight))
        branch_value, branch_pull = jax.vjp(jax.nn.gelu, branch)
        error_branch = branch_pull(grad_mixed * states)[0].astype(jnp.bfloat16)
        direct = grad_mixed * branch_act
        ahead = jnp.concatenate([decays[1:], jnp.ones_like(decays[:1])], axis=0)
        reach, partial_adj = lax.associative_scan(compose, (ahead, direct), axis=0, reverse=True)
        incoming = entering_2(
            (decays[0] * reach[0], decays[0] * partial_adj[0]), "seq", compose, identity, True
        )[1]
        adjoint = partial_adj + reach * incoming
        previous = jnp.concatenate([entering[None, :], states[:-1]], axis=0)
        conv_direct, grad_recall_pre, grad_admit_pre, grad_decay = gates_pull(
            (adjoint * previous, adjoint)
        )
        recall_all, admit_all = (
            lax.all_gather(grad_recall_pre.astype(jnp.bfloat16), "col", axis=1, tiled=True).astype(
                grad_recall_pre.dtype
            ),
            lax.all_gather(grad_admit_pre.astype(jnp.bfloat16), "col", axis=1, tiled=True).astype(
                grad_admit_pre.dtype
            ),
        )
        grad_slab, grad_recall, grad_admit = slab_pull((recall_all, admit_all))
        grad_conv_out = conv_direct + lax.dynamic_slice_in_dim(grad_slab, col_start, channels, 1)

        def local_conv(input_value, taps_value, border_value):
            return convolve(input_value, taps_value, offset, border_value)

        conv_value, conv_pull = jax.vjp(local_conv, rec_in, filter_taps, border)
        grad_rec_in, grad_taps, grad_border = conv_pull(grad_conv_out)
        from_next = passed_along(grad_border, "seq", -1)
        grad_rec_in = grad_rec_in + jnp.pad(from_next, ((tokens - (KW - 1), 0), (0, 0)))
        error_input = grad_rec_in.astype(jnp.bfloat16)
        in_err_all, branch_err_all = gather_col((error_input, error_branch))
        grad_input = matmul_rows(normed_all, in_err_all)
        grad_branch = matmul_rows(normed_all, branch_err_all)
        grad_normed = scatter_row(
            matmul_cols(in_err_all, input_weight) + matmul_cols(branch_err_all, branch_weight)
        )
        back_source, grad_mixer = norm_back(source, mixer_gain, factor_one, grad_normed)
        grads_in.append(grad_middle + back_source)
        local_grads = (
            grad_mixer,
            grad_input,
            grad_branch,
            grad_taps,
            grad_recall,
            grad_admit,
            grad_decay,
            grad_output,
            grad_feed,
            grad_gate,
            grad_up,
            grad_down,
        )
        local_grads = over_seq(local_grads)
        totals = tuple((acc + new for acc, new in zip(totals, local_grads)))
    return (jnp.stack(outputs), jnp.stack(grads_in)) + tuple(totals)


BF = jnp.bfloat16
F32 = jnp.float32
VMEM_LIMIT = 60 * 1024 * 1024
ROW_BLOCK = 256
GELU_A = 0.7978845608028654
GELU_B = 0.044715


def cost(flops, moved, trans=0):
    return pl.CostEstimate(flops=int(flops), bytes_accessed=int(moved), transcendentals=int(trans))


def params():
    return pltpu.CompilerParams(vmem_limit_bytes=VMEM_LIMIT, dimension_semantics=("arbitrary",))


def nbytes(*arrays):
    return sum(a.size * a.dtype.itemsize for a in arrays)


def gelu_pair(v):
    t = jnp.tanh(GELU_A * (v + GELU_B * v * v * v))
    value = 0.5 * v * (1.0 + t)
    slope = 0.5 * (1.0 + t) + 0.5 * v * (1.0 - t * t) * GELU_A * (1.0 + 3.0 * GELU_B * v * v)
    return value, slope


def minus_expm1(x):
    series = 1.0 + x * (1.0 / 7.0)
    for n in (6, 5, 4, 3, 2):
        series = 1.0 + x * (1.0 / n) * series
    return jnp.where(x > -0.3, -x * series, 1.0 - jnp.exp(x))


def pair_up(left, right):
    width = left.shape[1]
    lane = lax.broadcasted_iota(jnp.int32, left.shape, 1)
    low = lane < width // 2
    return (
        jnp.where(low, left, pltpu.roll(right, width // 2, 1)),
        jnp.where(low, pltpu.roll(left, width // 2, 1), right),
    )


def dot_nn(a, b, precision=None):
    return lax.dot_general(
        a, b, (((1,), (0,)), ((), ())), precision=precision, preferred_element_type=F32
    )


def dot_nt(a, b, precision=None):
    return lax.dot_general(
        a, b, (((1,), (1,)), ((), ())), precision=precision, preferred_element_type=F32
    )


def dot_tn(a, b, precision=None):
    return lax.dot_general(
        a, b, (((0,), (0,)), ((), ())), precision=precision, preferred_element_type=F32
    )


def rows_spec(block, width, start=0):
    return pl.BlockSpec((block, width), lambda i: (i + start, 0))


def whole_spec(shape):
    rank = len(shape)
    return pl.BlockSpec(shape, lambda i: (0,) * rank, pipeline_mode=pl.Buffered(1))


def head_spec(rows, width=128):
    return pl.BlockSpec((rows, width), lambda h: (0, h))


def sds(shape, dtype):
    return jax.ShapeDtypeStruct(shape, dtype)


MESH_ID = pl.DeviceIdType.MESH


def neighbour_x():
    return {"row": 1 - lax.axis_index("row")}


def neighbour_y():
    return {"col": lax.rem(lax.axis_index("col") + 2, 4)}


def greet():
    barrier = pltpu.get_barrier_semaphore()
    for device in (neighbour_x(), neighbour_y()):
        pl.semaphore_signal(barrier, inc=1, device_id=device, device_id_type=MESH_ID)
    pl.semaphore_wait(barrier, 2)


def message(src, dst, device, sems, n):
    send, recv = sems
    return pltpu.make_async_remote_copy(
        src_ref=src,
        dst_ref=dst,
        send_sem=send.at[n],
        recv_sem=recv.at[n],
        device_id=device,
        device_id_type=MESH_ID,
    )


def neighbour_core():
    col = lax.axis_index("col")
    return {"col": col + 1 - 2 * lax.rem(col, 2)}


def neighbour_end():
    seq = lax.axis_index("seq")
    return {"seq": seq + 1 - 2 * lax.rem(seq, 2)}


def neighbour_middle():
    return {"seq": 3 - lax.axis_index("seq")}


def greet_all(devices):
    barrier = pltpu.get_barrier_semaphore()
    for device in devices:
        pl.semaphore_signal(barrier, inc=1, device_id=device, device_id_type=MESH_ID)
    pl.semaphore_wait(barrier, len(devices))


def row_step(ref):
    rows, lanes = ref.shape
    step = 16
    while step * 2 * lanes <= 32768 and rows % (step * 2) == 0:
        step *= 2
    return step


def plus_in(dst, src):
    step = row_step(dst)

    def one(n, carry):
        at = pl.ds(pl.multiple_of(n * step, step), step)
        dst[at, :] = (dst[at, :].astype(F32) + src[at, :].astype(F32)).astype(dst.dtype)
        return carry

    lax.fori_loop(0, dst.shape[0] // step, one, 0)


def put_in(dst, src):
    step = row_step(dst)

    def one(n, carry):
        at = pl.ds(pl.multiple_of(n * step, step), step)
        dst[at, :] = src[at, :].astype(dst.dtype)
        return carry

    lax.fori_loop(0, dst.shape[0] // step, one, 0)


class SeqSum:
    def __init__(self, pieces, sems, base):
        self.pieces = pieces
        count = len(pieces)
        self.to_end = [message(s, a, neighbour_end(), sems, base + n) for n, (s, a, b) in enumerate(pieces)]
        self.across = [
            message(s, b, neighbour_middle(), sems, base + count + n) for n, (s, a, b) in enumerate(pieces)
        ]
        seq = lax.axis_index("seq")
        self.middle = (seq == 1) | (seq == 2)
        self.end = (seq == 0) | (seq == 3)

    def begin(self, n):
        @pl.when(self.end)
        def _():
            self.to_end[n].start()

    def relay(self, n):
        s, a, b = self.pieces[n]

        @pl.when(self.middle)
        def _():
            self.to_end[n].wait_recv()
            plus_in(s, a)
            self.across[n].start()

    def settle(self, n):
        s, a, b = self.pieces[n]

        @pl.when(self.middle)
        def _():
            self.across[n].wait_recv()
            self.across[n].wait_send()
            plus_in(s, b)
            self.to_end[n].start()

    def finish(self, n):
        s, a, b = self.pieces[n]

        @pl.when(self.end)
        def _():
            self.to_end[n].wait_recv()
            self.to_end[n].wait_send()
            put_in(s, a)

        @pl.when(self.middle)
        def _():
            self.to_end[n].wait_send()


def scatter_messages(q1, q2, q3, r3, rx, ry, sems, base):
    half = q1.shape[0] // 2
    a, b = pl.ds(0, half), pl.ds(half, half)
    x, y = neighbour_x(), neighbour_y()
    plan = ((q3, r3, a, x), (q3, r3, b, y), (q1, rx, a, x), (q2, ry, a, y), (q2, ry, b, y), (q1, rx, b, x))
    return [
        message(src.at[at, :], dst.at[at, :], dev, sems, base + n)
        for n, (src, dst, at, dev) in enumerate(plan)
    ]


def gather_messages(own, gx, gy, gd, sems, base):
    half = own.shape[0] // 2
    a, b = pl.ds(0, half), pl.ds(half, half)
    x, y = neighbour_x(), neighbour_y()
    plan = ((own, gx, a, x), (own, gy, a, y), (own, gx, b, x), (own, gy, b, y), (gx, gd, a, y), (gy, gd, b, x))
    return [
        message(src.at[at, :], dst.at[at, :], dev, sems, base + n)
        for n, (src, dst, at, dev) in enumerate(plan)
    ]


def gather_messages_by_x(own, gx, gy, gd, sems, base):
    half = own.shape[0] // 2
    a, b = pl.ds(0, half), pl.ds(half, half)
    x, y = neighbour_x(), neighbour_y()
    plan = ((own, gx, a, x), (own, gy, a, y), (own, gx, b, x), (own, gy, b, y), (gy, gd, a, x), (gy, gd, b, x))
    return [
        message(src.at[at, :], dst.at[at, :], dev, sems, base + n)
        for n, (src, dst, at, dev) in enumerate(plan)
    ]


def add_into(dst, src, start, rows):
    step = 128
    for r in range(start, start + rows, step):
        at = slice(r, r + step)
        dst[at, :] = (dst[at, :].astype(F32) + src[at, :].astype(F32)).astype(dst.dtype)


def load_rows(gate_w, up_w, sib_own, far, sib_far, dst, sem):
    width, lanes = far.shape
    part, units = width // 2, lanes // 2
    row = lax.axis_index("row")
    y = lax.div(lax.axis_index("col"), 2)
    own = pl.ds(pl.multiple_of(y * units, units), units)
    copies = []

    def copy(src, dst):
        copies.append(pltpu.make_async_copy(src, dst, sem.at[len(copies)]))
        copies[-1].start()

    for dx in (0, 1):
        rows = pl.ds(pl.multiple_of(part * (row + dx - 2 * row * dx), part), part)
        at = [pl.ds(((n // 2 * 2 + dx) * 2 + n % 2) * part, part) for n in range(4)]
        copy(gate_w.at[rows, own], dst.at[at[0], pl.ds(0, units)])
        copy(up_w.at[rows, own], dst.at[at[0], pl.ds(units, units)])
        for n, src in enumerate((sib_own, far, sib_far)):
            copy(src.at[rows, :], dst.at[at[n + 1], :])
    return copies


def comm_params(n):
    return pltpu.CompilerParams(
        vmem_limit_bytes=VMEM_LIMIT,
        dimension_semantics=("arbitrary",),
        collective_id=n,
        has_side_effects=True,
    )


def any_spec():
    return pl.BlockSpec(memory_space=pl.ANY)


def held_spec(block, width, last):
    return pl.BlockSpec((block, width), lambda i: (jnp.minimum(i, last), 0))


def full_spec(shape):
    rank = len(shape)
    return pl.BlockSpec(shape, lambda i: (0,) * rank)


def row_sums(values):
    return dot_nt(jnp.ones((8, values.shape[1]), F32), values, PRECISE)


def as_column(lanes, width):
    first = (lax.broadcasted_iota(jnp.int32, (8, width), 0) == 0).astype(F32)
    return dot_tn(lanes, first, PRECISE)


def chain(entries, count):
    state = entries[count - 1, 0, 1:2, :]
    for n in range(count - 2, -1, -1):
        state = entries[n, 0, 1:2, :] + entries[n, 0, 0:1, :] * state
    return state


def carried(entries, h, count):
    state = entries[count - 1, h, 1:2, :]
    for n in range(count - 2, -1, -1):
        state = entries[n, h, 1:2, :] + entries[n, h, 0:1, :] * state
    return state


class Messages:
    def __init__(self, sems):
        self.sems, self.used = sems, 0

    def new(self, src, dst, device):
        self.used += 1
        return message(src, dst, device, self.sems, self.used - 1)

    def block(self, maker, *refs):
        made = maker(*refs, self.sems, self.used)
        self.used += len(made)
        return made


FRONT_MESSAGES = 80


def front_body(heads, blocks, count, *refs):
    (stream, cot, in_w, br_w, out_w, gate_w, up_w, down_w) = refs[:8]
    (gains_in, small_in, recall_gate, admit_gate, off) = refs[8:13]
    (x, g, e_own, w_out, w_down, gains_out, small, s1, u, v, border_out, earlier_out, mid, own) = refs[13:27]
    (n1, conv, recall, admit, states, mixed) = refs[27:33]
    (ex, ey, ed, mx, my, md, far_gu, sib_own, sib_far, w_in_out) = refs[33:43]
    (x_own, x_recv, g_own, g_recv, gains_recv, small_recv, own_low, gx, gy, gd) = refs[43:53]
    (w_in, gains, border, earlier) = refs[53:57]
    (wo, wd, local, cum, ext, ends, q0, q1, q2, q3, r3, rx, ry, load, send, recv) = refs[57:]
    i = pl.program_id(0)
    seq, row, col = lax.axis_index("seq"), lax.axis_index("row"), lax.axis_index("col")
    y = lax.div(col, 2)
    core = lax.rem(col, 2)
    rows, width = x.shape
    part = width // 2
    half = rows // 2
    block = rows // blocks
    channels = u.shape[1]
    units = gate_w.shape[1] // 2
    to_x, to_y, to_core = neighbour_x(), neighbour_y(), neighbour_core()
    made = Messages((send, recv))
    copies = []

    def copy(src, dst):
        copies.append(pltpu.make_async_copy(src, dst, load.at[len(copies)]))
        return copies[-1]

    swap = [
        made.new(stream.at[1 - core], x_recv, to_core),
        made.new(gains_in, gains_recv, to_core),
        made.new(small_in, small_recv, to_core),
    ]
    swap_g = made.new(cot.at[1 - core], g_recv, to_core)
    x_copy, g_copy = copy(stream.at[core], x_own), copy(cot.at[core], g_own)
    gains_x = made.new(gains.at[:, pl.ds(0, width)], gains.at[:, pl.ds(width, width)], to_x)
    gains_y = made.new(gains.at[:, pl.ds(0, width)], gains.at[:, pl.ds(2 * width, width)], to_y)
    gains_d = made.new(gains.at[:, pl.ds(width, width)], gains.at[:, pl.ds(3 * width, width)], to_y)

    def place(dy, dx, dc):
        return pl.ds(pl.multiple_of(((dy * 2 + dx) * 2 + dc) * part, part), part)

    own_cols = pl.ds(pl.multiple_of(y * channels, channels), channels)
    other_cols = pl.ds(pl.multiple_of((1 - y) * channels, channels), channels)
    in_own, in_far, in_core, in_pass = [], [], [], []
    for n, w in enumerate((in_w, br_w)):
        lanes = pl.ds(n * channels, channels)
        for k in (0, 1):
            source = pl.ds(k * part, part)
            dx = row + k - 2 * row * k
            in_far.append(made.new(w.at[source, other_cols], w_in.at[place(1, dx, 0), lanes], to_y))
            in_own.append(copy(w.at[source, own_cols], w_in.at[place(0, dx, 0), lanes]))
            in_core.append(made.new(w.at[source, own_cols], w_in.at[place(0, dx, 1), lanes], to_core))
            in_pass.append(
                made.new(w_in.at[place(1, dx, 0), lanes], w_in.at[place(1, dx, 1), lanes], to_core)
            )

    own_rows = pl.ds(pl.multiple_of(y * channels, channels), channels)
    other_rows = pl.ds(pl.multiple_of((1 - y) * channels, channels), channels)
    wo_own = copy(out_w.at[own_rows, :], wo.at[0, 0])
    wo_far = made.new(out_w.at[other_rows, :], wo.at[1, 0], to_y)
    wo_core = made.new(out_w.at[own_rows, :], wo.at[0, 1], to_core)
    wo_pass = made.new(wo.at[1, 0], wo.at[1, 1], to_core)

    share, share_d = gate_w.shape[0] // (count + 1), units // (count + 1)
    own_units = pl.ds(pl.multiple_of(y * units, units), units)
    other_units = pl.ds(pl.multiple_of((1 - y) * units, units), units)
    at_seq = pl.ds(pl.multiple_of(seq * share, share), share)
    at_seq_d = pl.ds(pl.multiple_of(seq * share_d, share_d), share_d)
    far_d = wd.at[1, 0]
    first_lanes, last_lanes = pl.ds(0, units), pl.ds(units, units)
    from_d = pl.ds(pl.multiple_of((1 - y) * units + seq * share_d, share_d), share_d)
    ff_far = [
        made.new(down_w.at[from_d, :], far_d.at[at_seq_d, :], to_y),
        made.new(gate_w.at[at_seq, other_units], far_gu.at[at_seq, first_lanes], to_y),
        made.new(up_w.at[at_seq, other_units], far_gu.at[at_seq, last_lanes], to_y),
    ]
    others = [{"seq": lax.rem(seq + n, count + 1)} for n in range(1, count + 1)]
    ff_share = [made.new(far_d.at[at_seq_d, :], far_d.at[at_seq_d, :], device) for device in others]
    ff_share += [made.new(far_gu.at[at_seq, :], far_gu.at[at_seq, :], device) for device in others]
    ff_core = [
        made.new(gate_w.at[:, own_units], sib_own.at[:, first_lanes], to_core),
        made.new(up_w.at[:, own_units], sib_own.at[:, last_lanes], to_core),
        made.new(down_w.at[own_units, :], wd.at[0, 1], to_core),
    ]
    ff_pass = [made.new(far_gu, sib_far, to_core), made.new(far_d, wd.at[1, 1], to_core)]
    wd_own = copy(down_w.at[own_units, :], wd.at[0, 0])
    ahead = len(copies)
    w_in_store = copy(w_in, w_in_out)

    gather_n = made.block(gather_messages_by_x, own_low, gx, gy, gd)
    gather_e = made.block(gather_messages_by_x, e_own, ex, ey, ed)
    scatter = made.block(scatter_messages, q1, q2, q3, r3, rx, ry)
    gather_m = made.block(gather_messages, own, mx, my, md)
    edge = made.new(u.at[pl.ds(rows - 8, 8), :], border, {"seq": seq + 1})
    hand_on = [made.new(ends, earlier.at[n - 1], {"seq": seq + n}) for n in range(1, count + 1)]

    def put_together(left, right, full, low):
        step = 128
        for r in range(0, rows, step):
            at = slice(r, r + step)
            whole = jnp.concatenate([left[at, :], right[at, :]], axis=1)
            full[at, :] = whole
            low[at, :] = whole.astype(BF)

    @pl.when(i == 0)
    def _():
        for c in copies[:ahead]:
            c.start()
        border[...] = jnp.zeros_like(border)
        earlier[...] = jnp.zeros_like(earlier)
        greet_all(
            [to_x, to_y, to_core] + [{"seq": lax.rem(seq + n, count + 1)} for n in range(1, count + 1)]
        )
        for m in swap:
            m.start()
        for m in in_far:
            m.start()
        x_copy.wait()
        swap[0].wait_recv()
        put_together(x_own, x_recv, x, own_low)
        for m in gather_n[:4]:
            m.start()
        for m in in_core:
            m.start()
        swap[1].wait_recv()
        gains[:, 0:width] = jnp.concatenate([gains_in[...], gains_recv[...]], axis=1)
        gains_x.start()
        gains_y.start()
        swap[2].wait_recv()
        lane = small_in.shape[1]
        small[:, pl.ds(pl.multiple_of(core * lane, lane), lane)] = small_in[...]
        small[:, pl.ds(pl.multiple_of((1 - core) * lane, lane), lane)] = small_recv[...]
        swap_g.start()
        for m, n in zip(in_far, in_pass):
            m.wait_recv()
            n.start()
        gains_x.wait_recv()
        gains_d.start()
        gather_n[1].wait_recv()
        gather_n[4].start()
        wo_core.start()
        for m in ff_core:
            m.start()
        gather_n[3].wait_recv()
        gather_n[5].start()
        wo_far.start()
        for m in ff_far:
            m.start()
        g_copy.wait()
        swap_g.wait_recv()
        put_together(g_own, g_recv, g, e_own)
        for c in in_own:
            c.wait()
        for m in in_core + in_pass:
            m.wait_recv()
        gains_y.wait_recv()
        gains_d.wait_recv()
        w_in_store.start()
        gather_n[0].wait_recv()
        gather_n[4].wait_recv()
        for m in gather_e[:4]:
            m.start()

    @pl.when(i == blocks // 2)
    def _():
        gather_n[2].wait_recv()
        gather_n[5].wait_recv()

    @pl.when(i < blocks)
    def _():
        at = pl.ds(pl.multiple_of(i * block, block), block)
        parts = [r[at, :].astype(F32) for r in (own_low, gx, gy, gd)]
        total = sum(jnp.sum(p * p, axis=1, keepdims=True) for p in parts)
        s = lax.rsqrt(total / D + EPSILON)
        s1[at, :] = s
        normed = [p * s * gains[0:1, j * width : (j + 1) * width] for j, p in enumerate(parts)]
        acc = None
        for j, n in enumerate(normed):
            term = dot_nn(n.astype(BF), w_in[j * width : (j + 1) * width, :])
            acc = term if acc is None else acc + term
        u[at, :] = acc[:, :channels]
        v[at, :] = acc[:, channels:]
        for j in (0, 1):
            k, p = pair_up(normed[2 * j], normed[2 * j + 1])
            n1[:, j * width : (j + 1) * width] = k.astype(BF)
            n1[:, (j + 2) * width : (j + 3) * width] = p.astype(BF)

    @pl.when((i == blocks - 1) & (seq < count))
    def _():
        edge.start()

    @pl.when((i == blocks) & (seq > 0))
    def _():
        edge.wait_recv()

    @pl.when(i == blocks - 1)
    def _():
        ff_far[0].wait_recv()
        for m in ff_share[:count]:
            m.start()

    @pl.when((i >= blocks) & (i < blocks + heads))
    def _():
        h = i - blocks
        lane = pl.ds(pl.multiple_of(h * 128, 128), 128)
        state_h, cum_h = local.at[h], cum.at[h]
        ext[0:8, :] = border[:, lane]
        ext[8 : 8 + rows, :] = u[:, lane]
        sp = small[KW : KW + 1, lane]
        step = ROW_BLOCK
        for r in range(0, rows, step):
            o = off[8 + r : 8 + r + step, :]
            total = small[0:1, lane] * ext[8 + r : 8 + r + step, :]
            for k in range(1, KW):
                term = small[k : k + 1, lane] * ext[8 + r - k : 8 + r - k + step, :]
                total = total + jnp.where(o >= k, term, 0.0)
            conv[r : r + step, :] = total
            rec = jax.nn.sigmoid(dot_nn(total, recall_gate[y * heads + h], PRECISE))
            adm = jax.nn.sigmoid(dot_nn(total, admit_gate[y * heads + h], PRECISE))
            recall[r : r + step, :] = rec
            admit[r : r + step, :] = adm
            ell = -8.0 * rec * sp
            cum_h[r : r + step, :] = jnp.where(o > 0, jnp.exp(ell), 0.0)
            state_h[r : r + step, :] = jnp.sqrt(minus_expm1(2.0 * ell)) * adm * total
        seg = rows // 8

        def one(n, carry):
            h, p = carry
            at = pl.ds(n, 8, stride=seg)
            d = cum_h[at, :]
            h = d * h + state_h[at, :]
            p = d * p
            state_h[at, :] = h
            cum_h[at, :] = p
            return h, p

        zero = jnp.zeros((8, 128), F32)
        last, product = lax.fori_loop(0, seg, one, (zero, zero + 1.0), unroll=8)
        carry_h, carry_p = last[0:1, :], product[0:1, :]
        for s in range(1, 8):
            at = slice(s * seg, (s + 1) * seg)
            c = cum_h[at, :]
            state_h[at, :] = state_h[at, :] + c * carry_h
            cum_h[at, :] = c * carry_p
            carry_h = last[s : s + 1, :] + product[s : s + 1, :] * carry_h
            carry_p = product[s : s + 1, :] * carry_p
        ends[h, 0:1, :] = carry_p
        ends[h, 1:2, :] = carry_h
        ends[h, 2:8, :] = jnp.zeros((6, 128), F32)

    @pl.when(i == blocks + 1)
    def _():
        gather_e[1].wait_recv()
        gather_e[4].start()
        wo_far.wait_recv()
        wo_pass.start()

    @pl.when(i == blocks + 2)
    def _():
        gather_e[3].wait_recv()
        gather_e[5].start()

    def columns_in_order(pieces, out):
        size = out.shape[0]
        step = 128
        lower = row == 0

        def one(n, carry):
            at = pl.ds(pl.multiple_of(n * step, step), step)
            for dy in (0, 1):
                first, second = pair_up(pieces[dy, 0, at, :].astype(F32), pieces[dy, 1, at, :].astype(F32))
                near, far = jnp.where(lower, first, second), jnp.where(lower, second, first)
                out[at, 2 * dy * width : (2 * dy + 1) * width] = near.astype(BF)
                out[at, (2 * dy + 1) * width : (2 * dy + 2) * width] = far.astype(BF)
            return carry

        lax.fori_loop(0, size // step, one, 0)

    @pl.when(i == blocks + heads - 1)
    def _():
        wo_own.wait()
        wo_core.wait_recv()
        wo_pass.wait_recv()
        columns_in_order(wo, w_out)

    for n in range(1, count + 1):

        @pl.when((i == blocks + heads - 1) & (seq <= count - n))
        def _():
            hand_on[n - 1].start()

        @pl.when((i == blocks + heads) & (seq >= n))
        def _():
            hand_on[n - 1].wait_recv()

    @pl.when(i == blocks + heads)
    def _():
        for m in ff_far[1:]:
            m.wait_recv()
        for m in ff_share[count:]:
            m.start()

    third = blocks + heads

    @pl.when((i >= third) & (i < third + blocks))
    def _():
        at = pl.ds(pl.multiple_of((i - third) * block, block), block)
        st = jnp.concatenate(
            [local[h, at, :] + cum[h, at, :] * carried(earlier, h, count) for h in range(heads)], axis=1
        )
        states[...] = st
        m = (st * gelu_pair(v[at, :])[0]).astype(BF)
        mixed[...] = m
        for j, q in ((3, q3), (1, q1), (2, q2), (0, q0)):
            q[at, :] = dot_nn(m, w_out[:, j * width : (j + 1) * width]).astype(q.dtype)

    @pl.when(i == third + blocks // 2 - 1)
    def _():
        scatter[0].start()
        scatter[2].start()

    @pl.when(i == third + blocks - 1)
    def _():
        scatter[1].start()

    @pl.when(i == third + blocks)
    def _():
        scatter[0].wait_recv()
        add_into(q2, r3, 0, half)
        scatter[3].start()
        scatter[4].start()
        scatter[1].wait_recv()
        add_into(q1, r3, half, half)
        scatter[5].start()
        gains_out[...] = gains[...]
        border_out[...] = border[...]
        earlier_out[...] = earlier[...]
        w_in_store.wait()
        for m in ff_share:
            m.wait_recv()
        for m in ff_pass:
            m.start()
        for base, first in ((0, 2), (half, 4)):
            scatter[first].wait_recv()
            scatter[first + 1].wait_recv()
            for r in range(base, base + half, 128):
                at = slice(r, r + 128)
                total = x[at, :] + q0[at, :] + rx[at, :].astype(F32) + ry[at, :].astype(F32)
                mid[at, :] = total
                own[at, :] = total.astype(BF)
            start = 0 if base == 0 else 2
            gather_m[start].start()
            gather_m[start + 1].start()
        wd_own.wait()
        for m in ff_core + ff_pass:
            m.wait_recv()
        columns_in_order(wd, w_down)
        gather_m[0].wait_recv()
        gather_m[4].start()
        gather_m[3].wait_recv()
        gather_m[5].start()
        for n in (1, 2, 4, 5):
            gather_m[n].wait_recv()
        for n in (0, 2, 4, 5):
            gather_e[n].wait_recv()
        sent = swap + [swap_g, gains_x, gains_y, gains_d] + in_far + in_core + in_pass
        sent += [wo_far, wo_core, wo_pass] + ff_far + ff_share + ff_core + ff_pass
        for m in sent + gather_n + gather_e + scatter + gather_m:
            m.wait_send()

        @pl.when(seq < count)
        def _():
            edge.wait_send()

        for n in range(1, count + 1):

            @pl.when(seq <= count - n)
            def _():
                hand_on[n - 1].wait_send()


def front(stream, cot, in_w, br_w, out_w, gate_w, up_w, down_w, gains, small, recall_gate, admit_gate, off, count):
    rows, part = stream.shape[1:]
    width = 2 * part
    channels = in_w.shape[1] // 2
    units = gate_w.shape[1] // 2
    heads = channels // 128
    block = ROW_BLOCK
    blocks = rows // block

    def norm_at(i):
        return (jnp.minimum(i, blocks - 1), 0)

    def head_at(i):
        return (0, jnp.clip(i - blocks, 0, heads - 1))

    def mix_at(i):
        return (jnp.clip(i - blocks - heads, 0, blocks - 1), 0)

    chunk_low, chunk = sds((rows, width), BF), sds((rows, width), F32)
    wide = sds((rows, channels), F32)
    held = [
        chunk,
        chunk,
        chunk_low,
        sds((channels, 4 * width), BF),
        sds((units, 4 * width), BF),
        sds((8, 4 * width), F32),
        sds((8, channels), F32),
        sds((rows, 1), F32),
        wide,
        wide,
        sds((8, channels), F32),
        sds((count, heads, 8, 128), F32),
        chunk,
        chunk_low,
    ]
    blocked = [sds((rows, 4 * width), BF), wide, wide, wide, wide, sds((rows, channels), BF)]
    away = [chunk_low] * 6 + [sds((width, 2 * units), BF)] * 3 + [sds((4 * width, 2 * channels), BF)]
    piece = pltpu.VMEM((rows, width), BF)
    side = pltpu.VMEM((rows, part), F32)
    tall = pl.BlockSpec((rows, 128), head_at)
    return pl.pallas_call(
        functools.partial(front_body, heads, blocks, count),
        grid=(2 * blocks + heads + 1,),
        in_specs=[any_spec()] * 8
        + [whole_spec(a.shape) for a in (gains, small, recall_gate, admit_gate, off)],
        out_specs=[whole_spec(s.shape) for s in held]
        + [pl.BlockSpec((block, 4 * width), norm_at)]
        + [tall] * 3
        + [pl.BlockSpec((block, channels), mix_at)] * 2
        + [any_spec()] * 10,
        out_shape=held + blocked + away,
        scratch_shapes=[side] * 4
        + [pltpu.VMEM(gains.shape, F32), pltpu.VMEM(small.shape, F32)]
        + [piece] * 4
        + [
            pltpu.VMEM((4 * width, 2 * channels), BF),
            pltpu.VMEM((8, 4 * width), F32),
            pltpu.VMEM((8, channels), F32),
            pltpu.VMEM((count, heads, 8, 128), F32),
            pltpu.VMEM((2, 2, channels, width), BF),
            pltpu.VMEM((2, 2, units, width), BF),
            pltpu.VMEM((heads, rows, 128), F32),
            pltpu.VMEM((heads, rows, 128), F32),
            pltpu.VMEM((rows + 8, 128), F32),
            pltpu.VMEM((heads, 8, 128), F32),
            pltpu.VMEM((rows, width), F32),
        ]
        + [piece] * 6
        + [pltpu.SemaphoreType.DMA((9,))]
        + [pltpu.SemaphoreType.DMA((FRONT_MESSAGES,))] * 2,
        compiler_params=comm_params(1),
        cost_estimate=cost(200 * rows * in_w.size, rows * 40000),
        name="front",
    )(stream, cot, in_w, br_w, out_w, gate_w, up_w, down_w, gains, small, recall_gate, admit_gate, off)


def feed_body(blocks, *refs):
    (x0, x1, x2, x3, e0, e1, e2, e3, mid, cot, gain, wd) = refs[:12]
    weights = refs[12:17]
    outs = refs[17:21]
    (dx, own, gx, gy, gd, gain_grad, s_down, s_gu) = refs[21:29]
    (wgu, load, n2, hid, ee, err, scale, stage, c_down, c_gu) = refs[29:39]
    (q0, q1, q2, q3, r3, rx, ry, dots, dots_x, dots_y, send, recv) = refs[39:]
    i = pl.program_id(0)
    sems = (send, recv)
    scatter = scatter_messages(q1, q2, q3, r3, rx, ry, sems, 0)
    gather = gather_messages(own, gx, gy, gd, sems, 6)
    small_x = message(dots, dots_x, neighbour_x(), sems, 12)
    small_y = message(dots_x, dots_y, neighbour_y(), sems, 13)
    block, width = x0.shape
    rows = mid.shape[0]
    half = rows // 2
    units = hid.shape[1]

    @pl.when(i == 0)
    def _():
        copies = load_rows(*weights, wgu, load)
        greet_all((neighbour_x(), neighbour_y(), neighbour_core()))
        for c in copies:
            c.wait()

    @pl.when(i < blocks)
    def _():
        at = pl.ds(pl.multiple_of(i * block, block), block)
        parts = [r[...].astype(F32) for r in (x0, x1, x2, x3)]
        total = sum(jnp.sum(p * p, axis=1, keepdims=True) for p in parts)
        s = lax.rsqrt(total / D + EPSILON)
        scale[at, :] = s
        normed = [p * s * gain[1:2, j * width : (j + 1) * width] for j, p in enumerate(parts)]
        acc = None
        for j, n in enumerate(normed):
            term = dot_nn(n.astype(BF), wgu[j * width : (j + 1) * width, :])
            acc = term if acc is None else acc + term
        errs = [r[...] for r in (e0, e1, e2, e3)]
        wide = [e.astype(F32) for e in errs]
        for source, target in ((normed, n2), (wide, ee)):
            for j in (0, 1):
                k, p = pair_up(source[2 * j], source[2 * j + 1])
                target[at, j * width : (j + 1) * width] = k.astype(BF)
                target[at, (j + 2) * width : (j + 3) * width] = p.astype(BF)
        pre, up = acc[:, :units], acc[:, units:]
        act, slope = gelu_pair(pre)
        h = (act * up).astype(BF)
        hid[at, :] = h
        dh = None
        for j, e in enumerate(errs):
            term = dot_nt(e, wd[:, j * width : (j + 1) * width])
            dh = term if dh is None else dh + term
        g = (dh * up * slope).astype(BF)
        b = (dh * act).astype(BF)
        err[at, :units] = g
        err[at, units:] = b
        dots[:, at] = row_sums(g.astype(F32) * pre + b.astype(F32) * up)
        for j, q in ((3, q3), (1, q1), (2, q2), (0, q0)):
            rows_w = slice(j * width, (j + 1) * width)
            q[at, :] = (dot_nt(g, wgu[rows_w, :units]) + dot_nt(b, wgu[rows_w, units:])).astype(q.dtype)
        for j, q in enumerate(outs):
            q[...] = dot_nn(h, wd[:, j * width : (j + 1) * width]).astype(q.dtype)

    @pl.when(i == blocks // 2 - 1)
    def _():
        scatter[0].start()
        scatter[2].start()

    @pl.when(i == blocks - 1)
    def _():
        scatter[1].start()
        small_x.start()

    @pl.when(i == blocks)
    def _():
        scatter[0].wait_recv()
        add_into(q2, r3, 0, half)
        scatter[3].start()
        scatter[4].start()
        small_x.wait_recv()
        dots_x[...] = dots_x[...] + dots[...]
        small_y.start()

    @pl.when(i == blocks + 1)
    def _():
        scatter[1].wait_recv()
        add_into(q1, r3, half, half)
        scatter[5].start()

    def finish(base, first, start):
        scatter[first].wait_recv()
        scatter[first + 1].wait_recv()
        sum_grad = None
        for r in range(base, base + half, 128):
            at = slice(r, r + 128)
            d = q0[at, :] + rx[at, :].astype(F32) + ry[at, :].astype(F32)
            s, m = scale[at, :], mid[at, :]
            t = as_column(dots_x[:, at] + dots_y[:, at], width)
            new = cot[at, :] + s * own_gain * d - m * (s * s) * t * (1.0 / D)
            dx[at, :] = new
            own[at, :] = new.astype(BF)
            term = jnp.sum(d * m * s, axis=0, keepdims=True)
            sum_grad = term if sum_grad is None else sum_grad + term
        gather[start].start()
        gather[start + 1].start()
        return sum_grad

    own_gain = gain[1:2, :width]

    @pl.when(i == blocks + 2)
    def _():
        small_y.wait_recv()
        gain_grad[0:1, :] = finish(0, 2, 0)

    @pl.when(i == blocks + 4)
    def _():
        gain_grad[0:1, :] = gain_grad[0:1, :] + finish(half, 4, 2)

    @pl.when(i == blocks + 5)
    def _():
        gather[0].wait_recv()
        gather[4].start()

    @pl.when(i == blocks + 6)
    def _():
        gather[3].wait_recv()
        gather[5].start()

    tiles = units // width
    to_core = [
        message(stage, c_gu.at[pl.ds(n * width, width), :], neighbour_core(), sems, 14 + n) for n in (0, 1)
    ] + [
        message(
            stage.at[:, pl.ds(n * 2 * width, 2 * width)],
            c_down.at[pl.ds(n * width, width), :],
            neighbour_core(),
            sems,
            16 + n,
        )
        for n in range(tiles)
    ]

    def gu_tile(n):
        return dot_tn(n2[:, n * width : (n + 1) * width], err[...])

    for n in (0, 1):

        @pl.when(i == blocks + n)
        def _():
            g = gu_tile(2 + n).astype(BF)
            if n:
                to_core[0].wait_send()
            stage[...] = g
            to_core[n].start()

    for n in range(tiles):

        @pl.when(i == blocks + 2 + n)
        def _():
            at = slice(n * width, (n + 1) * width)
            g = dot_tn(hid[:, at], ee[...])
            if n == 0:
                to_core[1].wait_send()
            stage[:, n * 2 * width : (n + 1) * 2 * width] = g[:, 2 * width :].astype(BF)
            to_core[2 + n].start()
            s_down[at, :] = g[:, : 2 * width].astype(BF)

    for n in (1, 0):

        @pl.when(i == blocks + tiles + 3 - n)
        def _():
            to_core[n].wait_recv()
            at = slice(n * width, (n + 1) * width)
            s_gu[...] = (gu_tile(n) + c_gu[at, :].astype(F32)).astype(BF)

    @pl.when(i == blocks + tiles + 4)
    def _():
        for n in range(tiles):
            to_core[2 + n].wait_recv()
            to_core[2 + n].wait_send()
        plus_in(s_down, c_down)
        for n in (1, 2, 4, 5):
            gather[n].wait_recv()
        for m in scatter + gather + [small_x, small_y]:
            m.wait_send()


def feed(chunks, errs, mid, cot, gain, wd, weights):
    rows, width = chunks[0].shape
    units = wd.shape[0]
    block = ROW_BLOCK
    blocks = rows // block
    tiles = units // width
    held = functools.partial(held_spec, block, last=blocks - 1)
    chunk = pltpu.VMEM((rows, width), BF)
    lanes = pltpu.VMEM((8, rows), F32)
    gu_spec = pl.BlockSpec((width, 2 * units), lambda i: (jnp.where(i >= blocks + tiles + 3, 0, 1), 0))
    return pl.pallas_call(
        functools.partial(feed_body, blocks),
        grid=(blocks + tiles + 5,),
        in_specs=[held(width)] * 8
        + [whole_spec(mid.shape), whole_spec(cot.shape), whole_spec(gain.shape)]
        + [whole_spec(wd.shape)]
        + [any_spec()] * 5,
        out_specs=[held(width)] * 4
        + [whole_spec((rows, width))] * 2
        + [any_spec()] * 3
        + [whole_spec((8, width)), whole_spec((units, 2 * width)), gu_spec],
        out_shape=[sds((rows, width), F32)]
        + [sds((rows, width), BF)] * 3
        + [sds((rows, width), F32)]
        + [sds((rows, width), BF)] * 4
        + [sds((8, width), F32), sds((units, 2 * width), BF), sds((2 * width, 2 * units), BF)],
        scratch_shapes=[
            pltpu.VMEM((4 * width, 2 * units), BF),
            pltpu.SemaphoreType.DMA((10,)),
            pltpu.VMEM((rows, 4 * width), BF),
            pltpu.VMEM((rows, units), BF),
            pltpu.VMEM((rows, 4 * width), BF),
            pltpu.VMEM((rows, 2 * units), BF),
            pltpu.VMEM((rows, 1), F32),
            pltpu.VMEM((width, 2 * units), BF),
            pltpu.VMEM((units, 2 * width), BF),
            pltpu.VMEM((2 * width, 2 * units), BF),
            pltpu.VMEM((rows, width), F32),
        ]
        + [chunk] * 6
        + [lanes] * 3
        + [pltpu.SemaphoreType.DMA((16 + tiles,))] * 2,
        compiler_params=comm_params(3),
        cost_estimate=cost(48 * rows * wd.size, 3 * nbytes(wd) + rows * 30000, rows * units),
        name="feed",
    )(*chunks, *errs, mid, cot, gain, wd, *weights)


def back_body(heads, blocks, count, *refs):
    errs = refs[0:4]
    (w_out, states, branch, recall, conv, admit, u_head, off, soft) = refs[4:13]
    (taps, recall_w, admit_w, border, earlier, u, v, w, scale, x, dx, gain) = refs[13:25]
    (sum_gu, sum_down) = refs[25:27]
    (ev, paired, eu, grad, gain_grad, grad_recall, grad_admit, grad_small) = refs[27:35]
    (mine_gu, far_gu, mine_down, far_down) = refs[35:39]
    (part, reach, ext, st, uext, dc, ends, later, edge, from_later, load) = refs[39:50]
    (q0, q1, q2, q3, r3, rx, ry, dots, dots_x, dots_y) = refs[50:60]
    (s_gu, a_gu, b_gu, s_dn, a_dn, b_dn, store, send, recv) = refs[60:]
    i = pl.program_id(0)
    sems = (send, recv)
    seq = lax.axis_index("seq")
    rows, width = x.shape
    half = rows // 2
    step = ROW_BLOCK
    seg = rows // 8
    channels = heads * 128
    block = step

    scatter = scatter_messages(q1, q2, q3, r3, rx, ry, sems, 0)
    small_x = message(dots, dots_x, neighbour_x(), sems, 6)
    small_y = message(dots_x, dots_y, neighbour_y(), sems, 7)
    hand_on = [message(ends, later.at[n - 1], {"seq": seq - n}, sems, 7 + n) for n in range(1, count + 1)]
    base = 8 + count
    hand_edge = message(edge, from_later, {"seq": seq - 1}, sems, base)
    base += 1

    rows_gu, rows_dn = width // 4, sum_down.shape[0] // 2
    group_gu, group_dn = (s_gu, a_gu, b_gu), (s_dn, a_dn, b_dn)

    def gu_at(n):
        return pl.ds(n * rows_gu, rows_gu)

    def dn_at(n):
        return pl.ds(n * rows_dn, rows_dn)

    places = [("gu", n) for n in (4, 5, 6, 7)] + [("far", n) for n in (0, 1)]
    places += [("own", n) for n in (0, 1)] + [("gu", n) for n in (0, 1, 2, 3)]

    def view(kind, n, ref):
        if kind == "gu":
            return ref.at[gu_at(n), :]
        return ref.at[dn_at(n), pl.ds(width if kind == "far" else 0, width)]

    pieces = [
        [view(kind, n, r) for r in (group_gu if kind == "gu" else group_dn)] for kind, n in places
    ]
    total = SeqSum(pieces, sems, base)
    base += 2 * len(pieces)
    to_y, to_out = {}, {}
    for p, (kind, n) in enumerate(places):
        source = pieces[p][0]
        if kind == "far":
            to_y[p] = message(source, far_down.at[dn_at(n), :], neighbour_y(), sems, base + len(to_y))
        elif kind == "own":
            to_out[p] = pltpu.make_async_copy(source, mine_down.at[dn_at(n), :], store.at[len(to_out)])
        elif n >= 4:
            to_y[p] = message(source, far_gu.at[gu_at(n - 4), :], neighbour_y(), sems, base + len(to_y))
        else:
            to_out[p] = pltpu.make_async_copy(source, mine_gu.at[gu_at(n), :], store.at[len(to_out)])
    loads = [
        pltpu.make_async_copy(sum_gu, s_gu, load.at[0]),
        pltpu.make_async_copy(sum_down, s_dn, load.at[1]),
    ]

    def tick(t):
        if t + 2 < len(pieces):
            total.begin(t + 2)
        if t < len(pieces):
            total.relay(t)
        if 0 <= t - 1 < len(pieces):
            total.settle(t - 1)
        if 0 <= t - 2 < len(pieces):
            total.finish(t - 2)
            if t - 2 in to_y:
                to_y[t - 2].start()
            else:
                to_out[t - 2].start()

    @pl.when(i == 0)
    def _():
        for c in loads:
            c.start()
        later[...] = jnp.zeros_like(later)
        from_later[...] = jnp.zeros_like(from_later)
        greet_all(
            [neighbour_x(), neighbour_y()]
            + [{"seq": lax.rem(seq + n, count + 1)} for n in range(1, count + 1)]
        )
        for c in loads:
            c.wait()
        total.begin(0)
        total.begin(1)
        for r in range(0, rows, step):
            at = slice(r, r + step)
            for j in (0, 1):
                k, p = pair_up(errs[2 * j][at, :].astype(F32), errs[2 * j + 1][at, :].astype(F32))
                paired[at, j * width : (j + 1) * width] = k.astype(BF)
                paired[at, (j + 2) * width : (j + 3) * width] = p.astype(BF)

    @pl.when(i < heads)
    def _():
        sp = soft[0:1, :]
        part_h, reach_h = part.at[i], reach.at[i]
        lane = pl.ds(pl.multiple_of(i * 128, 128), 128)
        for r in range(0, rows, step):
            at = slice(r, r + step)
            o = off[8 + r : 8 + r + step, :]
            ext[at, :] = jnp.where(o > 0, jnp.exp(-8.0 * recall[at, :] * sp), 0.0)
            dm = None
            for j in range(4):
                term = dot_nt(errs[j][at, :], w_out[:, j * width : (j + 1) * width])
                dm = term if dm is None else dm + term
            act, slope = gelu_pair(branch[at, :])
            ev[at, lane] = (dm * states[at, :] * slope).astype(BF)
            part_h[at, :] = dm * act
        ext[rows : rows + 8, :] = jnp.ones((8, 128), F32)
        for r in range(0, rows, step):
            reach_h[r : r + step, :] = ext[r + 1 : r + 1 + step, :]

        def one(n, carry):
            h, p = carry
            at = pl.ds(seg - 1 - n, 8, stride=seg)
            d = reach_h[at, :]
            h = d * h + part_h[at, :]
            p = d * p
            part_h[at, :] = h
            reach_h[at, :] = p
            return h, p

        zero = jnp.zeros((8, 128), F32)
        h, p = lax.fori_loop(0, seg, one, (zero, zero + 1.0), unroll=8)
        carry_h, carry_p = h[7:8, :], p[7:8, :]
        for s in range(6, -1, -1):
            at = slice(s * seg, (s + 1) * seg)
            c = reach_h[at, :]
            part_h[at, :] = part_h[at, :] + c * carry_h
            reach_h[at, :] = c * carry_p
            carry_h = h[s : s + 1, :] + p[s : s + 1, :] * carry_h
            carry_p = p[s : s + 1, :] * carry_p
        first = ext[0:1, :]
        ends[i, 0:1, :] = first * carry_p
        ends[i, 1:2, :] = first * carry_h
        ends[i, 2:8, :] = jnp.zeros((6, 128), F32)

    for n in range(1, count + 1):

        @pl.when((i == heads - 1) & (seq >= n))
        def _():
            hand_on[n - 1].start()

        @pl.when((i == heads) & (seq <= count - n))
        def _():
            hand_on[n - 1].wait_recv()

    @pl.when((i >= heads) & (i < 2 * heads))
    def _():
        h = i - heads
        part_h, reach_h = part.at[h], reach.at[h]
        st[0:8, :] = jnp.broadcast_to(chain(earlier, count), (8, 128))
        st[8 : 8 + rows, :] = states[...]
        uext[0:8, :] = border[...]
        uext[8 : 8 + rows, :] = u_head[...]
        incoming = carried(later, h, count)
        sp = soft[0:1, :]
        dc[0:8, :] = jnp.zeros((8, 128), F32)
        dc[8 + rows : 16 + rows, :] = jnp.zeros((8, 128), F32)
        gr = ga = None
        sums = [None] * (KW + 1)

        def plus(total, term):
            return term if total is None else total + term

        for r in range(0, rows, step):
            at = slice(r, r + step)
            o = off[8 + r : 8 + r + step, :]
            adj = part_h[at, :] + reach_h[at, :] * incoming
            rec, adm, cv = recall[at, :], admit[at, :], conv[at, :]
            ell = -8.0 * rec * sp
            e = jnp.exp(ell)
            m = jnp.sqrt(minus_expm1(2.0 * ell))
            previous = jnp.where(o > 0, e * st[7 + r : 7 + r + step, :], 0.0)
            ac = adj * cv
            d_ell = adj * previous - ac * adm * (e * e) / m
            d_rp = -8.0 * sp * d_ell * rec * (1.0 - rec)
            d_ip = ac * m * adm * (1.0 - adm)
            d_conv = (
                adj * m * adm
                + dot_nt(d_rp, recall_w[0], PRECISE)
                + dot_nt(d_ip, admit_w[0], PRECISE)
            )
            dc[8 + r : 8 + r + step, :] = d_conv
            gr = plus(gr, dot_tn(cv, d_rp, PRECISE))
            ga = plus(ga, dot_tn(cv, d_ip, PRECISE))
            for k in range(KW):
                term = d_conv * uext[8 + r - k : 8 + r - k + step, :]
                if k:
                    term = jnp.where(o >= k, term, 0.0)
                sums[k] = plus(sums[k], jnp.sum(term, axis=0, keepdims=True))
            sums[KW] = plus(sums[KW], jnp.sum(rec * d_ell, axis=0, keepdims=True))
        grad_recall[0] = gr
        grad_admit[0] = ga
        for k in range(KW + 1):
            grad_small[k : k + 1, :] = sums[k]
        grad_small[KW + 1 : 8, :] = jnp.zeros((7 - KW, 128), F32)
        for r in range(0, rows, step):
            du = taps[0:1, :] * dc[8 + r : 8 + r + step, :]
            for k in range(1, KW):
                o = off[8 + r + k : 8 + r + k + step, :]
                term = taps[k : k + 1, :] * dc[8 + r + k : 8 + r + k + step, :]
                du = du + jnp.where(o >= k, term, 0.0)
            part_h[r : r + step, :] = du
        over = jnp.zeros((8, 128), F32)
        for k in range(1, KW):
            term = taps[k : k + 1, :] * dc[k : k + 8, :]
            over = over + jnp.where(off[k : k + 8, :] >= k, term, 0.0)
        edge[h] = over

    @pl.when((i == 2 * heads - 1) & (seq >= 1))
    def _():
        hand_edge.start()

    @pl.when((i == 2 * heads) & (seq < count))
    def _():
        hand_edge.wait_recv()

    third = 2 * heads

    @pl.when((i >= third) & (i < third + blocks))
    def _():
        at = pl.ds(pl.multiple_of((i - third) * block, block), block)
        d = jnp.concatenate([part[h, at, :] for h in range(heads)], axis=1)
        late = jnp.concatenate([from_later[h] for h in range(heads)], axis=1)
        extra = jnp.concatenate([jnp.zeros((block - 8, channels), F32), late], axis=0)
        d = d + jnp.where(i == third + blocks - 1, extra, 0.0)
        e = d.astype(BF)
        eu[...] = e
        b = ev[at, :]
        dots[:, at] = row_sums(e.astype(F32) * u[...] + b.astype(F32) * v[...])
        for j, q in ((3, q3), (1, q1), (2, q2), (0, q0)):
            rows_w = slice(j * width, (j + 1) * width)
            q[at, :] = (dot_nt(e, w[rows_w, :channels]) + dot_nt(b, w[rows_w, channels:])).astype(q.dtype)

    @pl.when(i == third + blocks // 2 - 1)
    def _():
        scatter[0].start()
        scatter[2].start()

    @pl.when(i == third + blocks - 1)
    def _():
        scatter[1].start()
        small_x.start()
        scatter[0].wait_recv()
        add_into(q2, r3, 0, half)
        scatter[3].start()
        scatter[4].start()

    last = third + blocks

    @pl.when(i == last)
    def _():
        small_x.wait_recv()
        dots_x[...] = dots_x[...] + dots[...]
        small_y.start()
        scatter[1].wait_recv()
        add_into(q1, r3, half, half)
        scatter[5].start()

    def finish(start, first):
        scatter[first].wait_recv()
        scatter[first + 1].wait_recv()
        sum_grad = None
        for r in range(start, start + half, 128):
            at = slice(r, r + 128)
            d = q0[at, :] + rx[at, :].astype(F32) + ry[at, :].astype(F32)
            s, m = scale[at, :], x[at, :]
            t = as_column(dots_x[:, at] + dots_y[:, at], width)
            grad[at, :] = dx[at, :] + s * gain[0:1, :width] * d - m * (s * s) * t * (1.0 / D)
            term = jnp.sum(d * m * s, axis=0, keepdims=True)
            sum_grad = term if sum_grad is None else sum_grad + term
        return sum_grad

    for t in range(len(pieces) + 2):

        @pl.when(i == t + 1)
        def _():
            tick(t)

    @pl.when(i == last + 1)
    def _():
        small_y.wait_recv()
        gain_grad[0:1, :] = finish(0, 2)

    @pl.when(i == last + 2)
    def _():
        gain_grad[0:1, :] = gain_grad[0:1, :] + finish(half, 4)
        for n in range(1, count + 1):

            @pl.when(seq >= n)
            def _():
                hand_on[n - 1].wait_send()

        @pl.when(seq >= 1)
        def _():
            hand_edge.wait_send()

        for m in to_y.values():
            m.wait_recv()
        for m in scatter + [small_x, small_y] + list(to_y.values()):
            m.wait_send()
        for c in to_out.values():
            c.wait()


def back(errs, w_out, states, v, recall, conv, admit, u, off, soft, taps, rw, aw, border, earlier, w, scale, x, dx, gain, sum_gu, sum_down):
    rows, channels = states.shape
    width = x.shape[1]
    heads = channels // 128
    block = ROW_BLOCK
    blocks = rows // block
    count = earlier.shape[0]
    steps = 2 * heads + blocks + 3
    assert steps >= 15

    def both(i):
        return jnp.where(i < heads, i, jnp.clip(i - heads, 0, heads - 1))

    def second(i):
        return jnp.clip(i - heads, 0, heads - 1)

    def on(shape, pick, axis):
        if axis == 0:
            return pl.BlockSpec(shape, lambda i: (pick(i),) + (0,) * (len(shape) - 1))
        return pl.BlockSpec(shape, lambda i: (0, pick(i)))

    def third(i):
        return jnp.clip(i - 2 * heads, 0, blocks - 1)

    def first(i):
        return jnp.minimum(i, heads - 1)

    tall = (rows, 128)
    gate = (1, 128, 128)
    own_gate = on(gate, second, 0)
    chunk = pltpu.VMEM((rows, width), BF)
    lanes = pltpu.VMEM((8, rows), F32)
    gu, dn = pltpu.VMEM(sum_gu.shape, BF), pltpu.VMEM(sum_down.shape, BF)
    piece = pltpu.VMEM((heads, 8, 128), F32)
    half_gu, half_dn = (sum_gu.shape[0] // 2, sum_gu.shape[1]), (sum_down.shape[0], width)
    count_sems = 8 + count + 1 + 24 + 6
    return pl.pallas_call(
        functools.partial(back_body, heads, blocks, count),
        grid=(steps,),
        in_specs=[whole_spec((rows, width))] * 4
        + [
            on((128, 4 * width), first, 0),
            on(tall, both, 1),
            on(tall, first, 1),
            on(tall, both, 1),
            on(tall, second, 1),
            on(tall, second, 1),
            on(tall, second, 1),
            whole_spec(off.shape),
            on((1, 128), both, 1),
            on((KW, 128), second, 1),
            own_gate,
            own_gate,
            on((8, 128), second, 1),
            pl.BlockSpec((count, 1, 8, 128), lambda i: (0, second(i), 0, 0)),
            on((block, channels), third, 0),
            on((block, channels), third, 0),
            whole_spec(w.shape),
            whole_spec(scale.shape),
            whole_spec(x.shape),
            whole_spec(dx.shape),
            whole_spec(gain.shape),
            any_spec(),
            any_spec(),
        ],
        out_specs=[
            whole_spec((rows, channels)),
            whole_spec((rows, 4 * width)),
            on((block, channels), third, 0),
            whole_spec((rows, width)),
            whole_spec((8, width)),
            on(gate, second, 0),
            on(gate, second, 0),
            on((8, 128), second, 1),
        ]
        + [any_spec()] * 4,
        out_shape=[
            sds((rows, channels), BF),
            sds((rows, 4 * width), BF),
            sds((rows, channels), BF),
            sds((rows, width), F32),
            sds((8, width), F32),
            sds((heads, 128, 128), F32),
            sds((heads, 128, 128), F32),
            sds((8, channels), F32),
            sds(half_gu, BF),
            sds(half_gu, BF),
            sds(half_dn, BF),
            sds(half_dn, BF),
        ],
        scratch_shapes=[pltpu.VMEM((heads, rows, 128), F32)] * 2
        + [
            pltpu.VMEM((rows + 8, 128), F32),
            pltpu.VMEM((rows + 8, 128), F32),
            pltpu.VMEM((rows + 8, 128), F32),
            pltpu.VMEM((rows + 16, 128), F32),
            piece,
            pltpu.VMEM((count, heads, 8, 128), F32),
            piece,
            piece,
            pltpu.SemaphoreType.DMA((2,)),
            pltpu.VMEM((rows, width), F32),
        ]
        + [chunk] * 6
        + [lanes] * 3
        + [gu] * 3
        + [dn] * 3
        + [pltpu.SemaphoreType.DMA((6,))]
        + [pltpu.SemaphoreType.DMA((count_sems,))] * 2,
        compiler_params=comm_params(4),
        cost_estimate=cost(64 * rows * w.size, rows * channels * 60, rows * channels * 8),
        name="back",
    )(
        *errs, w_out, states, v, recall, conv, admit, u, off, soft, taps, rw, aw, border, earlier,
        u, v, w, scale, x, dx, gain, sum_gu, sum_down,
    )


TAIL_MESSAGES = 48


def tail_body(*refs):
    (mixed, er, n1, eu, ev, grad_recall, grad_admit, grad_small, grad_mixer, grad_feed) = refs[:10]
    (p0, p1, p2, p3, mid, grad_chunk) = refs[10:16]
    (mine_in, far_in, mine_out, far_out, gates, tiny_out, out, grad) = refs[16:24]
    (n1_v, eu_v, ev_v, s_in, p_in, c_in, a_in, b_in, y_in, s_out, p_out, c_out, a_out, b_out, y_out) = refs[24:39]
    (s_gt, p_gt, c_gt, a_gt, b_gt, y_gt, s_ty, p_ty, c_ty, a_ty, b_ty) = refs[39:50]
    (q1, q2, q3, r3, rx, ry, own_a, other_a, own_b, other_b, load, send, recv) = refs[50:]
    made = Messages((send, recv))
    col = lax.axis_index("col")
    y, core = lax.div(col, 2), lax.rem(col, 2)
    to_core, to_y = neighbour_core(), neighbour_y()
    rows, width = p0.shape
    part = width // 2
    half_tokens = rows // 2
    channels = eu.shape[1]
    heads = grad_recall.shape[0]
    copies = []

    def copy(src, dst):
        copies.append(pltpu.make_async_copy(src, dst, load.at[len(copies)]))
        return copies[-1]

    outs_in = [copy(p3, q3), copy(p1, q1), copy(p2, q2)]
    late = [copy(n1, n1_v), copy(eu, eu_v), copy(ev, ev_v)]
    scatter = made.block(scatter_messages, q1, q2, q3, r3, rx, ry)
    half = width // 2
    a, b = pl.ds(0, half), pl.ds(half, half)
    c, d = pl.ds(2 * half, half), pl.ds(3 * half, half)
    inner = s_out.shape[0] // 2
    up, low = pl.ds(0, inner), pl.ds(inner, inner)
    lanes_far, lanes_own = pl.ds(width, width), pl.ds(0, width)
    group_in, group_out = (s_in, a_in, b_in), (s_out, a_out, b_out)
    pieces = [[s_ty, a_ty, b_ty], [s_gt, a_gt, b_gt]]
    pieces += [[r.at[at, lanes_far] for r in group_out] for at in (up, low)]
    pieces += [[r.at[at, lanes_own] for r in group_out] for at in (up, low)]
    pieces += [[r.at[at, :] for r in group_in] for at in (c, d, a, b)]
    count = len(pieces)
    total = SeqSum(pieces, (send, recv), made.used)
    made.used += 2 * count
    core_ty, core_gt = made.new(p_ty, c_ty, to_core), made.new(p_gt, c_gt, to_core)
    core_out = made.new(p_out, c_out, to_core)
    core_in = [made.new(p_in.at[at, :], c_in.at[at, :], to_core) for at in (c, d, a, b)]
    over_y = {
        1: made.new(s_gt, y_gt, to_y),
        2: made.new(s_out.at[up, lanes_far], y_out.at[up, :], to_y),
        3: made.new(s_out.at[low, lanes_far], y_out.at[low, :], to_y),
        6: made.new(s_in.at[c, :], y_in.at[a, :], to_y),
        7: made.new(s_in.at[d, :], y_in.at[b, :], to_y),
    }
    send_out, send_grad = made.new(other_a, out.at[core], to_core), made.new(other_b, grad.at[core], to_core)
    keep_out, keep_grad = copy(own_a, out.at[core]), copy(own_b, grad.at[core])

    for m in outs_in + late:
        m.start()
    greet_all((neighbour_x(), to_y, to_core, neighbour_end(), neighbour_middle()))

    for n, source in enumerate((grad_recall, grad_admit)):
        for h in range(heads):
            at = slice((n * heads + h) * 128, (n * heads + h + 1) * 128)
            p_gt[at, :] = source[h].astype(BF)
    core_gt.start()
    p_ty[...] = jnp.zeros_like(p_ty)
    p_ty[0:8, :] = grad_small[...]
    for n, source in enumerate((grad_mixer, grad_feed)):
        g = jnp.broadcast_to(source[0:1, :], (8, width))
        g = jnp.where(core == 0, g, pltpu.roll(g, part, 1))
        p_ty[8 + n : 9 + n, 0:width] = g[0:1, :]
    core_ty.start()
    for m in outs_in:
        m.wait()
    scatter[0].start()
    scatter[1].start()
    scatter[2].start()
    g = dot_tn(mixed[...], er[...])
    p_out[...] = g[:, 2 * width :].astype(BF)
    core_out.start()
    s_out[...] = g[:, : 2 * width].astype(BF)
    core_ty.wait_recv()
    s_ty[...] = p_ty[...] + c_ty[...]
    total.begin(0)
    core_gt.wait_recv()
    put_in(s_gt, p_gt)
    plus_in(s_gt, c_gt)
    total.begin(1)

    def tile(n, target, row):
        at = slice(n * width, (n + 1) * width)
        where = slice(row, row + width)
        target[where, :channels] = dot_tn(n1_v[:, at], eu_v[...]).astype(BF)
        target[where, channels:] = dot_tn(n1_v[:, at], ev_v[...]).astype(BF)

    core_out.wait_recv()
    plus_in(s_out, c_out)
    for n in range(2, 6):
        total.begin(n)
    for m in late:
        m.wait()
    tile(3, p_in, width)
    core_in[0].start()
    core_in[1].start()
    tile(1, s_in, width)
    total.relay(0)
    total.relay(1)
    total.settle(0)
    core_in[0].wait_recv()
    core_in[1].wait_recv()
    plus_in(s_in.at[pl.ds(width, width), :], c_in.at[pl.ds(width, width), :])
    total.begin(6)
    total.begin(7)
    total.relay(2)
    total.settle(1)
    total.finish(0)
    tile(2, p_in, 0)
    core_in[2].start()
    core_in[3].start()
    total.relay(3)
    total.settle(2)
    total.finish(1)
    over_y[1].start()
    tile(0, s_in, 0)
    core_in[2].wait_recv()
    core_in[3].wait_recv()
    plus_in(s_in.at[pl.ds(0, width), :], c_in.at[pl.ds(0, width), :])
    total.begin(8)
    total.begin(9)

    def chunk_out(value, own, other, at):
        own[at, :] = value[:, :part]
        other[at, :] = pltpu.roll(value, part, 1)[:, :part]

    def finish_out(start, first):
        scatter[first].wait_recv()
        scatter[first + 1].wait_recv()
        for r in range(start, start + half_tokens, 128):
            at = slice(r, r + 128)
            value = p0[at, :] + rx[at, :].astype(F32) + ry[at, :].astype(F32) + mid[at, :]
            chunk_out(value, own_a, other_a, at)

    for n in range(4, count + 2):
        if n < count:
            total.relay(n)
        if n - 1 < count:
            total.settle(n - 1)
        total.finish(n - 2)
        if n - 2 in over_y:
            over_y[n - 2].start()
        if n == 4:
            scatter[0].wait_recv()
            add_into(q2, r3, 0, half_tokens)
            scatter[3].start()
            scatter[4].start()
        if n == 5:
            scatter[1].wait_recv()
            add_into(q1, r3, half_tokens, half_tokens)
            scatter[5].start()
            for r in range(0, rows, 128):
                at = slice(r, r + 128)
                chunk_out(grad_chunk[at, :], own_b, other_b, at)
            send_grad.start()
            keep_grad.start()
        if n == 8:
            finish_out(0, 2)
        if n == 9:
            finish_out(half_tokens, 4)
            send_out.start()
            keep_out.start()
    put_in(tiny_out, s_ty)
    put_in(mine_in, s_in.at[pl.ds(0, width), :])
    put_in(mine_out, s_out.at[:, lanes_own])
    over_y[1].wait_recv()
    for n in (0, 1):
        for h in range(heads):
            at = slice((n * heads + h) * 128, (n * heads + h + 1) * 128)
            gates[n, y * heads + h] = s_gt[at, :].astype(F32)
            gates[n, (1 - y) * heads + h] = y_gt[at, :].astype(F32)
    for n in (2, 3, 6, 7):
        over_y[n].wait_recv()
    put_in(far_out, y_out)
    put_in(far_in, y_in)
    for m in (send_out, send_grad):
        m.wait_recv()
    for m in [core_ty, core_gt, core_out, send_out, send_grad] + core_in + list(over_y.values()) + scatter:
        m.wait_send()
    keep_out.wait()
    keep_grad.wait()


def tail(mixed, er, n1, eu, ev, grad_recall, grad_admit, grad_small, grad_mixer, grad_feed, parts, mid, grad_chunk):
    rows, channels = eu.shape
    width = mid.shape[1]
    part = width // 2
    heads = grad_recall.shape[0]
    inner = mixed.shape[1]
    big = pltpu.VMEM((2 * width, 2 * channels), BF)
    tall = pltpu.VMEM((inner, 2 * width), BF)
    gate = pltpu.VMEM((2 * heads * 128, 128), BF)
    tiny = pltpu.VMEM((16, channels), F32)
    piece = pltpu.VMEM((rows, width), BF)
    side = pltpu.VMEM((rows, part), F32)
    quarter_in, quarter_out = (width, 2 * channels), (inner, width)
    final = sds((2, rows, part), F32)
    return pl.pallas_call(
        tail_body,
        in_specs=[pl.BlockSpec(memory_space=pltpu.VMEM)] * 2
        + [any_spec()] * 3
        + [pl.BlockSpec(memory_space=pltpu.VMEM)] * 6
        + [any_spec()] * 3
        + [pl.BlockSpec(memory_space=pltpu.VMEM)] * 2,
        out_specs=[pl.BlockSpec(memory_space=pltpu.VMEM)] * 6 + [any_spec()] * 2,
        out_shape=[sds(quarter_in, BF)] * 2
        + [sds(quarter_out, BF)] * 2
        + [sds((2, 2 * heads, 128, 128), F32), sds((16, channels), F32), final, final],
        scratch_shapes=[
            pltpu.VMEM((rows, 4 * width), BF),
            pltpu.VMEM((rows, channels), BF),
            pltpu.VMEM((rows, channels), BF),
        ]
        + [big] * 5
        + [pltpu.VMEM(quarter_in, BF)]
        + [tall] * 5
        + [pltpu.VMEM(quarter_out, BF)]
        + [gate] * 6
        + [tiny] * 5
        + [piece] * 6
        + [side] * 4
        + [pltpu.SemaphoreType.DMA((8,))]
        + [pltpu.SemaphoreType.DMA((TAIL_MESSAGES,))] * 2,
        compiler_params=pltpu.CompilerParams(
            vmem_limit_bytes=VMEM_LIMIT, collective_id=6, has_side_effects=True
        ),
        cost_estimate=cost(60 * rows * width * channels * 4, nbytes(n1, eu, ev, mixed, er)),
        name="tail",
    )(mixed, er, n1, eu, ev, grad_recall, grad_admit, grad_small, grad_mixer, grad_feed, *parts, mid, grad_chunk)


def arrange_body(place, mine_gu, far_gu, mine_dn, far_dn, mine_in, far_in, mine_out, far_out, *outs):
    gate, up, down, inp, branch, out = outs
    row, y = place[0], place[1]
    first = pl.program_id(0) == 0

    def side_by_side(mine, far, left, right):
        lanes = left.shape[1] // 2
        for target, at in ((left, 0), (right, mine.shape[1] // 2)):
            m = mine[:, at : at + lanes].astype(F32)
            t = far[:, at : at + lanes].astype(F32)
            target[:, :lanes] = jnp.where(y == 0, m, t)
            target[:, lanes:] = jnp.where(y == 0, t, m)

    def stack_up(mine, far, target):
        value = jnp.where(first, mine[...].astype(F32), far[...].astype(F32))
        target[...] = jnp.where(row == 0, value, pltpu.roll(value, value.shape[1] // 2, 1))

    side_by_side(mine_gu, far_gu, gate, up)
    side_by_side(mine_in, far_in, inp, branch)
    stack_up(mine_dn, far_dn, down)
    stack_up(mine_out, far_out, out)


def arrange(place, mine_gu, far_gu, mine_dn, far_dn, mine_in, far_in, mine_out, far_out):
    width, units = mine_dn.shape[1], mine_dn.shape[0]
    inner = mine_out.shape[0]
    lanes_gu, lanes_in = mine_gu.shape[1], mine_in.shape[1]
    quarter = width // 4

    def rows_in(i, j, place):
        return (2 * i + j, 0)

    def rows_to(i, j, place):
        return (2 * (i + place[0] - 2 * i * place[0]) + j, 0)

    def near(i, j, place):
        return (jnp.where(i == 0, j, 1), 0)

    def far(i, j, place):
        return (jnp.where(i == 0, 0, j), 0)

    def stack_to(i, j, place):
        return (2 * (i + place[1] - 2 * i * place[1]) + j, 0)

    def spec(rows, lanes, at):
        return pl.BlockSpec((rows, lanes), at)

    shapes = [(width, lanes_gu)] * 2 + [(2 * units, width)] + [(width, lanes_in)] * 2 + [(2 * inner, width)]
    return pl.pallas_call(
        arrange_body,
        grid_spec=pltpu.PrefetchScalarGridSpec(
            num_scalar_prefetch=1,
            grid=(2, 2),
            in_specs=[
                spec(quarter, lanes_gu, rows_in),
                spec(quarter, lanes_gu, rows_in),
                spec(units // 2, width, near),
                spec(units // 2, width, far),
                spec(quarter, lanes_in, rows_in),
                spec(quarter, lanes_in, rows_in),
                spec(inner // 2, width, near),
                spec(inner // 2, width, far),
            ],
            out_specs=[spec(quarter, lanes_gu, rows_to)] * 2
            + [spec(units // 2, width, stack_to)]
            + [spec(quarter, lanes_in, rows_to)] * 2
            + [spec(inner // 2, width, stack_to)],
        ),
        out_shape=[sds(s, F32) for s in shapes],
        compiler_params=pltpu.CompilerParams(vmem_limit_bytes=VMEM_LIMIT),
        cost_estimate=cost(1000000, 24000000),
        name="arrange",
    )(place, mine_gu, far_gu, mine_dn, far_dn, mine_in, far_in, mine_out, far_out)


def local_fast(
    stream_in,
    cotangent,
    doc_lengths,
    mixer_gain,
    input_weight,
    branch_weight,
    filter_taps,
    recall_gate,
    admit_gate,
    decay_param,
    output_weight,
    feed_gain,
    gate_weight,
    up_weight,
    down_weight,
):
    tokens = stream_in.shape[1]
    count = lax.axis_size("seq")
    part = stream_in.shape[2]
    seq = lax.axis_index("seq")
    row = lax.axis_index("row")
    col = lax.axis_index("col")
    y, core = col // 2, col % 2
    heads = recall_gate.shape[0] // 2
    rw = lax.dynamic_slice_in_dim(recall_gate, y * heads, heads, 0)
    aw = lax.dynamic_slice_in_dim(admit_gate, y * heads, heads, 0)
    soft_own = jax.nn.softplus(-decay_param)[None]
    small = jnp.concatenate(
        [filter_taps, soft_own, decay_param[None], jnp.zeros((2,) + decay_param.shape, F32)]
    )
    gains = jnp.concatenate([mixer_gain[None], feed_gain[None], jnp.zeros((6, part), F32)])

    lengths = lax.dynamic_index_in_dim(doc_lengths, core, 0, False)
    offset = doc_offset(lengths, seq * tokens, tokens)
    edge = jnp.full((8,), -1, jnp.int32)
    off = jnp.concatenate([edge, offset, edge])[:, None]

    (
        x, g, g_low, w_out, w_down, gains_all, small, s1, u, v, border, earlier, mid, mid_low,
        n1, conv, recall, admit, states, mixed, ex, ey, ed, mx, my, md, far_w, sib_own, sib_far, w_in,
    ) = front(
        stream_in, cotangent, input_weight, branch_weight, output_weight, gate_weight, up_weight, down_weight,
        gains, small, recall_gate, admit_gate, off, count - 1,
    )
    taps, soft, decay = small[:KW], small[KW : KW + 1], small[KW + 1 : KW + 2]
    p0, p1, p2, p3, dx2, *dx_all, grad_feed, sum_down, sum_gu = feed(
        (mid_low, mx, my, md), (g_low, ex, ey, ed), mid, g, gains_all, w_down,
        (gate_weight, up_weight, sib_own, far_w, sib_far),
    )
    (
        ev, er, eu, grad_chunk, grad_mixer, grad_recall, grad_admit, grad_small, mine_gu, far_gu, mine_down, far_down
    ) = back(
        dx_all, w_out, states, v, recall, conv, admit, u, off, soft, taps, rw, aw, border, earlier,
        w_in, s1, x, dx2, gains_all, sum_gu, sum_down,
    )

    mine_in, far_in, mine_out, far_out, gates, tiny, out, grad = tail(
        mixed, er, n1, eu, ev, grad_recall, grad_admit, grad_small, grad_mixer, grad_feed,
        (p0, p1, p2, p3), mid, grad_chunk,
    )
    place = jnp.stack([row, y]).astype(jnp.int32)
    grad_gate, grad_up, grad_down, grad_input, grad_branch, grad_output = arrange(
        place, mine_gu, far_gu, mine_down, far_down, mine_in, far_in, mine_out, far_out
    )
    own = taps.shape[1] // 2
    mine = lax.dynamic_slice_in_dim(tiny[:8], core * own, own, 1)
    gain_grads = lax.dynamic_slice_in_dim(tiny[8:10, : 2 * part], core * part, part, 1)
    return (
        out,
        grad,
        gain_grads[0],
        grad_input,
        grad_branch,
        mine[:KW],
        gates[0],
        gates[1],
        mine[KW] * 8.0 * jax.nn.sigmoid(-decay_param),
        grad_output,
        gain_grads[1],
        grad_gate,
        grad_up,
        grad_down,
    )


def solution(mesh):
    in_specs = (
        P(None, "seq", ("col", "row")),
        P(None, "seq", ("col", "row")),
        P(),
        P(("col", "row")),
        P("col", "row"),
        P("col", "row"),
        P(None, ("row", "col")),
        P("row", None, None),
        P("row", None, None),
        P(("row", "col")),
        P("row", "col"),
        P(("col", "row")),
        P("col", "row"),
        P("col", "row"),
        P("row", "col"),
    )
    out_specs = (
        P(None, "seq", ("col", "row")),
        P(None, "seq", ("col", "row")),
        P(("col", "row")),
        P("col", "row"),
        P("col", "row"),
        P(None, ("row", "col")),
        P("row", None, None),
        P("row", None, None),
        P(("row", "col")),
        P("row", "col"),
        P(("col", "row")),
        P("col", "row"),
        P("col", "row"),
        P("row", "col"),
    )
    plan = local_fast if dict(mesh.shape) == {"seq": 4, "row": 2, "col": 4} else local
    return jax.shard_map(plan, mesh=mesh, in_specs=in_specs, out_specs=out_specs, check_vma=False)
```

```python
import functools

import jax
import jax.numpy as jnp
from jax import lax
from jax.experimental import pallas as pl
from jax.experimental.pallas import tpu as pltpu
from jax.sharding import PartitionSpec as P

D = 1536
KW = 4


EPSILON = 1e-06
PRECISE = lax.Precision.HIGHEST
SUM_ROWS = (((0,), (0,)), ((), ()))
SUM_COLS = (((1,), (1,)), ((), ()))


def as_sent(value):
    return jax.tree.map(lambda a: a.astype(jnp.bfloat16) if a.dtype == jnp.float32 else a, value)


def passed_along(block, axis, distance):
    devices = range(lax.axis_size(axis))
    route = [(i - distance, i) for i in devices if i - distance in devices]
    return lax.ppermute(block, axis, route)


def entering_2(part, axis, combine, identity, reverse):
    count = lax.axis_size(axis)
    place = lax.axis_index(axis)
    ahead = count - 1 - place if reverse else place
    gathered = jax.tree.map(lambda a: lax.all_gather(a, axis), part)
    state = jax.tree.map(lambda a, e: jnp.zeros_like(a) + jnp.asarray(e, a.dtype), part, identity)

    def one(hop, state):
        source = count - 1 - hop if reverse else hop
        return combine(
            state, jax.tree.map(lambda a: lax.dynamic_index_in_dim(a, source, 0, False), gathered)
        )

    return lax.fori_loop(0, ahead, one, state)


def compose(first, second):
    return (first[0] * second[0], second[0] * first[1] + second[1])


def convolve(source, taps, offset, border):
    tokens = source.shape[0]
    extended = jnp.concatenate([border, source], axis=0)
    result = jnp.zeros_like(source)
    for lag_index in range(KW):
        anchor = KW - 1 - lag_index
        valid = (offset >= lag_index).astype(jnp.float32)[:, None]
        result = result + taps[lag_index] * extended[anchor : anchor + tokens] * valid
    return result


def slab_pre(conv_value, recall_value, admit_value):
    tokens = conv_value.shape[0]
    blocks = conv_value.reshape(tokens, recall_value.shape[0], recall_value.shape[1])
    recall_pre = jnp.einsum("thi,hij->thj", blocks, recall_value, precision=PRECISE).reshape(
        tokens, -1
    )
    admit_pre = jnp.einsum("thi,hij->thj", blocks, admit_value, precision=PRECISE).reshape(
        tokens, -1
    )
    return (recall_pre, admit_pre)


def own_terms(conv_value, recall_pre, admit_pre, decay_value, resume):
    recall = jax.nn.sigmoid(recall_pre)
    admit = jax.nn.sigmoid(admit_pre)
    log_decay = -8.0 * recall * jax.nn.softplus(-decay_value)
    decays = jnp.exp(log_decay) * resume[:, None]
    drives = jnp.sqrt(-jnp.expm1(2.0 * log_decay)) * admit * conv_value
    return (decays, drives)


def width_total(partial_value):
    return lax.psum(partial_value, ("row", "col"))


def gather_row(source):
    return lax.all_gather(source, "row", axis=1, tiled=True)


def gather_col(source):
    return jax.tree.map(
        lambda part, own: part.astype(own.dtype),
        lax.all_gather(as_sent(source), "col", axis=1, tiled=True),
        source,
    )


def scatter_col(source):
    return (
        lax.psum_scatter(source[0], "col", scatter_dimension=1, tiled=True),
        lax.psum_scatter(source[1], "col", scatter_dimension=1, tiled=True),
    )


def scatter_col_back(source):
    return lax.psum_scatter(source, "col", scatter_dimension=1, tiled=True)


def scatter_row(source):
    return lax.psum_scatter(source, "row", scatter_dimension=1, tiled=True)


def over_seq(grads):
    return (
        lax.psum(grads[0].astype(jnp.bfloat16), "seq").astype(jnp.float32),
        lax.psum(grads[1].astype(jnp.bfloat16), "seq").astype(jnp.float32),
        lax.psum(grads[2].astype(jnp.bfloat16), "seq").astype(jnp.float32),
        lax.psum(grads[3].astype(jnp.bfloat16), "seq").astype(jnp.float32),
        lax.psum(grads[4].astype(jnp.bfloat16), "seq").astype(jnp.float32),
        lax.psum(grads[5].astype(jnp.bfloat16), "seq").astype(jnp.float32),
        lax.psum(grads[6].astype(jnp.bfloat16), "seq").astype(jnp.float32),
        lax.psum(grads[7].astype(jnp.bfloat16), "seq").astype(jnp.float32),
        lax.psum(grads[8].astype(jnp.bfloat16), "seq").astype(jnp.float32),
        lax.psum(grads[9].astype(jnp.bfloat16), "seq").astype(jnp.float32),
        lax.psum(grads[10].astype(jnp.bfloat16), "seq").astype(jnp.float32),
        lax.psum(grads[11].astype(jnp.bfloat16), "seq").astype(jnp.float32),
    )


def normalize(source, scales):
    factor = lax.rsqrt(width_total(jnp.sum(source * source, axis=1)) / D + EPSILON)
    return (source * factor[:, None] * scales, factor)


def norm_back(source, scales, factor, grad_norm):
    weighted = scales * grad_norm
    summed = width_total(jnp.sum(weighted * source, axis=1))
    grad_source = (
        factor[:, None] * weighted - source * (factor * factor * factor * summed / D)[:, None]
    )
    grad_scales = jnp.sum(grad_norm * source * factor[:, None], axis=0)
    return (grad_source, grad_scales)


def doc_offset(lengths, anchor, tokens):
    starts = jnp.cumsum(lengths, dtype=jnp.int32) - lengths
    places = anchor + jnp.arange(tokens, dtype=jnp.int32)
    begins = jnp.max(jnp.where(starts[None, :] <= places[:, None], starts[None, :], 0), axis=1)
    return places - begins


def matmul_rows(left, right):
    return lax.dot_general(left, right, SUM_ROWS, preferred_element_type=jnp.float32)


def matmul_cols(left, right):
    return lax.dot_general(left, right, SUM_COLS, preferred_element_type=jnp.float32)


def local(
    stream_in,
    cotangent,
    doc_lengths,
    mixer_gain,
    input_weight,
    branch_weight,
    filter_taps,
    recall_gate,
    admit_gate,
    decay_param,
    output_weight,
    feed_gain,
    gate_weight,
    up_weight,
    down_weight,
):
    tokens = stream_in.shape[1]
    anchor = lax.axis_index("seq") * tokens
    channels = decay_param.shape[0]
    col_start = lax.axis_index("col") * channels
    params = (
        mixer_gain,
        input_weight,
        branch_weight,
        filter_taps,
        recall_gate,
        admit_gate,
        decay_param,
        output_weight,
        feed_gain,
        gate_weight,
        up_weight,
        down_weight,
    )
    totals = tuple((jnp.zeros(w.shape, jnp.float32) for w in params))
    identity = (jnp.ones_like(decay_param), jnp.zeros_like(decay_param))
    outputs = []
    grads_in = []
    for micro in range(stream_in.shape[0]):
        offset = doc_offset(doc_lengths[micro], anchor, tokens)
        resume = (offset > 0).astype(jnp.float32)
        source = stream_in[micro]
        normed, factor_one = normalize(source, mixer_gain)
        normed_low = normed.astype(jnp.bfloat16)
        normed_all = gather_row(normed_low)
        rec_in, branch = scatter_col(
            (
                jnp.dot(normed_all, input_weight, preferred_element_type=jnp.float32),
                jnp.dot(normed_all, branch_weight, preferred_element_type=jnp.float32),
            )
        )
        border = passed_along(rec_in[tokens - (KW - 1) :], "seq", 1)
        conv_out = convolve(rec_in, filter_taps, offset, border)
        conv_slab = lax.all_gather(conv_out, "col", axis=1, tiled=True)
        slab_values, slab_pull = jax.vjp(slab_pre, conv_slab, recall_gate, admit_gate)
        recall_pre = lax.dynamic_slice_in_dim(slab_values[0], col_start, channels, 1)
        admit_pre = lax.dynamic_slice_in_dim(slab_values[1], col_start, channels, 1)

        def local_gates(conv_value, recall_value, admit_value, decay_value):
            return own_terms(conv_value, recall_value, admit_value, decay_value, resume)

        (decays, drives), gates_pull = jax.vjp(
            local_gates, conv_out, recall_pre, admit_pre, decay_param
        )
        cum_decay, local_state = lax.associative_scan(compose, (decays, drives), axis=0)
        entering = entering_2((cum_decay[-1], local_state[-1]), "seq", compose, identity, False)[1]
        states = local_state + cum_decay * entering
        branch_act = jax.nn.gelu(branch)
        mixed_all = gather_col((states * branch_act).astype(jnp.bfloat16))
        middle = source + scatter_row(
            jnp.dot(mixed_all, output_weight, preferred_element_type=jnp.float32)
        )
        normed_two, factor_two = normalize(middle, feed_gain)
        normed_two_low = normed_two.astype(jnp.bfloat16)
        normed_two_all = gather_row(normed_two_low)
        gate_pre, up_pre = scatter_col(
            (
                jnp.dot(normed_two_all, gate_weight, preferred_element_type=jnp.float32),
                jnp.dot(normed_two_all, up_weight, preferred_element_type=jnp.float32),
            )
        )
        gate_act = jax.nn.gelu(gate_pre)
        hidden_all = gather_col((gate_act * up_pre).astype(jnp.bfloat16))
        outputs.append(
            middle
            + scatter_row(jnp.dot(hidden_all, down_weight, preferred_element_type=jnp.float32))
        )
        upstream = cotangent[micro]
        upstream_all = gather_row(upstream.astype(jnp.bfloat16))
        grad_down = matmul_rows(hidden_all, upstream_all)
        grad_hidden = scatter_col_back(matmul_cols(upstream_all, down_weight))
        gate_value, gelu_pull = jax.vjp(jax.nn.gelu, gate_pre)
        error_gate = gelu_pull(grad_hidden * up_pre)[0].astype(jnp.bfloat16)
        error_up = (grad_hidden * gate_act).astype(jnp.bfloat16)
        gate_err_all, up_err_all = gather_col((error_gate, error_up))
        grad_gate = matmul_rows(normed_two_all, gate_err_all)
        grad_up = matmul_rows(normed_two_all, up_err_all)
        grad_normed_two = scatter_row(
            matmul_cols(gate_err_all, gate_weight) + matmul_cols(up_err_all, up_weight)
        )
        back_middle, grad_feed = norm_back(middle, feed_gain, factor_two, grad_normed_two)
        grad_middle = upstream + back_middle
        rec_err_all = gather_row(grad_middle.astype(jnp.bfloat16))
        grad_output = matmul_rows(mixed_all, rec_err_all)
        grad_mixed = scatter_col_back(matmul_cols(rec_err_all, output_weight))
        branch_value, branch_pull = jax.vjp(jax.nn.gelu, branch)
        error_branch = branch_pull(grad_mixed * states)[0].astype(jnp.bfloat16)
        direct = grad_mixed * branch_act
        ahead = jnp.concatenate([decays[1:], jnp.ones_like(decays[:1])], axis=0)
        reach, partial_adj = lax.associative_scan(compose, (ahead, direct), axis=0, reverse=True)
        incoming = entering_2(
            (decays[0] * reach[0], decays[0] * partial_adj[0]), "seq", compose, identity, True
        )[1]
        adjoint = partial_adj + reach * incoming
        previous = jnp.concatenate([entering[None, :], states[:-1]], axis=0)
        conv_direct, grad_recall_pre, grad_admit_pre, grad_decay = gates_pull(
            (adjoint * previous, adjoint)
        )
        recall_all, admit_all = (
            lax.all_gather(grad_recall_pre.astype(jnp.bfloat16), "col", axis=1, tiled=True).astype(
                grad_recall_pre.dtype
            ),
            lax.all_gather(grad_admit_pre.astype(jnp.bfloat16), "col", axis=1, tiled=True).astype(
                grad_admit_pre.dtype
            ),
        )
        grad_slab, grad_recall, grad_admit = slab_pull((recall_all, admit_all))
        grad_conv_out = conv_direct + lax.dynamic_slice_in_dim(grad_slab, col_start, channels, 1)

        def local_conv(input_value, taps_value, border_value):
            return convolve(input_value, taps_value, offset, border_value)

        conv_value, conv_pull = jax.vjp(local_conv, rec_in, filter_taps, border)
        grad_rec_in, grad_taps, grad_border = conv_pull(grad_conv_out)
        from_next = passed_along(grad_border, "seq", -1)
        grad_rec_in = grad_rec_in + jnp.pad(from_next, ((tokens - (KW - 1), 0), (0, 0)))
        error_input = grad_rec_in.astype(jnp.bfloat16)
        in_err_all, branch_err_all = gather_col((error_input, error_branch))
        grad_input = matmul_rows(normed_all, in_err_all)
        grad_branch = matmul_rows(normed_all, branch_err_all)
        grad_normed = scatter_row(
            matmul_cols(in_err_all, input_weight) + matmul_cols(branch_err_all, branch_weight)
        )
        back_source, grad_mixer = norm_back(source, mixer_gain, factor_one, grad_normed)
        grads_in.append(grad_middle + back_source)
        local_grads = (
            grad_mixer,
            grad_input,
            grad_branch,
            grad_taps,
            grad_recall,
            grad_admit,
            grad_decay,
            grad_output,
            grad_feed,
            grad_gate,
            grad_up,
            grad_down,
        )
        local_grads = over_seq(local_grads)
        totals = tuple((acc + new for acc, new in zip(totals, local_grads)))
    return (jnp.stack(outputs), jnp.stack(grads_in)) + tuple(totals)


BF = jnp.bfloat16
F32 = jnp.float32
VMEM_LIMIT = 62 * 1024 * 1024
ROW_BLOCK = 256
GELU_A = 0.7978845608028654
GELU_B = 0.044715


def cost(flops, moved, trans=0):
    return pl.CostEstimate(flops=int(flops), bytes_accessed=int(moved), transcendentals=int(trans))


def params():
    return pltpu.CompilerParams(vmem_limit_bytes=VMEM_LIMIT, dimension_semantics=("arbitrary",))


def nbytes(*arrays):
    return sum(a.size * a.dtype.itemsize for a in arrays)


def gelu_pair(v):
    t = jnp.tanh(GELU_A * (v + GELU_B * v * v * v))
    value = 0.5 * v * (1.0 + t)
    slope = 0.5 * (1.0 + t) + 0.5 * v * (1.0 - t * t) * GELU_A * (1.0 + 3.0 * GELU_B * v * v)
    return value, slope


def minus_expm1(x):
    series = 1.0 + x * (1.0 / 7.0)
    for n in (6, 5, 4, 3, 2):
        series = 1.0 + x * (1.0 / n) * series
    return jnp.where(x > -0.3, -x * series, 1.0 - jnp.exp(x))


def pair_up(left, right):
    width = left.shape[1]
    lane = lax.broadcasted_iota(jnp.int32, left.shape, 1)
    low = lane < width // 2
    return (
        jnp.where(low, left, pltpu.roll(right, width // 2, 1)),
        jnp.where(low, pltpu.roll(left, width // 2, 1), right),
    )


def dot_nn(a, b, precision=None):
    return lax.dot_general(
        a, b, (((1,), (0,)), ((), ())), precision=precision, preferred_element_type=F32
    )


def dot_nt(a, b, precision=None):
    return lax.dot_general(
        a, b, (((1,), (1,)), ((), ())), precision=precision, preferred_element_type=F32
    )


def dot_tn(a, b, precision=None):
    return lax.dot_general(
        a, b, (((0,), (0,)), ((), ())), precision=precision, preferred_element_type=F32
    )


def rows_spec(block, width, start=0):
    return pl.BlockSpec((block, width), lambda i: (i + start, 0))


def whole_spec(shape):
    rank = len(shape)
    return pl.BlockSpec(shape, lambda i: (0,) * rank, pipeline_mode=pl.Buffered(1))


def head_spec(rows, width=128):
    return pl.BlockSpec((rows, width), lambda h: (0, h))


def sds(shape, dtype):
    return jax.ShapeDtypeStruct(shape, dtype)


MESH_ID = pl.DeviceIdType.MESH


def neighbour_x():
    return {"row": 1 - lax.axis_index("row")}


def neighbour_y():
    return {"col": lax.rem(lax.axis_index("col") + 2, 4)}


def greet():
    barrier = pltpu.get_barrier_semaphore()
    for device in (neighbour_x(), neighbour_y()):
        pl.semaphore_signal(barrier, inc=1, device_id=device, device_id_type=MESH_ID)
    pl.semaphore_wait(barrier, 2)


def message(src, dst, device, sems, n):
    send, recv = sems
    return pltpu.make_async_remote_copy(
        src_ref=src,
        dst_ref=dst,
        send_sem=send.at[n],
        recv_sem=recv.at[n],
        device_id=device,
        device_id_type=MESH_ID,
    )


def neighbour_core():
    col = lax.axis_index("col")
    return {"col": col + 1 - 2 * lax.rem(col, 2)}


def neighbour_end():
    seq = lax.axis_index("seq")
    return {"seq": seq + 1 - 2 * lax.rem(seq, 2)}


def neighbour_middle():
    return {"seq": 3 - lax.axis_index("seq")}


def greet_all(devices):
    barrier = pltpu.get_barrier_semaphore()
    for device in devices:
        pl.semaphore_signal(barrier, inc=1, device_id=device, device_id_type=MESH_ID)
    pl.semaphore_wait(barrier, len(devices))


def row_step(ref):
    rows, lanes = ref.shape
    step = 16
    while step * 2 * lanes <= 32768 and rows % (step * 2) == 0:
        step *= 2
    return step


def plus_in(dst, src):
    step = row_step(dst)

    def one(n, carry):
        at = pl.ds(pl.multiple_of(n * step, step), step)
        dst[at, :] = (dst[at, :].astype(F32) + src[at, :].astype(F32)).astype(dst.dtype)
        return carry

    lax.fori_loop(0, dst.shape[0] // step, one, 0)


def put_sum(dst, left, right):
    step = row_step(dst)

    def one(n, carry):
        at = pl.ds(pl.multiple_of(n * step, step), step)
        dst[at, :] = (left[at, :].astype(F32) + right[at, :].astype(F32)).astype(dst.dtype)
        return carry

    lax.fori_loop(0, dst.shape[0] // step, one, 0)


def put_in(dst, src):
    step = row_step(dst)

    def one(n, carry):
        at = pl.ds(pl.multiple_of(n * step, step), step)
        dst[at, :] = src[at, :].astype(dst.dtype)
        return carry

    lax.fori_loop(0, dst.shape[0] // step, one, 0)


class SeqSum:
    def __init__(self, pieces, sems, base):
        self.pieces = pieces
        count = len(pieces)
        self.to_end = [message(s, a, neighbour_end(), sems, base + n) for n, (s, a, b) in enumerate(pieces)]
        self.across = [
            message(s, b, neighbour_middle(), sems, base + count + n) for n, (s, a, b) in enumerate(pieces)
        ]
        seq = lax.axis_index("seq")
        self.middle = (seq == 1) | (seq == 2)
        self.end = (seq == 0) | (seq == 3)

    def begin(self, n):
        @pl.when(self.end)
        def _():
            self.to_end[n].start()

    def relay(self, n):
        s, a, b = self.pieces[n]

        @pl.when(self.middle)
        def _():
            self.to_end[n].wait_recv()
            plus_in(s, a)
            self.across[n].start()

    def settle(self, n):
        s, a, b = self.pieces[n]

        @pl.when(self.middle)
        def _():
            self.across[n].wait_recv()
            self.across[n].wait_send()
            plus_in(s, b)
            self.to_end[n].start()

    def finish(self, n):
        s, a, b = self.pieces[n]

        @pl.when(self.end)
        def _():
            self.to_end[n].wait_recv()
            self.to_end[n].wait_send()
            put_in(s, a)

        @pl.when(self.middle)
        def _():
            self.to_end[n].wait_send()


def scatter_messages(q1, q2, q3, r3, rx, ry, sems, base):
    half = q1.shape[0] // 2
    a, b = pl.ds(0, half), pl.ds(half, half)
    x, y = neighbour_x(), neighbour_y()
    plan = ((q3, r3, a, x), (q3, r3, b, y), (q1, rx, a, x), (q2, ry, a, y), (q2, ry, b, y), (q1, rx, b, x))
    return [
        message(src.at[at, :], dst.at[at, :], dev, sems, base + n)
        for n, (src, dst, at, dev) in enumerate(plan)
    ]


def gather_messages(own, gx, gy, gd, sems, base):
    half = own.shape[0] // 2
    a, b = pl.ds(0, half), pl.ds(half, half)
    x, y = neighbour_x(), neighbour_y()
    plan = ((own, gx, a, x), (own, gy, a, y), (own, gx, b, x), (own, gy, b, y), (gx, gd, a, y), (gy, gd, b, x))
    return [
        message(src.at[at, :], dst.at[at, :], dev, sems, base + n)
        for n, (src, dst, at, dev) in enumerate(plan)
    ]


def gather_messages_by_x(own, gx, gy, gd, sems, base):
    half = own.shape[0] // 2
    a, b = pl.ds(0, half), pl.ds(half, half)
    x, y = neighbour_x(), neighbour_y()
    plan = ((own, gx, a, x), (own, gy, a, y), (own, gx, b, x), (own, gy, b, y), (gy, gd, a, x), (gy, gd, b, x))
    return [
        message(src.at[at, :], dst.at[at, :], dev, sems, base + n)
        for n, (src, dst, at, dev) in enumerate(plan)
    ]


def add_into(dst, src, start, rows):
    plus_in(dst.at[pl.ds(start, rows), :], src.at[pl.ds(start, rows), :])


def load_rows(gate_w, up_w, sib_own, far, sib_far, dst, sem):
    width, lanes = far.shape
    part, units = width // 2, lanes // 2
    row = lax.axis_index("row")
    y = lax.div(lax.axis_index("col"), 2)
    own = pl.ds(pl.multiple_of(y * units, units), units)
    copies = []

    def copy(src, dst):
        copies.append(pltpu.make_async_copy(src, dst, sem.at[len(copies)]))
        copies[-1].start()

    for dx in (0, 1):
        rows = pl.ds(pl.multiple_of(part * (row + dx - 2 * row * dx), part), part)
        at = [pl.ds(((n // 2 * 2 + dx) * 2 + n % 2) * part, part) for n in range(4)]
        copy(gate_w.at[rows, own], dst.at[at[0], pl.ds(0, units)])
        copy(up_w.at[rows, own], dst.at[at[0], pl.ds(units, units)])
        for n, src in enumerate((sib_own, far, sib_far)):
            copy(src.at[rows, :], dst.at[at[n + 1], :])
    return copies


def comm_params(n):
    return pltpu.CompilerParams(
        vmem_limit_bytes=VMEM_LIMIT,
        dimension_semantics=("arbitrary",),
        collective_id=n,
        has_side_effects=True,
    )


def any_spec():
    return pl.BlockSpec(memory_space=pl.ANY)


def held_spec(block, width, last):
    return pl.BlockSpec((block, width), lambda i: (jnp.minimum(i, last), 0))


def full_spec(shape):
    rank = len(shape)
    return pl.BlockSpec(shape, lambda i: (0,) * rank)


def row_sums(values):
    folded = values[:, :128]
    for n in range(128, values.shape[1], 128):
        folded = folded + values[:, n : n + 128]
    return dot_nt(jnp.ones((8, 128), F32), folded, PRECISE)


def as_column(lanes, width):
    first = (lax.broadcasted_iota(jnp.int32, (8, 128), 0) == 0).astype(F32)
    column = dot_tn(lanes, first, PRECISE)
    return jnp.concatenate([column] * (width // 128), axis=1)


def norm_back_rows(start, rows, own_sum, low_x, low_y, dots_x, dots_y, scale, source, gain, base, out, low):
    width = source.shape[1]
    step = 128

    def one(n, sum_grad):
        at = pl.ds(pl.multiple_of(start + n * step, step), step)
        d = own_sum[at, :] + low_x[at, :].astype(F32) + low_y[at, :].astype(F32)
        s, m = scale[at, :], source[at, :]
        t = as_column(dots_x[:, at] + dots_y[:, at], width)
        new = base[at, :] + s * gain * d - m * (s * s) * t * (1.0 / D)
        out[at, :] = new
        if low is not None:
            low[at, :] = new.astype(BF)
        return sum_grad + jnp.sum(d * m * s, axis=0, keepdims=True)

    return lax.fori_loop(0, rows // step, one, jnp.zeros((1, width), F32))


def chain(entries, count):
    state = entries[count - 1, 0, 1:2, :]
    for n in range(count - 2, -1, -1):
        state = entries[n, 0, 1:2, :] + entries[n, 0, 0:1, :] * state
    return state


def carried(entries, h, count):
    state = entries[count - 1, h, 1:2, :]
    for n in range(count - 2, -1, -1):
        state = entries[n, h, 1:2, :] + entries[n, h, 0:1, :] * state
    return state


class Messages:
    def __init__(self, sems):
        self.sems, self.used = sems, 0

    def new(self, src, dst, device):
        self.used += 1
        return message(src, dst, device, self.sems, self.used - 1)

    def block(self, maker, *refs):
        made = maker(*refs, self.sems, self.used)
        self.used += len(made)
        return made


FRONT_MESSAGES = 80


def front_body(heads, blocks, count, *refs):
    (stream, cot, in_w, br_w, out_w, gate_w, up_w, down_w) = refs[:8]
    (gains_in, small_in, recall_gate, admit_gate, off) = refs[8:13]
    (x, g, e_own, w_out, w_down, gains_out, small, s1, u, v, border_out, earlier_out, mid, own) = refs[13:27]
    (n1, conv, recall, admit, states, mixed) = refs[27:33]
    (mx, my, md, far_gu, sib_own, sib_far, w_in_out) = refs[33:40]
    (x_own, x_recv, g_own, g_recv, gains_recv, small_recv, own_low, gx, gy, gd) = refs[40:50]
    (w_in, gains, border, earlier) = refs[50:54]
    (wo, wd, local, cum, ext, ends, q0, q1, q2, q3, r3, rx, ry, load, send, recv) = refs[54:]
    i = pl.program_id(0)
    seq, row, col = lax.axis_index("seq"), lax.axis_index("row"), lax.axis_index("col")
    y = lax.div(col, 2)
    core = lax.rem(col, 2)
    rows, width = x.shape
    part = width // 2
    half = rows // 2
    block = rows // blocks
    channels = u.shape[1]
    units = gate_w.shape[1] // 2
    to_x, to_y, to_core = neighbour_x(), neighbour_y(), neighbour_core()
    made = Messages((send, recv))
    copies = []

    def copy(src, dst):
        copies.append(pltpu.make_async_copy(src, dst, load.at[len(copies)]))
        return copies[-1]

    swap = [
        made.new(stream.at[1 - core], x_recv, to_core),
        made.new(gains_in, gains_recv, to_core),
        made.new(small_in, small_recv, to_core),
    ]
    swap_g = made.new(cot.at[1 - core], g_recv, to_core)
    x_copy, g_copy = copy(stream.at[core], x_own), copy(cot.at[core], g_own)
    gains_x = made.new(gains.at[:, pl.ds(0, width)], gains.at[:, pl.ds(width, width)], to_x)
    gains_y = made.new(gains.at[:, pl.ds(0, width)], gains.at[:, pl.ds(2 * width, width)], to_y)
    gains_d = made.new(gains.at[:, pl.ds(width, width)], gains.at[:, pl.ds(3 * width, width)], to_y)

    def place(dy, dx, dc):
        return pl.ds(pl.multiple_of(((dy * 2 + dx) * 2 + dc) * part, part), part)

    own_cols = pl.ds(pl.multiple_of(y * channels, channels), channels)
    other_cols = pl.ds(pl.multiple_of((1 - y) * channels, channels), channels)
    in_own, in_far, in_core, in_pass = [], [], [], []
    for n, w in enumerate((in_w, br_w)):
        lanes = pl.ds(n * channels, channels)
        for k in (0, 1):
            source = pl.ds(k * part, part)
            dx = row + k - 2 * row * k
            in_far.append(made.new(w.at[source, other_cols], w_in.at[place(1, dx, 0), lanes], to_y))
            in_own.append(copy(w.at[source, own_cols], w_in.at[place(0, dx, 0), lanes]))
            in_core.append(made.new(w.at[source, own_cols], w_in.at[place(0, dx, 1), lanes], to_core))
            in_pass.append(
                made.new(w_in.at[place(1, dx, 0), lanes], w_in.at[place(1, dx, 1), lanes], to_core)
            )

    own_rows = pl.ds(pl.multiple_of(y * channels, channels), channels)
    other_rows = pl.ds(pl.multiple_of((1 - y) * channels, channels), channels)
    wo_own = copy(out_w.at[own_rows, :], wo.at[0, 0])
    wo_far = made.new(out_w.at[other_rows, :], wo.at[1, 0], to_y)
    wo_core = made.new(out_w.at[own_rows, :], wo.at[0, 1], to_core)
    wo_pass = made.new(wo.at[1, 0], wo.at[1, 1], to_core)

    share, share_d = gate_w.shape[0] // (count + 1), units // (count + 1)
    own_units = pl.ds(pl.multiple_of(y * units, units), units)
    other_units = pl.ds(pl.multiple_of((1 - y) * units, units), units)
    at_seq = pl.ds(pl.multiple_of(seq * share, share), share)
    at_seq_d = pl.ds(pl.multiple_of(seq * share_d, share_d), share_d)
    far_d = wd.at[1, 0]
    first_lanes, last_lanes = pl.ds(0, units), pl.ds(units, units)
    from_d = pl.ds(pl.multiple_of((1 - y) * units + seq * share_d, share_d), share_d)
    ff_far = [
        made.new(down_w.at[from_d, :], far_d.at[at_seq_d, :], to_y),
        made.new(gate_w.at[at_seq, other_units], far_gu.at[at_seq, first_lanes], to_y),
        made.new(up_w.at[at_seq, other_units], far_gu.at[at_seq, last_lanes], to_y),
    ]
    others = [{"seq": lax.rem(seq + n, count + 1)} for n in range(1, count + 1)]
    ff_share = [made.new(far_d.at[at_seq_d, :], far_d.at[at_seq_d, :], device) for device in others]
    ff_share += [made.new(far_gu.at[at_seq, :], far_gu.at[at_seq, :], device) for device in others]
    ff_core = [
        made.new(gate_w.at[:, own_units], sib_own.at[:, first_lanes], to_core),
        made.new(up_w.at[:, own_units], sib_own.at[:, last_lanes], to_core),
        made.new(down_w.at[own_units, :], wd.at[0, 1], to_core),
    ]
    ff_pass = [made.new(far_gu, sib_far, to_core), made.new(far_d, wd.at[1, 1], to_core)]
    wd_own = copy(down_w.at[own_units, :], wd.at[0, 0])
    ahead = len(copies)
    w_in_store = copy(w_in, w_in_out)

    gather_n = made.block(gather_messages_by_x, own_low, gx, gy, gd)
    scatter = made.block(scatter_messages, q1, q2, q3, r3, rx, ry)
    gather_m = made.block(gather_messages, own, mx, my, md)
    edge = made.new(u.at[pl.ds(rows - 8, 8), :], border, {"seq": seq + 1})
    hand_on = [made.new(ends, earlier.at[n - 1], {"seq": seq + n}) for n in range(1, count + 1)]

    def put_together(left, right, full, low):
        step = 128

        def one(n, carry):
            at = pl.ds(pl.multiple_of(n * step, step), step)
            whole = jnp.concatenate([left[at, :], right[at, :]], axis=1)
            full[at, :] = whole
            low[at, :] = whole.astype(BF)
            return carry

        lax.fori_loop(0, rows // step, one, 0)

    @pl.when(i == 0)
    def _():
        for c in copies[:ahead]:
            c.start()
        border[...] = jnp.zeros_like(border)
        earlier[...] = jnp.zeros_like(earlier)
        greet_all(
            [to_x, to_y, to_core] + [{"seq": lax.rem(seq + n, count + 1)} for n in range(1, count + 1)]
        )
        for m in swap:
            m.start()
        x_copy.wait()
        swap[0].wait_recv()
        put_together(x_own, x_recv, x, own_low)
        for m in gather_n[:4]:
            m.start()
        for m in in_core:
            m.start()
        swap[1].wait_recv()
        gains[:, 0:width] = jnp.concatenate([gains_in[...], gains_recv[...]], axis=1)
        gains_x.start()
        gains_y.start()
        swap[2].wait_recv()
        lane = small_in.shape[1]
        small[:, pl.ds(pl.multiple_of(core * lane, lane), lane)] = small_in[...]
        small[:, pl.ds(pl.multiple_of((1 - core) * lane, lane), lane)] = small_recv[...]
        swap_g.start()
        gains_x.wait_recv()
        gains_d.start()
        gather_n[1].wait_recv()
        gather_n[4].start()
        wo_core.start()
        for m in ff_core:
            m.start()
        gather_n[3].wait_recv()
        gather_n[5].start()
        for m in in_far:
            m.start()
        for m, n in zip(in_far, in_pass):
            m.wait_recv()
            n.start()
        wo_far.start()
        for m in ff_far:
            m.start()
        for c in in_own:
            c.wait()
        for m in in_core + in_pass:
            m.wait_recv()
        gains_y.wait_recv()
        gains_d.wait_recv()
        w_in_store.start()
        gather_n[0].wait_recv()
        gather_n[4].wait_recv()

    @pl.when(i == 1)
    def _():
        g_copy.wait()
        swap_g.wait_recv()
        put_together(g_own, g_recv, g, e_own)

    @pl.when(i == blocks // 2)
    def _():
        gather_n[2].wait_recv()
        gather_n[5].wait_recv()

    @pl.when(i < blocks)
    def _():
        at = pl.ds(pl.multiple_of(i * block, block), block)
        parts = [r[at, :].astype(F32) for r in (own_low, gx, gy, gd)]
        total = sum(jnp.sum(p * p, axis=1, keepdims=True) for p in parts)
        s = lax.rsqrt(total / D + EPSILON)
        s1[at, :] = s
        normed = [p * s * gains[0:1, j * width : (j + 1) * width] for j, p in enumerate(parts)]
        acc = None
        for j, n in enumerate(normed):
            term = dot_nn(n.astype(BF), w_in[j * width : (j + 1) * width, :])
            acc = term if acc is None else acc + term
        u[at, :] = acc[:, :channels]
        v[at, :] = acc[:, channels:]
        for j in (0, 1):
            k, p = pair_up(normed[2 * j], normed[2 * j + 1])
            n1[:, j * width : (j + 1) * width] = k.astype(BF)
            n1[:, (j + 2) * width : (j + 3) * width] = p.astype(BF)

    @pl.when((i == blocks - 1) & (seq < count))
    def _():
        edge.start()

    @pl.when((i == blocks) & (seq > 0))
    def _():
        edge.wait_recv()

    @pl.when(i == blocks - 1)
    def _():
        ff_far[0].wait_recv()
        for m in ff_share[:count]:
            m.start()

    @pl.when((i >= blocks) & (i < blocks + heads))
    def _():
        h = i - blocks
        lane = pl.ds(pl.multiple_of(h * 128, 128), 128)
        state_h, cum_h = local.at[h], cum.at[h]
        ext[0:8, :] = border[:, lane]
        ext[8 : 8 + rows, :] = u[:, lane]
        sp = small[KW : KW + 1, lane]
        step = ROW_BLOCK
        for r in range(0, rows, step):
            o = off[8 + r : 8 + r + step, :]
            total = small[0:1, lane] * ext[8 + r : 8 + r + step, :]
            for k in range(1, KW):
                term = small[k : k + 1, lane] * ext[8 + r - k : 8 + r - k + step, :]
                total = total + jnp.where(o >= k, term, 0.0)
            conv[r : r + step, :] = total
            rec = jax.nn.sigmoid(dot_nn(total, recall_gate[y * heads + h], PRECISE))
            adm = jax.nn.sigmoid(dot_nn(total, admit_gate[y * heads + h], PRECISE))
            recall[r : r + step, :] = rec
            admit[r : r + step, :] = adm
            ell = -8.0 * rec * sp
            cum_h[r : r + step, :] = jnp.where(o > 0, jnp.exp(ell), 0.0)
            state_h[r : r + step, :] = jnp.sqrt(minus_expm1(2.0 * ell)) * adm * total
        seg = rows // 8

        def one(n, carry):
            h, p = carry
            at = pl.ds(n, 8, stride=seg)
            d = cum_h[at, :]
            h = d * h + state_h[at, :]
            p = d * p
            state_h[at, :] = h
            cum_h[at, :] = p
            return h, p

        zero = jnp.zeros((8, 128), F32)
        last, product = lax.fori_loop(0, seg, one, (zero, zero + 1.0), unroll=8)
        carry_h, carry_p = last[0:1, :], product[0:1, :]
        for s in range(1, 8):
            at = slice(s * seg, (s + 1) * seg)
            c = cum_h[at, :]
            state_h[at, :] = state_h[at, :] + c * carry_h
            cum_h[at, :] = c * carry_p
            carry_h = last[s : s + 1, :] + product[s : s + 1, :] * carry_h
            carry_p = product[s : s + 1, :] * carry_p
        ends[h, 0:1, :] = carry_p
        ends[h, 1:2, :] = carry_h
        ends[h, 2:8, :] = jnp.zeros((6, 128), F32)

    @pl.when(i == blocks + 1)
    def _():
        wo_far.wait_recv()
        wo_pass.start()

    def columns_in_order(pieces, out):
        size = out.shape[0]
        step = 128
        lower = row == 0

        def one(n, carry):
            at = pl.ds(pl.multiple_of(n * step, step), step)
            for dy in (0, 1):
                first, second = pair_up(pieces[dy, 0, at, :].astype(F32), pieces[dy, 1, at, :].astype(F32))
                near, far = jnp.where(lower, first, second), jnp.where(lower, second, first)
                out[at, 2 * dy * width : (2 * dy + 1) * width] = near.astype(BF)
                out[at, (2 * dy + 1) * width : (2 * dy + 2) * width] = far.astype(BF)
            return carry

        lax.fori_loop(0, size // step, one, 0)

    @pl.when(i == blocks + heads - 1)
    def _():
        wo_own.wait()
        wo_core.wait_recv()
        wo_pass.wait_recv()
        columns_in_order(wo, w_out)

    for n in range(1, count + 1):

        @pl.when((i == blocks + heads - 1) & (seq <= count - n))
        def _():
            hand_on[n - 1].start()

        @pl.when((i == blocks + heads) & (seq >= n))
        def _():
            hand_on[n - 1].wait_recv()

    @pl.when(i == blocks + heads)
    def _():
        for m in ff_far[1:]:
            m.wait_recv()
        for m in ff_share[count:]:
            m.start()

    third = blocks + heads

    @pl.when((i >= third) & (i < third + blocks))
    def _():
        at = pl.ds(pl.multiple_of((i - third) * block, block), block)
        st = jnp.concatenate(
            [local[h, at, :] + cum[h, at, :] * carried(earlier, h, count) for h in range(heads)], axis=1
        )
        states[...] = st
        m = (st * gelu_pair(v[at, :])[0]).astype(BF)
        mixed[...] = m
        for j, q in ((3, q3), (1, q1), (2, q2), (0, q0)):
            q[at, :] = dot_nn(m, w_out[:, j * width : (j + 1) * width]).astype(q.dtype)

    @pl.when(i == third + blocks // 2 - 1)
    def _():
        scatter[0].start()
        scatter[2].start()

    @pl.when(i == third + blocks - 1)
    def _():
        scatter[1].start()

    @pl.when(i == third + blocks)
    def _():
        scatter[0].wait_recv()
        add_into(q2, r3, 0, half)
        scatter[3].start()
        scatter[4].start()
        scatter[1].wait_recv()
        add_into(q1, r3, half, half)
        scatter[5].start()
        gains_out[...] = gains[...]
        border_out[...] = border[...]
        earlier_out[...] = earlier[...]
        w_in_store.wait()
        for m in ff_share:
            m.wait_recv()
        for m in ff_pass:
            m.start()
        for base, first in ((0, 2), (half, 4)):
            scatter[first].wait_recv()
            scatter[first + 1].wait_recv()

            def one(n, carry):
                at = pl.ds(pl.multiple_of(base + n * 128, 128), 128)
                total = x[at, :] + q0[at, :] + rx[at, :].astype(F32) + ry[at, :].astype(F32)
                mid[at, :] = total
                own[at, :] = total.astype(BF)
                return carry

            lax.fori_loop(0, half // 128, one, 0)
            start = 0 if base == 0 else 2
            gather_m[start].start()
            gather_m[start + 1].start()
        wd_own.wait()
        for m in ff_core + ff_pass:
            m.wait_recv()
        columns_in_order(wd, w_down)
        gather_m[0].wait_recv()
        gather_m[4].start()
        gather_m[3].wait_recv()
        gather_m[5].start()
        for n in (1, 2, 4, 5):
            gather_m[n].wait_recv()
        sent = swap + [swap_g, gains_x, gains_y, gains_d] + in_far + in_core + in_pass
        sent += [wo_far, wo_core, wo_pass] + ff_far + ff_share + ff_core + ff_pass
        for m in sent + gather_n + scatter + gather_m:
            m.wait_send()

        @pl.when(seq < count)
        def _():
            edge.wait_send()

        for n in range(1, count + 1):

            @pl.when(seq <= count - n)
            def _():
                hand_on[n - 1].wait_send()


def front(stream, cot, in_w, br_w, out_w, gate_w, up_w, down_w, gains, small, recall_gate, admit_gate, off, count):
    rows, part = stream.shape[1:]
    width = 2 * part
    channels = in_w.shape[1] // 2
    units = gate_w.shape[1] // 2
    heads = channels // 128
    block = ROW_BLOCK
    blocks = rows // block

    def norm_at(i):
        return (jnp.minimum(i, blocks - 1), 0)

    def head_at(i):
        return (0, jnp.clip(i - blocks, 0, heads - 1))

    def mix_at(i):
        return (jnp.clip(i - blocks - heads, 0, blocks - 1), 0)

    chunk_low, chunk = sds((rows, width), BF), sds((rows, width), F32)
    wide = sds((rows, channels), F32)
    held = [
        chunk,
        chunk,
        chunk_low,
        sds((channels, 4 * width), BF),
        sds((units, 4 * width), BF),
        sds((8, 4 * width), F32),
        sds((8, channels), F32),
        sds((rows, 1), F32),
        wide,
        wide,
        sds((8, channels), F32),
        sds((count, heads, 8, 128), F32),
        chunk,
        chunk_low,
    ]
    blocked = [sds((rows, 4 * width), BF), wide, wide, wide, wide, sds((rows, channels), BF)]
    away = [chunk_low] * 3 + [sds((width, 2 * units), BF)] * 3 + [sds((4 * width, 2 * channels), BF)]
    piece = pltpu.VMEM((rows, width), BF)
    side = pltpu.VMEM((rows, part), F32)
    tall = pl.BlockSpec((rows, 128), head_at)
    return pl.pallas_call(
        functools.partial(front_body, heads, blocks, count),
        grid=(2 * blocks + heads + 1,),
        in_specs=[any_spec()] * 8
        + [whole_spec(a.shape) for a in (gains, small, recall_gate, admit_gate, off)],
        out_specs=[whole_spec(s.shape) for s in held]
        + [pl.BlockSpec((block, 4 * width), norm_at)]
        + [tall] * 3
        + [pl.BlockSpec((block, channels), mix_at)] * 2
        + [any_spec()] * 7,
        out_shape=held + blocked + away,
        scratch_shapes=[side] * 4
        + [pltpu.VMEM(gains.shape, F32), pltpu.VMEM(small.shape, F32)]
        + [piece] * 4
        + [
            pltpu.VMEM((4 * width, 2 * channels), BF),
            pltpu.VMEM((8, 4 * width), F32),
            pltpu.VMEM((8, channels), F32),
            pltpu.VMEM((count, heads, 8, 128), F32),
            pltpu.VMEM((2, 2, channels, width), BF),
            pltpu.VMEM((2, 2, units, width), BF),
            pltpu.VMEM((heads, rows, 128), F32),
            pltpu.VMEM((heads, rows, 128), F32),
            pltpu.VMEM((rows + 8, 128), F32),
            pltpu.VMEM((heads, 8, 128), F32),
            pltpu.VMEM((rows, width), F32),
        ]
        + [piece] * 6
        + [pltpu.SemaphoreType.DMA((9,))]
        + [pltpu.SemaphoreType.DMA((FRONT_MESSAGES,))] * 2,
        compiler_params=comm_params(1),
        cost_estimate=cost(200 * rows * in_w.size, rows * 40000),
        name="front",
    )(stream, cot, in_w, br_w, out_w, gate_w, up_w, down_w, gains, small, recall_gate, admit_gate, off)


FEED_MESSAGES = 64
FEED_CUTS = 4


def feed_body(blocks, *refs):
    (x0, x1, x2, x3, e_own, mid, cot, gain, wd_in) = refs[:9]
    weights = refs[9:14]
    outs = refs[14:18]
    (dx, own, gx, gy, gd, gain_grad, s_down, s_gu) = refs[18:26]
    (wgu, wd, ex, ey, ed, load, n2, hid, ee, err, scale, stage, c_down, c_gu, a_down, b_down) = refs[26:42]
    (a_gu, b_gu, free, q0, q1, q2, q3, r3, rx, ry, dots, dots_x, dots_y, send, recv) = refs[42:]
    i = pl.program_id(0)
    made = Messages((send, recv))
    block, width = x0.shape
    rows = mid.shape[0]
    half = rows // 2
    units = hid.shape[1]
    tiles = units // width
    scatter = made.block(scatter_messages, q1, q2, q3, r3, rx, ry)
    gather = made.block(gather_messages, own, gx, gy, gd)
    halves = (pl.ds(0, half), pl.ds(half, half))
    small_x = [made.new(dots.at[:, at], dots_x.at[:, at], neighbour_x()) for at in halves]
    small_y = [made.new(dots_x.at[:, at], dots_y.at[:, at], neighbour_y()) for at in halves]
    gu_core = [made.new(stage, c_gu, neighbour_core()) for n in (0, 1)]
    down_core = [
        made.new(
            stage.at[:, pl.ds(n * 2 * width, 2 * width)], c_down.at[pl.ds(n * width, width), :], neighbour_core()
        )
        for n in range(tiles)
    ]
    part_d = units // 2
    pieces = [
        [r.at[pl.ds(n * part_d, part_d), pl.ds(lane, width)] for r in (s_down, a_down, b_down)]
        for lane in (width, 0)
        for n in range(2)
    ]
    cut = 2 * width // 8
    for n in range(FEED_CUTS // 2):
        at = pl.ds(n * cut, cut)
        pieces.append([s_gu.at[pl.ds(width + n * cut, cut), :], a_gu.at[at, :], b_gu.at[at, :]])
    total = SeqSum(pieces, (send, recv), made.used)
    made.used += 2 * len(pieces)

    gather_e = made.block(gather_messages, e_own, ex, ey, ed)
    load_d = pltpu.make_async_copy(wd_in, wd, load.at[10])
    load_cot = pltpu.make_async_copy(cot, dx, load.at[11])
    second = blocks + tiles
    third = second + blocks

    @pl.when(i == 0)
    def _():
        copies = load_rows(*weights, wgu, load)
        load_d.start()
        load_cot.start()
        greet_all(
            (neighbour_x(), neighbour_y(), neighbour_core(), neighbour_end(), neighbour_middle())
        )
        for m in gather_e[:4]:
            m.start()
        for c in copies:
            c.wait()
        load_d.wait()

    @pl.when(i < blocks)
    def _():
        at = pl.ds(pl.multiple_of(i * block, block), block)
        parts = [r[...].astype(F32) for r in (x0, x1, x2, x3)]
        total = sum(jnp.sum(p * p, axis=1, keepdims=True) for p in parts)
        s = lax.rsqrt(total / D + EPSILON)
        scale[at, :] = s
        normed = [p * s * gain[1:2, j * width : (j + 1) * width] for j, p in enumerate(parts)]
        acc = None
        for j, n in enumerate(normed):
            term = dot_nn(n.astype(BF), wgu[j * width : (j + 1) * width, :])
            acc = term if acc is None else acc + term
        for j in (0, 1):
            k, p = pair_up(normed[2 * j], normed[2 * j + 1])
            n2[at, j * width : (j + 1) * width] = k.astype(BF)
            n2[at, (j + 2) * width : (j + 3) * width] = p.astype(BF)
        pre, up = acc[:, :units], acc[:, units:]
        err[at, :units] = pre.astype(BF)
        err[at, units:] = up.astype(BF)
        h = (gelu_pair(pre)[0] * up).astype(BF)
        hid[at, :] = h
        for j, q in enumerate(outs):
            q[...] = dot_nn(h, wd[:, j * width : (j + 1) * width]).astype(q.dtype)

    @pl.when(i == blocks - 2)
    def _():
        gather_e[0].wait_recv()
        gather_e[4].start()

    @pl.when(i == blocks - 1)
    def _():
        gather_e[3].wait_recv()
        gather_e[5].start()

    @pl.when(i == blocks)
    def _():
        for n in (1, 2, 4, 5):
            gather_e[n].wait_recv()
        step = 128

        def one(n, carry):
            at = pl.ds(pl.multiple_of(n * step, step), step)
            wide = [r[at, :].astype(F32) for r in (e_own, ex, ey, ed)]
            for j in (0, 1):
                k, p = pair_up(wide[2 * j], wide[2 * j + 1])
                ee[at, j * width : (j + 1) * width] = k.astype(BF)
                ee[at, (j + 2) * width : (j + 3) * width] = p.astype(BF)
            return carry

        lax.fori_loop(0, rows // step, one, 0)

    @pl.when((i >= second) & (i < third))
    def _():
        at = pl.ds(pl.multiple_of((i - second) * block, block), block)
        pre, up = err[at, :units].astype(F32), err[at, units:].astype(F32)
        act, slope = gelu_pair(pre)
        dh = None
        for j, r in enumerate((e_own, ex, ey, ed)):
            term = dot_nt(r[at, :], wd[:, j * width : (j + 1) * width])
            dh = term if dh is None else dh + term
        g = (dh * up * slope).astype(BF)
        b = (dh * act).astype(BF)
        err[at, :units] = g
        err[at, units:] = b
        dots[:, at] = row_sums(g.astype(F32) * pre + b.astype(F32) * up)
        for j, q in ((3, q3), (1, q1), (2, q2), (0, q0)):
            rows_w = slice(j * width, (j + 1) * width)
            q[at, :] = (dot_nt(g, wgu[rows_w, :units]) + dot_nt(b, wgu[rows_w, units:])).astype(q.dtype)

    def hand_dots(n):
        small_x[n].wait_recv()
        dots_x[:, halves[n]] = dots_x[:, halves[n]] + dots[:, halves[n]]
        small_y[n].start()

    own_gain = gain[1:2, :width]

    def finish(start, first):
        scatter[first].wait_recv()
        scatter[first + 1].wait_recv()
        return norm_back_rows(
            start, half, q0, rx, ry, dots_x, dots_y, scale, mid, own_gain, dx, dx, own
        )

    @pl.when(i == second + blocks // 2 - 1)
    def _():
        scatter[0].start()
        scatter[2].start()
        small_x[0].start()

    @pl.when(i == third - 2)
    def _():
        scatter[0].wait_recv()
        add_into(q2, r3, 0, half)
        scatter[3].start()
        hand_dots(0)

    @pl.when(i == third - 1)
    def _():
        scatter[1].start()
        small_x[1].start()
        scatter[4].start()
        load_cot.wait()
        small_y[0].wait_recv()
        gain_grad[0:1, :] = finish(0, 2)
        gather[0].start()
        gather[1].start()

    @pl.when((i >= blocks) & (i < blocks + tiles))
    def _():
        k = i - blocks
        at = pl.ds(pl.multiple_of(k * width, width), width)
        g = dot_tn(hid[:, at], ee[...])
        stage[:, pl.ds(pl.multiple_of(k * 2 * width, 2 * width), 2 * width)] = g[:, 2 * width :].astype(BF)
        s_down[at, :] = g[:, : 2 * width].astype(BF)

    for n in range(tiles):

        @pl.when(i == blocks + n)
        def _():
            down_core[n].start()

    @pl.when(i == second)
    def _():
        for n in range(tiles):
            down_core[n].wait_recv()
            down_core[n].wait_send()
        plus_in(s_down, c_down)
        for n in range(3):
            total.begin(n)

    for n in (0, 1):

        @pl.when(i == third + 1 + 2 * n)
        def _():
            gu_core[n].wait_send()

    @pl.when((i >= third) & (i < third + 4))
    def _():
        k = i - third
        n = jnp.where(k < 2, 3 - 2 * k, 6 - 2 * k)
        at = pl.ds(pl.multiple_of(n * width, width), width)
        stage[...] = dot_tn(n2[:, at], err[...]).astype(BF)

    for n in (0, 1):

        @pl.when(i == third + 2 * n)
        def _():
            if n:
                pl.semaphore_wait(free, 1)
            gu_core[n].start()

        @pl.when(i == third + 2 * n + 1)
        def _():
            gu_core[n].wait_recv()
            target = s_gu.at[pl.ds((1 - n) * width, width), :]
            put_sum(target, stage, c_gu)
            if not n:
                pl.semaphore_signal(free, inc=1, device_id=neighbour_core(), device_id_type=MESH_ID)

    @pl.when(i == third + 1)
    def _():
        for n in range(4, len(pieces)):
            total.begin(n)

    ticks = [second + 1, second + 3] + [third + 1 + n for n in range(len(pieces))]
    for t, where in enumerate(ticks):

        @pl.when(i == where)
        def _():
            if t + 3 < 4:
                total.begin(t + 3)
            if t < len(pieces):
                total.relay(t)
            if 0 <= t - 1 < len(pieces):
                total.settle(t - 1)
            if t >= 2:
                total.finish(t - 2)

    @pl.when(i == third)
    def _():
        scatter[1].wait_recv()
        add_into(q1, r3, half, half)
        scatter[5].start()
        hand_dots(1)

    @pl.when(i == third + 2)
    def _():
        small_y[1].wait_recv()
        gain_grad[0:1, :] = gain_grad[0:1, :] + finish(half, 4)
        gather[2].start()
        gather[3].start()
        gather[0].wait_recv()
        gather[4].start()

    @pl.when(i == third + 4)
    def _():
        gather[3].wait_recv()
        gather[5].start()

    @pl.when(i == third + 2 + len(pieces))
    def _():
        for n in (1, 2, 4, 5):
            gather[n].wait_recv()
        for m in scatter + gather + gather_e + small_x + small_y:
            m.wait_send()


def feed(chunks, err_own, mid, cot, gain, wd, weights):
    rows, width = chunks[0].shape
    units = wd.shape[0]
    block = ROW_BLOCK
    blocks = rows // block
    tiles = units // width
    held = functools.partial(held_spec, block, last=blocks - 1)
    chunk = pltpu.VMEM((rows, width), BF)
    lanes = pltpu.VMEM((8, rows), F32)
    landing = pltpu.VMEM((units, 2 * width), BF)
    return pl.pallas_call(
        functools.partial(feed_body, blocks),
        grid=(2 * blocks + tiles + 7 + FEED_CUTS // 2,),
        in_specs=[held(width)] * 4
        + [whole_spec(err_own.shape), whole_spec(mid.shape), any_spec(), whole_spec(gain.shape)]
        + [any_spec()] * 6,
        out_specs=[held(width)] * 4
        + [whole_spec((rows, width))] * 2
        + [any_spec()] * 3
        + [whole_spec((8, width)), whole_spec((units, 2 * width)), whole_spec((2 * width, 2 * units))],
        out_shape=[sds((rows, width), F32)]
        + [sds((rows, width), BF)] * 3
        + [sds((rows, width), F32)]
        + [sds((rows, width), BF)] * 4
        + [sds((8, width), F32), sds((units, 2 * width), BF), sds((2 * width, 2 * units), BF)],
        scratch_shapes=[
            pltpu.VMEM((4 * width, 2 * units), BF),
            pltpu.VMEM(wd.shape, BF),
            chunk,
            chunk,
            chunk,
            pltpu.SemaphoreType.DMA((12,)),
            pltpu.VMEM((rows, 4 * width), BF),
            pltpu.VMEM((rows, units), BF),
            pltpu.VMEM((rows, 4 * width), BF),
            pltpu.VMEM((rows, 2 * units), BF),
            pltpu.VMEM((rows, 1), F32),
            pltpu.VMEM((width, 2 * units), BF),
            landing,
            pltpu.VMEM((width, 2 * units), BF),
            landing,
            landing,
            pltpu.VMEM((FEED_CUTS * width // 8, 2 * units), BF),
            pltpu.VMEM((FEED_CUTS * width // 8, 2 * units), BF),
            pltpu.SemaphoreType.REGULAR,
            pltpu.VMEM((rows, width), F32),
        ]
        + [chunk] * 6
        + [lanes] * 3
        + [pltpu.SemaphoreType.DMA((FEED_MESSAGES,))] * 2,
        compiler_params=comm_params(3),
        cost_estimate=cost(48 * rows * wd.size, 3 * nbytes(wd) + rows * 30000, rows * units),
        name="feed",
    )(*chunks, err_own, mid, cot, gain, wd, *weights)


def back_body(heads, blocks, count, *refs):
    errs = refs[0:4]
    (w_out, states, branch, recall, conv, admit, u_head, off, soft) = refs[4:13]
    (taps, recall_w, admit_w, border, earlier, u, v, w_hbm, scale, x_hbm, dx_hbm, gain) = refs[13:25]
    (sum_gu, sum_down, mixed) = refs[25:28]
    (ev, eu, grad, gain_grad, grad_small) = refs[28:33]
    (mine_gu, far_gu, far_down, mine_out, far_out, gates) = refs[33:39]
    (w, x, dx, paired, part, reach, ext, st, uext, dc, ends, later, edge, from_later, load) = refs[39:54]
    (q0, q1, q2, q3, r3, rx, ry, dots, dots_x, dots_y) = refs[54:64]
    (s_gu, a_gu, b_gu, s_out, p_out, c_out, a_out, b_out) = refs[64:72]
    (s_gt, p_gt, c_gt, a_gt, b_gt, store, send, recv) = refs[72:]
    i = pl.program_id(0)
    sems = (send, recv)
    seq = lax.axis_index("seq")
    rows, width = x.shape
    half = rows // 2
    step = ROW_BLOCK
    seg = rows // 8
    channels = heads * 128
    block = step

    scatter = scatter_messages(q1, q2, q3, r3, rx, ry, sems, 0)
    small_x = message(dots, dots_x, neighbour_x(), sems, 6)
    small_y = message(dots_x, dots_y, neighbour_y(), sems, 7)
    hand_on = [message(ends, later.at[n - 1], {"seq": seq - n}, sems, 7 + n) for n in range(1, count + 1)]
    base = 8 + count
    hand_edge = message(edge, from_later, {"seq": seq - 1}, sems, base)
    base += 1

    cut, rows_out = width // 8, channels
    y = lax.div(lax.axis_index("col"), 2)
    to_side, to_core = neighbour_y(), neighbour_core()
    size = heads * 128
    pieces, to_y, to_out, stores = [], {}, {}, []

    def store_copy(src, dst):
        stores.append(pltpu.make_async_copy(src, dst, store.at[len(stores)]))
        return stores[-1]

    made = Messages(sems)
    made.used = base
    done = FEED_CUTS * cut
    early_y = [
        made.new(sum_down.at[:, pl.ds(width, width)], far_down, to_side),
        made.new(sum_gu.at[pl.ds(width, done), :], far_gu.at[pl.ds(0, done), :], to_side),
    ]
    for start, rows_gu in ((12, 1), (13, 2), (15, 1), (0, 2), (2, 2), (4, 2), (6, 2)):
        p = len(pieces)
        at = pl.ds(start * cut, rows_gu * cut)
        pieces.append([r.at[at, :] for r in (s_gu, a_gu, b_gu)])
        if start >= 8:
            target = far_gu.at[pl.ds((start - 8) * cut, rows_gu * cut), :]
            to_y[p] = [made.new(pieces[p][0], target, to_side)]
        else:
            to_out[p] = [store_copy(pieces[p][0], mine_gu.at[at, :])]
    for lane in (width, 0):
        for n in (0,):
            p = len(pieces)
            at = pl.ds(n * rows_out, rows_out)
            pieces.append([r.at[at, pl.ds(lane, width)] for r in (s_out, a_out, b_out)])
            if lane:
                to_y[p] = [made.new(pieces[p][0], far_out.at[at, :], to_side)]
            else:
                to_out[p] = [store_copy(pieces[p][0], mine_out.at[at, :])]
    p = len(pieces)
    pieces.append([s_gt, a_gt, b_gt])
    to_y[p], to_out[p] = [], []
    for n in (0, 1):
        source = s_gt.at[pl.ds(n * size, size), :]
        target = gates.at[pl.ds(pl.multiple_of((2 * n + y) * size, size), size), :]
        to_y[p].append(made.new(source, target, to_side))
        to_out[p].append(store_copy(source, target))
    total = SeqSum(pieces, sems, made.used)
    made.used += 2 * len(pieces)
    core_out, core_gt = made.new(p_out, c_out, to_core), made.new(p_gt, c_gt, to_core)
    load_gu = pltpu.make_async_copy(sum_gu, s_gu, load.at[0])
    loads = [
        pltpu.make_async_copy(source, target, load.at[n + 1])
        for n, (source, target) in enumerate(((w_hbm, w), (x_hbm, x), (dx_hbm, dx)))
    ]

    def tick(t):
        if t + 3 < len(pieces):
            total.begin(t + 3)
        if t < len(pieces):
            total.relay(t)
        if 0 <= t - 1 < len(pieces):
            total.settle(t - 1)
        if 0 <= t - 2 < len(pieces):
            total.finish(t - 2)
            for m in to_y.get(t - 2, []) + to_out.get(t - 2, []):
                m.start()

    @pl.when(i == 0)
    def _():
        load_gu.start()
        later[...] = jnp.zeros_like(later)
        from_later[...] = jnp.zeros_like(from_later)
        greet_all(
            [neighbour_x(), neighbour_y(), neighbour_core()]
            + [{"seq": lax.rem(seq + n, count + 1)} for n in range(1, count + 1)]
        )
        load_gu.wait()
        for n in range(3):
            total.begin(n)
        for c in loads:
            c.start()
        for m in early_y:
            m.start()
        for r in range(0, rows, step):
            at = slice(r, r + step)
            for j in (0, 1):
                k, p = pair_up(errs[2 * j][at, :].astype(F32), errs[2 * j + 1][at, :].astype(F32))
                paired[at, j * width : (j + 1) * width] = k.astype(BF)
                paired[at, (j + 2) * width : (j + 3) * width] = p.astype(BF)

    @pl.when(i == 3)
    def _():
        core_out.wait_recv()
        plus_in(s_out, c_out)

    @pl.when(i == 2 * heads + 1)
    def _():
        core_gt.wait_recv()
        put_in(s_gt, p_gt)
        plus_in(s_gt, c_gt)

    for t in range(len(pieces) + 2):

        @pl.when(i == (2 * t + 2 if t <= heads else t + heads + 3))
        def _():
            tick(t)

    @pl.when(i == 1)
    def _():
        g = dot_tn(mixed[...], paired[...])
        p_out[...] = g[:, 2 * width :].astype(BF)
        core_out.start()
        s_out[...] = g[:, : 2 * width].astype(BF)

    @pl.when(i < heads)
    def _():
        sp = soft[0:1, :]
        part_h, reach_h = part.at[i], reach.at[i]
        lane = pl.ds(pl.multiple_of(i * 128, 128), 128)
        for r in range(0, rows, step):
            at = slice(r, r + step)
            o = off[8 + r : 8 + r + step, :]
            ext[at, :] = jnp.where(o > 0, jnp.exp(-8.0 * recall[at, :] * sp), 0.0)
            dm = None
            for j in range(4):
                term = dot_nt(errs[j][at, :], w_out[:, j * width : (j + 1) * width])
                dm = term if dm is None else dm + term
            act, slope = gelu_pair(branch[at, :])
            ev[at, lane] = (dm * states[at, :] * slope).astype(BF)
            part_h[at, :] = dm * act
        ext[rows : rows + 8, :] = jnp.ones((8, 128), F32)
        for r in range(0, rows, step):
            reach_h[r : r + step, :] = ext[r + 1 : r + 1 + step, :]

        def one(n, carry):
            h, p = carry
            at = pl.ds(seg - 1 - n, 8, stride=seg)
            d = reach_h[at, :]
            h = d * h + part_h[at, :]
            p = d * p
            part_h[at, :] = h
            reach_h[at, :] = p
            return h, p

        zero = jnp.zeros((8, 128), F32)
        h, p = lax.fori_loop(0, seg, one, (zero, zero + 1.0), unroll=8)
        carry_h, carry_p = h[7:8, :], p[7:8, :]
        for s in range(6, -1, -1):
            at = slice(s * seg, (s + 1) * seg)
            c = reach_h[at, :]
            part_h[at, :] = part_h[at, :] + c * carry_h
            reach_h[at, :] = c * carry_p
            carry_h = h[s : s + 1, :] + p[s : s + 1, :] * carry_h
            carry_p = p[s : s + 1, :] * carry_p
        first = ext[0:1, :]
        ends[i, 0:1, :] = first * carry_p
        ends[i, 1:2, :] = first * carry_h
        ends[i, 2:8, :] = jnp.zeros((6, 128), F32)

    for n in range(1, count + 1):

        @pl.when((i == heads - 1) & (seq >= n))
        def _():
            hand_on[n - 1].start()

        @pl.when((i == heads) & (seq <= count - n))
        def _():
            hand_on[n - 1].wait_recv()

    @pl.when((i >= heads) & (i < 2 * heads))
    def _():
        h = i - heads
        part_h, reach_h = part.at[h], reach.at[h]
        st[0:8, :] = jnp.broadcast_to(chain(earlier, count), (8, 128))
        st[8 : 8 + rows, :] = states[...]
        uext[0:8, :] = border[...]
        uext[8 : 8 + rows, :] = u_head[...]
        incoming = carried(later, h, count)
        sp = soft[0:1, :]
        dc[0:8, :] = jnp.zeros((8, 128), F32)
        dc[8 + rows : 16 + rows, :] = jnp.zeros((8, 128), F32)
        gr = ga = None
        sums = [None] * (KW + 1)

        def plus(total, term):
            return term if total is None else total + term

        for r in range(0, rows, step):
            at = slice(r, r + step)
            o = off[8 + r : 8 + r + step, :]
            adj = part_h[at, :] + reach_h[at, :] * incoming
            rec, adm, cv = recall[at, :], admit[at, :], conv[at, :]
            ell = -8.0 * rec * sp
            e = jnp.exp(ell)
            m = jnp.sqrt(minus_expm1(2.0 * ell))
            previous = jnp.where(o > 0, e * st[7 + r : 7 + r + step, :], 0.0)
            ac = adj * cv
            d_ell = adj * previous - ac * adm * (e * e) / m
            d_rp = -8.0 * sp * d_ell * rec * (1.0 - rec)
            d_ip = ac * m * adm * (1.0 - adm)
            d_conv = (
                adj * m * adm
                + dot_nt(d_rp, recall_w[0], PRECISE)
                + dot_nt(d_ip, admit_w[0], PRECISE)
            )
            dc[8 + r : 8 + r + step, :] = d_conv
            gr = plus(gr, dot_tn(cv, d_rp, PRECISE))
            ga = plus(ga, dot_tn(cv, d_ip, PRECISE))
            for k in range(KW):
                term = d_conv * uext[8 + r - k : 8 + r - k + step, :]
                if k:
                    term = jnp.where(o >= k, term, 0.0)
                sums[k] = plus(sums[k], jnp.sum(term, axis=0, keepdims=True))
            sums[KW] = plus(sums[KW], jnp.sum(rec * d_ell, axis=0, keepdims=True))
        for n, value in enumerate((gr, ga)):
            p_gt[pl.ds(pl.multiple_of(n * size + h * 128, 128), 128), :] = value.astype(BF)
        for k in range(KW + 1):
            grad_small[k : k + 1, :] = sums[k]
        grad_small[KW + 1 : 8, :] = jnp.zeros((7 - KW, 128), F32)
        for r in range(0, rows, step):
            du = taps[0:1, :] * dc[8 + r : 8 + r + step, :]
            for k in range(1, KW):
                o = off[8 + r + k : 8 + r + k + step, :]
                term = taps[k : k + 1, :] * dc[8 + r + k : 8 + r + k + step, :]
                du = du + jnp.where(o >= k, term, 0.0)
            part_h[r : r + step, :] = du
        over = jnp.zeros((8, 128), F32)
        for k in range(1, KW):
            term = taps[k : k + 1, :] * dc[k : k + 8, :]
            over = over + jnp.where(off[k : k + 8, :] >= k, term, 0.0)
        edge[h] = over

    @pl.when((i == 2 * heads - 1) & (seq >= 1))
    def _():
        hand_edge.start()

    @pl.when(i == 2 * heads - 1)
    def _():
        core_gt.start()


    @pl.when((i == 2 * heads) & (seq < count))
    def _():
        hand_edge.wait_recv()

    third = 2 * heads

    @pl.when(i == third)
    def _():
        for c in loads:
            c.wait()

    @pl.when((i >= third) & (i < third + blocks))
    def _():
        at = pl.ds(pl.multiple_of((i - third) * block, block), block)
        d = jnp.concatenate([part[h, at, :] for h in range(heads)], axis=1)
        late = jnp.concatenate([from_later[h] for h in range(heads)], axis=1)
        extra = jnp.concatenate([jnp.zeros((block - 8, channels), F32), late], axis=0)
        d = d + jnp.where(i == third + blocks - 1, extra, 0.0)
        e = d.astype(BF)
        eu[...] = e
        b = ev[at, :]
        dots[:, at] = row_sums(e.astype(F32) * u[...] + b.astype(F32) * v[...])
        for j, q in ((3, q3), (1, q1), (2, q2), (0, q0)):
            rows_w = slice(j * width, (j + 1) * width)
            q[at, :] = (dot_nt(e, w[rows_w, :channels]) + dot_nt(b, w[rows_w, channels:])).astype(q.dtype)

    @pl.when(i == third + blocks // 2 - 1)
    def _():
        scatter[0].start()
        scatter[2].start()

    @pl.when(i == third + blocks - 1)
    def _():
        scatter[1].start()
        small_x.start()
        scatter[0].wait_recv()
        add_into(q2, r3, 0, half)
        scatter[3].start()
        scatter[4].start()

    last = third + blocks

    @pl.when(i == last)
    def _():
        small_x.wait_recv()
        dots_x[...] = dots_x[...] + dots[...]
        small_y.start()
        scatter[1].wait_recv()
        add_into(q1, r3, half, half)
        scatter[5].start()

    def finish(start, first):
        scatter[first].wait_recv()
        scatter[first + 1].wait_recv()
        return norm_back_rows(
            start, half, q0, rx, ry, dots_x, dots_y, scale, x, gain[0:1, :width], dx, grad, None
        )

    @pl.when(i == last + 1)
    def _():
        small_y.wait_recv()
        gain_grad[0:1, :] = finish(0, 2)

    @pl.when(i == last + 2)
    def _():
        gain_grad[0:1, :] = gain_grad[0:1, :] + finish(half, 4)
        for n in range(1, count + 1):

            @pl.when(seq >= n)
            def _():
                hand_on[n - 1].wait_send()

        @pl.when(seq >= 1)
        def _():
            hand_edge.wait_send()


    @pl.when(i == pl.num_programs(0) - 1)
    def _():
        sent_y = [m for group in to_y.values() for m in group] + early_y
        for m in sent_y:
            m.wait_recv()
        for m in scatter + [small_x, small_y, core_out, core_gt] + sent_y:
            m.wait_send()
        for c in stores:
            c.wait()


def back(errs, w_out, states, v, recall, conv, admit, u, off, soft, taps, rw, aw, border, earlier, w, scale, x, dx, gain, sum_gu, sum_down, mixed):
    rows, channels = states.shape
    width = x.shape[1]
    heads = channels // 128
    block = ROW_BLOCK
    blocks = rows // block
    count = earlier.shape[0]
    steps = 2 * heads + blocks + 8

    def both(i):
        return jnp.where(i < heads, i, jnp.clip(i - heads, 0, heads - 1))

    def second(i):
        return jnp.clip(i - heads, 0, heads - 1)

    def on(shape, pick, axis):
        if axis == 0:
            return pl.BlockSpec(shape, lambda i: (pick(i),) + (0,) * (len(shape) - 1))
        return pl.BlockSpec(shape, lambda i: (0, pick(i)))

    def third(i):
        return jnp.clip(i - 2 * heads, 0, blocks - 1)

    def first(i):
        return jnp.minimum(i, heads - 1)

    tall = (rows, 128)
    gate = (1, 128, 128)
    own_gate = on(gate, second, 0)
    chunk = pltpu.VMEM((rows, width), BF)
    lanes = pltpu.VMEM((8, rows), F32)
    gu = pltpu.VMEM(sum_gu.shape, BF)
    pair, gate_sum = pltpu.VMEM((channels, 2 * width), BF), pltpu.VMEM((2 * channels, 128), BF)
    piece = pltpu.VMEM((heads, 8, 128), F32)
    half_gu, half_dn = (sum_gu.shape[0] // 2, sum_gu.shape[1]), (sum_down.shape[0], width)
    half_out = (channels, width)
    count_sems = 88
    return pl.pallas_call(
        functools.partial(back_body, heads, blocks, count),
        grid=(steps,),
        in_specs=[whole_spec((rows, width))] * 4
        + [
            on((128, 4 * width), first, 0),
            on(tall, both, 1),
            on(tall, first, 1),
            on(tall, both, 1),
            on(tall, second, 1),
            on(tall, second, 1),
            on(tall, second, 1),
            whole_spec(off.shape),
            on((1, 128), both, 1),
            on((KW, 128), second, 1),
            own_gate,
            own_gate,
            on((8, 128), second, 1),
            pl.BlockSpec((count, 1, 8, 128), lambda i: (0, second(i), 0, 0)),
            on((block, channels), third, 0),
            on((block, channels), third, 0),
            any_spec(),
            whole_spec(scale.shape),
            any_spec(),
            any_spec(),
            whole_spec(gain.shape),
            any_spec(),
            any_spec(),
            whole_spec(mixed.shape),
        ],
        out_specs=[
            whole_spec((rows, channels)),
            on((block, channels), third, 0),
            whole_spec((rows, width)),
            whole_spec((8, width)),
            on((8, 128), second, 1),
        ]
        + [any_spec()] * 6,
        out_shape=[
            sds((rows, channels), BF),
            sds((rows, channels), BF),
            sds((rows, width), F32),
            sds((8, width), F32),
            sds((8, channels), F32),
            sds(half_gu, BF),
            sds(half_gu, BF),
            sds(half_dn, BF),
            sds(half_out, BF),
            sds(half_out, BF),
            sds((4 * channels, 128), BF),
        ],
        scratch_shapes=[
            pltpu.VMEM(w.shape, BF),
            pltpu.VMEM((rows, width), F32),
            pltpu.VMEM((rows, width), F32),
            pltpu.VMEM((rows, 4 * width), BF),
        ]
        + [pltpu.VMEM((heads, rows, 128), F32)] * 2
        + [
            pltpu.VMEM((rows + 8, 128), F32),
            pltpu.VMEM((rows + 8, 128), F32),
            pltpu.VMEM((rows + 8, 128), F32),
            pltpu.VMEM((rows + 16, 128), F32),
            piece,
            pltpu.VMEM((count, heads, 8, 128), F32),
            piece,
            piece,
            pltpu.SemaphoreType.DMA((4,)),
            pltpu.VMEM((rows, width), F32),
        ]
        + [chunk] * 6
        + [lanes] * 3
        + [gu] * 3
        + [pair] * 5
        + [gate_sum] * 5
        + [pltpu.SemaphoreType.DMA((12,))]
        + [pltpu.SemaphoreType.DMA((count_sems,))] * 2,
        compiler_params=comm_params(4),
        cost_estimate=cost(64 * rows * w.size, rows * channels * 60, rows * channels * 8),
        name="back",
    )(
        *errs, w_out, states, v, recall, conv, admit, u, off, soft, taps, rw, aw, border, earlier,
        u, v, w, scale, x, dx, gain, sum_gu, sum_down, mixed,
    )


TAIL_MESSAGES = 48


def tail_body(*refs):
    (n1, eu, ev, grad_small, grad_mixer, grad_feed) = refs[:6]
    (p0, p1, p2, p3, mid, grad_chunk) = refs[6:12]
    (mine_in, far_in, tiny_out, out, grad) = refs[12:17]
    (s_in, p_in, c_in, a_in, b_in, s_ty, p_ty, c_ty, a_ty, b_ty) = refs[17:27]
    (q0, md, gc, q1, q2, q3, r3, rx, ry, own_a, other_a, own_b, other_b, load, send, recv) = refs[27:]
    made = Messages((send, recv))
    col = lax.axis_index("col")
    core = lax.rem(col, 2)
    to_core, to_y = neighbour_core(), neighbour_y()
    rows, width = p0.shape
    part = width // 2
    half_tokens = rows // 2
    channels = eu.shape[1]
    copies = []

    def copy(src, dst):
        copies.append(pltpu.make_async_copy(src, dst, load.at[len(copies)]))
        return copies[-1]

    outs_in = [copy(p3, q3), copy(p1, q1), copy(p2, q2)]
    late = [copy(p0, q0), copy(mid, md), copy(grad_chunk, gc)]
    scatter = made.block(scatter_messages, q1, q2, q3, r3, rx, ry)
    cut = width // 4
    order = [pl.ds(n * cut, cut) for n in (4, 5, 6, 7, 0, 1, 2, 3)]
    pieces = [[s_ty, a_ty, b_ty]] + [[r.at[at, :] for r in (s_in, a_in, b_in)] for at in order]
    count = len(pieces)
    total = SeqSum(pieces, (send, recv), made.used)
    made.used += 2 * count
    core_ty = made.new(p_ty, c_ty, to_core)
    far_rows, own_rows = pl.ds(width, width), pl.ds(0, width)
    core_in = [made.new(p_in.at[at, :], c_in.at[at, :], to_core) for at in (far_rows, own_rows)]
    over_y = {
        n + 1: made.new(s_in.at[order[n], :], far_in.at[pl.ds(n * cut, cut), :], to_y) for n in range(4)
    }
    send_out, send_grad = made.new(other_a, out.at[core], to_core), made.new(other_b, grad.at[core], to_core)
    keep_out, keep_grad = copy(own_a, out.at[core]), copy(own_b, grad.at[core])
    keep_in = {n + 1: copy(s_in.at[order[n], :], mine_in.at[pl.ds((n - 4) * cut, cut), :]) for n in range(4, 8)}

    for m in outs_in:
        m.start()
    greet_all((neighbour_x(), to_y, to_core, neighbour_end(), neighbour_middle()))
    p_ty[...] = jnp.zeros_like(p_ty)
    p_ty[0:8, :] = grad_small[...]
    for n, source in enumerate((grad_mixer, grad_feed)):
        g = jnp.broadcast_to(source[0:1, :], (8, width))
        g = jnp.where(core == 0, g, pltpu.roll(g, part, 1))
        p_ty[8 + n : 9 + n, 0:width] = g[0:1, :]
    core_ty.start()

    def tile(n, target, row):
        sub = width // 3

        def one(k, carry):
            at = pl.ds(pl.multiple_of(n * width + k * sub, sub), sub)
            where = pl.ds(pl.multiple_of(row + k * sub, sub), sub)
            left = n1[:, at]
            target[where, :channels] = dot_tn(left, eu[...]).astype(BF)
            target[where, channels:] = dot_tn(left, ev[...]).astype(BF)
            return carry

        lax.fori_loop(0, 3, one, 0)

    def gather_core(n, at):
        core_in[n].wait_recv()
        plus_in(s_in.at[at, :], c_in.at[at, :])

    tile(3, p_in, width)
    core_in[0].start()
    for m in outs_in:
        m.wait()
    for m in late:
        m.start()
    for m in scatter[:3]:
        m.start()
    tile(1, s_in, width)
    core_ty.wait_recv()
    s_ty[...] = p_ty[...] + c_ty[...]
    total.begin(0)
    gather_core(0, far_rows)
    for n in range(1, 5):
        total.begin(n)
    tile(2, p_in, 0)
    core_in[1].start()
    total.relay(0)
    total.relay(1)
    total.settle(0)
    tile(0, s_in, 0)
    gather_core(1, own_rows)
    for n in range(5, count):
        total.begin(n)

    def chunk_out(value, own, other, at):
        own[at, :] = value[:, :part]
        other[at, :] = pltpu.roll(value, part, 1)[:, :part]

    def in_steps(start, size, body):
        def one(n, carry):
            body(pl.ds(pl.multiple_of(start + n * 128, 128), 128))
            return carry

        lax.fori_loop(0, size // 128, one, 0)

    def finish_out(start, first):
        scatter[first].wait_recv()
        scatter[first + 1].wait_recv()

        def body(at):
            value = q0[at, :] + rx[at, :].astype(F32) + ry[at, :].astype(F32) + md[at, :]
            chunk_out(value, own_a, other_a, at)

        in_steps(start, half_tokens, body)

    for n in range(2, count + 2):
        if n < count:
            total.relay(n)
        if n - 1 < count:
            total.settle(n - 1)
        total.finish(n - 2)
        if n - 2 in over_y:
            over_y[n - 2].start()
        if n - 2 in keep_in:
            keep_in[n - 2].start()
        if n == 2:
            scatter[0].wait_recv()
            add_into(q2, r3, 0, half_tokens)
            scatter[3].start()
            scatter[4].start()
        if n == 3:
            scatter[1].wait_recv()
            add_into(q1, r3, half_tokens, half_tokens)
            scatter[5].start()
            for m in late:
                m.wait()
            in_steps(0, rows, lambda at: chunk_out(gc[at, :], own_b, other_b, at))
            send_grad.start()
            keep_grad.start()
        if n == 7:
            finish_out(0, 2)
        if n == 8:
            finish_out(half_tokens, 4)
            send_out.start()
            keep_out.start()
    put_in(tiny_out, s_ty)
    received = list(over_y.values()) + [send_out, send_grad]
    for m in received:
        m.wait_recv()
    for m in [core_ty] + core_in + received + scatter:
        m.wait_send()
    for c in [keep_out, keep_grad] + list(keep_in.values()):
        c.wait()


def tail(n1, eu, ev, grad_small, grad_mixer, grad_feed, parts, mid, grad_chunk):
    rows, channels = eu.shape
    width = mid.shape[1]
    part = width // 2
    big = pltpu.VMEM((2 * width, 2 * channels), BF)
    tiny = pltpu.VMEM((16, channels), F32)
    piece = pltpu.VMEM((rows, width), BF)
    full = pltpu.VMEM((rows, width), F32)
    side = pltpu.VMEM((rows, part), F32)
    quarter_in = (width, 2 * channels)
    final = sds((2, rows, part), F32)
    return pl.pallas_call(
        tail_body,
        in_specs=[pl.BlockSpec(memory_space=pltpu.VMEM)] * 6 + [any_spec()] * 6,
        out_specs=[any_spec()] * 2 + [pl.BlockSpec(memory_space=pltpu.VMEM)] + [any_spec()] * 2,
        out_shape=[sds(quarter_in, BF)] * 2 + [sds((16, channels), F32), final, final],
        scratch_shapes=[big] * 5
        + [tiny] * 5
        + [full] * 3
        + [piece] * 6
        + [side] * 4
        + [pltpu.SemaphoreType.DMA((12,))]
        + [pltpu.SemaphoreType.DMA((TAIL_MESSAGES,))] * 2,
        compiler_params=pltpu.CompilerParams(
            vmem_limit_bytes=VMEM_LIMIT, collective_id=6, has_side_effects=True
        ),
        cost_estimate=cost(60 * rows * width * channels * 4, nbytes(n1, eu, ev)),
        name="tail",
    )(n1, eu, ev, grad_small, grad_mixer, grad_feed, *parts, mid, grad_chunk)


def arrange_body(place, mine_gu, far_gu, mine_dn, far_dn, mine_in, far_in, mine_out, far_out, *outs):
    gate, up, down, inp, branch, out = outs
    row, y = place[0], place[1]
    first = pl.program_id(0) == 0

    def side_by_side(mine, far, left, right):
        lanes = left.shape[1] // 2
        for target, at in ((left, 0), (right, mine.shape[1] // 2)):
            m = mine[:, at : at + lanes].astype(F32)
            t = far[:, at : at + lanes].astype(F32)
            target[:, :lanes] = jnp.where(y == 0, m, t)
            target[:, lanes:] = jnp.where(y == 0, t, m)

    def stack_up(mine, far, target):
        value = jnp.where(first, mine[...].astype(F32), far[...].astype(F32))
        target[...] = jnp.where(row == 0, value, pltpu.roll(value, value.shape[1] // 2, 1))

    side_by_side(mine_gu, far_gu, gate, up)
    side_by_side(mine_in, far_in, inp, branch)
    stack_up(mine_dn, far_dn, down)
    stack_up(mine_out, far_out, out)


def arrange(place, mine_gu, far_gu, mine_dn, far_dn, mine_in, far_in, mine_out, far_out):
    width, units = far_dn.shape[1], far_dn.shape[0]
    inner = mine_out.shape[0]
    lanes_gu, lanes_in = mine_gu.shape[1], mine_in.shape[1]
    quarter = width // 4

    def rows_in(i, j, place):
        return (2 * i + j, 0)

    def rows_to(i, j, place):
        return (2 * (i + place[0] - 2 * i * place[0]) + j, 0)

    def near(i, j, place):
        return (jnp.where(i == 0, j, 1), 0)

    def far(i, j, place):
        return (jnp.where(i == 0, 0, j), 0)

    def stack_to(i, j, place):
        return (2 * (i + place[1] - 2 * i * place[1]) + j, 0)

    def spec(rows, lanes, at):
        return pl.BlockSpec((rows, lanes), at)

    shapes = [(width, lanes_gu)] * 2 + [(2 * units, width)] + [(width, lanes_in)] * 2 + [(2 * inner, width)]
    return pl.pallas_call(
        arrange_body,
        grid_spec=pltpu.PrefetchScalarGridSpec(
            num_scalar_prefetch=1,
            grid=(2, 2),
            in_specs=[
                spec(quarter, lanes_gu, rows_in),
                spec(quarter, lanes_gu, rows_in),
                spec(units // 2, width, near),
                spec(units // 2, width, far),
                spec(quarter, lanes_in, rows_in),
                spec(quarter, lanes_in, rows_in),
                spec(inner // 2, width, near),
                spec(inner // 2, width, far),
            ],
            out_specs=[spec(quarter, lanes_gu, rows_to)] * 2
            + [spec(units // 2, width, stack_to)]
            + [spec(quarter, lanes_in, rows_to)] * 2
            + [spec(inner // 2, width, stack_to)],
        ),
        out_shape=[sds(s, F32) for s in shapes],
        compiler_params=pltpu.CompilerParams(vmem_limit_bytes=VMEM_LIMIT),
        cost_estimate=cost(1000000, 24000000),
        name="arrange",
    )(place, mine_gu, far_gu, mine_dn, far_dn, mine_in, far_in, mine_out, far_out)


def local_fast(
    stream_in,
    cotangent,
    doc_lengths,
    mixer_gain,
    input_weight,
    branch_weight,
    filter_taps,
    recall_gate,
    admit_gate,
    decay_param,
    output_weight,
    feed_gain,
    gate_weight,
    up_weight,
    down_weight,
):
    tokens = stream_in.shape[1]
    count = lax.axis_size("seq")
    part = stream_in.shape[2]
    seq = lax.axis_index("seq")
    row = lax.axis_index("row")
    col = lax.axis_index("col")
    y, core = col // 2, col % 2
    heads = recall_gate.shape[0] // 2
    rw = lax.dynamic_slice_in_dim(recall_gate, y * heads, heads, 0)
    aw = lax.dynamic_slice_in_dim(admit_gate, y * heads, heads, 0)
    soft_own = jax.nn.softplus(-decay_param)[None]
    small = jnp.concatenate(
        [filter_taps, soft_own, decay_param[None], jnp.zeros((2,) + decay_param.shape, F32)]
    )
    gains = jnp.concatenate([mixer_gain[None], feed_gain[None], jnp.zeros((6, part), F32)])

    lengths = lax.dynamic_index_in_dim(doc_lengths, core, 0, False)
    offset = doc_offset(lengths, seq * tokens, tokens)
    edge = jnp.full((8,), -1, jnp.int32)
    off = jnp.concatenate([edge, offset, edge])[:, None]

    (
        x, g, g_low, w_out, w_down, gains_all, small, s1, u, v, border, earlier, mid, mid_low,
        n1, conv, recall, admit, states, mixed, mx, my, md, far_w, sib_own, sib_far, w_in,
    ) = front(
        stream_in, cotangent, input_weight, branch_weight, output_weight, gate_weight, up_weight, down_weight,
        gains, small, recall_gate, admit_gate, off, count - 1,
    )
    taps, soft, decay = small[:KW], small[KW : KW + 1], small[KW + 1 : KW + 2]
    p0, p1, p2, p3, dx2, *dx_all, grad_feed, sum_down, sum_gu = feed(
        (mid_low, mx, my, md), g_low, mid, g, gains_all, w_down,
        (gate_weight, up_weight, sib_own, far_w, sib_far),
    )
    (
        ev, eu, grad_chunk, grad_mixer, grad_small, mine_gu, far_gu, far_down, mine_out, far_out, gates
    ) = back(
        dx_all, w_out, states, v, recall, conv, admit, u, off, soft, taps, rw, aw, border, earlier,
        w_in, s1, x, dx2, gains_all, sum_gu, sum_down, mixed,
    )
    mine_in, far_in, tiny, out, grad = tail(
        n1, eu, ev, grad_small, grad_mixer, grad_feed, (p0, p1, p2, p3), mid, grad_chunk
    )
    place = jnp.stack([row, y]).astype(jnp.int32)
    grad_gate, grad_up, grad_down, grad_input, grad_branch, grad_output = arrange(
        place, mine_gu, far_gu, sum_down, far_down, mine_in, far_in, mine_out, far_out
    )
    gates = gates.astype(F32).reshape((2,) + recall_gate.shape)
    own = taps.shape[1] // 2
    mine = lax.dynamic_slice_in_dim(tiny[:8], core * own, own, 1)
    gain_grads = lax.dynamic_slice_in_dim(tiny[8:10, : 2 * part], core * part, part, 1)
    return (
        out,
        grad,
        gain_grads[0],
        grad_input,
        grad_branch,
        mine[:KW],
        gates[0],
        gates[1],
        mine[KW] * 8.0 * jax.nn.sigmoid(-decay_param),
        grad_output,
        gain_grads[1],
        grad_gate,
        grad_up,
        grad_down,
    )


def solution(mesh):
    in_specs = (
        P(None, "seq", ("col", "row")),
        P(None, "seq", ("col", "row")),
        P(),
        P(("col", "row")),
        P("col", "row"),
        P("col", "row"),
        P(None, ("row", "col")),
        P("row", None, None),
        P("row", None, None),
        P(("row", "col")),
        P("row", "col"),
        P(("col", "row")),
        P("col", "row"),
        P("col", "row"),
        P("row", "col"),
    )
    out_specs = (
        P(None, "seq", ("col", "row")),
        P(None, "seq", ("col", "row")),
        P(("col", "row")),
        P("col", "row"),
        P("col", "row"),
        P(None, ("row", "col")),
        P("row", None, None),
        P("row", None, None),
        P(("row", "col")),
        P("row", "col"),
        P(("col", "row")),
        P("col", "row"),
        P("col", "row"),
        P("row", "col"),
    )
    plan = local_fast if dict(mesh.shape) == {"seq": 4, "row": 2, "col": 4} else local
    return jax.shard_map(plan, mesh=mesh, in_specs=in_specs, out_specs=out_specs, check_vma=False)
```

```python
import functools

import jax
import jax.numpy as jnp
from jax import lax
from jax.experimental import pallas as pl
from jax.experimental.pallas import tpu as pltpu
from jax.sharding import PartitionSpec as P

D = 1536
KW = 4


EPSILON = 1e-06
PRECISE = lax.Precision.HIGHEST
SUM_ROWS = (((0,), (0,)), ((), ()))
SUM_COLS = (((1,), (1,)), ((), ()))


def as_sent(value):
    return jax.tree.map(lambda a: a.astype(jnp.bfloat16) if a.dtype == jnp.float32 else a, value)


def passed_along(block, axis, distance):
    devices = range(lax.axis_size(axis))
    route = [(i - distance, i) for i in devices if i - distance in devices]
    return lax.ppermute(block, axis, route)


def entering_2(part, axis, combine, identity, reverse):
    count = lax.axis_size(axis)
    place = lax.axis_index(axis)
    ahead = count - 1 - place if reverse else place
    gathered = jax.tree.map(lambda a: lax.all_gather(a, axis), part)
    state = jax.tree.map(lambda a, e: jnp.zeros_like(a) + jnp.asarray(e, a.dtype), part, identity)

    def one(hop, state):
        source = count - 1 - hop if reverse else hop
        return combine(
            state, jax.tree.map(lambda a: lax.dynamic_index_in_dim(a, source, 0, False), gathered)
        )

    return lax.fori_loop(0, ahead, one, state)


def compose(first, second):
    return (first[0] * second[0], second[0] * first[1] + second[1])


def convolve(source, taps, offset, border):
    tokens = source.shape[0]
    extended = jnp.concatenate([border, source], axis=0)
    result = jnp.zeros_like(source)
    for lag_index in range(KW):
        anchor = KW - 1 - lag_index
        valid = (offset >= lag_index).astype(jnp.float32)[:, None]
        result = result + taps[lag_index] * extended[anchor : anchor + tokens] * valid
    return result


def slab_pre(conv_value, recall_value, admit_value):
    tokens = conv_value.shape[0]
    blocks = conv_value.reshape(tokens, recall_value.shape[0], recall_value.shape[1])
    recall_pre = jnp.einsum("thi,hij->thj", blocks, recall_value, precision=PRECISE).reshape(
        tokens, -1
    )
    admit_pre = jnp.einsum("thi,hij->thj", blocks, admit_value, precision=PRECISE).reshape(
        tokens, -1
    )
    return (recall_pre, admit_pre)


def own_terms(conv_value, recall_pre, admit_pre, decay_value, resume):
    recall = jax.nn.sigmoid(recall_pre)
    admit = jax.nn.sigmoid(admit_pre)
    log_decay = -8.0 * recall * jax.nn.softplus(-decay_value)
    decays = jnp.exp(log_decay) * resume[:, None]
    drives = jnp.sqrt(-jnp.expm1(2.0 * log_decay)) * admit * conv_value
    return (decays, drives)


def width_total(partial_value):
    return lax.psum(partial_value, ("row", "col"))


def gather_row(source):
    return lax.all_gather(source, "row", axis=1, tiled=True)


def gather_col(source):
    return jax.tree.map(
        lambda part, own: part.astype(own.dtype),
        lax.all_gather(as_sent(source), "col", axis=1, tiled=True),
        source,
    )


def scatter_col(source):
    return (
        lax.psum_scatter(source[0], "col", scatter_dimension=1, tiled=True),
        lax.psum_scatter(source[1], "col", scatter_dimension=1, tiled=True),
    )


def scatter_col_back(source):
    return lax.psum_scatter(source, "col", scatter_dimension=1, tiled=True)


def scatter_row(source):
    return lax.psum_scatter(source, "row", scatter_dimension=1, tiled=True)


def over_seq(grads):
    return (
        lax.psum(grads[0].astype(jnp.bfloat16), "seq").astype(jnp.float32),
        lax.psum(grads[1].astype(jnp.bfloat16), "seq").astype(jnp.float32),
        lax.psum(grads[2].astype(jnp.bfloat16), "seq").astype(jnp.float32),
        lax.psum(grads[3].astype(jnp.bfloat16), "seq").astype(jnp.float32),
        lax.psum(grads[4].astype(jnp.bfloat16), "seq").astype(jnp.float32),
        lax.psum(grads[5].astype(jnp.bfloat16), "seq").astype(jnp.float32),
        lax.psum(grads[6].astype(jnp.bfloat16), "seq").astype(jnp.float32),
        lax.psum(grads[7].astype(jnp.bfloat16), "seq").astype(jnp.float32),
        lax.psum(grads[8].astype(jnp.bfloat16), "seq").astype(jnp.float32),
        lax.psum(grads[9].astype(jnp.bfloat16), "seq").astype(jnp.float32),
        lax.psum(grads[10].astype(jnp.bfloat16), "seq").astype(jnp.float32),
        lax.psum(grads[11].astype(jnp.bfloat16), "seq").astype(jnp.float32),
    )


def normalize(source, scales):
    factor = lax.rsqrt(width_total(jnp.sum(source * source, axis=1)) / D + EPSILON)
    return (source * factor[:, None] * scales, factor)


def norm_back(source, scales, factor, grad_norm):
    weighted = scales * grad_norm
    summed = width_total(jnp.sum(weighted * source, axis=1))
    grad_source = (
        factor[:, None] * weighted - source * (factor * factor * factor * summed / D)[:, None]
    )
    grad_scales = jnp.sum(grad_norm * source * factor[:, None], axis=0)
    return (grad_source, grad_scales)


def doc_offset(lengths, anchor, tokens):
    starts = jnp.cumsum(lengths, dtype=jnp.int32) - lengths
    places = anchor + jnp.arange(tokens, dtype=jnp.int32)
    begins = jnp.max(jnp.where(starts[None, :] <= places[:, None], starts[None, :], 0), axis=1)
    return places - begins


def matmul_rows(left, right):
    return lax.dot_general(left, right, SUM_ROWS, preferred_element_type=jnp.float32)


def matmul_cols(left, right):
    return lax.dot_general(left, right, SUM_COLS, preferred_element_type=jnp.float32)


def local(
    stream_in,
    cotangent,
    doc_lengths,
    mixer_gain,
    input_weight,
    branch_weight,
    filter_taps,
    recall_gate,
    admit_gate,
    decay_param,
    output_weight,
    feed_gain,
    gate_weight,
    up_weight,
    down_weight,
):
    tokens = stream_in.shape[1]
    anchor = lax.axis_index("seq") * tokens
    channels = decay_param.shape[0]
    col_start = lax.axis_index("col") * channels
    params = (
        mixer_gain,
        input_weight,
        branch_weight,
        filter_taps,
        recall_gate,
        admit_gate,
        decay_param,
        output_weight,
        feed_gain,
        gate_weight,
        up_weight,
        down_weight,
    )
    totals = tuple((jnp.zeros(w.shape, jnp.float32) for w in params))
    identity = (jnp.ones_like(decay_param), jnp.zeros_like(decay_param))
    outputs = []
    grads_in = []
    for micro in range(stream_in.shape[0]):
        offset = doc_offset(doc_lengths[micro], anchor, tokens)
        resume = (offset > 0).astype(jnp.float32)
        source = stream_in[micro]
        normed, factor_one = normalize(source, mixer_gain)
        normed_low = normed.astype(jnp.bfloat16)
        normed_all = gather_row(normed_low)
        rec_in, branch = scatter_col(
            (
                jnp.dot(normed_all, input_weight, preferred_element_type=jnp.float32),
                jnp.dot(normed_all, branch_weight, preferred_element_type=jnp.float32),
            )
        )
        border = passed_along(rec_in[tokens - (KW - 1) :], "seq", 1)
        conv_out = convolve(rec_in, filter_taps, offset, border)
        conv_slab = lax.all_gather(conv_out, "col", axis=1, tiled=True)
        slab_values, slab_pull = jax.vjp(slab_pre, conv_slab, recall_gate, admit_gate)
        recall_pre = lax.dynamic_slice_in_dim(slab_values[0], col_start, channels, 1)
        admit_pre = lax.dynamic_slice_in_dim(slab_values[1], col_start, channels, 1)

        def local_gates(conv_value, recall_value, admit_value, decay_value):
            return own_terms(conv_value, recall_value, admit_value, decay_value, resume)

        (decays, drives), gates_pull = jax.vjp(
            local_gates, conv_out, recall_pre, admit_pre, decay_param
        )
        cum_decay, local_state = lax.associative_scan(compose, (decays, drives), axis=0)
        entering = entering_2((cum_decay[-1], local_state[-1]), "seq", compose, identity, False)[1]
        states = local_state + cum_decay * entering
        branch_act = jax.nn.gelu(branch)
        mixed_all = gather_col((states * branch_act).astype(jnp.bfloat16))
        middle = source + scatter_row(
            jnp.dot(mixed_all, output_weight, preferred_element_type=jnp.float32)
        )
        normed_two, factor_two = normalize(middle, feed_gain)
        normed_two_low = normed_two.astype(jnp.bfloat16)
        normed_two_all = gather_row(normed_two_low)
        gate_pre, up_pre = scatter_col(
            (
                jnp.dot(normed_two_all, gate_weight, preferred_element_type=jnp.float32),
                jnp.dot(normed_two_all, up_weight, preferred_element_type=jnp.float32),
            )
        )
        gate_act = jax.nn.gelu(gate_pre)
        hidden_all = gather_col((gate_act * up_pre).astype(jnp.bfloat16))
        outputs.append(
            middle
            + scatter_row(jnp.dot(hidden_all, down_weight, preferred_element_type=jnp.float32))
        )
        upstream = cotangent[micro]
        upstream_all = gather_row(upstream.astype(jnp.bfloat16))
        grad_down = matmul_rows(hidden_all, upstream_all)
        grad_hidden = scatter_col_back(matmul_cols(upstream_all, down_weight))
        gate_value, gelu_pull = jax.vjp(jax.nn.gelu, gate_pre)
        error_gate = gelu_pull(grad_hidden * up_pre)[0].astype(jnp.bfloat16)
        error_up = (grad_hidden * gate_act).astype(jnp.bfloat16)
        gate_err_all, up_err_all = gather_col((error_gate, error_up))
        grad_gate = matmul_rows(normed_two_all, gate_err_all)
        grad_up = matmul_rows(normed_two_all, up_err_all)
        grad_normed_two = scatter_row(
            matmul_cols(gate_err_all, gate_weight) + matmul_cols(up_err_all, up_weight)
        )
        back_middle, grad_feed = norm_back(middle, feed_gain, factor_two, grad_normed_two)
        grad_middle = upstream + back_middle
        rec_err_all = gather_row(grad_middle.astype(jnp.bfloat16))
        grad_output = matmul_rows(mixed_all, rec_err_all)
        grad_mixed = scatter_col_back(matmul_cols(rec_err_all, output_weight))
        branch_value, branch_pull = jax.vjp(jax.nn.gelu, branch)
        error_branch = branch_pull(grad_mixed * states)[0].astype(jnp.bfloat16)
        direct = grad_mixed * branch_act
        ahead = jnp.concatenate([decays[1:], jnp.ones_like(decays[:1])], axis=0)
        reach, partial_adj = lax.associative_scan(compose, (ahead, direct), axis=0, reverse=True)
        incoming = entering_2(
            (decays[0] * reach[0], decays[0] * partial_adj[0]), "seq", compose, identity, True
        )[1]
        adjoint = partial_adj + reach * incoming
        previous = jnp.concatenate([entering[None, :], states[:-1]], axis=0)
        conv_direct, grad_recall_pre, grad_admit_pre, grad_decay = gates_pull(
            (adjoint * previous, adjoint)
        )
        recall_all, admit_all = (
            lax.all_gather(grad_recall_pre.astype(jnp.bfloat16), "col", axis=1, tiled=True).astype(
                grad_recall_pre.dtype
            ),
            lax.all_gather(grad_admit_pre.astype(jnp.bfloat16), "col", axis=1, tiled=True).astype(
                grad_admit_pre.dtype
            ),
        )
        grad_slab, grad_recall, grad_admit = slab_pull((recall_all, admit_all))
        grad_conv_out = conv_direct + lax.dynamic_slice_in_dim(grad_slab, col_start, channels, 1)

        def local_conv(input_value, taps_value, border_value):
            return convolve(input_value, taps_value, offset, border_value)

        conv_value, conv_pull = jax.vjp(local_conv, rec_in, filter_taps, border)
        grad_rec_in, grad_taps, grad_border = conv_pull(grad_conv_out)
        from_next = passed_along(grad_border, "seq", -1)
        grad_rec_in = grad_rec_in + jnp.pad(from_next, ((tokens - (KW - 1), 0), (0, 0)))
        error_input = grad_rec_in.astype(jnp.bfloat16)
        in_err_all, branch_err_all = gather_col((error_input, error_branch))
        grad_input = matmul_rows(normed_all, in_err_all)
        grad_branch = matmul_rows(normed_all, branch_err_all)
        grad_normed = scatter_row(
            matmul_cols(in_err_all, input_weight) + matmul_cols(branch_err_all, branch_weight)
        )
        back_source, grad_mixer = norm_back(source, mixer_gain, factor_one, grad_normed)
        grads_in.append(grad_middle + back_source)
        local_grads = (
            grad_mixer,
            grad_input,
            grad_branch,
            grad_taps,
            grad_recall,
            grad_admit,
            grad_decay,
            grad_output,
            grad_feed,
            grad_gate,
            grad_up,
            grad_down,
        )
        local_grads = over_seq(local_grads)
        totals = tuple((acc + new for acc, new in zip(totals, local_grads)))
    return (jnp.stack(outputs), jnp.stack(grads_in)) + tuple(totals)


BF = jnp.bfloat16
F32 = jnp.float32
VMEM_LIMIT = 62 * 1024 * 1024
ROW_BLOCK = 256
GELU_A = 0.7978845608028654
GELU_B = 0.044715


def cost(flops, moved, trans=0):
    return pl.CostEstimate(flops=int(flops), bytes_accessed=int(moved), transcendentals=int(trans))


def params():
    return pltpu.CompilerParams(vmem_limit_bytes=VMEM_LIMIT, dimension_semantics=("arbitrary",))


def nbytes(*arrays):
    return sum(a.size * a.dtype.itemsize for a in arrays)


def gelu_pair(v):
    t = jnp.tanh(GELU_A * (v + GELU_B * v * v * v))
    value = 0.5 * v * (1.0 + t)
    slope = 0.5 * (1.0 + t) + 0.5 * v * (1.0 - t * t) * GELU_A * (1.0 + 3.0 * GELU_B * v * v)
    return value, slope


def minus_expm1(x):
    series = 1.0 + x * (1.0 / 7.0)
    for n in (6, 5, 4, 3, 2):
        series = 1.0 + x * (1.0 / n) * series
    return jnp.where(x > -0.3, -x * series, 1.0 - jnp.exp(x))


def pair_up(left, right):
    width = left.shape[1]
    lane = lax.broadcasted_iota(jnp.int32, left.shape, 1)
    low = lane < width // 2
    return (
        jnp.where(low, left, pltpu.roll(right, width // 2, 1)),
        jnp.where(low, pltpu.roll(left, width // 2, 1), right),
    )


def dot_nn(a, b, precision=None):
    return lax.dot_general(
        a, b, (((1,), (0,)), ((), ())), precision=precision, preferred_element_type=F32
    )


def dot_nt(a, b, precision=None):
    return lax.dot_general(
        a, b, (((1,), (1,)), ((), ())), precision=precision, preferred_element_type=F32
    )


def dot_tn(a, b, precision=None):
    return lax.dot_general(
        a, b, (((0,), (0,)), ((), ())), precision=precision, preferred_element_type=F32
    )


def rows_spec(block, width, start=0):
    return pl.BlockSpec((block, width), lambda i: (i + start, 0))


def whole_spec(shape):
    rank = len(shape)
    return pl.BlockSpec(shape, lambda i: (0,) * rank, pipeline_mode=pl.Buffered(1))


def head_spec(rows, width=128):
    return pl.BlockSpec((rows, width), lambda h: (0, h))


def sds(shape, dtype):
    return jax.ShapeDtypeStruct(shape, dtype)


MESH_ID = pl.DeviceIdType.MESH


def neighbour_x():
    return {"row": 1 - lax.axis_index("row")}


def neighbour_y():
    return {"col": lax.rem(lax.axis_index("col") + 2, 4)}


def greet():
    barrier = pltpu.get_barrier_semaphore()
    for device in (neighbour_x(), neighbour_y()):
        pl.semaphore_signal(barrier, inc=1, device_id=device, device_id_type=MESH_ID)
    pl.semaphore_wait(barrier, 2)


def message(src, dst, device, sems, n):
    send, recv = sems
    return pltpu.make_async_remote_copy(
        src_ref=src,
        dst_ref=dst,
        send_sem=send.at[n],
        recv_sem=recv.at[n],
        device_id=device,
        device_id_type=MESH_ID,
    )


def neighbour_core():
    col = lax.axis_index("col")
    return {"col": col + 1 - 2 * lax.rem(col, 2)}


def neighbour_end():
    seq = lax.axis_index("seq")
    return {"seq": seq + 1 - 2 * lax.rem(seq, 2)}


def neighbour_middle():
    return {"seq": 3 - lax.axis_index("seq")}


def greet_all(devices):
    barrier = pltpu.get_barrier_semaphore()
    for device in devices:
        pl.semaphore_signal(barrier, inc=1, device_id=device, device_id_type=MESH_ID)
    pl.semaphore_wait(barrier, len(devices))


def row_step(ref):
    rows, lanes = ref.shape
    step = 16
    while step * 2 * lanes <= 32768 and rows % (step * 2) == 0:
        step *= 2
    return step


def plus_in(dst, src):
    step = row_step(dst)

    def one(n, carry):
        at = pl.ds(pl.multiple_of(n * step, step), step)
        dst[at, :] = (dst[at, :].astype(F32) + src[at, :].astype(F32)).astype(dst.dtype)
        return carry

    lax.fori_loop(0, dst.shape[0] // step, one, 0)


def put_sum(dst, left, right):
    step = row_step(dst)

    def one(n, carry):
        at = pl.ds(pl.multiple_of(n * step, step), step)
        dst[at, :] = (left[at, :].astype(F32) + right[at, :].astype(F32)).astype(dst.dtype)
        return carry

    lax.fori_loop(0, dst.shape[0] // step, one, 0)


def put_in(dst, src):
    step = row_step(dst)

    def one(n, carry):
        at = pl.ds(pl.multiple_of(n * step, step), step)
        dst[at, :] = src[at, :].astype(dst.dtype)
        return carry

    lax.fori_loop(0, dst.shape[0] // step, one, 0)


class SeqSum:
    def __init__(self, pieces, sems, base):
        self.pieces = pieces
        count = len(pieces)
        self.to_end = [message(s, a, neighbour_end(), sems, base + n) for n, (s, a, b) in enumerate(pieces)]
        self.across = [
            message(s, b, neighbour_middle(), sems, base + count + n) for n, (s, a, b) in enumerate(pieces)
        ]
        seq = lax.axis_index("seq")
        self.middle = (seq == 1) | (seq == 2)
        self.end = (seq == 0) | (seq == 3)

    def begin(self, n):
        @pl.when(self.end)
        def _():
            self.to_end[n].start()

    def relay(self, n):
        s, a, b = self.pieces[n]

        @pl.when(self.middle)
        def _():
            self.to_end[n].wait_recv()
            plus_in(s, a)
            self.across[n].start()

    def settle(self, n):
        s, a, b = self.pieces[n]

        @pl.when(self.middle)
        def _():
            self.across[n].wait_recv()
            self.across[n].wait_send()
            plus_in(s, b)
            self.to_end[n].start()

    def finish(self, n):
        s, a, b = self.pieces[n]

        @pl.when(self.end)
        def _():
            self.to_end[n].wait_recv()
            self.to_end[n].wait_send()
            put_in(s, a)

        @pl.when(self.middle)
        def _():
            self.to_end[n].wait_send()


def scatter_messages(q1, q2, q3, r3, rx, ry, sems, base):
    half = q1.shape[0] // 2
    a, b = pl.ds(0, half), pl.ds(half, half)
    x, y = neighbour_x(), neighbour_y()
    plan = ((q3, r3, a, x), (q3, r3, b, y), (q1, rx, a, x), (q2, ry, a, y), (q2, ry, b, y), (q1, rx, b, x))
    return [
        message(src.at[at, :], dst.at[at, :], dev, sems, base + n)
        for n, (src, dst, at, dev) in enumerate(plan)
    ]


def gather_messages(own, gx, gy, gd, sems, base):
    half = own.shape[0] // 2
    a, b = pl.ds(0, half), pl.ds(half, half)
    x, y = neighbour_x(), neighbour_y()
    plan = ((own, gx, a, x), (own, gy, a, y), (own, gx, b, x), (own, gy, b, y), (gx, gd, a, y), (gy, gd, b, x))
    return [
        message(src.at[at, :], dst.at[at, :], dev, sems, base + n)
        for n, (src, dst, at, dev) in enumerate(plan)
    ]


def gather_messages_by_x(own, gx, gy, gd, sems, base):
    half = own.shape[0] // 2
    a, b = pl.ds(0, half), pl.ds(half, half)
    x, y = neighbour_x(), neighbour_y()
    plan = ((own, gx, a, x), (own, gy, a, y), (own, gx, b, x), (own, gy, b, y), (gy, gd, a, x), (gy, gd, b, x))
    return [
        message(src.at[at, :], dst.at[at, :], dev, sems, base + n)
        for n, (src, dst, at, dev) in enumerate(plan)
    ]


def add_into(dst, src, start, rows):
    plus_in(dst.at[pl.ds(start, rows), :], src.at[pl.ds(start, rows), :])


def load_rows(gate_w, up_w, sib_own, far, sib_far, dst, sem):
    width, lanes = far.shape
    part, units = width // 2, lanes // 2
    row = lax.axis_index("row")
    y = lax.div(lax.axis_index("col"), 2)
    own = pl.ds(pl.multiple_of(y * units, units), units)
    copies = []

    def copy(src, dst):
        copies.append(pltpu.make_async_copy(src, dst, sem.at[len(copies)]))
        copies[-1].start()

    for dx in (0, 1):
        rows = pl.ds(pl.multiple_of(part * (row + dx - 2 * row * dx), part), part)
        at = [pl.ds(((n // 2 * 2 + dx) * 2 + n % 2) * part, part) for n in range(4)]
        copy(gate_w.at[rows, own], dst.at[at[0], pl.ds(0, units)])
        copy(up_w.at[rows, own], dst.at[at[0], pl.ds(units, units)])
        for n, src in enumerate((sib_own, far, sib_far)):
            copy(src.at[rows, :], dst.at[at[n + 1], :])
    return copies


def comm_params(n):
    return pltpu.CompilerParams(
        vmem_limit_bytes=VMEM_LIMIT,
        dimension_semantics=("arbitrary",),
        collective_id=n,
        has_side_effects=True,
    )


def any_spec():
    return pl.BlockSpec(memory_space=pl.ANY)


def held_spec(block, width, last):
    return pl.BlockSpec((block, width), lambda i: (jnp.minimum(i, last), 0))


def full_spec(shape):
    rank = len(shape)
    return pl.BlockSpec(shape, lambda i: (0,) * rank)


def row_sums(values):
    folded = values[:, :128]
    for n in range(128, values.shape[1], 128):
        folded = folded + values[:, n : n + 128]
    return dot_nt(jnp.ones((8, 128), F32), folded, PRECISE)


def as_column(lanes, width):
    first = (lax.broadcasted_iota(jnp.int32, (8, 128), 0) == 0).astype(F32)
    column = dot_tn(lanes, first, PRECISE)
    return jnp.concatenate([column] * (width // 128), axis=1)


def norm_back_rows(start, rows, own_sum, low_x, low_y, dots_x, dots_y, scale, source, gain, base, out, low):
    width = source.shape[1]
    step = 128

    def one(n, sum_grad):
        at = pl.ds(pl.multiple_of(start + n * step, step), step)
        d = own_sum[at, :] + low_x[at, :].astype(F32) + low_y[at, :].astype(F32)
        s, m = scale[at, :], source[at, :]
        t = as_column(dots_x[:, at] + dots_y[:, at], width)
        new = base[at, :] + s * gain * d - m * (s * s) * t * (1.0 / D)
        out[at, :] = new
        if low is not None:
            low[at, :] = new.astype(BF)
        return sum_grad + jnp.sum(d * m * s, axis=0, keepdims=True)

    return lax.fori_loop(0, rows // step, one, jnp.zeros((1, width), F32))


def chain(entries, count):
    state = entries[count - 1, 0, 1:2, :]
    for n in range(count - 2, -1, -1):
        state = entries[n, 0, 1:2, :] + entries[n, 0, 0:1, :] * state
    return state


def carried(entries, h, count):
    state = entries[count - 1, h, 1:2, :]
    for n in range(count - 2, -1, -1):
        state = entries[n, h, 1:2, :] + entries[n, h, 0:1, :] * state
    return state


class Messages:
    def __init__(self, sems):
        self.sems, self.used = sems, 0

    def new(self, src, dst, device):
        self.used += 1
        return message(src, dst, device, self.sems, self.used - 1)

    def block(self, maker, *refs):
        made = maker(*refs, self.sems, self.used)
        self.used += len(made)
        return made


FRONT_MESSAGES = 80


def front_body(heads, blocks, count, *refs):
    (stream, cot, in_w, br_w, out_w, gate_w, up_w, down_w) = refs[:8]
    (gains_in, small_in, recall_gate, admit_gate, off) = refs[8:13]
    (e_own, w_down, gains_out, small, s1, border_out, earlier_out, mid, own) = refs[13:22]
    (n1, conv, recall, admit, states, mixed) = refs[22:28]
    (mx, my, md, far_gu, sib_own, sib_far, w_in_out, x_out, g_out, w_out_out, u_out, v_out) = refs[28:40]
    (x_own, x_recv, g_own, g_recv, gains_recv, small_recv, own_low, gx, gy, gd) = refs[40:50]
    (w_in, gains, border, earlier, x, g, w_out, u, v) = refs[50:59]
    (wo, wd, local, cum, ext, ends, q0, q1, q2, q3, r3, rx, ry, load, send, recv) = refs[59:]
    i = pl.program_id(0)
    seq, row, col = lax.axis_index("seq"), lax.axis_index("row"), lax.axis_index("col")
    y = lax.div(col, 2)
    core = lax.rem(col, 2)
    rows, width = x.shape
    part = width // 2
    half = rows // 2
    block = rows // blocks
    channels = u.shape[1]
    units = gate_w.shape[1] // 2
    to_x, to_y, to_core = neighbour_x(), neighbour_y(), neighbour_core()
    made = Messages((send, recv))
    copies = []

    def copy(src, dst):
        copies.append(pltpu.make_async_copy(src, dst, load.at[len(copies)]))
        return copies[-1]

    swap = [
        made.new(stream.at[1 - core], x_recv, to_core),
        made.new(gains_in, gains_recv, to_core),
        made.new(small_in, small_recv, to_core),
    ]
    swap_g = made.new(cot.at[1 - core], g_recv, to_core)
    x_copy, g_copy = copy(stream.at[core], x_own), copy(cot.at[core], g_own)
    gains_x = made.new(gains.at[:, pl.ds(0, width)], gains.at[:, pl.ds(width, width)], to_x)
    gains_y = made.new(gains.at[:, pl.ds(0, width)], gains.at[:, pl.ds(2 * width, width)], to_y)
    gains_d = made.new(gains.at[:, pl.ds(width, width)], gains.at[:, pl.ds(3 * width, width)], to_y)

    def place(dy, dx, dc):
        return pl.ds(pl.multiple_of(((dy * 2 + dx) * 2 + dc) * part, part), part)

    own_cols = pl.ds(pl.multiple_of(y * channels, channels), channels)
    other_cols = pl.ds(pl.multiple_of((1 - y) * channels, channels), channels)
    in_own, in_far, in_core, in_pass = [], [], [], []
    for n, w in enumerate((in_w, br_w)):
        lanes = pl.ds(n * channels, channels)
        for k in (0, 1):
            source = pl.ds(k * part, part)
            dx = row + k - 2 * row * k
            in_far.append(made.new(w.at[source, other_cols], w_in.at[place(1, dx, 0), lanes], to_y))
            in_own.append(copy(w.at[source, own_cols], w_in.at[place(0, dx, 0), lanes]))
            in_core.append(made.new(w.at[source, own_cols], w_in.at[place(0, dx, 1), lanes], to_core))
            in_pass.append(
                made.new(w_in.at[place(1, dx, 0), lanes], w_in.at[place(1, dx, 1), lanes], to_core)
            )

    own_rows = pl.ds(pl.multiple_of(y * channels, channels), channels)
    other_rows = pl.ds(pl.multiple_of((1 - y) * channels, channels), channels)
    wo_own = copy(out_w.at[own_rows, :], wo.at[0, 0])
    wo_far = made.new(out_w.at[other_rows, :], wo.at[1, 0], to_y)
    wo_core = made.new(out_w.at[own_rows, :], wo.at[0, 1], to_core)
    wo_pass = made.new(wo.at[1, 0], wo.at[1, 1], to_core)

    share, share_d = gate_w.shape[0] // (count + 1), units // (count + 1)
    own_units = pl.ds(pl.multiple_of(y * units, units), units)
    other_units = pl.ds(pl.multiple_of((1 - y) * units, units), units)
    at_seq = pl.ds(pl.multiple_of(seq * share, share), share)
    at_seq_d = pl.ds(pl.multiple_of(seq * share_d, share_d), share_d)
    far_d = wd.at[1, 0]
    first_lanes, last_lanes = pl.ds(0, units), pl.ds(units, units)
    from_d = pl.ds(pl.multiple_of((1 - y) * units + seq * share_d, share_d), share_d)
    ff_far = [
        made.new(down_w.at[from_d, :], far_d.at[at_seq_d, :], to_y),
        made.new(gate_w.at[at_seq, other_units], far_gu.at[at_seq, first_lanes], to_y),
        made.new(up_w.at[at_seq, other_units], far_gu.at[at_seq, last_lanes], to_y),
    ]
    others = [{"seq": lax.rem(seq + n, count + 1)} for n in range(1, count + 1)]
    ff_share = [made.new(far_d.at[at_seq_d, :], far_d.at[at_seq_d, :], device) for device in others]
    ff_share += [made.new(far_gu.at[at_seq, :], far_gu.at[at_seq, :], device) for device in others]
    ff_core = [
        made.new(gate_w.at[:, own_units], sib_own.at[:, first_lanes], to_core),
        made.new(up_w.at[:, own_units], sib_own.at[:, last_lanes], to_core),
        made.new(down_w.at[own_units, :], wd.at[0, 1], to_core),
    ]
    ff_pass = [made.new(far_gu, sib_far, to_core), made.new(far_d, wd.at[1, 1], to_core)]
    wd_own = copy(down_w.at[own_units, :], wd.at[0, 0])
    ahead = len(copies)
    w_in_store = copy(w_in, w_in_out)
    x_store, g_store, w_out_store = copy(x, x_out), copy(g, g_out), copy(w_out, w_out_out)
    u_store, v_store = copy(u, u_out), copy(v, v_out)

    gather_n = made.block(gather_messages_by_x, own_low, gx, gy, gd)
    scatter = made.block(scatter_messages, q1, q2, q3, r3, rx, ry)
    gather_m = made.block(gather_messages, own, mx, my, md)
    edge = made.new(u.at[pl.ds(rows - 8, 8), :], border, {"seq": seq + 1})
    hand_on = [made.new(ends, earlier.at[n - 1], {"seq": seq + n}) for n in range(1, count + 1)]

    def put_together(left, right, full, low):
        step = 128

        def one(n, carry):
            at = pl.ds(pl.multiple_of(n * step, step), step)
            whole = jnp.concatenate([left[:, at], right[:, at]], axis=0).T
            full[at, :] = whole
            low[at, :] = whole.astype(BF)
            return carry

        lax.fori_loop(0, rows // step, one, 0)

    @pl.when(i == 0)
    def _():
        for c in copies[:ahead]:
            c.start()
        border[...] = jnp.zeros_like(border)
        earlier[...] = jnp.zeros_like(earlier)
        greet_all(
            [to_x, to_y, to_core] + [{"seq": lax.rem(seq + n, count + 1)} for n in range(1, count + 1)]
        )
        for m in swap:
            m.start()
        x_copy.wait()
        swap[0].wait_recv()
        put_together(x_own, x_recv, x, own_low)
        x_store.start()
        for m in gather_n[:4]:
            m.start()
        for m in in_core:
            m.start()
        swap[1].wait_recv()
        gains[:, 0:width] = jnp.concatenate([gains_in[...], gains_recv[...]], axis=1)
        gains_x.start()
        gains_y.start()
        swap[2].wait_recv()
        lane = small_in.shape[1]
        small[:, pl.ds(pl.multiple_of(core * lane, lane), lane)] = small_in[...]
        small[:, pl.ds(pl.multiple_of((1 - core) * lane, lane), lane)] = small_recv[...]
        swap_g.start()
        gains_x.wait_recv()
        gains_d.start()
        gather_n[1].wait_recv()
        gather_n[4].start()
        wo_core.start()
        for m in ff_core:
            m.start()
        gather_n[3].wait_recv()
        gather_n[5].start()
        for m in in_far:
            m.start()
        for m, n in zip(in_far, in_pass):
            m.wait_recv()
            n.start()
        wo_far.start()
        for m in ff_far:
            m.start()
        for c in in_own:
            c.wait()
        for m in in_core + in_pass:
            m.wait_recv()
        gains_y.wait_recv()
        gains_d.wait_recv()
        w_in_store.start()
        gather_n[0].wait_recv()
        gather_n[4].wait_recv()

    @pl.when(i == 1)
    def _():
        g_copy.wait()
        swap_g.wait_recv()
        put_together(g_own, g_recv, g, e_own)
        g_store.start()

    @pl.when(i == blocks // 2)
    def _():
        gather_n[2].wait_recv()
        gather_n[5].wait_recv()

    @pl.when(i < blocks)
    def _():
        at = pl.ds(pl.multiple_of(i * block, block), block)
        parts = [r[at, :].astype(F32) for r in (own_low, gx, gy, gd)]
        total = sum(jnp.sum(p * p, axis=1, keepdims=True) for p in parts)
        s = lax.rsqrt(total / D + EPSILON)
        s1[at, :] = s
        normed = [p * s * gains[0:1, j * width : (j + 1) * width] for j, p in enumerate(parts)]
        acc = None
        for j, n in enumerate(normed):
            term = dot_nn(n.astype(BF), w_in[j * width : (j + 1) * width, :])
            acc = term if acc is None else acc + term
        u[at, :] = acc[:, :channels]
        v[at, :] = acc[:, channels:]
        for j in (0, 1):
            k, p = pair_up(normed[2 * j], normed[2 * j + 1])
            n1[:, j * width : (j + 1) * width] = k.astype(BF)
            n1[:, (j + 2) * width : (j + 3) * width] = p.astype(BF)

    @pl.when((i == blocks - 1) & (seq < count))
    def _():
        edge.start()

    @pl.when((i == blocks) & (seq > 0))
    def _():
        edge.wait_recv()

    @pl.when(i == blocks)
    def _():
        u_store.start()
        v_store.start()

    @pl.when(i == blocks - 1)
    def _():
        ff_far[0].wait_recv()
        for m in ff_share[:count]:
            m.start()

    @pl.when((i >= blocks) & (i < blocks + heads))
    def _():
        h = i - blocks
        lane = pl.ds(pl.multiple_of(h * 128, 128), 128)
        state_h, cum_h = local.at[h], cum.at[h]
        ext[0:8, :] = border[:, lane]
        ext[8 : 8 + rows, :] = u[:, lane]
        sp = small[KW : KW + 1, lane]
        step = ROW_BLOCK
        for r in range(0, rows, step):
            o = off[8 + r : 8 + r + step, :]
            total = small[0:1, lane] * ext[8 + r : 8 + r + step, :]
            for k in range(1, KW):
                term = small[k : k + 1, lane] * ext[8 + r - k : 8 + r - k + step, :]
                total = total + jnp.where(o >= k, term, 0.0)
            conv[r : r + step, :] = total
            rec = jax.nn.sigmoid(dot_nn(total, recall_gate[y * heads + h], PRECISE))
            adm = jax.nn.sigmoid(dot_nn(total, admit_gate[y * heads + h], PRECISE))
            recall[r : r + step, :] = rec
            admit[r : r + step, :] = adm
            ell = -8.0 * rec * sp
            cum_h[r : r + step, :] = jnp.where(o > 0, jnp.exp(ell), 0.0)
            state_h[r : r + step, :] = jnp.sqrt(minus_expm1(2.0 * ell)) * adm * total
        seg = rows // 8

        def one(n, carry):
            h, p = carry
            at = pl.ds(n, 8, stride=seg)
            d = cum_h[at, :]
            h = d * h + state_h[at, :]
            p = d * p
            state_h[at, :] = h
            cum_h[at, :] = p
            return h, p

        zero = jnp.zeros((8, 128), F32)
        last, product = lax.fori_loop(0, seg, one, (zero, zero + 1.0), unroll=8)
        carry_h, carry_p = last[0:1, :], product[0:1, :]
        for s in range(1, 8):
            at = slice(s * seg, (s + 1) * seg)
            c = cum_h[at, :]
            state_h[at, :] = state_h[at, :] + c * carry_h
            cum_h[at, :] = c * carry_p
            carry_h = last[s : s + 1, :] + product[s : s + 1, :] * carry_h
            carry_p = product[s : s + 1, :] * carry_p
        ends[h, 0:1, :] = carry_p
        ends[h, 1:2, :] = carry_h
        ends[h, 2:8, :] = jnp.zeros((6, 128), F32)

    @pl.when(i == blocks + 1)
    def _():
        wo_far.wait_recv()
        wo_pass.start()

    def columns_in_order(pieces, out):
        size = out.shape[0]
        step = 128
        lower = row == 0

        def one(n, carry):
            at = pl.ds(pl.multiple_of(n * step, step), step)
            for dy in (0, 1):
                first, second = pair_up(pieces[dy, 0, at, :].astype(F32), pieces[dy, 1, at, :].astype(F32))
                near, far = jnp.where(lower, first, second), jnp.where(lower, second, first)
                out[at, 2 * dy * width : (2 * dy + 1) * width] = near.astype(BF)
                out[at, (2 * dy + 1) * width : (2 * dy + 2) * width] = far.astype(BF)
            return carry

        lax.fori_loop(0, size // step, one, 0)

    @pl.when(i == blocks + heads - 1)
    def _():
        wo_own.wait()
        wo_core.wait_recv()
        wo_pass.wait_recv()
        columns_in_order(wo, w_out)
        w_out_store.start()

    for n in range(1, count + 1):

        @pl.when((i == blocks + heads - 1) & (seq <= count - n))
        def _():
            hand_on[n - 1].start()

        @pl.when((i == blocks + heads) & (seq >= n))
        def _():
            hand_on[n - 1].wait_recv()

    @pl.when(i == blocks + heads)
    def _():
        for m in ff_far[1:]:
            m.wait_recv()
        for m in ff_share[count:]:
            m.start()

    third = blocks + heads

    @pl.when((i >= third) & (i < third + blocks))
    def _():
        at = pl.ds(pl.multiple_of((i - third) * block, block), block)
        st = jnp.concatenate(
            [local[h, at, :] + cum[h, at, :] * carried(earlier, h, count) for h in range(heads)], axis=1
        )
        states[...] = st
        m = (st * gelu_pair(v[at, :])[0]).astype(BF)
        mixed[...] = m
        for j, q in ((3, q3), (1, q1), (2, q2), (0, q0)):
            q[at, :] = dot_nn(m, w_out[:, j * width : (j + 1) * width]).astype(q.dtype)

    @pl.when(i == third + blocks // 2 - 1)
    def _():
        scatter[0].start()
        scatter[2].start()

    @pl.when(i == third + blocks - 1)
    def _():
        scatter[1].start()

    @pl.when(i == third + blocks)
    def _():
        scatter[0].wait_recv()
        add_into(q2, r3, 0, half)
        scatter[3].start()
        scatter[4].start()
        scatter[1].wait_recv()
        add_into(q1, r3, half, half)
        scatter[5].start()
        gains_out[...] = gains[...]
        border_out[...] = border[...]
        earlier_out[...] = earlier[...]
        for base, first in ((0, 2), (half, 4)):
            scatter[first].wait_recv()
            scatter[first + 1].wait_recv()

            def one(n, carry):
                at = pl.ds(pl.multiple_of(base + n * 128, 128), 128)
                total = x[at, :] + q0[at, :] + rx[at, :].astype(F32) + ry[at, :].astype(F32)
                mid[at, :] = total
                own[at, :] = total.astype(BF)
                return carry

            lax.fori_loop(0, half // 128, one, 0)
            start = 0 if base == 0 else 2
            gather_m[start].start()
            gather_m[start + 1].start()
        for m in ff_share:
            m.wait_recv()
        for m in ff_pass:
            m.start()
        gather_m[0].wait_recv()
        gather_m[4].start()
        gather_m[3].wait_recv()
        gather_m[5].start()
        wd_own.wait()
        for m in ff_core + ff_pass:
            m.wait_recv()
        columns_in_order(wd, w_down)
        for c in copies[ahead:]:
            c.wait()
        for n in (1, 2, 4, 5):
            gather_m[n].wait_recv()
        sent = swap + [swap_g, gains_x, gains_y, gains_d] + in_far + in_core + in_pass
        sent += [wo_far, wo_core, wo_pass] + ff_far + ff_share + ff_core + ff_pass
        for m in sent + gather_n + scatter + gather_m:
            m.wait_send()

        @pl.when(seq < count)
        def _():
            edge.wait_send()

        for n in range(1, count + 1):

            @pl.when(seq <= count - n)
            def _():
                hand_on[n - 1].wait_send()


def front(stream, cot, in_w, br_w, out_w, gate_w, up_w, down_w, gains, small, recall_gate, admit_gate, off, count):
    part, rows = stream.shape[1:]
    width = 2 * part
    channels = in_w.shape[1] // 2
    units = gate_w.shape[1] // 2
    heads = channels // 128
    block = ROW_BLOCK
    blocks = rows // block

    def norm_at(i):
        return (jnp.minimum(i, blocks - 1), 0)

    def head_at(i):
        return (0, jnp.clip(i - blocks, 0, heads - 1))

    def mix_at(i):
        return (jnp.clip(i - blocks - heads, 0, blocks - 1), 0)

    chunk_low, chunk = sds((rows, width), BF), sds((rows, width), F32)
    wide = sds((rows, channels), F32)
    held = [
        chunk_low,
        sds((units, 4 * width), BF),
        sds((8, 4 * width), F32),
        sds((8, channels), F32),
        sds((rows, 1), F32),
        sds((8, channels), F32),
        sds((count, heads, 8, 128), F32),
        chunk,
        chunk_low,
    ]
    blocked = [sds((rows, 4 * width), BF), wide, wide, wide, wide, sds((rows, channels), BF)]
    away = [chunk_low] * 3 + [sds((width, 2 * units), BF)] * 3 + [sds((4 * width, 2 * channels), BF)]
    away += [chunk, chunk, sds((channels, 4 * width), BF), wide, wide]
    piece = pltpu.VMEM((rows, width), BF)
    side = pltpu.VMEM((part, rows), F32)
    tall = pl.BlockSpec((rows, 128), head_at)
    return pl.pallas_call(
        functools.partial(front_body, heads, blocks, count),
        grid=(2 * blocks + heads + 1,),
        in_specs=[any_spec()] * 8
        + [whole_spec(a.shape) for a in (gains, small, recall_gate, admit_gate, off)],
        out_specs=[whole_spec(s.shape) for s in held]
        + [pl.BlockSpec((block, 4 * width), norm_at)]
        + [tall] * 3
        + [pl.BlockSpec((block, channels), mix_at)] * 2
        + [any_spec()] * len(away),
        out_shape=held + blocked + away,
        scratch_shapes=[side] * 4
        + [pltpu.VMEM(gains.shape, F32), pltpu.VMEM(small.shape, F32)]
        + [piece] * 4
        + [
            pltpu.VMEM((4 * width, 2 * channels), BF),
            pltpu.VMEM((8, 4 * width), F32),
            pltpu.VMEM((8, channels), F32),
            pltpu.VMEM((count, heads, 8, 128), F32),
            pltpu.VMEM((rows, width), F32),
            pltpu.VMEM((rows, width), F32),
            pltpu.VMEM((channels, 4 * width), BF),
            pltpu.VMEM((rows, channels), F32),
            pltpu.VMEM((rows, channels), F32),
            pltpu.VMEM((2, 2, channels, width), BF),
            pltpu.VMEM((2, 2, units, width), BF),
            pltpu.VMEM((heads, rows, 128), F32),
            pltpu.VMEM((heads, rows, 128), F32),
            pltpu.VMEM((rows + 8, 128), F32),
            pltpu.VMEM((heads, 8, 128), F32),
            pltpu.VMEM((rows, width), F32),
        ]
        + [piece] * 6
        + [pltpu.SemaphoreType.DMA((14,))]
        + [pltpu.SemaphoreType.DMA((FRONT_MESSAGES,))] * 2,
        compiler_params=comm_params(1),
        cost_estimate=cost(200 * rows * in_w.size, rows * 40000),
        name="front",
    )(stream, cot, in_w, br_w, out_w, gate_w, up_w, down_w, gains, small, recall_gate, admit_gate, off)


FEED_MESSAGES = 64
FEED_CUTS = 4


def feed_body(blocks, *refs):
    (x0, x1, x2, x3, e_own, mid, cot, gain, wd_in) = refs[:9]
    weights = refs[9:14]
    outs = refs[14:18]
    (dx, own, gx, gy, gd, gain_grad, s_down, s_gu) = refs[18:26]
    (wgu, wd, ex, ey, ed, load, n2, hid, ee, err, scale, stage, c_down, c_gu, a_down, b_down) = refs[26:42]
    (a_gu, b_gu, free, q0, q1, q2, q3, r3, rx, ry, dots, dots_x, dots_y, send, recv) = refs[42:]
    i = pl.program_id(0)
    made = Messages((send, recv))
    block, width = x0.shape
    rows = mid.shape[0]
    half = rows // 2
    units = hid.shape[1]
    tiles = units // width
    scatter = made.block(scatter_messages, q1, q2, q3, r3, rx, ry)
    gather = made.block(gather_messages, own, gx, gy, gd)
    halves = (pl.ds(0, half), pl.ds(half, half))
    small_x = [made.new(dots.at[:, at], dots_x.at[:, at], neighbour_x()) for at in halves]
    small_y = [made.new(dots_x.at[:, at], dots_y.at[:, at], neighbour_y()) for at in halves]
    gu_core = [made.new(stage, c_gu, neighbour_core()) for n in (0, 1)]
    down_core = [
        made.new(
            stage.at[:, pl.ds(n * 2 * width, 2 * width)], c_down.at[pl.ds(n * width, width), :], neighbour_core()
        )
        for n in range(tiles)
    ]
    part_d = units // 2
    pieces = [
        [r.at[pl.ds(n * part_d, part_d), pl.ds(lane, width)] for r in (s_down, a_down, b_down)]
        for lane in (width, 0)
        for n in range(2)
    ]
    cut = width // 8
    for n in range(FEED_CUTS):
        at = pl.ds(n * cut, cut)
        pieces.append([s_gu.at[pl.ds(width + n * cut, cut), :], a_gu.at[at, :], b_gu.at[at, :]])
    total = SeqSum(pieces, (send, recv), made.used)
    made.used += 2 * len(pieces)

    gather_e = made.block(gather_messages, e_own, ex, ey, ed)
    load_d = pltpu.make_async_copy(wd_in, wd, load.at[10])
    load_cot = pltpu.make_async_copy(cot, dx, load.at[11])
    second = blocks + tiles
    third = second + blocks

    @pl.when(i == 0)
    def _():
        copies = load_rows(*weights, wgu, load)
        load_d.start()
        load_cot.start()
        greet_all(
            (neighbour_x(), neighbour_y(), neighbour_core(), neighbour_end(), neighbour_middle())
        )
        for m in gather_e[:4]:
            m.start()
        for c in copies:
            c.wait()
        load_d.wait()

    @pl.when(i < blocks)
    def _():
        at = pl.ds(pl.multiple_of(i * block, block), block)
        parts = [r[...].astype(F32) for r in (x0, x1, x2, x3)]
        total = sum(jnp.sum(p * p, axis=1, keepdims=True) for p in parts)
        s = lax.rsqrt(total / D + EPSILON)
        scale[at, :] = s
        normed = [p * s * gain[1:2, j * width : (j + 1) * width] for j, p in enumerate(parts)]
        acc = None
        for j, n in enumerate(normed):
            term = dot_nn(n.astype(BF), wgu[j * width : (j + 1) * width, :])
            acc = term if acc is None else acc + term
        for j in (0, 1):
            k, p = pair_up(normed[2 * j], normed[2 * j + 1])
            n2[at, j * width : (j + 1) * width] = k.astype(BF)
            n2[at, (j + 2) * width : (j + 3) * width] = p.astype(BF)
        pre, up = acc[:, :units], acc[:, units:]
        err[at, :units] = pre.astype(BF)
        err[at, units:] = up.astype(BF)
        h = (gelu_pair(pre)[0] * up).astype(BF)
        hid[at, :] = h
        for j, q in enumerate(outs):
            q[...] = dot_nn(h, wd[:, j * width : (j + 1) * width]).astype(q.dtype)

    @pl.when(i == blocks - 2)
    def _():
        gather_e[0].wait_recv()
        gather_e[4].start()

    @pl.when(i == blocks - 1)
    def _():
        gather_e[3].wait_recv()
        gather_e[5].start()

    @pl.when(i == blocks)
    def _():
        for n in (1, 2, 4, 5):
            gather_e[n].wait_recv()
        step = 128

        def one(n, carry):
            at = pl.ds(pl.multiple_of(n * step, step), step)
            wide = [r[at, :].astype(F32) for r in (e_own, ex, ey, ed)]
            for j in (0, 1):
                k, p = pair_up(wide[2 * j], wide[2 * j + 1])
                ee[at, j * width : (j + 1) * width] = k.astype(BF)
                ee[at, (j + 2) * width : (j + 3) * width] = p.astype(BF)
            return carry

        lax.fori_loop(0, rows // step, one, 0)

    @pl.when((i >= second) & (i < third))
    def _():
        at = pl.ds(pl.multiple_of((i - second) * block, block), block)
        pre, up = err[at, :units].astype(F32), err[at, units:].astype(F32)
        act, slope = gelu_pair(pre)
        dh = None
        for j, r in enumerate((e_own, ex, ey, ed)):
            term = dot_nt(r[at, :], wd[:, j * width : (j + 1) * width])
            dh = term if dh is None else dh + term
        g = (dh * up * slope).astype(BF)
        b = (dh * act).astype(BF)
        err[at, :units] = g
        err[at, units:] = b
        dots[:, at] = row_sums(g.astype(F32) * pre + b.astype(F32) * up)
        for j, q in ((3, q3), (1, q1), (2, q2), (0, q0)):
            rows_w = slice(j * width, (j + 1) * width)
            q[at, :] = (dot_nt(g, wgu[rows_w, :units]) + dot_nt(b, wgu[rows_w, units:])).astype(q.dtype)

    def hand_dots(n):
        small_x[n].wait_recv()
        dots_x[:, halves[n]] = dots_x[:, halves[n]] + dots[:, halves[n]]
        small_y[n].start()

    own_gain = gain[1:2, :width]

    def finish(start, first):
        scatter[first].wait_recv()
        scatter[first + 1].wait_recv()
        return norm_back_rows(
            start, half, q0, rx, ry, dots_x, dots_y, scale, mid, own_gain, dx, dx, own
        )

    @pl.when(i == second + blocks // 2 - 1)
    def _():
        scatter[0].start()
        scatter[2].start()
        small_x[0].start()

    @pl.when(i == third - 2)
    def _():
        scatter[0].wait_recv()
        add_into(q2, r3, 0, half)
        scatter[3].start()
        hand_dots(0)

    @pl.when(i == third - 1)
    def _():
        scatter[1].start()
        small_x[1].start()
        scatter[4].start()
        load_cot.wait()
        small_y[0].wait_recv()
        gain_grad[0:1, :] = finish(0, 2)
        gather[0].start()
        gather[1].start()

    @pl.when((i >= blocks) & (i < blocks + tiles))
    def _():
        k = i - blocks
        at = pl.ds(pl.multiple_of(k * width, width), width)
        g = dot_tn(hid[:, at], ee[...])
        stage[:, pl.ds(pl.multiple_of(k * 2 * width, 2 * width), 2 * width)] = g[:, 2 * width :].astype(BF)
        s_down[at, :] = g[:, : 2 * width].astype(BF)

    for n in range(tiles):

        @pl.when(i == blocks + n)
        def _():
            down_core[n].start()

    @pl.when(i == second)
    def _():
        for n in range(tiles):
            down_core[n].wait_recv()
            down_core[n].wait_send()
        plus_in(s_down, c_down)
        for n in range(3):
            total.begin(n)

    for n in (0, 1):

        @pl.when(i == third + 1 + 2 * n)
        def _():
            gu_core[n].wait_send()

    @pl.when((i >= third) & (i < third + 4))
    def _():
        k = i - third
        n = jnp.where(k < 2, 3 - 2 * k, 6 - 2 * k)
        at = pl.ds(pl.multiple_of(n * width, width), width)
        stage[...] = dot_tn(n2[:, at], err[...]).astype(BF)

    for n in (0, 1):

        @pl.when(i == third + 2 * n)
        def _():
            if n:
                pl.semaphore_wait(free, 1)
            gu_core[n].start()

        @pl.when(i == third + 2 * n + 1)
        def _():
            gu_core[n].wait_recv()
            target = s_gu.at[pl.ds((1 - n) * width, width), :]
            put_sum(target, stage, c_gu)
            if not n:
                pl.semaphore_signal(free, inc=1, device_id=neighbour_core(), device_id_type=MESH_ID)

    @pl.when(i == third + 1)
    def _():
        for n in range(4, len(pieces)):
            total.begin(n)

    ticks = [second + 1, second + 3] + [third + 1 + n for n in range(len(pieces))]
    for t, where in enumerate(ticks):

        @pl.when(i == where)
        def _():
            if t + 3 < 4:
                total.begin(t + 3)
            if t < len(pieces):
                total.relay(t)
            if 0 <= t - 1 < len(pieces):
                total.settle(t - 1)
            if t >= 2:
                total.finish(t - 2)

    @pl.when(i == third)
    def _():
        scatter[1].wait_recv()
        add_into(q1, r3, half, half)
        scatter[5].start()
        hand_dots(1)

    @pl.when(i == third + 2)
    def _():
        small_y[1].wait_recv()
        gain_grad[0:1, :] = gain_grad[0:1, :] + finish(half, 4)
        gather[2].start()
        gather[3].start()
        gather[0].wait_recv()
        gather[4].start()

    @pl.when(i == third + 4)
    def _():
        gather[3].wait_recv()
        gather[5].start()

    @pl.when(i == third + 2 + len(pieces))
    def _():
        for n in (1, 2, 4, 5):
            gather[n].wait_recv()
        for m in scatter + gather + gather_e + small_x + small_y:
            m.wait_send()


def feed(chunks, err_own, mid, cot, gain, wd, weights):
    rows, width = chunks[0].shape
    units = wd.shape[0]
    block = ROW_BLOCK
    blocks = rows // block
    tiles = units // width
    held = functools.partial(held_spec, block, last=blocks - 1)
    chunk = pltpu.VMEM((rows, width), BF)
    lanes = pltpu.VMEM((8, rows), F32)
    landing = pltpu.VMEM((units, 2 * width), BF)
    return pl.pallas_call(
        functools.partial(feed_body, blocks),
        grid=(2 * blocks + tiles + 7 + FEED_CUTS,),
        in_specs=[held(width)] * 4
        + [whole_spec(err_own.shape), whole_spec(mid.shape), any_spec(), whole_spec(gain.shape)]
        + [any_spec()] * 6,
        out_specs=[held(width)] * 4
        + [whole_spec((rows, width))] * 2
        + [any_spec()] * 3
        + [whole_spec((8, width)), whole_spec((units, 2 * width)), whole_spec((2 * width, 2 * units))],
        out_shape=[sds((rows, width), F32)]
        + [sds((rows, width), BF)] * 3
        + [sds((rows, width), F32)]
        + [sds((rows, width), BF)] * 4
        + [sds((8, width), F32), sds((units, 2 * width), BF), sds((2 * width, 2 * units), BF)],
        scratch_shapes=[
            pltpu.VMEM((4 * width, 2 * units), BF),
            pltpu.VMEM(wd.shape, BF),
            chunk,
            chunk,
            chunk,
            pltpu.SemaphoreType.DMA((12,)),
            pltpu.VMEM((rows, 4 * width), BF),
            pltpu.VMEM((rows, units), BF),
            pltpu.VMEM((rows, 4 * width), BF),
            pltpu.VMEM((rows, 2 * units), BF),
            pltpu.VMEM((rows, 1), F32),
            pltpu.VMEM((width, 2 * units), BF),
            landing,
            pltpu.VMEM((width, 2 * units), BF),
            landing,
            landing,
            pltpu.VMEM((FEED_CUTS * width // 8, 2 * units), BF),
            pltpu.VMEM((FEED_CUTS * width // 8, 2 * units), BF),
            pltpu.SemaphoreType.REGULAR,
            pltpu.VMEM((rows, width), F32),
        ]
        + [chunk] * 6
        + [lanes] * 3
        + [pltpu.SemaphoreType.DMA((FEED_MESSAGES,))] * 2,
        compiler_params=comm_params(3),
        cost_estimate=cost(48 * rows * wd.size, 3 * nbytes(wd) + rows * 30000, rows * units),
        name="feed",
    )(*chunks, err_own, mid, cot, gain, wd, *weights)


def back_body(heads, blocks, count, *refs):
    errs = refs[0:4]
    (w_out, states, branch, recall, conv, admit, u_head, off, soft) = refs[4:13]
    (taps, recall_w, admit_w, border, earlier, u, v, w_hbm, scale, x_hbm, dx_hbm, gain) = refs[13:25]
    (sum_gu, sum_down, mixed) = refs[25:28]
    (euv, grad, gain_grad, grad_small) = refs[28:32]
    (mine_gu, far_gu, far_down, mine_out, far_out, gates) = refs[32:38]
    (w, x, dx, paired, part, reach, ext, st, uext, dc, ends, later, edge, from_later, load) = refs[38:53]
    (q0, q1, q2, q3, r3, rx, ry, dots, dots_x, dots_y) = refs[53:63]
    (s_gu, a_gu, b_gu, s_out, p_out, c_out, a_out, b_out) = refs[63:71]
    (s_gt, p_gt, c_gt, a_gt, b_gt, store, send, recv) = refs[71:]
    i = pl.program_id(0)
    sems = (send, recv)
    seq = lax.axis_index("seq")
    rows, width = x.shape
    half = rows // 2
    step = ROW_BLOCK
    seg = rows // 8
    channels = heads * 128
    block = step

    scatter = scatter_messages(q1, q2, q3, r3, rx, ry, sems, 0)
    small_x = message(dots, dots_x, neighbour_x(), sems, 6)
    small_y = message(dots_x, dots_y, neighbour_y(), sems, 7)
    hand_on = [message(ends, later.at[n - 1], {"seq": seq - n}, sems, 7 + n) for n in range(1, count + 1)]
    base = 8 + count
    hand_edge = message(edge, from_later, {"seq": seq - 1}, sems, base)
    base += 1

    cut, rows_out = width // 8, channels
    y = lax.div(lax.axis_index("col"), 2)
    to_side, to_core = neighbour_y(), neighbour_core()
    size = heads * 128
    pieces, to_y, to_out, stores = [], {}, {}, []

    def store_copy(src, dst):
        stores.append(pltpu.make_async_copy(src, dst, store.at[len(stores)]))
        return stores[-1]

    made = Messages(sems)
    made.used = base
    done = FEED_CUTS * cut
    early_y = [
        made.new(sum_down.at[:, pl.ds(width, width)], far_down, to_side),
        made.new(sum_gu.at[pl.ds(width, done), :], far_gu.at[pl.ds(0, done), :], to_side),
    ]
    for start, rows_gu in ((12, 1), (13, 2), (15, 1), (0, 2), (2, 2), (4, 2), (6, 2)):
        p = len(pieces)
        at = pl.ds(start * cut, rows_gu * cut)
        pieces.append([r.at[at, :] for r in (s_gu, a_gu, b_gu)])
        if start >= 8:
            target = far_gu.at[pl.ds((start - 8) * cut, rows_gu * cut), :]
            to_y[p] = [made.new(pieces[p][0], target, to_side)]
        else:
            to_out[p] = [store_copy(pieces[p][0], mine_gu.at[at, :])]
    for lane in (width, 0):
        for n in (0,):
            p = len(pieces)
            at = pl.ds(n * rows_out, rows_out)
            pieces.append([r.at[at, pl.ds(lane, width)] for r in (s_out, a_out, b_out)])
            if lane:
                to_y[p] = [made.new(pieces[p][0], far_out.at[at, :], to_side)]
            else:
                to_out[p] = [store_copy(pieces[p][0], mine_out.at[at, :])]
    p = len(pieces)
    pieces.append([s_gt, a_gt, b_gt])
    to_y[p], to_out[p] = [], []
    for n in (0, 1):
        source = s_gt.at[pl.ds(n * size, size), :]
        target = gates.at[pl.ds(pl.multiple_of((2 * n + y) * size, size), size), :]
        to_y[p].append(made.new(source, target, to_side))
        to_out[p].append(store_copy(source, target))
    total = SeqSum(pieces, sems, made.used)
    made.used += 2 * len(pieces)
    core_out, core_gt = made.new(p_out, c_out, to_core), made.new(p_gt, c_gt, to_core)
    load_gu = pltpu.make_async_copy(sum_gu, s_gu, load.at[0])
    loads = [
        pltpu.make_async_copy(source, target, load.at[n + 1])
        for n, (source, target) in enumerate(((w_hbm, w), (x_hbm, x), (dx_hbm, dx)))
    ]

    def tick(t):
        if t + 3 < len(pieces):
            total.begin(t + 3)
        if t < len(pieces):
            total.relay(t)
        if 0 <= t - 1 < len(pieces):
            total.settle(t - 1)
        if 0 <= t - 2 < len(pieces):
            total.finish(t - 2)
            for m in to_y.get(t - 2, []) + to_out.get(t - 2, []):
                m.start()

    @pl.when(i == 0)
    def _():
        load_gu.start()
        later[...] = jnp.zeros_like(later)
        from_later[...] = jnp.zeros_like(from_later)
        greet_all(
            [neighbour_x(), neighbour_y(), neighbour_core()]
            + [{"seq": lax.rem(seq + n, count + 1)} for n in range(1, count + 1)]
        )
        load_gu.wait()
        for n in range(3):
            total.begin(n)
        for c in loads:
            c.start()
        for m in early_y:
            m.start()
        for r in range(0, rows, step):
            at = slice(r, r + step)
            for j in (0, 1):
                k, p = pair_up(errs[2 * j][at, :].astype(F32), errs[2 * j + 1][at, :].astype(F32))
                paired[at, j * width : (j + 1) * width] = k.astype(BF)
                paired[at, (j + 2) * width : (j + 3) * width] = p.astype(BF)

    @pl.when(i == 3)
    def _():
        core_out.wait_recv()
        plus_in(s_out, c_out)

    @pl.when(i == 2 * heads + 1)
    def _():
        core_gt.wait_recv()
        put_in(s_gt, p_gt)
        plus_in(s_gt, c_gt)

    for t in range(len(pieces) + 2):

        @pl.when(i == (1 if t == 0 else 2 * t if t <= heads + 1 else t + heads + 2))
        def _():
            tick(t)

    @pl.when(i == 1)
    def _():
        g = dot_tn(mixed[...], paired[...])
        p_out[...] = g[:, 2 * width :].astype(BF)
        core_out.start()
        s_out[...] = g[:, : 2 * width].astype(BF)

    @pl.when(i < heads)
    def _():
        sp = soft[0:1, :]
        part_h, reach_h = part.at[i], reach.at[i]
        lane = pl.ds(pl.multiple_of(channels + i * 128, 128), 128)
        for r in range(0, rows, step):
            at = slice(r, r + step)
            o = off[8 + r : 8 + r + step, :]
            ext[at, :] = jnp.where(o > 0, jnp.exp(-8.0 * recall[at, :] * sp), 0.0)
            dm = None
            for j in range(4):
                term = dot_nt(errs[j][at, :], w_out[:, j * width : (j + 1) * width])
                dm = term if dm is None else dm + term
            act, slope = gelu_pair(branch[at, :])
            euv[at, lane] = (dm * states[at, :] * slope).astype(BF)
            part_h[at, :] = dm * act
        ext[rows : rows + 8, :] = jnp.ones((8, 128), F32)
        for r in range(0, rows, step):
            reach_h[r : r + step, :] = ext[r + 1 : r + 1 + step, :]

        def one(n, carry):
            h, p = carry
            at = pl.ds(seg - 1 - n, 8, stride=seg)
            d = reach_h[at, :]
            h = d * h + part_h[at, :]
            p = d * p
            part_h[at, :] = h
            reach_h[at, :] = p
            return h, p

        zero = jnp.zeros((8, 128), F32)
        h, p = lax.fori_loop(0, seg, one, (zero, zero + 1.0), unroll=8)
        carry_h, carry_p = h[7:8, :], p[7:8, :]
        for s in range(6, -1, -1):
            at = slice(s * seg, (s + 1) * seg)
            c = reach_h[at, :]
            part_h[at, :] = part_h[at, :] + c * carry_h
            reach_h[at, :] = c * carry_p
            carry_h = h[s : s + 1, :] + p[s : s + 1, :] * carry_h
            carry_p = p[s : s + 1, :] * carry_p
        first = ext[0:1, :]
        ends[i, 0:1, :] = first * carry_p
        ends[i, 1:2, :] = first * carry_h
        ends[i, 2:8, :] = jnp.zeros((6, 128), F32)

    for n in range(1, count + 1):

        @pl.when((i == heads - 1) & (seq >= n))
        def _():
            hand_on[n - 1].start()

        @pl.when((i == heads) & (seq <= count - n))
        def _():
            hand_on[n - 1].wait_recv()

    @pl.when((i >= heads) & (i < 2 * heads))
    def _():
        h = i - heads
        part_h, reach_h = part.at[h], reach.at[h]
        st[0:8, :] = jnp.broadcast_to(chain(earlier, count), (8, 128))
        st[8 : 8 + rows, :] = states[...]
        uext[0:8, :] = border[...]
        uext[8 : 8 + rows, :] = u_head[...]
        incoming = carried(later, h, count)
        sp = soft[0:1, :]
        dc[0:8, :] = jnp.zeros((8, 128), F32)
        dc[8 + rows : 16 + rows, :] = jnp.zeros((8, 128), F32)
        gr = ga = None
        sums = [None] * (KW + 1)

        def plus(total, term):
            return term if total is None else total + term

        for r in range(0, rows, step):
            at = slice(r, r + step)
            o = off[8 + r : 8 + r + step, :]
            adj = part_h[at, :] + reach_h[at, :] * incoming
            rec, adm, cv = recall[at, :], admit[at, :], conv[at, :]
            ell = -8.0 * rec * sp
            e = jnp.exp(ell)
            m = jnp.sqrt(minus_expm1(2.0 * ell))
            previous = jnp.where(o > 0, e * st[7 + r : 7 + r + step, :], 0.0)
            ac = adj * cv
            d_ell = adj * previous - ac * adm * (e * e) / m
            d_rp = -8.0 * sp * d_ell * rec * (1.0 - rec)
            d_ip = ac * m * adm * (1.0 - adm)
            d_conv = (
                adj * m * adm
                + dot_nt(d_rp, recall_w[0], PRECISE)
                + dot_nt(d_ip, admit_w[0], PRECISE)
            )
            dc[8 + r : 8 + r + step, :] = d_conv
            gr = plus(gr, dot_tn(cv, d_rp, PRECISE))
            ga = plus(ga, dot_tn(cv, d_ip, PRECISE))
            for k in range(KW):
                term = d_conv * uext[8 + r - k : 8 + r - k + step, :]
                if k:
                    term = jnp.where(o >= k, term, 0.0)
                sums[k] = plus(sums[k], jnp.sum(term, axis=0, keepdims=True))
            sums[KW] = plus(sums[KW], jnp.sum(rec * d_ell, axis=0, keepdims=True))
        for n, value in enumerate((gr, ga)):
            p_gt[pl.ds(pl.multiple_of(n * size + h * 128, 128), 128), :] = value.astype(BF)
        for k in range(KW + 1):
            grad_small[k : k + 1, :] = sums[k]
        grad_small[KW + 1 : 8, :] = jnp.zeros((7 - KW, 128), F32)
        for r in range(0, rows, step):
            du = taps[0:1, :] * dc[8 + r : 8 + r + step, :]
            for k in range(1, KW):
                o = off[8 + r + k : 8 + r + k + step, :]
                term = taps[k : k + 1, :] * dc[8 + r + k : 8 + r + k + step, :]
                du = du + jnp.where(o >= k, term, 0.0)
            part_h[r : r + step, :] = du
        over = jnp.zeros((8, 128), F32)
        for k in range(1, KW):
            term = taps[k : k + 1, :] * dc[k : k + 8, :]
            over = over + jnp.where(off[k : k + 8, :] >= k, term, 0.0)
        edge[h] = over

    @pl.when((i == 2 * heads - 1) & (seq >= 1))
    def _():
        hand_edge.start()

    @pl.when(i == 2 * heads - 1)
    def _():
        core_gt.start()


    @pl.when((i == 2 * heads) & (seq < count))
    def _():
        hand_edge.wait_recv()

    third = 2 * heads

    @pl.when(i == third)
    def _():
        for c in loads:
            c.wait()

    @pl.when((i >= third) & (i < third + blocks))
    def _():
        at = pl.ds(pl.multiple_of((i - third) * block, block), block)
        d = jnp.concatenate([part[h, at, :] for h in range(heads)], axis=1)
        late = jnp.concatenate([from_later[h] for h in range(heads)], axis=1)
        extra = jnp.concatenate([jnp.zeros((block - 8, channels), F32), late], axis=0)
        d = d + jnp.where(i == third + blocks - 1, extra, 0.0)
        e = d.astype(BF)
        euv[at, :channels] = e
        b = euv[at, channels:]
        dots[:, at] = row_sums(e.astype(F32) * u[...] + b.astype(F32) * v[...])
        for j, q in ((3, q3), (1, q1), (2, q2), (0, q0)):
            rows_w = slice(j * width, (j + 1) * width)
            q[at, :] = (dot_nt(e, w[rows_w, :channels]) + dot_nt(b, w[rows_w, channels:])).astype(q.dtype)

    @pl.when(i == third + blocks // 2 - 1)
    def _():
        scatter[0].start()
        scatter[2].start()

    @pl.when(i == third + blocks - 1)
    def _():
        scatter[1].start()
        small_x.start()
        scatter[0].wait_recv()
        add_into(q2, r3, 0, half)
        scatter[3].start()
        scatter[4].start()

    last = third + blocks

    @pl.when(i == last)
    def _():
        small_x.wait_recv()
        dots_x[...] = dots_x[...] + dots[...]
        small_y.start()
        scatter[1].wait_recv()
        add_into(q1, r3, half, half)
        scatter[5].start()

    def finish(start, first):
        scatter[first].wait_recv()
        scatter[first + 1].wait_recv()
        return norm_back_rows(
            start, half, q0, rx, ry, dots_x, dots_y, scale, x, gain[0:1, :width], dx, grad, None
        )

    @pl.when(i == last + 1)
    def _():
        small_y.wait_recv()
        gain_grad[0:1, :] = finish(0, 2)

    @pl.when(i == last + 2)
    def _():
        gain_grad[0:1, :] = gain_grad[0:1, :] + finish(half, 4)
        for n in range(1, count + 1):

            @pl.when(seq >= n)
            def _():
                hand_on[n - 1].wait_send()

        @pl.when(seq >= 1)
        def _():
            hand_edge.wait_send()


    @pl.when(i == pl.num_programs(0) - 1)
    def _():
        sent_y = [m for group in to_y.values() for m in group] + early_y
        for m in sent_y:
            m.wait_recv()
        for m in scatter + [small_x, small_y, core_out, core_gt] + sent_y:
            m.wait_send()
        for c in stores:
            c.wait()


def back(errs, w_out, states, v, recall, conv, admit, u, off, soft, taps, rw, aw, border, earlier, w, scale, x, dx, gain, sum_gu, sum_down, mixed):
    rows, channels = states.shape
    width = x.shape[1]
    heads = channels // 128
    block = ROW_BLOCK
    blocks = rows // block
    count = earlier.shape[0]
    steps = 2 * heads + blocks + 8

    def both(i):
        return jnp.where(i < heads, i, jnp.clip(i - heads, 0, heads - 1))

    def second(i):
        return jnp.clip(i - heads, 0, heads - 1)

    def on(shape, pick, axis):
        if axis == 0:
            return pl.BlockSpec(shape, lambda i: (pick(i),) + (0,) * (len(shape) - 1))
        return pl.BlockSpec(shape, lambda i: (0, pick(i)))

    def third(i):
        return jnp.clip(i - 2 * heads, 0, blocks - 1)

    def first(i):
        return jnp.minimum(i, heads - 1)

    tall = (rows, 128)
    gate = (1, 128, 128)
    own_gate = on(gate, second, 0)
    chunk = pltpu.VMEM((rows, width), BF)
    lanes = pltpu.VMEM((8, rows), F32)
    gu = pltpu.VMEM(sum_gu.shape, BF)
    pair, gate_sum = pltpu.VMEM((channels, 2 * width), BF), pltpu.VMEM((2 * channels, 128), BF)
    piece = pltpu.VMEM((heads, 8, 128), F32)
    half_gu, half_dn = (sum_gu.shape[0] // 2, sum_gu.shape[1]), (sum_down.shape[0], width)
    half_out = (channels, width)
    count_sems = 88
    return pl.pallas_call(
        functools.partial(back_body, heads, blocks, count),
        grid=(steps,),
        in_specs=[whole_spec((rows, width))] * 4
        + [
            on((128, 4 * width), first, 0),
            on(tall, both, 1),
            on(tall, first, 1),
            on(tall, both, 1),
            on(tall, second, 1),
            on(tall, second, 1),
            on(tall, second, 1),
            whole_spec(off.shape),
            on((1, 128), both, 1),
            on((KW, 128), second, 1),
            own_gate,
            own_gate,
            on((8, 128), second, 1),
            pl.BlockSpec((count, 1, 8, 128), lambda i: (0, second(i), 0, 0)),
            on((block, channels), third, 0),
            on((block, channels), third, 0),
            any_spec(),
            whole_spec(scale.shape),
            any_spec(),
            any_spec(),
            whole_spec(gain.shape),
            any_spec(),
            any_spec(),
            whole_spec(mixed.shape),
        ],
        out_specs=[
            whole_spec((rows, 2 * channels)),
            whole_spec((rows, width)),
            whole_spec((8, width)),
            on((8, 128), second, 1),
        ]
        + [any_spec()] * 6,
        out_shape=[
            sds((rows, 2 * channels), BF),
            sds((rows, width), F32),
            sds((8, width), F32),
            sds((8, channels), F32),
            sds(half_gu, BF),
            sds(half_gu, BF),
            sds(half_dn, BF),
            sds(half_out, BF),
            sds(half_out, BF),
            sds((4 * channels, 128), BF),
        ],
        scratch_shapes=[
            pltpu.VMEM(w.shape, BF),
            pltpu.VMEM((rows, width), F32),
            pltpu.VMEM((rows, width), F32),
            pltpu.VMEM((rows, 4 * width), BF),
        ]
        + [pltpu.VMEM((heads, rows, 128), F32)] * 2
        + [
            pltpu.VMEM((rows + 8, 128), F32),
            pltpu.VMEM((rows + 8, 128), F32),
            pltpu.VMEM((rows + 8, 128), F32),
            pltpu.VMEM((rows + 16, 128), F32),
            piece,
            pltpu.VMEM((count, heads, 8, 128), F32),
            piece,
            piece,
            pltpu.SemaphoreType.DMA((4,)),
            pltpu.VMEM((rows, width), F32),
        ]
        + [chunk] * 6
        + [lanes] * 3
        + [gu] * 3
        + [pair] * 5
        + [gate_sum] * 5
        + [pltpu.SemaphoreType.DMA((12,))]
        + [pltpu.SemaphoreType.DMA((count_sems,))] * 2,
        compiler_params=comm_params(4),
        cost_estimate=cost(64 * rows * w.size, rows * channels * 60, rows * channels * 8),
        name="back",
    )(
        *errs, w_out, states, v, recall, conv, admit, u, off, soft, taps, rw, aw, border, earlier,
        u, v, w, scale, x, dx, gain, sum_gu, sum_down, mixed,
    )


TAIL_MESSAGES = 48


def tail_body(*refs):
    (n1, euv, grad_small, grad_mixer, grad_feed) = refs[:5]
    (p0, p1, p2, p3, mid, grad_chunk) = refs[5:11]
    (mine_in, far_in, tiny_out, out, grad) = refs[11:16]
    (s_in, p_in, c_in, a_in, b_in, s_ty, p_ty, c_ty, a_ty, b_ty) = refs[16:26]
    (q0, md, gc, q1, q2, q3, r3, rx, ry, own_a, other_a, own_b, other_b, load, send, recv) = refs[26:]
    made = Messages((send, recv))
    col = lax.axis_index("col")
    core = lax.rem(col, 2)
    to_core, to_y = neighbour_core(), neighbour_y()
    rows, width = p0.shape
    part = width // 2
    half_tokens = rows // 2
    copies = []

    def copy(src, dst):
        copies.append(pltpu.make_async_copy(src, dst, load.at[len(copies)]))
        return copies[-1]

    outs_in = [copy(p3, q3), copy(p1, q1), copy(p2, q2)]
    late = [copy(p0, q0), copy(mid, md), copy(grad_chunk, gc)]
    scatter = made.block(scatter_messages, q1, q2, q3, r3, rx, ry)
    cut = width // 4
    order = [pl.ds(n * cut, cut) for n in (4, 5, 6, 7, 0, 1, 2, 3)]
    pieces = [[s_ty, a_ty, b_ty]] + [[r.at[at, :] for r in (s_in, a_in, b_in)] for at in order]
    count = len(pieces)
    total = SeqSum(pieces, (send, recv), made.used)
    made.used += 2 * count
    core_ty = made.new(p_ty, c_ty, to_core)
    far_rows, own_rows = pl.ds(width, width), pl.ds(0, width)
    core_in = [made.new(p_in.at[at, :], c_in.at[at, :], to_core) for at in (far_rows, own_rows)]
    over_y = {
        n + 1: made.new(s_in.at[order[n], :], far_in.at[pl.ds(n * cut, cut), :], to_y) for n in range(4)
    }
    send_out, send_grad = made.new(other_a, out.at[core], to_core), made.new(other_b, grad.at[core], to_core)
    keep_out, keep_grad = copy(own_a, out.at[core]), copy(own_b, grad.at[core])
    keep_in = {n + 1: copy(s_in.at[order[n], :], mine_in.at[pl.ds((n - 4) * cut, cut), :]) for n in range(4, 8)}

    for m in outs_in:
        m.start()
    greet_all((neighbour_x(), to_y, to_core, neighbour_end(), neighbour_middle()))
    p_ty[...] = jnp.zeros_like(p_ty)
    p_ty[0:8, :] = grad_small[...]
    for n, source in enumerate((grad_mixer, grad_feed)):
        g = jnp.broadcast_to(source[0:1, :], (8, width))
        g = jnp.where(core == 0, g, pltpu.roll(g, part, 1))
        p_ty[8 + n : 9 + n, 0:width] = g[0:1, :]
    core_ty.start()

    def tile(n, target, row):
        sub = width // 3

        def one(k, carry):
            at = pl.ds(pl.multiple_of(n * width + k * sub, sub), sub)
            where = pl.ds(pl.multiple_of(row + k * sub, sub), sub)
            target[where, :] = dot_tn(n1[:, at], euv[...]).astype(BF)
            return carry

        lax.fori_loop(0, 3, one, 0)

    def gather_core(n, at):
        core_in[n].wait_recv()
        plus_in(s_in.at[at, :], c_in.at[at, :])

    tile(3, p_in, width)
    core_in[0].start()
    for m in outs_in:
        m.wait()
    for m in late:
        m.start()
    for m in scatter[:3]:
        m.start()
    tile(1, s_in, width)
    core_ty.wait_recv()
    s_ty[...] = p_ty[...] + c_ty[...]
    total.begin(0)
    gather_core(0, far_rows)
    for n in range(1, 5):
        total.begin(n)
    tile(2, p_in, 0)
    core_in[1].start()
    total.relay(0)
    total.relay(1)
    total.settle(0)
    tile(0, s_in, 0)
    gather_core(1, own_rows)
    for n in range(5, count):
        total.begin(n)

    def chunk_out(value, own, other, at):
        turned = value.T
        own[:, at] = turned[:part]
        other[:, at] = turned[part:]

    def in_steps(start, size, body):
        def one(n, carry):
            body(pl.ds(pl.multiple_of(start + n * 128, 128), 128))
            return carry

        lax.fori_loop(0, size // 128, one, 0)

    def finish_out(start, first):
        scatter[first].wait_recv()
        scatter[first + 1].wait_recv()

        def body(at):
            value = q0[at, :] + rx[at, :].astype(F32) + ry[at, :].astype(F32) + md[at, :]
            chunk_out(value, own_a, other_a, at)

        in_steps(start, half_tokens, body)

    for n in range(2, count + 2):
        if n < count:
            total.relay(n)
        if n - 1 < count:
            total.settle(n - 1)
        total.finish(n - 2)
        if n - 2 in over_y:
            over_y[n - 2].start()
        if n - 2 in keep_in:
            keep_in[n - 2].start()
        if n == 2:
            scatter[0].wait_recv()
            add_into(q2, r3, 0, half_tokens)
            scatter[3].start()
            scatter[4].start()
        if n == 3:
            scatter[1].wait_recv()
            add_into(q1, r3, half_tokens, half_tokens)
            scatter[5].start()
            for m in late:
                m.wait()
            in_steps(0, rows, lambda at: chunk_out(gc[at, :], own_b, other_b, at))
            send_grad.start()
            keep_grad.start()
        if n == 7:
            finish_out(0, 2)
        if n == 8:
            finish_out(half_tokens, 4)
            send_out.start()
            keep_out.start()
    put_in(tiny_out, s_ty)
    received = list(over_y.values()) + [send_out, send_grad]
    for m in received:
        m.wait_recv()
    for m in [core_ty] + core_in + received + scatter:
        m.wait_send()
    for c in [keep_out, keep_grad] + list(keep_in.values()):
        c.wait()


def tail(n1, euv, grad_small, grad_mixer, grad_feed, parts, mid, grad_chunk):
    rows, channels = euv.shape[0], euv.shape[1] // 2
    width = mid.shape[1]
    part = width // 2
    big = pltpu.VMEM((2 * width, 2 * channels), BF)
    tiny = pltpu.VMEM((16, channels), F32)
    piece = pltpu.VMEM((rows, width), BF)
    full = pltpu.VMEM((rows, width), F32)
    side = pltpu.VMEM((part, rows), F32)
    quarter_in = (width, 2 * channels)
    final = sds((2, part, rows), F32)
    return pl.pallas_call(
        tail_body,
        in_specs=[pl.BlockSpec(memory_space=pltpu.VMEM)] * 5 + [any_spec()] * 6,
        out_specs=[any_spec()] * 2 + [pl.BlockSpec(memory_space=pltpu.VMEM)] + [any_spec()] * 2,
        out_shape=[sds(quarter_in, BF)] * 2 + [sds((16, channels), F32), final, final],
        scratch_shapes=[big] * 5
        + [tiny] * 5
        + [full] * 3
        + [piece] * 6
        + [side] * 4
        + [pltpu.SemaphoreType.DMA((12,))]
        + [pltpu.SemaphoreType.DMA((TAIL_MESSAGES,))] * 2,
        compiler_params=pltpu.CompilerParams(
            vmem_limit_bytes=VMEM_LIMIT, collective_id=6, has_side_effects=True
        ),
        cost_estimate=cost(60 * rows * width * channels * 4, nbytes(n1, euv)),
        name="tail",
    )(n1, euv, grad_small, grad_mixer, grad_feed, *parts, mid, grad_chunk)


def arrange_body(place, mine_gu, far_gu, mine_dn, far_dn, mine_in, far_in, mine_out, far_out, *outs):
    gate, up, down, inp, branch, out = outs
    row, y = place[0], place[1]
    first = pl.program_id(0) == 0

    def side_by_side(mine, far, left, right):
        lanes = left.shape[1] // 2
        for target, at in ((left, 0), (right, mine.shape[1] // 2)):
            m = mine[:, at : at + lanes].astype(F32)
            t = far[:, at : at + lanes].astype(F32)
            target[:, :lanes] = jnp.where(y == 0, m, t)
            target[:, lanes:] = jnp.where(y == 0, t, m)

    def stack_up(mine, far, target):
        value = jnp.where(first, mine[...].astype(F32), far[...].astype(F32))
        target[...] = jnp.where(row == 0, value, pltpu.roll(value, value.shape[1] // 2, 1))

    side_by_side(mine_gu, far_gu, gate, up)
    side_by_side(mine_in, far_in, inp, branch)
    stack_up(mine_dn, far_dn, down)
    stack_up(mine_out, far_out, out)


def arrange(place, mine_gu, far_gu, mine_dn, far_dn, mine_in, far_in, mine_out, far_out):
    width, units = far_dn.shape[1], far_dn.shape[0]
    inner = mine_out.shape[0]
    lanes_gu, lanes_in = mine_gu.shape[1], mine_in.shape[1]
    cuts = 2
    piece = width // (2 * cuts)

    def rows_in(i, j, place):
        return (cuts * i + j, 0)

    def rows_to(i, j, place):
        return (cuts * (i + place[0] - 2 * i * place[0]) + j, 0)

    def near(i, j, place):
        return (jnp.where(i == 0, j, cuts - 1), 0)

    def far(i, j, place):
        return (jnp.where(i == 0, 0, j), 0)

    def stack_to(i, j, place):
        return (cuts * (i + place[1] - 2 * i * place[1]) + j, 0)

    def spec(rows, lanes, at):
        return pl.BlockSpec((rows, lanes), at)

    shapes = [(width, lanes_gu)] * 2 + [(2 * units, width)] + [(width, lanes_in)] * 2 + [(2 * inner, width)]
    return pl.pallas_call(
        arrange_body,
        grid_spec=pltpu.PrefetchScalarGridSpec(
            num_scalar_prefetch=1,
            grid=(2, cuts),
            in_specs=[
                spec(piece, lanes_gu, rows_in),
                spec(piece, lanes_gu, rows_in),
                spec(units // cuts, width, near),
                spec(units // cuts, width, far),
                spec(piece, lanes_in, rows_in),
                spec(piece, lanes_in, rows_in),
                spec(inner // cuts, width, near),
                spec(inner // cuts, width, far),
            ],
            out_specs=[spec(piece, lanes_gu, rows_to)] * 2
            + [spec(units // cuts, width, stack_to)]
            + [spec(piece, lanes_in, rows_to)] * 2
            + [spec(inner // cuts, width, stack_to)],
        ),
        out_shape=[sds(s, F32) for s in shapes],
        compiler_params=pltpu.CompilerParams(vmem_limit_bytes=VMEM_LIMIT),
        cost_estimate=cost(1000000, 24000000),
        name="arrange",
    )(place, mine_gu, far_gu, mine_dn, far_dn, mine_in, far_in, mine_out, far_out)


def local_fast(
    stream_in,
    cotangent,
    doc_lengths,
    mixer_gain,
    input_weight,
    branch_weight,
    filter_taps,
    recall_gate,
    admit_gate,
    decay_param,
    output_weight,
    feed_gain,
    gate_weight,
    up_weight,
    down_weight,
):
    tokens = stream_in.shape[1]
    count = lax.axis_size("seq")
    part = stream_in.shape[2]
    seq = lax.axis_index("seq")
    row = lax.axis_index("row")
    col = lax.axis_index("col")
    y, core = col // 2, col % 2
    heads = recall_gate.shape[0] // 2
    rw = lax.dynamic_slice_in_dim(recall_gate, y * heads, heads, 0)
    aw = lax.dynamic_slice_in_dim(admit_gate, y * heads, heads, 0)
    soft_own = jax.nn.softplus(-decay_param)[None]
    small = jnp.concatenate(
        [filter_taps, soft_own, decay_param[None], jnp.zeros((2,) + decay_param.shape, F32)]
    )
    gains = jnp.concatenate([mixer_gain[None], feed_gain[None], jnp.zeros((6, part), F32)])

    lengths = lax.dynamic_index_in_dim(doc_lengths, core, 0, False)
    offset = doc_offset(lengths, seq * tokens, tokens)
    edge = jnp.full((8,), -1, jnp.int32)
    off = jnp.concatenate([edge, offset, edge])[:, None]

    (
        g_low, w_down, gains_all, small, s1, border, earlier, mid, mid_low,
        n1, conv, recall, admit, states, mixed, mx, my, md, far_w, sib_own, sib_far, w_in,
        x, g, w_out, u, v,
    ) = front(
        jnp.swapaxes(stream_in, 1, 2), jnp.swapaxes(cotangent, 1, 2), input_weight, branch_weight, output_weight, gate_weight, up_weight, down_weight,
        gains, small, recall_gate, admit_gate, off, count - 1,
    )
    taps, soft, decay = small[:KW], small[KW : KW + 1], small[KW + 1 : KW + 2]
    p0, p1, p2, p3, dx2, *dx_all, grad_feed, sum_down, sum_gu = feed(
        (mid_low, mx, my, md), g_low, mid, g, gains_all, w_down,
        (gate_weight, up_weight, sib_own, far_w, sib_far),
    )
    (
        euv, grad_chunk, grad_mixer, grad_small, mine_gu, far_gu, far_down, mine_out, far_out, gates
    ) = back(
        dx_all, w_out, states, v, recall, conv, admit, u, off, soft, taps, rw, aw, border, earlier,
        w_in, s1, x, dx2, gains_all, sum_gu, sum_down, mixed,
    )
    mine_in, far_in, tiny, out, grad = tail(
        n1, euv, grad_small, grad_mixer, grad_feed, (p0, p1, p2, p3), mid, grad_chunk
    )
    place = jnp.stack([row, y]).astype(jnp.int32)
    grad_gate, grad_up, grad_down, grad_input, grad_branch, grad_output = arrange(
        place, mine_gu, far_gu, sum_down, far_down, mine_in, far_in, mine_out, far_out
    )
    gates = gates.astype(F32).reshape((2,) + recall_gate.shape)
    own = taps.shape[1] // 2
    mine = lax.dynamic_slice_in_dim(tiny[:8], core * own, own, 1)
    gain_grads = lax.dynamic_slice_in_dim(tiny[8:10, : 2 * part], core * part, part, 1)
    return (
        jnp.swapaxes(out, 1, 2),
        jnp.swapaxes(grad, 1, 2),
        gain_grads[0],
        grad_input,
        grad_branch,
        mine[:KW],
        gates[0],
        gates[1],
        mine[KW] * 8.0 * jax.nn.sigmoid(-decay_param),
        grad_output,
        gain_grads[1],
        grad_gate,
        grad_up,
        grad_down,
    )


def solution(mesh):
    in_specs = (
        P(None, "seq", ("col", "row")),
        P(None, "seq", ("col", "row")),
        P(),
        P(("col", "row")),
        P("col", "row"),
        P("col", "row"),
        P(None, ("row", "col")),
        P("row", None, None),
        P("row", None, None),
        P(("row", "col")),
        P("row", "col"),
        P(("col", "row")),
        P("col", "row"),
        P("col", "row"),
        P("row", "col"),
    )
    out_specs = (
        P(None, "seq", ("col", "row")),
        P(None, "seq", ("col", "row")),
        P(("col", "row")),
        P("col", "row"),
        P("col", "row"),
        P(None, ("row", "col")),
        P("row", None, None),
        P("row", None, None),
        P(("row", "col")),
        P("row", "col"),
        P(("col", "row")),
        P("col", "row"),
        P("col", "row"),
        P("row", "col"),
    )
    plan = local_fast if dict(mesh.shape) == {"seq": 4, "row": 2, "col": 4} else local
    return jax.shard_map(plan, mesh=mesh, in_specs=in_specs, out_specs=out_specs, check_vma=False)
```

```python
import functools

import jax
import jax.numpy as jnp
from jax import lax
from jax.experimental import pallas as pl
from jax.experimental.pallas import tpu as pltpu
from jax.sharding import PartitionSpec as P

D = 1536
KW = 4


EPSILON = 1e-06
PRECISE = lax.Precision.HIGHEST
SUM_ROWS = (((0,), (0,)), ((), ()))
SUM_COLS = (((1,), (1,)), ((), ()))


def as_sent(value):
    return jax.tree.map(lambda a: a.astype(jnp.bfloat16) if a.dtype == jnp.float32 else a, value)


def passed_along(block, axis, distance):
    devices = range(lax.axis_size(axis))
    route = [(i - distance, i) for i in devices if i - distance in devices]
    return lax.ppermute(block, axis, route)


def entering_2(part, axis, combine, identity, reverse):
    count = lax.axis_size(axis)
    place = lax.axis_index(axis)
    ahead = count - 1 - place if reverse else place
    gathered = jax.tree.map(lambda a: lax.all_gather(a, axis), part)
    state = jax.tree.map(lambda a, e: jnp.zeros_like(a) + jnp.asarray(e, a.dtype), part, identity)

    def one(hop, state):
        source = count - 1 - hop if reverse else hop
        return combine(
            state, jax.tree.map(lambda a: lax.dynamic_index_in_dim(a, source, 0, False), gathered)
        )

    return lax.fori_loop(0, ahead, one, state)


def compose(first, second):
    return (first[0] * second[0], second[0] * first[1] + second[1])


def convolve(source, taps, offset, border):
    tokens = source.shape[0]
    extended = jnp.concatenate([border, source], axis=0)
    result = jnp.zeros_like(source)
    for lag_index in range(KW):
        anchor = KW - 1 - lag_index
        valid = (offset >= lag_index).astype(jnp.float32)[:, None]
        result = result + taps[lag_index] * extended[anchor : anchor + tokens] * valid
    return result


def slab_pre(conv_value, recall_value, admit_value):
    tokens = conv_value.shape[0]
    blocks = conv_value.reshape(tokens, recall_value.shape[0], recall_value.shape[1])
    recall_pre = jnp.einsum("thi,hij->thj", blocks, recall_value, precision=PRECISE).reshape(
        tokens, -1
    )
    admit_pre = jnp.einsum("thi,hij->thj", blocks, admit_value, precision=PRECISE).reshape(
        tokens, -1
    )
    return (recall_pre, admit_pre)


def own_terms(conv_value, recall_pre, admit_pre, decay_value, resume):
    recall = jax.nn.sigmoid(recall_pre)
    admit = jax.nn.sigmoid(admit_pre)
    log_decay = -8.0 * recall * jax.nn.softplus(-decay_value)
    decays = jnp.exp(log_decay) * resume[:, None]
    drives = jnp.sqrt(-jnp.expm1(2.0 * log_decay)) * admit * conv_value
    return (decays, drives)


def width_total(partial_value):
    return lax.psum(partial_value, ("row", "col"))


def gather_row(source):
    return lax.all_gather(source, "row", axis=1, tiled=True)


def gather_col(source):
    return jax.tree.map(
        lambda part, own: part.astype(own.dtype),
        lax.all_gather(as_sent(source), "col", axis=1, tiled=True),
        source,
    )


def scatter_col(source):
    return (
        lax.psum_scatter(source[0], "col", scatter_dimension=1, tiled=True),
        lax.psum_scatter(source[1], "col", scatter_dimension=1, tiled=True),
    )


def scatter_col_back(source):
    return lax.psum_scatter(source, "col", scatter_dimension=1, tiled=True)


def scatter_row(source):
    return lax.psum_scatter(source, "row", scatter_dimension=1, tiled=True)


def over_seq(grads):
    return (
        lax.psum(grads[0].astype(jnp.bfloat16), "seq").astype(jnp.float32),
        lax.psum(grads[1].astype(jnp.bfloat16), "seq").astype(jnp.float32),
        lax.psum(grads[2].astype(jnp.bfloat16), "seq").astype(jnp.float32),
        lax.psum(grads[3].astype(jnp.bfloat16), "seq").astype(jnp.float32),
        lax.psum(grads[4].astype(jnp.bfloat16), "seq").astype(jnp.float32),
        lax.psum(grads[5].astype(jnp.bfloat16), "seq").astype(jnp.float32),
        lax.psum(grads[6].astype(jnp.bfloat16), "seq").astype(jnp.float32),
        lax.psum(grads[7].astype(jnp.bfloat16), "seq").astype(jnp.float32),
        lax.psum(grads[8].astype(jnp.bfloat16), "seq").astype(jnp.float32),
        lax.psum(grads[9].astype(jnp.bfloat16), "seq").astype(jnp.float32),
        lax.psum(grads[10].astype(jnp.bfloat16), "seq").astype(jnp.float32),
        lax.psum(grads[11].astype(jnp.bfloat16), "seq").astype(jnp.float32),
    )


def normalize(source, scales):
    factor = lax.rsqrt(width_total(jnp.sum(source * source, axis=1)) / D + EPSILON)
    return (source * factor[:, None] * scales, factor)


def norm_back(source, scales, factor, grad_norm):
    weighted = scales * grad_norm
    summed = width_total(jnp.sum(weighted * source, axis=1))
    grad_source = (
        factor[:, None] * weighted - source * (factor * factor * factor * summed / D)[:, None]
    )
    grad_scales = jnp.sum(grad_norm * source * factor[:, None], axis=0)
    return (grad_source, grad_scales)


def doc_offset(lengths, anchor, tokens):
    starts = jnp.cumsum(lengths, dtype=jnp.int32) - lengths
    places = anchor + jnp.arange(tokens, dtype=jnp.int32)
    begins = jnp.max(jnp.where(starts[None, :] <= places[:, None], starts[None, :], 0), axis=1)
    return places - begins


def matmul_rows(left, right):
    return lax.dot_general(left, right, SUM_ROWS, preferred_element_type=jnp.float32)


def matmul_cols(left, right):
    return lax.dot_general(left, right, SUM_COLS, preferred_element_type=jnp.float32)


def local(
    stream_in,
    cotangent,
    doc_lengths,
    mixer_gain,
    input_weight,
    branch_weight,
    filter_taps,
    recall_gate,
    admit_gate,
    decay_param,
    output_weight,
    feed_gain,
    gate_weight,
    up_weight,
    down_weight,
):
    tokens = stream_in.shape[1]
    anchor = lax.axis_index("seq") * tokens
    channels = decay_param.shape[0]
    col_start = lax.axis_index("col") * channels
    params = (
        mixer_gain,
        input_weight,
        branch_weight,
        filter_taps,
        recall_gate,
        admit_gate,
        decay_param,
        output_weight,
        feed_gain,
        gate_weight,
        up_weight,
        down_weight,
    )
    totals = tuple((jnp.zeros(w.shape, jnp.float32) for w in params))
    identity = (jnp.ones_like(decay_param), jnp.zeros_like(decay_param))
    outputs = []
    grads_in = []
    for micro in range(stream_in.shape[0]):
        offset = doc_offset(doc_lengths[micro], anchor, tokens)
        resume = (offset > 0).astype(jnp.float32)
        source = stream_in[micro]
        normed, factor_one = normalize(source, mixer_gain)
        normed_low = normed.astype(jnp.bfloat16)
        normed_all = gather_row(normed_low)
        rec_in, branch = scatter_col(
            (
                jnp.dot(normed_all, input_weight, preferred_element_type=jnp.float32),
                jnp.dot(normed_all, branch_weight, preferred_element_type=jnp.float32),
            )
        )
        border = passed_along(rec_in[tokens - (KW - 1) :], "seq", 1)
        conv_out = convolve(rec_in, filter_taps, offset, border)
        conv_slab = lax.all_gather(conv_out, "col", axis=1, tiled=True)
        slab_values, slab_pull = jax.vjp(slab_pre, conv_slab, recall_gate, admit_gate)
        recall_pre = lax.dynamic_slice_in_dim(slab_values[0], col_start, channels, 1)
        admit_pre = lax.dynamic_slice_in_dim(slab_values[1], col_start, channels, 1)

        def local_gates(conv_value, recall_value, admit_value, decay_value):
            return own_terms(conv_value, recall_value, admit_value, decay_value, resume)

        (decays, drives), gates_pull = jax.vjp(
            local_gates, conv_out, recall_pre, admit_pre, decay_param
        )
        cum_decay, local_state = lax.associative_scan(compose, (decays, drives), axis=0)
        entering = entering_2((cum_decay[-1], local_state[-1]), "seq", compose, identity, False)[1]
        states = local_state + cum_decay * entering
        branch_act = jax.nn.gelu(branch)
        mixed_all = gather_col((states * branch_act).astype(jnp.bfloat16))
        middle = source + scatter_row(
            jnp.dot(mixed_all, output_weight, preferred_element_type=jnp.float32)
        )
        normed_two, factor_two = normalize(middle, feed_gain)
        normed_two_low = normed_two.astype(jnp.bfloat16)
        normed_two_all = gather_row(normed_two_low)
        gate_pre, up_pre = scatter_col(
            (
                jnp.dot(normed_two_all, gate_weight, preferred_element_type=jnp.float32),
                jnp.dot(normed_two_all, up_weight, preferred_element_type=jnp.float32),
            )
        )
        gate_act = jax.nn.gelu(gate_pre)
        hidden_all = gather_col((gate_act * up_pre).astype(jnp.bfloat16))
        outputs.append(
            middle
            + scatter_row(jnp.dot(hidden_all, down_weight, preferred_element_type=jnp.float32))
        )
        upstream = cotangent[micro]
        upstream_all = gather_row(upstream.astype(jnp.bfloat16))
        grad_down = matmul_rows(hidden_all, upstream_all)
        grad_hidden = scatter_col_back(matmul_cols(upstream_all, down_weight))
        gate_value, gelu_pull = jax.vjp(jax.nn.gelu, gate_pre)
        error_gate = gelu_pull(grad_hidden * up_pre)[0].astype(jnp.bfloat16)
        error_up = (grad_hidden * gate_act).astype(jnp.bfloat16)
        gate_err_all, up_err_all = gather_col((error_gate, error_up))
        grad_gate = matmul_rows(normed_two_all, gate_err_all)
        grad_up = matmul_rows(normed_two_all, up_err_all)
        grad_normed_two = scatter_row(
            matmul_cols(gate_err_all, gate_weight) + matmul_cols(up_err_all, up_weight)
        )
        back_middle, grad_feed = norm_back(middle, feed_gain, factor_two, grad_normed_two)
        grad_middle = upstream + back_middle
        rec_err_all = gather_row(grad_middle.astype(jnp.bfloat16))
        grad_output = matmul_rows(mixed_all, rec_err_all)
        grad_mixed = scatter_col_back(matmul_cols(rec_err_all, output_weight))
        branch_value, branch_pull = jax.vjp(jax.nn.gelu, branch)
        error_branch = branch_pull(grad_mixed * states)[0].astype(jnp.bfloat16)
        direct = grad_mixed * branch_act
        ahead = jnp.concatenate([decays[1:], jnp.ones_like(decays[:1])], axis=0)
        reach, partial_adj = lax.associative_scan(compose, (ahead, direct), axis=0, reverse=True)
        incoming = entering_2(
            (decays[0] * reach[0], decays[0] * partial_adj[0]), "seq", compose, identity, True
        )[1]
        adjoint = partial_adj + reach * incoming
        previous = jnp.concatenate([entering[None, :], states[:-1]], axis=0)
        conv_direct, grad_recall_pre, grad_admit_pre, grad_decay = gates_pull(
            (adjoint * previous, adjoint)
        )
        recall_all, admit_all = (
            lax.all_gather(grad_recall_pre.astype(jnp.bfloat16), "col", axis=1, tiled=True).astype(
                grad_recall_pre.dtype
            ),
            lax.all_gather(grad_admit_pre.astype(jnp.bfloat16), "col", axis=1, tiled=True).astype(
                grad_admit_pre.dtype
            ),
        )
        grad_slab, grad_recall, grad_admit = slab_pull((recall_all, admit_all))
        grad_conv_out = conv_direct + lax.dynamic_slice_in_dim(grad_slab, col_start, channels, 1)

        def local_conv(input_value, taps_value, border_value):
            return convolve(input_value, taps_value, offset, border_value)

        conv_value, conv_pull = jax.vjp(local_conv, rec_in, filter_taps, border)
        grad_rec_in, grad_taps, grad_border = conv_pull(grad_conv_out)
        from_next = passed_along(grad_border, "seq", -1)
        grad_rec_in = grad_rec_in + jnp.pad(from_next, ((tokens - (KW - 1), 0), (0, 0)))
        error_input = grad_rec_in.astype(jnp.bfloat16)
        in_err_all, branch_err_all = gather_col((error_input, error_branch))
        grad_input = matmul_rows(normed_all, in_err_all)
        grad_branch = matmul_rows(normed_all, branch_err_all)
        grad_normed = scatter_row(
            matmul_cols(in_err_all, input_weight) + matmul_cols(branch_err_all, branch_weight)
        )
        back_source, grad_mixer = norm_back(source, mixer_gain, factor_one, grad_normed)
        grads_in.append(grad_middle + back_source)
        local_grads = (
            grad_mixer,
            grad_input,
            grad_branch,
            grad_taps,
            grad_recall,
            grad_admit,
            grad_decay,
            grad_output,
            grad_feed,
            grad_gate,
            grad_up,
            grad_down,
        )
        local_grads = over_seq(local_grads)
        totals = tuple((acc + new for acc, new in zip(totals, local_grads)))
    return (jnp.stack(outputs), jnp.stack(grads_in)) + tuple(totals)


BF = jnp.bfloat16
F32 = jnp.float32
VMEM_LIMIT = 62 * 1024 * 1024
ROW_BLOCK = 256
GELU_A = 0.7978845608028654
GELU_B = 0.044715


def cost(flops, moved, trans=0):
    return pl.CostEstimate(flops=int(flops), bytes_accessed=int(moved), transcendentals=int(trans))


def params():
    return pltpu.CompilerParams(vmem_limit_bytes=VMEM_LIMIT, dimension_semantics=("arbitrary",))


def nbytes(*arrays):
    return sum(a.size * a.dtype.itemsize for a in arrays)


def gelu_pair(v):
    t = jnp.tanh(GELU_A * (v + GELU_B * v * v * v))
    value = 0.5 * v * (1.0 + t)
    slope = 0.5 * (1.0 + t) + 0.5 * v * (1.0 - t * t) * GELU_A * (1.0 + 3.0 * GELU_B * v * v)
    return value, slope


def minus_expm1(x):
    series = 1.0 + x * (1.0 / 7.0)
    for n in (6, 5, 4, 3, 2):
        series = 1.0 + x * (1.0 / n) * series
    return jnp.where(x > -0.3, -x * series, 1.0 - jnp.exp(x))


def pair_up(left, right):
    width = left.shape[1]
    lane = lax.broadcasted_iota(jnp.int32, left.shape, 1)
    low = lane < width // 2
    return (
        jnp.where(low, left, pltpu.roll(right, width // 2, 1)),
        jnp.where(low, pltpu.roll(left, width // 2, 1), right),
    )


def dot_nn(a, b, precision=None):
    return lax.dot_general(
        a, b, (((1,), (0,)), ((), ())), precision=precision, preferred_element_type=F32
    )


def dot_nt(a, b, precision=None):
    return lax.dot_general(
        a, b, (((1,), (1,)), ((), ())), precision=precision, preferred_element_type=F32
    )


def dot_tn(a, b, precision=None):
    return lax.dot_general(
        a, b, (((0,), (0,)), ((), ())), precision=precision, preferred_element_type=F32
    )


def rows_spec(block, width, start=0):
    return pl.BlockSpec((block, width), lambda i: (i + start, 0))


def whole_spec(shape):
    rank = len(shape)
    return pl.BlockSpec(shape, lambda i: (0,) * rank, pipeline_mode=pl.Buffered(1))


def head_spec(rows, width=128):
    return pl.BlockSpec((rows, width), lambda h: (0, h))


def sds(shape, dtype):
    return jax.ShapeDtypeStruct(shape, dtype)


MESH_ID = pl.DeviceIdType.MESH


def neighbour_x():
    return {"row": 1 - lax.axis_index("row")}


def neighbour_y():
    return {"col": lax.rem(lax.axis_index("col") + 2, 4)}


def greet():
    barrier = pltpu.get_barrier_semaphore()
    for device in (neighbour_x(), neighbour_y()):
        pl.semaphore_signal(barrier, inc=1, device_id=device, device_id_type=MESH_ID)
    pl.semaphore_wait(barrier, 2)


def message(src, dst, device, sems, n):
    send, recv = sems
    return pltpu.make_async_remote_copy(
        src_ref=src,
        dst_ref=dst,
        send_sem=send.at[n],
        recv_sem=recv.at[n],
        device_id=device,
        device_id_type=MESH_ID,
    )


def neighbour_core():
    col = lax.axis_index("col")
    return {"col": col + 1 - 2 * lax.rem(col, 2)}


def neighbour_end():
    seq = lax.axis_index("seq")
    return {"seq": seq + 1 - 2 * lax.rem(seq, 2)}


def neighbour_middle():
    return {"seq": 3 - lax.axis_index("seq")}


def greet_all(devices):
    barrier = pltpu.get_barrier_semaphore()
    for device in devices:
        pl.semaphore_signal(barrier, inc=1, device_id=device, device_id_type=MESH_ID)
    pl.semaphore_wait(barrier, len(devices))


def row_step(ref):
    rows, lanes = ref.shape
    step = 16
    while step * 2 * lanes <= 32768 and rows % (step * 2) == 0:
        step *= 2
    return step


def plus_in(dst, src):
    step = row_step(dst)

    def one(n, carry):
        at = pl.ds(pl.multiple_of(n * step, step), step)
        dst[at, :] = (dst[at, :].astype(F32) + src[at, :].astype(F32)).astype(dst.dtype)
        return carry

    lax.fori_loop(0, dst.shape[0] // step, one, 0)


def put_sum(dst, left, right):
    step = row_step(dst)

    def one(n, carry):
        at = pl.ds(pl.multiple_of(n * step, step), step)
        dst[at, :] = (left[at, :].astype(F32) + right[at, :].astype(F32)).astype(dst.dtype)
        return carry

    lax.fori_loop(0, dst.shape[0] // step, one, 0)


def put_in(dst, src):
    step = row_step(dst)

    def one(n, carry):
        at = pl.ds(pl.multiple_of(n * step, step), step)
        dst[at, :] = src[at, :].astype(dst.dtype)
        return carry

    lax.fori_loop(0, dst.shape[0] // step, one, 0)


class SeqSum:
    def __init__(self, pieces, sems, base):
        self.pieces = pieces
        count = len(pieces)
        self.to_end = [message(s, a, neighbour_end(), sems, base + n) for n, (s, a, b) in enumerate(pieces)]
        self.across = [
            message(s, b, neighbour_middle(), sems, base + count + n) for n, (s, a, b) in enumerate(pieces)
        ]
        seq = lax.axis_index("seq")
        self.middle = (seq == 1) | (seq == 2)
        self.end = (seq == 0) | (seq == 3)

    def begin(self, n):
        @pl.when(self.end)
        def _():
            self.to_end[n].start()

    def relay(self, n):
        s, a, b = self.pieces[n]

        @pl.when(self.middle)
        def _():
            self.to_end[n].wait_recv()
            plus_in(s, a)
            self.across[n].start()

    def settle(self, n):
        s, a, b = self.pieces[n]

        @pl.when(self.middle)
        def _():
            self.across[n].wait_recv()
            self.across[n].wait_send()
            plus_in(s, b)
            self.to_end[n].start()

    def finish(self, n):
        s, a, b = self.pieces[n]

        @pl.when(self.end)
        def _():
            self.to_end[n].wait_recv()
            self.to_end[n].wait_send()
            put_in(s, a)

        @pl.when(self.middle)
        def _():
            self.to_end[n].wait_send()


def scatter_messages(q1, q2, q3, r3, rx, ry, sems, base):
    half = q1.shape[0] // 2
    a, b = pl.ds(0, half), pl.ds(half, half)
    x, y = neighbour_x(), neighbour_y()
    plan = ((q3, r3, a, x), (q3, r3, b, y), (q1, rx, a, x), (q2, ry, a, y), (q2, ry, b, y), (q1, rx, b, x))
    return [
        message(src.at[at, :], dst.at[at, :], dev, sems, base + n)
        for n, (src, dst, at, dev) in enumerate(plan)
    ]


def gather_messages(own, gx, gy, gd, sems, base):
    half = own.shape[0] // 2
    a, b = pl.ds(0, half), pl.ds(half, half)
    x, y = neighbour_x(), neighbour_y()
    plan = ((own, gx, a, x), (own, gy, a, y), (own, gx, b, x), (own, gy, b, y), (gx, gd, a, y), (gy, gd, b, x))
    return [
        message(src.at[at, :], dst.at[at, :], dev, sems, base + n)
        for n, (src, dst, at, dev) in enumerate(plan)
    ]


def gather_messages_by_x(own, gx, gy, gd, sems, base):
    half = own.shape[0] // 2
    a, b = pl.ds(0, half), pl.ds(half, half)
    x, y = neighbour_x(), neighbour_y()
    plan = ((own, gx, a, x), (own, gy, a, y), (own, gx, b, x), (own, gy, b, y), (gy, gd, a, x), (gy, gd, b, x))
    return [
        message(src.at[at, :], dst.at[at, :], dev, sems, base + n)
        for n, (src, dst, at, dev) in enumerate(plan)
    ]


def add_into(dst, src, start, rows):
    plus_in(dst.at[pl.ds(start, rows), :], src.at[pl.ds(start, rows), :])


def load_rows(gate_w, up_w, sib_own, far, sib_far, dst, sem):
    width, lanes = far.shape
    part, units = width // 2, lanes // 2
    row = lax.axis_index("row")
    y = lax.div(lax.axis_index("col"), 2)
    own = pl.ds(pl.multiple_of(y * units, units), units)
    copies = []

    def copy(src, dst):
        copies.append(pltpu.make_async_copy(src, dst, sem.at[len(copies)]))
        copies[-1].start()

    for dx in (0, 1):
        rows = pl.ds(pl.multiple_of(part * (row + dx - 2 * row * dx), part), part)
        at = [pl.ds(((n // 2 * 2 + dx) * 2 + n % 2) * part, part) for n in range(4)]
        copy(gate_w.at[rows, own], dst.at[at[0], pl.ds(0, units)])
        copy(up_w.at[rows, own], dst.at[at[0], pl.ds(units, units)])
        for n, src in enumerate((sib_own, far, sib_far)):
            copy(src.at[rows, :], dst.at[at[n + 1], :])
    return copies


def comm_params(n):
    return pltpu.CompilerParams(
        vmem_limit_bytes=VMEM_LIMIT,
        dimension_semantics=("arbitrary",),
        collective_id=n,
        has_side_effects=True,
    )


def any_spec():
    return pl.BlockSpec(memory_space=pl.ANY)


def held_spec(block, width, last):
    return pl.BlockSpec((block, width), lambda i: (jnp.minimum(i, last), 0))


def full_spec(shape):
    rank = len(shape)
    return pl.BlockSpec(shape, lambda i: (0,) * rank)


def row_sums(values):
    folded = values[:, :128]
    for n in range(128, values.shape[1], 128):
        folded = folded + values[:, n : n + 128]
    return dot_nt(jnp.ones((8, 128), F32), folded, PRECISE)


def as_column(lanes, width):
    first = (lax.broadcasted_iota(jnp.int32, (8, 128), 0) == 0).astype(F32)
    column = dot_tn(lanes, first, PRECISE)
    return jnp.concatenate([column] * (width // 128), axis=1)


def norm_back_rows(start, rows, own_sum, low_x, low_y, dots_x, dots_y, scale, source, gain, base, out, low):
    width = source.shape[1]
    step = 128

    def one(n, sum_grad):
        at = pl.ds(pl.multiple_of(start + n * step, step), step)
        d = own_sum[at, :] + low_x[at, :].astype(F32) + low_y[at, :].astype(F32)
        s, m = scale[at, :], source[at, :]
        t = as_column(dots_x[:, at] + dots_y[:, at], width)
        new = base[at, :] + s * gain * d - m * (s * s) * t * (1.0 / D)
        out[at, :] = new
        if low is not None:
            low[at, :] = new.astype(BF)
        return sum_grad + jnp.sum(d * m * s, axis=0, keepdims=True)

    return lax.fori_loop(0, rows // step, one, jnp.zeros((1, width), F32))


def chain(entries, count):
    state = entries[count - 1, 0, 1:2, :]
    for n in range(count - 2, -1, -1):
        state = entries[n, 0, 1:2, :] + entries[n, 0, 0:1, :] * state
    return state


def carried(entries, h, count):
    state = entries[count - 1, h, 1:2, :]
    for n in range(count - 2, -1, -1):
        state = entries[n, h, 1:2, :] + entries[n, h, 0:1, :] * state
    return state


class Messages:
    def __init__(self, sems):
        self.sems, self.used = sems, 0

    def new(self, src, dst, device):
        self.used += 1
        return message(src, dst, device, self.sems, self.used - 1)

    def block(self, maker, *refs):
        made = maker(*refs, self.sems, self.used)
        self.used += len(made)
        return made


FRONT_MESSAGES = 80


def front_body(heads, blocks, count, *refs):
    (stream, cot, in_w, br_w, out_w, gate_w, up_w, down_w) = refs[:8]
    (gains_in, small_in, recall_gate, admit_gate, off) = refs[8:13]
    (e_own, w_down, gains_out, small, s1, border_out, earlier_out, mid, own) = refs[13:22]
    (n1, conv, recall, admit, states, mixed) = refs[22:28]
    (mx, my, md, far_gu, sib_own, sib_far, w_in_out, x_out, g_out, w_out_out, u_out, v_out) = refs[28:40]
    (x_own, x_recv, g_own, g_recv, gains_recv, small_recv, own_low, gx, gy, gd) = refs[40:50]
    (w_in, gains, border, earlier, x, g, w_out, u, v) = refs[50:59]
    (wo, wd, local, cum, ext, ends, q0, q1, q2, q3, r3, rx, ry, load, send, recv) = refs[59:]
    i = pl.program_id(0)
    seq, row, col = lax.axis_index("seq"), lax.axis_index("row"), lax.axis_index("col")
    y = lax.div(col, 2)
    core = lax.rem(col, 2)
    rows, width = x.shape
    part = width // 2
    half = rows // 2
    block = rows // blocks
    channels = u.shape[1]
    units = gate_w.shape[1] // 2
    to_x, to_y, to_core = neighbour_x(), neighbour_y(), neighbour_core()
    made = Messages((send, recv))
    copies = []

    def copy(src, dst):
        copies.append(pltpu.make_async_copy(src, dst, load.at[len(copies)]))
        return copies[-1]

    swap = [
        made.new(stream.at[1 - core], x_recv, to_core),
        made.new(gains_in, gains_recv, to_core),
        made.new(small_in, small_recv, to_core),
    ]
    swap_g = made.new(cot.at[1 - core], g_recv, to_core)
    x_copy, g_copy = copy(stream.at[core], x_own), copy(cot.at[core], g_own)
    gains_x = made.new(gains.at[:, pl.ds(0, width)], gains.at[:, pl.ds(width, width)], to_x)
    gains_y = made.new(gains.at[:, pl.ds(0, width)], gains.at[:, pl.ds(2 * width, width)], to_y)
    gains_d = made.new(gains.at[:, pl.ds(width, width)], gains.at[:, pl.ds(3 * width, width)], to_y)

    def place(dy, dx, dc):
        return pl.ds(pl.multiple_of(((dy * 2 + dx) * 2 + dc) * part, part), part)

    own_cols = pl.ds(pl.multiple_of(y * channels, channels), channels)
    other_cols = pl.ds(pl.multiple_of((1 - y) * channels, channels), channels)
    in_own, in_far, in_core, in_pass = [], [], [], []
    for n, w in enumerate((in_w, br_w)):
        lanes = pl.ds(n * channels, channels)
        for k in (0, 1):
            source = pl.ds(k * part, part)
            dx = row + k - 2 * row * k
            in_far.append(made.new(w.at[source, other_cols], w_in.at[place(1, dx, 0), lanes], to_y))
            in_own.append(copy(w.at[source, own_cols], w_in.at[place(0, dx, 0), lanes]))
            in_core.append(made.new(w.at[source, own_cols], w_in.at[place(0, dx, 1), lanes], to_core))
            in_pass.append(
                made.new(w_in.at[place(1, dx, 0), lanes], w_in.at[place(1, dx, 1), lanes], to_core)
            )

    own_rows = pl.ds(pl.multiple_of(y * channels, channels), channels)
    other_rows = pl.ds(pl.multiple_of((1 - y) * channels, channels), channels)
    wo_own = copy(out_w.at[own_rows, :], wo.at[0, 0])
    wo_far = made.new(out_w.at[other_rows, :], wo.at[1, 0], to_y)
    wo_core = made.new(out_w.at[own_rows, :], wo.at[0, 1], to_core)
    wo_pass = made.new(wo.at[1, 0], wo.at[1, 1], to_core)

    share, share_d = gate_w.shape[0] // (count + 1), units // (count + 1)
    own_units = pl.ds(pl.multiple_of(y * units, units), units)
    other_units = pl.ds(pl.multiple_of((1 - y) * units, units), units)
    at_seq = pl.ds(pl.multiple_of(seq * share, share), share)
    at_seq_d = pl.ds(pl.multiple_of(seq * share_d, share_d), share_d)
    far_d = wd.at[1, 0]
    first_lanes, last_lanes = pl.ds(0, units), pl.ds(units, units)
    from_d = pl.ds(pl.multiple_of((1 - y) * units + seq * share_d, share_d), share_d)
    ff_far = [
        made.new(down_w.at[from_d, :], far_d.at[at_seq_d, :], to_y),
        made.new(gate_w.at[at_seq, other_units], far_gu.at[at_seq, first_lanes], to_y),
        made.new(up_w.at[at_seq, other_units], far_gu.at[at_seq, last_lanes], to_y),
    ]
    others = [{"seq": lax.rem(seq + n, count + 1)} for n in range(1, count + 1)]
    ff_share = [made.new(far_d.at[at_seq_d, :], far_d.at[at_seq_d, :], device) for device in others]
    ff_share += [made.new(far_gu.at[at_seq, :], far_gu.at[at_seq, :], device) for device in others]
    ff_core = [
        made.new(gate_w.at[:, own_units], sib_own.at[:, first_lanes], to_core),
        made.new(up_w.at[:, own_units], sib_own.at[:, last_lanes], to_core),
        made.new(down_w.at[own_units, :], wd.at[0, 1], to_core),
    ]
    ff_pass = [made.new(far_gu, sib_far, to_core), made.new(far_d, wd.at[1, 1], to_core)]
    wd_own = copy(down_w.at[own_units, :], wd.at[0, 0])
    ahead = len(copies)
    w_in_store = copy(w_in, w_in_out)
    x_store, g_store, w_out_store = copy(x, x_out), copy(g, g_out), copy(w_out, w_out_out)
    u_store, v_store = copy(u, u_out), copy(v, v_out)

    gather_n = made.block(gather_messages_by_x, own_low, gx, gy, gd)
    scatter = made.block(scatter_messages, q1, q2, q3, r3, rx, ry)
    gather_m = made.block(gather_messages, own, mx, my, md)
    edge = made.new(u.at[pl.ds(rows - 8, 8), :], border, {"seq": seq + 1})
    hand_on = [made.new(ends, earlier.at[n - 1], {"seq": seq + n}) for n in range(1, count + 1)]

    def put_together(left, right, full, low):
        step = 128

        def one(n, carry):
            at = pl.ds(pl.multiple_of(n * step, step), step)
            whole = jnp.concatenate([left[:, at], right[:, at]], axis=0).T
            full[at, :] = whole
            low[at, :] = whole.astype(BF)
            return carry

        lax.fori_loop(0, rows // step, one, 0)

    @pl.when(i == 0)
    def _():
        for c in copies[:ahead]:
            c.start()
        border[...] = jnp.zeros_like(border)
        earlier[...] = jnp.zeros_like(earlier)
        greet_all(
            [to_x, to_y, to_core] + [{"seq": lax.rem(seq + n, count + 1)} for n in range(1, count + 1)]
        )
        for m in swap:
            m.start()
        x_copy.wait()
        swap[0].wait_recv()
        put_together(x_own, x_recv, x, own_low)
        x_store.start()
        for m in gather_n[:4]:
            m.start()
        for m in in_core:
            m.start()
        swap[1].wait_recv()
        gains[:, 0:width] = jnp.concatenate([gains_in[...], gains_recv[...]], axis=1)
        gains_x.start()
        gains_y.start()
        swap[2].wait_recv()
        lane = small_in.shape[1]
        small[:, pl.ds(pl.multiple_of(core * lane, lane), lane)] = small_in[...]
        small[:, pl.ds(pl.multiple_of((1 - core) * lane, lane), lane)] = small_recv[...]
        swap_g.start()
        gains_x.wait_recv()
        gains_d.start()
        gather_n[1].wait_recv()
        gather_n[4].start()
        wo_core.start()
        for m in ff_core:
            m.start()
        gather_n[3].wait_recv()
        gather_n[5].start()
        for m in in_far:
            m.start()
        for m, n in zip(in_far, in_pass):
            m.wait_recv()
            n.start()
        wo_far.start()
        for m in ff_far:
            m.start()
        for c in in_own:
            c.wait()
        for m in in_core + in_pass:
            m.wait_recv()
        gains_y.wait_recv()
        gains_d.wait_recv()
        w_in_store.start()
        gather_n[0].wait_recv()
        gather_n[4].wait_recv()

    @pl.when(i == 1)
    def _():
        g_copy.wait()
        swap_g.wait_recv()
        put_together(g_own, g_recv, g, e_own)
        g_store.start()

    @pl.when(i == blocks // 2)
    def _():
        gather_n[2].wait_recv()
        gather_n[5].wait_recv()

    @pl.when(i < blocks)
    def _():
        at = pl.ds(pl.multiple_of(i * block, block), block)
        parts = [r[at, :].astype(F32) for r in (own_low, gx, gy, gd)]
        total = sum(jnp.sum(p * p, axis=1, keepdims=True) for p in parts)
        s = lax.rsqrt(total / D + EPSILON)
        s1[at, :] = s
        normed = [p * s * gains[0:1, j * width : (j + 1) * width] for j, p in enumerate(parts)]
        acc = None
        for j, n in enumerate(normed):
            term = dot_nn(n.astype(BF), w_in[j * width : (j + 1) * width, :])
            acc = term if acc is None else acc + term
        u[at, :] = acc[:, :channels]
        v[at, :] = acc[:, channels:]
        for j in (0, 1):
            k, p = pair_up(normed[2 * j], normed[2 * j + 1])
            n1[:, j * width : (j + 1) * width] = k.astype(BF)
            n1[:, (j + 2) * width : (j + 3) * width] = p.astype(BF)

    @pl.when((i == blocks - 1) & (seq < count))
    def _():
        edge.start()

    @pl.when((i == blocks) & (seq > 0))
    def _():
        edge.wait_recv()

    @pl.when(i == blocks)
    def _():
        u_store.start()
        v_store.start()

    @pl.when(i == blocks - 1)
    def _():
        ff_far[0].wait_recv()
        for m in ff_share[:count]:
            m.start()

    @pl.when((i >= blocks) & (i < blocks + heads))
    def _():
        h = i - blocks
        lane = pl.ds(pl.multiple_of(h * 128, 128), 128)
        state_h, cum_h = local.at[h], cum.at[h]
        ext[0:8, :] = border[:, lane]
        ext[8 : 8 + rows, :] = u[:, lane]
        sp = small[KW : KW + 1, lane]
        step = ROW_BLOCK
        for r in range(0, rows, step):
            o = off[8 + r : 8 + r + step, :]
            total = small[0:1, lane] * ext[8 + r : 8 + r + step, :]
            for k in range(1, KW):
                term = small[k : k + 1, lane] * ext[8 + r - k : 8 + r - k + step, :]
                total = total + jnp.where(o >= k, term, 0.0)
            conv[r : r + step, :] = total
            rec = jax.nn.sigmoid(dot_nn(total, recall_gate[y * heads + h], PRECISE))
            adm = jax.nn.sigmoid(dot_nn(total, admit_gate[y * heads + h], PRECISE))
            recall[r : r + step, :] = rec
            admit[r : r + step, :] = adm
            ell = -8.0 * rec * sp
            cum_h[r : r + step, :] = jnp.where(o > 0, jnp.exp(ell), 0.0)
            state_h[r : r + step, :] = jnp.sqrt(minus_expm1(2.0 * ell)) * adm * total
        seg = rows // 8

        def one(n, carry):
            h, p = carry
            at = pl.ds(n, 8, stride=seg)
            d = cum_h[at, :]
            h = d * h + state_h[at, :]
            p = d * p
            state_h[at, :] = h
            cum_h[at, :] = p
            return h, p

        zero = jnp.zeros((8, 128), F32)
        last, product = lax.fori_loop(0, seg, one, (zero, zero + 1.0), unroll=8)
        carry_h, carry_p = last[0:1, :], product[0:1, :]
        for s in range(1, 8):
            at = slice(s * seg, (s + 1) * seg)
            c = cum_h[at, :]
            state_h[at, :] = state_h[at, :] + c * carry_h
            cum_h[at, :] = c * carry_p
            carry_h = last[s : s + 1, :] + product[s : s + 1, :] * carry_h
            carry_p = product[s : s + 1, :] * carry_p
        ends[h, 0:1, :] = carry_p
        ends[h, 1:2, :] = carry_h
        ends[h, 2:8, :] = jnp.zeros((6, 128), F32)

    @pl.when(i == blocks + 1)
    def _():
        wo_far.wait_recv()
        wo_pass.start()

    def columns_in_order(pieces, out):
        size = out.shape[0]
        step = 128
        lower = row == 0

        def one(n, carry):
            at = pl.ds(pl.multiple_of(n * step, step), step)
            for dy in (0, 1):
                first, second = pair_up(pieces[dy, 0, at, :].astype(F32), pieces[dy, 1, at, :].astype(F32))
                near, far = jnp.where(lower, first, second), jnp.where(lower, second, first)
                out[at, 2 * dy * width : (2 * dy + 1) * width] = near.astype(BF)
                out[at, (2 * dy + 1) * width : (2 * dy + 2) * width] = far.astype(BF)
            return carry

        lax.fori_loop(0, size // step, one, 0)

    @pl.when(i == blocks + heads - 1)
    def _():
        wo_own.wait()
        wo_core.wait_recv()
        wo_pass.wait_recv()
        columns_in_order(wo, w_out)
        w_out_store.start()

    for n in range(1, count + 1):

        @pl.when((i == blocks + heads - 1) & (seq <= count - n))
        def _():
            hand_on[n - 1].start()

        @pl.when((i == blocks + heads) & (seq >= n))
        def _():
            hand_on[n - 1].wait_recv()

    @pl.when(i == blocks + heads)
    def _():
        for m in ff_far[1:]:
            m.wait_recv()
        for m in ff_share[count:]:
            m.start()

    third = blocks + heads

    @pl.when((i >= third) & (i < third + blocks))
    def _():
        at = pl.ds(pl.multiple_of((i - third) * block, block), block)
        st = jnp.concatenate(
            [local[h, at, :] + cum[h, at, :] * carried(earlier, h, count) for h in range(heads)], axis=1
        )
        states[...] = st
        m = (st * gelu_pair(v[at, :])[0]).astype(BF)
        mixed[...] = m
        for j, q in ((3, q3), (1, q1), (2, q2), (0, q0)):
            q[at, :] = dot_nn(m, w_out[:, j * width : (j + 1) * width]).astype(q.dtype)

    @pl.when(i == third + blocks // 2 - 1)
    def _():
        scatter[0].start()
        scatter[2].start()

    @pl.when(i == third + blocks - 1)
    def _():
        scatter[1].start()

    @pl.when(i == third + blocks)
    def _():
        scatter[0].wait_recv()
        add_into(q2, r3, 0, half)
        scatter[3].start()
        scatter[4].start()
        scatter[1].wait_recv()
        add_into(q1, r3, half, half)
        scatter[5].start()
        gains_out[...] = gains[...]
        border_out[...] = border[...]
        earlier_out[...] = earlier[...]
        for base, first in ((0, 2), (half, 4)):
            scatter[first].wait_recv()
            scatter[first + 1].wait_recv()

            def one(n, carry):
                at = pl.ds(pl.multiple_of(base + n * 128, 128), 128)
                total = x[at, :] + q0[at, :] + rx[at, :].astype(F32) + ry[at, :].astype(F32)
                mid[at, :] = total
                own[at, :] = total.astype(BF)
                return carry

            lax.fori_loop(0, half // 128, one, 0)
            start = 0 if base == 0 else 2
            gather_m[start].start()
            gather_m[start + 1].start()
        for m in ff_share:
            m.wait_recv()
        for m in ff_pass:
            m.start()
        gather_m[0].wait_recv()
        gather_m[4].start()
        gather_m[3].wait_recv()
        gather_m[5].start()
        wd_own.wait()
        for m in ff_core + ff_pass:
            m.wait_recv()
        columns_in_order(wd, w_down)
        for c in copies[ahead:]:
            c.wait()
        for n in (1, 2, 4, 5):
            gather_m[n].wait_recv()
        sent = swap + [swap_g, gains_x, gains_y, gains_d] + in_far + in_core + in_pass
        sent += [wo_far, wo_core, wo_pass] + ff_far + ff_share + ff_core + ff_pass
        for m in sent + gather_n + scatter + gather_m:
            m.wait_send()

        @pl.when(seq < count)
        def _():
            edge.wait_send()

        for n in range(1, count + 1):

            @pl.when(seq <= count - n)
            def _():
                hand_on[n - 1].wait_send()


def front(stream, cot, in_w, br_w, out_w, gate_w, up_w, down_w, gains, small, recall_gate, admit_gate, off, count):
    part, rows = stream.shape[1:]
    width = 2 * part
    channels = in_w.shape[1] // 2
    units = gate_w.shape[1] // 2
    heads = channels // 128
    block = ROW_BLOCK
    blocks = rows // block

    def norm_at(i):
        return (jnp.minimum(i, blocks - 1), 0)

    def head_at(i):
        return (0, jnp.clip(i - blocks, 0, heads - 1))

    def mix_at(i):
        return (jnp.clip(i - blocks - heads, 0, blocks - 1), 0)

    chunk_low, chunk = sds((rows, width), BF), sds((rows, width), F32)
    wide = sds((rows, channels), F32)
    held = [
        chunk_low,
        sds((units, 4 * width), BF),
        sds((8, 4 * width), F32),
        sds((8, channels), F32),
        sds((rows, 1), F32),
        sds((8, channels), F32),
        sds((count, heads, 8, 128), F32),
        chunk,
        chunk_low,
    ]
    blocked = [sds((rows, 4 * width), BF), wide, wide, wide, wide, sds((rows, channels), BF)]
    away = [chunk_low] * 3 + [sds((width, 2 * units), BF)] * 3 + [sds((4 * width, 2 * channels), BF)]
    away += [chunk, chunk, sds((channels, 4 * width), BF), wide, wide]
    piece = pltpu.VMEM((rows, width), BF)
    side = pltpu.VMEM((part, rows), F32)
    tall = pl.BlockSpec((rows, 128), head_at)
    return pl.pallas_call(
        functools.partial(front_body, heads, blocks, count),
        grid=(2 * blocks + heads + 1,),
        in_specs=[any_spec()] * 8
        + [whole_spec(a.shape) for a in (gains, small, recall_gate, admit_gate, off)],
        out_specs=[whole_spec(s.shape) for s in held]
        + [pl.BlockSpec((block, 4 * width), norm_at)]
        + [tall] * 3
        + [pl.BlockSpec((block, channels), mix_at)] * 2
        + [any_spec()] * len(away),
        out_shape=held + blocked + away,
        scratch_shapes=[side] * 4
        + [pltpu.VMEM(gains.shape, F32), pltpu.VMEM(small.shape, F32)]
        + [piece] * 4
        + [
            pltpu.VMEM((4 * width, 2 * channels), BF),
            pltpu.VMEM((8, 4 * width), F32),
            pltpu.VMEM((8, channels), F32),
            pltpu.VMEM((count, heads, 8, 128), F32),
            pltpu.VMEM((rows, width), F32),
            pltpu.VMEM((rows, width), F32),
            pltpu.VMEM((channels, 4 * width), BF),
            pltpu.VMEM((rows, channels), F32),
            pltpu.VMEM((rows, channels), F32),
            pltpu.VMEM((2, 2, channels, width), BF),
            pltpu.VMEM((2, 2, units, width), BF),
            pltpu.VMEM((heads, rows, 128), F32),
            pltpu.VMEM((heads, rows, 128), F32),
            pltpu.VMEM((rows + 8, 128), F32),
            pltpu.VMEM((heads, 8, 128), F32),
            pltpu.VMEM((rows, width), F32),
        ]
        + [piece] * 6
        + [pltpu.SemaphoreType.DMA((14,))]
        + [pltpu.SemaphoreType.DMA((FRONT_MESSAGES,))] * 2,
        compiler_params=comm_params(1),
        cost_estimate=cost(200 * rows * in_w.size, rows * 40000),
        name="front",
    )(stream, cot, in_w, br_w, out_w, gate_w, up_w, down_w, gains, small, recall_gate, admit_gate, off)


FEED_MESSAGES = 64
FEED_CUTS = 4


def feed_body(blocks, *refs):
    (x0, x1, x2, x3, e_own, mid, cot, gain, wd_in) = refs[:9]
    weights = refs[9:14]
    outs = refs[14:18]
    (dx, own, gx, gy, gd, gain_grad, s_down, s_gu) = refs[18:26]
    (wgu, wd, ex, ey, ed, load, n2, hid, ee, err, scale, stage, c_down, c_gu, a_down, b_down) = refs[26:42]
    (a_gu, b_gu, free, q0, q1, q2, q3, r3, rx, ry, dots, dots_x, dots_y, send, recv) = refs[42:]
    i = pl.program_id(0)
    made = Messages((send, recv))
    block, width = x0.shape
    rows = mid.shape[0]
    half = rows // 2
    units = hid.shape[1]
    tiles = units // width
    scatter = made.block(scatter_messages, q1, q2, q3, r3, rx, ry)
    gather = made.block(gather_messages, own, gx, gy, gd)
    halves = (pl.ds(0, half), pl.ds(half, half))
    small_x = [made.new(dots.at[:, at], dots_x.at[:, at], neighbour_x()) for at in halves]
    small_y = [made.new(dots_x.at[:, at], dots_y.at[:, at], neighbour_y()) for at in halves]
    gu_core = [made.new(stage, c_gu, neighbour_core()) for n in (0, 1)]
    down_core = [
        made.new(
            stage.at[:, pl.ds(n * 2 * width, 2 * width)], c_down.at[pl.ds(n * width, width), :], neighbour_core()
        )
        for n in range(tiles)
    ]
    part_d = units // 2
    pieces = [
        [r.at[pl.ds(n * part_d, part_d), pl.ds(lane, width)] for r in (s_down, a_down, b_down)]
        for lane in (width, 0)
        for n in range(2)
    ]
    cut = width // 8
    spans = [(n * cut, cut) for n in range(FEED_CUTS - 1)]
    spans += [((FEED_CUTS - 1) * cut, 2 * cut // 3), (FEED_CUTS * cut - cut // 3, cut // 3)]
    for start, size in spans:
        at = pl.ds(start, size)
        pieces.append([s_gu.at[pl.ds(width + start, size), :], a_gu.at[at, :], b_gu.at[at, :]])
    total = SeqSum(pieces, (send, recv), made.used)
    made.used += 2 * len(pieces)

    gather_e = made.block(gather_messages, e_own, ex, ey, ed)
    load_d = pltpu.make_async_copy(wd_in, wd, load.at[10])
    load_cot = pltpu.make_async_copy(cot, dx, load.at[11])
    second = blocks + tiles
    third = second + blocks

    @pl.when(i == 0)
    def _():
        copies = load_rows(*weights, wgu, load)
        load_d.start()
        load_cot.start()
        greet_all(
            (neighbour_x(), neighbour_y(), neighbour_core(), neighbour_end(), neighbour_middle())
        )
        for m in gather_e[:4]:
            m.start()
        for c in copies:
            c.wait()
        load_d.wait()

    @pl.when(i < blocks)
    def _():
        at = pl.ds(pl.multiple_of(i * block, block), block)
        parts = [r[...].astype(F32) for r in (x0, x1, x2, x3)]
        total = sum(jnp.sum(p * p, axis=1, keepdims=True) for p in parts)
        s = lax.rsqrt(total / D + EPSILON)
        scale[at, :] = s
        normed = [p * s * gain[1:2, j * width : (j + 1) * width] for j, p in enumerate(parts)]
        acc = None
        for j, n in enumerate(normed):
            term = dot_nn(n.astype(BF), wgu[j * width : (j + 1) * width, :])
            acc = term if acc is None else acc + term
        for j in (0, 1):
            k, p = pair_up(normed[2 * j], normed[2 * j + 1])
            n2[at, j * width : (j + 1) * width] = k.astype(BF)
            n2[at, (j + 2) * width : (j + 3) * width] = p.astype(BF)
        pre, up = acc[:, :units], acc[:, units:]
        err[at, :units] = pre.astype(BF)
        err[at, units:] = up.astype(BF)
        h = (gelu_pair(pre)[0] * up).astype(BF)
        hid[at, :] = h
        for j, q in enumerate(outs):
            q[...] = dot_nn(h, wd[:, j * width : (j + 1) * width]).astype(q.dtype)

    @pl.when(i == blocks - 2)
    def _():
        gather_e[0].wait_recv()
        gather_e[4].start()

    @pl.when(i == blocks - 1)
    def _():
        gather_e[3].wait_recv()
        gather_e[5].start()

    @pl.when(i == blocks)
    def _():
        for n in (1, 2, 4, 5):
            gather_e[n].wait_recv()
        step = 128

        def one(n, carry):
            at = pl.ds(pl.multiple_of(n * step, step), step)
            wide = [r[at, :].astype(F32) for r in (e_own, ex, ey, ed)]
            for j in (0, 1):
                k, p = pair_up(wide[2 * j], wide[2 * j + 1])
                ee[at, j * width : (j + 1) * width] = k.astype(BF)
                ee[at, (j + 2) * width : (j + 3) * width] = p.astype(BF)
            return carry

        lax.fori_loop(0, rows // step, one, 0)

    @pl.when((i >= second) & (i < third))
    def _():
        at = pl.ds(pl.multiple_of((i - second) * block, block), block)
        pre, up = err[at, :units].astype(F32), err[at, units:].astype(F32)
        act, slope = gelu_pair(pre)
        dh = None
        for j, r in enumerate((e_own, ex, ey, ed)):
            term = dot_nt(r[at, :], wd[:, j * width : (j + 1) * width])
            dh = term if dh is None else dh + term
        g = (dh * up * slope).astype(BF)
        b = (dh * act).astype(BF)
        err[at, :units] = g
        err[at, units:] = b
        dots[:, at] = row_sums(g.astype(F32) * pre + b.astype(F32) * up)
        for j, q in ((3, q3), (1, q1), (2, q2), (0, q0)):
            rows_w = slice(j * width, (j + 1) * width)
            q[at, :] = (dot_nt(g, wgu[rows_w, :units]) + dot_nt(b, wgu[rows_w, units:])).astype(q.dtype)

    def hand_dots(n):
        small_x[n].wait_recv()
        dots_x[:, halves[n]] = dots_x[:, halves[n]] + dots[:, halves[n]]
        small_y[n].start()

    own_gain = gain[1:2, :width]

    def finish(start, first):
        scatter[first].wait_recv()
        scatter[first + 1].wait_recv()
        return norm_back_rows(
            start, half, q0, rx, ry, dots_x, dots_y, scale, mid, own_gain, dx, dx, own
        )

    @pl.when(i == second + blocks // 2 - 1)
    def _():
        scatter[0].start()
        scatter[2].start()
        small_x[0].start()

    @pl.when(i == third - 2)
    def _():
        scatter[0].wait_recv()
        add_into(q2, r3, 0, half)
        scatter[3].start()
        hand_dots(0)

    @pl.when(i == third - 1)
    def _():
        scatter[1].start()
        small_x[1].start()
        scatter[4].start()
        load_cot.wait()
        small_y[0].wait_recv()
        gain_grad[0:1, :] = finish(0, 2)
        gather[0].start()
        gather[1].start()

    @pl.when((i >= blocks) & (i < blocks + tiles))
    def _():
        k = i - blocks
        at = pl.ds(pl.multiple_of(k * width, width), width)
        g = dot_tn(hid[:, at], ee[...])
        stage[:, pl.ds(pl.multiple_of(k * 2 * width, 2 * width), 2 * width)] = g[:, 2 * width :].astype(BF)
        s_down[at, :] = g[:, : 2 * width].astype(BF)

    for n in range(tiles):

        @pl.when(i == blocks + n)
        def _():
            down_core[n].start()

    @pl.when(i == second)
    def _():
        for n in range(tiles):
            down_core[n].wait_recv()
            down_core[n].wait_send()
        plus_in(s_down, c_down)
        for n in range(3):
            total.begin(n)

    for n in (0, 1):

        @pl.when(i == third + 1 + 2 * n)
        def _():
            gu_core[n].wait_send()

    @pl.when((i >= third) & (i < third + 4))
    def _():
        k = i - third
        n = jnp.where(k < 2, 3 - 2 * k, 6 - 2 * k)
        at = pl.ds(pl.multiple_of(n * width, width), width)
        stage[...] = dot_tn(n2[:, at], err[...]).astype(BF)

    for n in (0, 1):

        @pl.when(i == third + 2 * n)
        def _():
            if n:
                pl.semaphore_wait(free, 1)
            gu_core[n].start()

        @pl.when(i == third + 2 * n + 1)
        def _():
            gu_core[n].wait_recv()
            target = s_gu.at[pl.ds((1 - n) * width, width), :]
            put_sum(target, stage, c_gu)
            if not n:
                pl.semaphore_signal(free, inc=1, device_id=neighbour_core(), device_id_type=MESH_ID)

    @pl.when(i == third + 1)
    def _():
        for n in range(4, len(pieces)):
            total.begin(n)

    ticks = [second + 1, second + 3] + [third + 1 + n for n in range(len(pieces))]
    for t, where in enumerate(ticks):

        @pl.when(i == where)
        def _():
            if t + 3 < 4:
                total.begin(t + 3)
            if t < len(pieces):
                total.relay(t)
            if 0 <= t - 1 < len(pieces):
                total.settle(t - 1)
            if t >= 2:
                total.finish(t - 2)

    @pl.when(i == third)
    def _():
        scatter[1].wait_recv()
        add_into(q1, r3, half, half)
        scatter[5].start()
        hand_dots(1)

    @pl.when(i == third + 2)
    def _():
        small_y[1].wait_recv()
        gain_grad[0:1, :] = gain_grad[0:1, :] + finish(half, 4)
        gather[2].start()
        gather[3].start()
        gather[0].wait_recv()
        gather[4].start()

    @pl.when(i == third + 4)
    def _():
        gather[3].wait_recv()
        gather[5].start()

    @pl.when(i == third + 2 + len(pieces))
    def _():
        for n in (1, 2, 4, 5):
            gather[n].wait_recv()
        for m in scatter + gather + gather_e + small_x + small_y:
            m.wait_send()


def feed(chunks, err_own, mid, cot, gain, wd, weights):
    rows, width = chunks[0].shape
    units = wd.shape[0]
    block = ROW_BLOCK
    blocks = rows // block
    tiles = units // width
    held = functools.partial(held_spec, block, last=blocks - 1)
    chunk = pltpu.VMEM((rows, width), BF)
    lanes = pltpu.VMEM((8, rows), F32)
    landing = pltpu.VMEM((units, 2 * width), BF)
    return pl.pallas_call(
        functools.partial(feed_body, blocks),
        grid=(2 * blocks + tiles + 8 + FEED_CUTS,),
        in_specs=[held(width)] * 4
        + [whole_spec(err_own.shape), whole_spec(mid.shape), any_spec(), whole_spec(gain.shape)]
        + [any_spec()] * 6,
        out_specs=[held(width)] * 4
        + [whole_spec((rows, width))] * 2
        + [any_spec()] * 3
        + [whole_spec((8, width)), whole_spec((units, 2 * width)), whole_spec((2 * width, 2 * units))],
        out_shape=[sds((rows, width), F32)]
        + [sds((rows, width), BF)] * 3
        + [sds((rows, width), F32)]
        + [sds((rows, width), BF)] * 4
        + [sds((8, width), F32), sds((units, 2 * width), BF), sds((2 * width, 2 * units), BF)],
        scratch_shapes=[
            pltpu.VMEM((4 * width, 2 * units), BF),
            pltpu.VMEM(wd.shape, BF),
            chunk,
            chunk,
            chunk,
            pltpu.SemaphoreType.DMA((12,)),
            pltpu.VMEM((rows, 4 * width), BF),
            pltpu.VMEM((rows, units), BF),
            pltpu.VMEM((rows, 4 * width), BF),
            pltpu.VMEM((rows, 2 * units), BF),
            pltpu.VMEM((rows, 1), F32),
            pltpu.VMEM((width, 2 * units), BF),
            landing,
            pltpu.VMEM((width, 2 * units), BF),
            landing,
            landing,
            pltpu.VMEM((FEED_CUTS * width // 8, 2 * units), BF),
            pltpu.VMEM((FEED_CUTS * width // 8, 2 * units), BF),
            pltpu.SemaphoreType.REGULAR,
            pltpu.VMEM((rows, width), F32),
        ]
        + [chunk] * 6
        + [lanes] * 3
        + [pltpu.SemaphoreType.DMA((FEED_MESSAGES,))] * 2,
        compiler_params=comm_params(3),
        cost_estimate=cost(48 * rows * wd.size, 3 * nbytes(wd) + rows * 30000, rows * units),
        name="feed",
    )(*chunks, err_own, mid, cot, gain, wd, *weights)


def back_body(heads, blocks, count, *refs):
    errs = refs[0:4]
    (w_out, states, branch, recall, conv, admit, u_head, off, soft) = refs[4:13]
    (taps, recall_w, admit_w, border, earlier, u, v, w_hbm, scale, x_hbm, dx_hbm, gain) = refs[13:25]
    (sum_gu, sum_down, mixed) = refs[25:28]
    (euv, grad, gain_grad, grad_small) = refs[28:32]
    (mine_gu, far_gu, far_down, mine_out, far_out, gates) = refs[32:38]
    (w, x, dx, paired, part, reach, ext, st, uext, dc, ends, later, edge, from_later, load) = refs[38:53]
    (q0, q1, q2, q3, r3, rx, ry, dots, dots_x, dots_y) = refs[53:63]
    (s_gu, a_gu, b_gu, s_out, p_out, c_out, a_out, b_out) = refs[63:71]
    (s_gt, p_gt, c_gt, a_gt, b_gt, store, send, recv) = refs[71:]
    i = pl.program_id(0)
    sems = (send, recv)
    seq = lax.axis_index("seq")
    rows, width = x.shape
    half = rows // 2
    step = ROW_BLOCK
    seg = rows // 8
    channels = heads * 128
    block = step

    scatter = scatter_messages(q1, q2, q3, r3, rx, ry, sems, 0)
    small_x = message(dots, dots_x, neighbour_x(), sems, 6)
    small_y = message(dots_x, dots_y, neighbour_y(), sems, 7)
    hand_on = [message(ends, later.at[n - 1], {"seq": seq - n}, sems, 7 + n) for n in range(1, count + 1)]
    base = 8 + count
    hand_edge = message(edge, from_later, {"seq": seq - 1}, sems, base)
    base += 1

    cut, rows_out = width // 8, channels
    y = lax.div(lax.axis_index("col"), 2)
    to_side, to_core = neighbour_y(), neighbour_core()
    size = heads * 128
    pieces, to_y, to_out, stores = [], {}, {}, []

    def store_copy(src, dst):
        stores.append(pltpu.make_async_copy(src, dst, store.at[len(stores)]))
        return stores[-1]

    made = Messages(sems)
    made.used = base
    done = FEED_CUTS * cut
    early_y = [
        made.new(sum_down.at[:, pl.ds(width, width)], far_down, to_side),
        made.new(sum_gu.at[pl.ds(width, done), :], far_gu.at[pl.ds(0, done), :], to_side),
    ]
    for start, rows_gu in ((12, 1), (13, 2), (15, 1), (0, 2), (2, 2), (4, 2), (6, 2)):
        p = len(pieces)
        at = pl.ds(start * cut, rows_gu * cut)
        pieces.append([r.at[at, :] for r in (s_gu, a_gu, b_gu)])
        if start >= 8:
            target = far_gu.at[pl.ds((start - 8) * cut, rows_gu * cut), :]
            to_y[p] = [made.new(pieces[p][0], target, to_side)]
        else:
            to_out[p] = [store_copy(pieces[p][0], mine_gu.at[at, :])]
    pieces.append([r.at[:, pl.ds(width, width)] for r in (s_out, a_out, b_out)])
    to_y[len(pieces) - 1] = [made.new(pieces[-1][0], far_out, to_side)]
    p = len(pieces)
    pieces.append([s_gt, a_gt, b_gt])
    to_y[p], to_out[p] = [], []
    for n in (0, 1):
        source = s_gt.at[pl.ds(n * size, size), :]
        target = gates.at[pl.ds(pl.multiple_of((2 * n + y) * size, size), size), :]
        to_y[p].append(made.new(source, target, to_side))
        to_out[p].append(store_copy(source, target))
    for n in (0, 1):
        at = pl.ds(n * (rows_out // 2), rows_out // 2)
        pieces.append([r.at[at, pl.ds(0, width)] for r in (s_out, a_out, b_out)])
        to_out[len(pieces) - 1] = [store_copy(pieces[-1][0], mine_out.at[at, :])]
    total = SeqSum(pieces, sems, made.used)
    made.used += 2 * len(pieces)
    core_out, core_gt = made.new(p_out, c_out, to_core), made.new(p_gt, c_gt, to_core)
    load_gu = pltpu.make_async_copy(sum_gu, s_gu, load.at[0])
    loads = [
        pltpu.make_async_copy(source, target, load.at[n + 1])
        for n, (source, target) in enumerate(((w_hbm, w), (x_hbm, x), (dx_hbm, dx)))
    ]

    def tick(t):
        if t + 3 < len(pieces):
            total.begin(t + 3)
        if t < len(pieces):
            total.relay(t)
        if 0 <= t - 1 < len(pieces):
            total.settle(t - 1)
        if 0 <= t - 2 < len(pieces):
            total.finish(t - 2)
            for m in to_y.get(t - 2, []) + to_out.get(t - 2, []):
                m.start()

    @pl.when(i == 0)
    def _():
        load_gu.start()
        later[...] = jnp.zeros_like(later)
        from_later[...] = jnp.zeros_like(from_later)
        greet_all(
            [neighbour_x(), neighbour_y(), neighbour_core()]
            + [{"seq": lax.rem(seq + n, count + 1)} for n in range(1, count + 1)]
        )
        load_gu.wait()
        for n in range(3):
            total.begin(n)
        for c in loads:
            c.start()
        for m in early_y:
            m.start()
        for r in range(0, rows, step):
            at = slice(r, r + step)
            for j in (0, 1):
                k, p = pair_up(errs[2 * j][at, :].astype(F32), errs[2 * j + 1][at, :].astype(F32))
                paired[at, j * width : (j + 1) * width] = k.astype(BF)
                paired[at, (j + 2) * width : (j + 3) * width] = p.astype(BF)

    @pl.when(i == 3)
    def _():
        core_out.wait_recv()
        plus_in(s_out, c_out)

    @pl.when(i == 2 * heads + 1)
    def _():
        core_gt.wait_recv()
        put_in(s_gt, p_gt)
        plus_in(s_gt, c_gt)

    for t in range(len(pieces) + 2):

        @pl.when(i == (1 if t == 0 else 2 * t if t <= heads + 1 else t + heads + 2))
        def _():
            tick(t)

    @pl.when(i == 1)
    def _():
        g = dot_tn(mixed[...], paired[...])
        p_out[...] = g[:, 2 * width :].astype(BF)
        core_out.start()
        s_out[...] = g[:, : 2 * width].astype(BF)

    @pl.when(i < heads)
    def _():
        sp = soft[0:1, :]
        part_h, reach_h = part.at[i], reach.at[i]
        lane = pl.ds(pl.multiple_of(channels + i * 128, 128), 128)
        for r in range(0, rows, step):
            at = slice(r, r + step)
            o = off[8 + r : 8 + r + step, :]
            ext[at, :] = jnp.where(o > 0, jnp.exp(-8.0 * recall[at, :] * sp), 0.0)
            dm = None
            for j in range(4):
                term = dot_nt(errs[j][at, :], w_out[:, j * width : (j + 1) * width])
                dm = term if dm is None else dm + term
            act, slope = gelu_pair(branch[at, :])
            euv[at, lane] = (dm * states[at, :] * slope).astype(BF)
            part_h[at, :] = dm * act
        ext[rows : rows + 8, :] = jnp.ones((8, 128), F32)
        for r in range(0, rows, step):
            reach_h[r : r + step, :] = ext[r + 1 : r + 1 + step, :]

        def one(n, carry):
            h, p = carry
            at = pl.ds(seg - 1 - n, 8, stride=seg)
            d = reach_h[at, :]
            h = d * h + part_h[at, :]
            p = d * p
            part_h[at, :] = h
            reach_h[at, :] = p
            return h, p

        zero = jnp.zeros((8, 128), F32)
        h, p = lax.fori_loop(0, seg, one, (zero, zero + 1.0), unroll=8)
        carry_h, carry_p = h[7:8, :], p[7:8, :]
        for s in range(6, -1, -1):
            at = slice(s * seg, (s + 1) * seg)
            c = reach_h[at, :]
            part_h[at, :] = part_h[at, :] + c * carry_h
            reach_h[at, :] = c * carry_p
            carry_h = h[s : s + 1, :] + p[s : s + 1, :] * carry_h
            carry_p = p[s : s + 1, :] * carry_p
        first = ext[0:1, :]
        ends[i, 0:1, :] = first * carry_p
        ends[i, 1:2, :] = first * carry_h
        ends[i, 2:8, :] = jnp.zeros((6, 128), F32)

    for n in range(1, count + 1):

        @pl.when((i == heads - 1) & (seq >= n))
        def _():
            hand_on[n - 1].start()

        @pl.when((i == heads) & (seq <= count - n))
        def _():
            hand_on[n - 1].wait_recv()

    @pl.when((i >= heads) & (i < 2 * heads))
    def _():
        h = i - heads
        part_h, reach_h = part.at[h], reach.at[h]
        st[0:8, :] = jnp.broadcast_to(chain(earlier, count), (8, 128))
        st[8 : 8 + rows, :] = states[...]
        uext[0:8, :] = border[...]
        uext[8 : 8 + rows, :] = u_head[...]
        incoming = carried(later, h, count)
        sp = soft[0:1, :]
        dc[0:8, :] = jnp.zeros((8, 128), F32)
        dc[8 + rows : 16 + rows, :] = jnp.zeros((8, 128), F32)
        gr = ga = None
        sums = [None] * (KW + 1)

        def plus(total, term):
            return term if total is None else total + term

        for r in range(0, rows, step):
            at = slice(r, r + step)
            o = off[8 + r : 8 + r + step, :]
            adj = part_h[at, :] + reach_h[at, :] * incoming
            rec, adm, cv = recall[at, :], admit[at, :], conv[at, :]
            ell = -8.0 * rec * sp
            e = jnp.exp(ell)
            m = jnp.sqrt(minus_expm1(2.0 * ell))
            previous = jnp.where(o > 0, e * st[7 + r : 7 + r + step, :], 0.0)
            ac = adj * cv
            d_ell = adj * previous - ac * adm * (e * e) / m
            d_rp = -8.0 * sp * d_ell * rec * (1.0 - rec)
            d_ip = ac * m * adm * (1.0 - adm)
            d_conv = (
                adj * m * adm
                + dot_nt(d_rp, recall_w[0], PRECISE)
                + dot_nt(d_ip, admit_w[0], PRECISE)
            )
            dc[8 + r : 8 + r + step, :] = d_conv
            gr = plus(gr, dot_tn(cv, d_rp, PRECISE))
            ga = plus(ga, dot_tn(cv, d_ip, PRECISE))
            for k in range(KW):
                term = d_conv * uext[8 + r - k : 8 + r - k + step, :]
                if k:
                    term = jnp.where(o >= k, term, 0.0)
                sums[k] = plus(sums[k], jnp.sum(term, axis=0, keepdims=True))
            sums[KW] = plus(sums[KW], jnp.sum(rec * d_ell, axis=0, keepdims=True))
        for n, value in enumerate((gr, ga)):
            p_gt[pl.ds(pl.multiple_of(n * size + h * 128, 128), 128), :] = value.astype(BF)
        for k in range(KW + 1):
            grad_small[k : k + 1, :] = sums[k]
        grad_small[KW + 1 : 8, :] = jnp.zeros((7 - KW, 128), F32)
        for r in range(0, rows, step):
            du = taps[0:1, :] * dc[8 + r : 8 + r + step, :]
            for k in range(1, KW):
                o = off[8 + r + k : 8 + r + k + step, :]
                term = taps[k : k + 1, :] * dc[8 + r + k : 8 + r + k + step, :]
                du = du + jnp.where(o >= k, term, 0.0)
            part_h[r : r + step, :] = du
        over = jnp.zeros((8, 128), F32)
        for k in range(1, KW):
            term = taps[k : k + 1, :] * dc[k : k + 8, :]
            over = over + jnp.where(off[k : k + 8, :] >= k, term, 0.0)
        edge[h] = over

    @pl.when((i == 2 * heads - 1) & (seq >= 1))
    def _():
        hand_edge.start()

    @pl.when(i == 2 * heads - 1)
    def _():
        core_gt.start()


    @pl.when((i == 2 * heads) & (seq < count))
    def _():
        hand_edge.wait_recv()

    third = 2 * heads

    @pl.when(i == third)
    def _():
        for c in loads:
            c.wait()

    @pl.when((i >= third) & (i < third + blocks))
    def _():
        at = pl.ds(pl.multiple_of((i - third) * block, block), block)
        d = jnp.concatenate([part[h, at, :] for h in range(heads)], axis=1)
        late = jnp.concatenate([from_later[h] for h in range(heads)], axis=1)
        extra = jnp.concatenate([jnp.zeros((block - 8, channels), F32), late], axis=0)
        d = d + jnp.where(i == third + blocks - 1, extra, 0.0)
        e = d.astype(BF)
        euv[at, :channels] = e
        b = euv[at, channels:]
        dots[:, at] = row_sums(e.astype(F32) * u[...] + b.astype(F32) * v[...])
        for j, q in ((3, q3), (1, q1), (2, q2), (0, q0)):
            rows_w = slice(j * width, (j + 1) * width)
            q[at, :] = (dot_nt(e, w[rows_w, :channels]) + dot_nt(b, w[rows_w, channels:])).astype(q.dtype)

    @pl.when(i == third + blocks // 2 - 1)
    def _():
        scatter[0].start()
        scatter[2].start()

    @pl.when(i == third + blocks - 1)
    def _():
        scatter[1].start()
        small_x.start()
        scatter[0].wait_recv()
        add_into(q2, r3, 0, half)
        scatter[3].start()
        scatter[4].start()

    last = third + blocks

    @pl.when(i == last)
    def _():
        small_x.wait_recv()
        dots_x[...] = dots_x[...] + dots[...]
        small_y.start()
        scatter[1].wait_recv()
        add_into(q1, r3, half, half)
        scatter[5].start()

    def finish(start, first):
        scatter[first].wait_recv()
        scatter[first + 1].wait_recv()
        return norm_back_rows(
            start, half, q0, rx, ry, dots_x, dots_y, scale, x, gain[0:1, :width], dx, grad, None
        )

    @pl.when(i == last + 1)
    def _():
        small_y.wait_recv()
        gain_grad[0:1, :] = finish(0, 2)

    @pl.when(i == last + 2)
    def _():
        gain_grad[0:1, :] = gain_grad[0:1, :] + finish(half, 4)
        for n in range(1, count + 1):

            @pl.when(seq >= n)
            def _():
                hand_on[n - 1].wait_send()

        @pl.when(seq >= 1)
        def _():
            hand_edge.wait_send()


    @pl.when(i == pl.num_programs(0) - 1)
    def _():
        sent_y = [m for group in to_y.values() for m in group] + early_y
        for m in sent_y:
            m.wait_recv()
        for m in scatter + [small_x, small_y, core_out, core_gt] + sent_y:
            m.wait_send()
        for c in stores:
            c.wait()


def back(errs, w_out, states, v, recall, conv, admit, u, off, soft, taps, rw, aw, border, earlier, w, scale, x, dx, gain, sum_gu, sum_down, mixed):
    rows, channels = states.shape
    width = x.shape[1]
    heads = channels // 128
    block = ROW_BLOCK
    blocks = rows // block
    count = earlier.shape[0]
    steps = 2 * heads + blocks + 8

    def both(i):
        return jnp.where(i < heads, i, jnp.clip(i - heads, 0, heads - 1))

    def second(i):
        return jnp.clip(i - heads, 0, heads - 1)

    def on(shape, pick, axis):
        if axis == 0:
            return pl.BlockSpec(shape, lambda i: (pick(i),) + (0,) * (len(shape) - 1))
        return pl.BlockSpec(shape, lambda i: (0, pick(i)))

    def third(i):
        return jnp.clip(i - 2 * heads, 0, blocks - 1)

    def first(i):
        return jnp.minimum(i, heads - 1)

    tall = (rows, 128)
    gate = (1, 128, 128)
    own_gate = on(gate, second, 0)
    chunk = pltpu.VMEM((rows, width), BF)
    lanes = pltpu.VMEM((8, rows), F32)
    gu = pltpu.VMEM(sum_gu.shape, BF)
    pair, gate_sum = pltpu.VMEM((channels, 2 * width), BF), pltpu.VMEM((2 * channels, 128), BF)
    piece = pltpu.VMEM((heads, 8, 128), F32)
    half_gu, half_dn = (sum_gu.shape[0] // 2, sum_gu.shape[1]), (sum_down.shape[0], width)
    half_out = (channels, width)
    count_sems = 88
    return pl.pallas_call(
        functools.partial(back_body, heads, blocks, count),
        grid=(steps,),
        in_specs=[whole_spec((rows, width))] * 4
        + [
            on((128, 4 * width), first, 0),
            on(tall, both, 1),
            on(tall, first, 1),
            on(tall, both, 1),
            on(tall, second, 1),
            on(tall, second, 1),
            on(tall, second, 1),
            whole_spec(off.shape),
            on((1, 128), both, 1),
            on((KW, 128), second, 1),
            own_gate,
            own_gate,
            on((8, 128), second, 1),
            pl.BlockSpec((count, 1, 8, 128), lambda i: (0, second(i), 0, 0)),
            on((block, channels), third, 0),
            on((block, channels), third, 0),
            any_spec(),
            whole_spec(scale.shape),
            any_spec(),
            any_spec(),
            whole_spec(gain.shape),
            any_spec(),
            any_spec(),
            whole_spec(mixed.shape),
        ],
        out_specs=[
            whole_spec((rows, 2 * channels)),
            whole_spec((rows, width)),
            whole_spec((8, width)),
            on((8, 128), second, 1),
        ]
        + [any_spec()] * 6,
        out_shape=[
            sds((rows, 2 * channels), BF),
            sds((rows, width), F32),
            sds((8, width), F32),
            sds((8, channels), F32),
            sds(half_gu, BF),
            sds(half_gu, BF),
            sds(half_dn, BF),
            sds(half_out, BF),
            sds(half_out, BF),
            sds((4 * channels, 128), BF),
        ],
        scratch_shapes=[
            pltpu.VMEM(w.shape, BF),
            pltpu.VMEM((rows, width), F32),
            pltpu.VMEM((rows, width), F32),
            pltpu.VMEM((rows, 4 * width), BF),
        ]
        + [pltpu.VMEM((heads, rows, 128), F32)] * 2
        + [
            pltpu.VMEM((rows + 8, 128), F32),
            pltpu.VMEM((rows + 8, 128), F32),
            pltpu.VMEM((rows + 8, 128), F32),
            pltpu.VMEM((rows + 16, 128), F32),
            piece,
            pltpu.VMEM((count, heads, 8, 128), F32),
            piece,
            piece,
            pltpu.SemaphoreType.DMA((4,)),
            pltpu.VMEM((rows, width), F32),
        ]
        + [chunk] * 6
        + [lanes] * 3
        + [gu] * 3
        + [pair] * 5
        + [gate_sum] * 5
        + [pltpu.SemaphoreType.DMA((12,))]
        + [pltpu.SemaphoreType.DMA((count_sems,))] * 2,
        compiler_params=comm_params(4),
        cost_estimate=cost(64 * rows * w.size, rows * channels * 60, rows * channels * 8),
        name="back",
    )(
        *errs, w_out, states, v, recall, conv, admit, u, off, soft, taps, rw, aw, border, earlier,
        u, v, w, scale, x, dx, gain, sum_gu, sum_down, mixed,
    )


TAIL_MESSAGES = 48


def tail_body(*refs):
    (n1, euv, grad_small, grad_mixer, grad_feed) = refs[:5]
    (p0, p1, p2, p3, mid, grad_chunk) = refs[5:11]
    (mine_in, far_in, tiny_out, out, grad) = refs[11:16]
    (s_in, p_in, c_in, a_in, b_in, s_ty, p_ty, c_ty, a_ty, b_ty) = refs[16:26]
    (q0, md, gc, q1, q2, q3, r3, rx, ry, own_a, other_a, own_b, other_b, load, send, recv) = refs[26:]
    made = Messages((send, recv))
    col = lax.axis_index("col")
    core = lax.rem(col, 2)
    to_core, to_y = neighbour_core(), neighbour_y()
    rows, width = p0.shape
    part = width // 2
    half_tokens = rows // 2
    copies = []

    def copy(src, dst):
        copies.append(pltpu.make_async_copy(src, dst, load.at[len(copies)]))
        return copies[-1]

    outs_in = [copy(p3, q3), copy(p1, q1), copy(p2, q2)]
    late = [copy(p0, q0), copy(mid, md), copy(grad_chunk, gc)]
    scatter = made.block(scatter_messages, q1, q2, q3, r3, rx, ry)
    cut = width // 4
    spans = [(n * cut, cut) for n in (4, 5, 6, 7, 0, 1, 2)]
    spans += [(3 * cut, cut // 2), (3 * cut + cut // 2, cut // 2)]
    order = [pl.ds(*span) for span in spans]
    pieces = [[s_ty, a_ty, b_ty]] + [[r.at[at, :] for r in (s_in, a_in, b_in)] for at in order]
    count = len(pieces)
    total = SeqSum(pieces, (send, recv), made.used)
    made.used += 2 * count
    core_ty = made.new(p_ty, c_ty, to_core)
    far_rows, own_rows = pl.ds(width, width), pl.ds(0, width)
    core_in = [made.new(p_in.at[at, :], c_in.at[at, :], to_core) for at in (far_rows, own_rows)]
    over_y = {
        n + 1: made.new(s_in.at[order[n], :], far_in.at[pl.ds(n * cut, cut), :], to_y) for n in range(4)
    }
    send_out, send_grad = made.new(other_a, out.at[core], to_core), made.new(other_b, grad.at[core], to_core)
    keep_out, keep_grad = copy(own_a, out.at[core]), copy(own_b, grad.at[core])
    keep_in = {n + 1: copy(s_in.at[order[n], :], mine_in.at[order[n], :]) for n in range(4, len(order))}

    for m in outs_in:
        m.start()
    greet_all((neighbour_x(), to_y, to_core, neighbour_end(), neighbour_middle()))
    p_ty[...] = jnp.zeros_like(p_ty)
    p_ty[0:8, :] = grad_small[...]
    for n, source in enumerate((grad_mixer, grad_feed)):
        g = jnp.broadcast_to(source[0:1, :], (8, width))
        g = jnp.where(core == 0, g, pltpu.roll(g, part, 1))
        p_ty[8 + n : 9 + n, 0:width] = g[0:1, :]
    core_ty.start()

    def tile(n, target, row):
        sub = width // 3

        def one(k, carry):
            at = pl.ds(pl.multiple_of(n * width + k * sub, sub), sub)
            where = pl.ds(pl.multiple_of(row + k * sub, sub), sub)
            target[where, :] = dot_tn(n1[:, at], euv[...]).astype(BF)
            return carry

        lax.fori_loop(0, 3, one, 0)

    def gather_core(n, at):
        core_in[n].wait_recv()
        plus_in(s_in.at[at, :], c_in.at[at, :])

    tile(3, p_in, width)
    core_in[0].start()
    for m in outs_in:
        m.wait()
    for m in late:
        m.start()
    for m in scatter[:3]:
        m.start()
    tile(1, s_in, width)
    core_ty.wait_recv()
    s_ty[...] = p_ty[...] + c_ty[...]
    total.begin(0)
    gather_core(0, far_rows)
    for n in range(1, 5):
        total.begin(n)
    tile(2, p_in, 0)
    core_in[1].start()
    total.relay(0)
    total.relay(1)
    total.settle(0)
    tile(0, s_in, 0)
    gather_core(1, own_rows)
    for n in range(5, count):
        total.begin(n)

    def chunk_out(value, own, other, at):
        turned = value.T
        own[:, at] = turned[:part]
        other[:, at] = turned[part:]

    def in_steps(start, size, body):
        def one(n, carry):
            body(pl.ds(pl.multiple_of(start + n * 128, 128), 128))
            return carry

        lax.fori_loop(0, size // 128, one, 0)

    def finish_out(start, first):
        scatter[first].wait_recv()
        scatter[first + 1].wait_recv()

        def body(at):
            value = q0[at, :] + rx[at, :].astype(F32) + ry[at, :].astype(F32) + md[at, :]
            chunk_out(value, own_a, other_a, at)

        in_steps(start, half_tokens, body)

    for n in range(2, count + 2):
        if n < count:
            total.relay(n)
        if n - 1 < count:
            total.settle(n - 1)
        total.finish(n - 2)
        if n - 2 in over_y:
            over_y[n - 2].start()
        if n - 2 in keep_in:
            keep_in[n - 2].start()
        if n == 2:
            scatter[0].wait_recv()
            add_into(q2, r3, 0, half_tokens)
            scatter[3].start()
            scatter[4].start()
        if n == 3:
            scatter[1].wait_recv()
            add_into(q1, r3, half_tokens, half_tokens)
            scatter[5].start()
            for m in late:
                m.wait()
            in_steps(0, rows, lambda at: chunk_out(gc[at, :], own_b, other_b, at))
            send_grad.start()
            keep_grad.start()
        if n == 7:
            finish_out(0, 2)
        if n == 8:
            finish_out(half_tokens, 4)
            send_out.start()
            keep_out.start()
    put_in(tiny_out, s_ty)
    received = list(over_y.values()) + [send_out, send_grad]
    for m in received:
        m.wait_recv()
    for m in [core_ty] + core_in + received + scatter:
        m.wait_send()
    for c in [keep_out, keep_grad] + list(keep_in.values()):
        c.wait()


def tail(n1, euv, grad_small, grad_mixer, grad_feed, parts, mid, grad_chunk):
    rows, channels = euv.shape[0], euv.shape[1] // 2
    width = mid.shape[1]
    part = width // 2
    big = pltpu.VMEM((2 * width, 2 * channels), BF)
    tiny = pltpu.VMEM((16, channels), F32)
    piece = pltpu.VMEM((rows, width), BF)
    full = pltpu.VMEM((rows, width), F32)
    side = pltpu.VMEM((part, rows), F32)
    quarter_in = (width, 2 * channels)
    final = sds((2, part, rows), F32)
    return pl.pallas_call(
        tail_body,
        in_specs=[pl.BlockSpec(memory_space=pltpu.VMEM)] * 5 + [any_spec()] * 6,
        out_specs=[any_spec()] * 2 + [pl.BlockSpec(memory_space=pltpu.VMEM)] + [any_spec()] * 2,
        out_shape=[sds(quarter_in, BF)] * 2 + [sds((16, channels), F32), final, final],
        scratch_shapes=[big] * 5
        + [tiny] * 5
        + [full] * 3
        + [piece] * 6
        + [side] * 4
        + [pltpu.SemaphoreType.DMA((13,))]
        + [pltpu.SemaphoreType.DMA((TAIL_MESSAGES,))] * 2,
        compiler_params=pltpu.CompilerParams(
            vmem_limit_bytes=VMEM_LIMIT, collective_id=6, has_side_effects=True
        ),
        cost_estimate=cost(60 * rows * width * channels * 4, nbytes(n1, euv)),
        name="tail",
    )(n1, euv, grad_small, grad_mixer, grad_feed, *parts, mid, grad_chunk)


def arrange_body(place, mine_gu, far_gu, mine_dn, far_dn, mine_in, far_in, mine_out, far_out, *outs):
    gate, up, down, inp, branch, out = outs
    row, y = place[0], place[1]
    first = pl.program_id(0) == 0

    def side_by_side(mine, far, left, right):
        lanes = left.shape[1] // 2
        for target, at in ((left, 0), (right, mine.shape[1] // 2)):
            m = mine[:, at : at + lanes].astype(F32)
            t = far[:, at : at + lanes].astype(F32)
            target[:, :lanes] = jnp.where(y == 0, m, t)
            target[:, lanes:] = jnp.where(y == 0, t, m)

    def stack_up(mine, far, target):
        value = jnp.where(first, mine[...].astype(F32), far[...].astype(F32))
        target[...] = jnp.where(row == 0, value, pltpu.roll(value, value.shape[1] // 2, 1))

    side_by_side(mine_gu, far_gu, gate, up)
    side_by_side(mine_in, far_in, inp, branch)
    stack_up(mine_dn, far_dn, down)
    stack_up(mine_out, far_out, out)


def arrange(place, mine_gu, far_gu, mine_dn, far_dn, mine_in, far_in, mine_out, far_out):
    width, units = far_dn.shape[1], far_dn.shape[0]
    inner = mine_out.shape[0]
    lanes_gu, lanes_in = mine_gu.shape[1], mine_in.shape[1]
    cuts = 2
    piece = width // (2 * cuts)

    def rows_in(i, j, place):
        return (cuts * i + j, 0)

    def rows_to(i, j, place):
        return (cuts * (i + place[0] - 2 * i * place[0]) + j, 0)

    def near(i, j, place):
        return (jnp.where(i == 0, j, cuts - 1), 0)

    def far(i, j, place):
        return (jnp.where(i == 0, 0, j), 0)

    def stack_to(i, j, place):
        return (cuts * (i + place[1] - 2 * i * place[1]) + j, 0)

    def spec(rows, lanes, at):
        return pl.BlockSpec((rows, lanes), at)

    shapes = [(width, lanes_gu)] * 2 + [(2 * units, width)] + [(width, lanes_in)] * 2 + [(2 * inner, width)]
    return pl.pallas_call(
        arrange_body,
        grid_spec=pltpu.PrefetchScalarGridSpec(
            num_scalar_prefetch=1,
            grid=(2, cuts),
            in_specs=[
                spec(piece, lanes_gu, rows_in),
                spec(piece, lanes_gu, rows_in),
                spec(units // cuts, width, near),
                spec(units // cuts, width, far),
                spec(piece, lanes_in, rows_in),
                spec(piece, lanes_in, rows_in),
                spec(inner // cuts, width, near),
                spec(inner // cuts, width, far),
            ],
            out_specs=[spec(piece, lanes_gu, rows_to)] * 2
            + [spec(units // cuts, width, stack_to)]
            + [spec(piece, lanes_in, rows_to)] * 2
            + [spec(inner // cuts, width, stack_to)],
        ),
        out_shape=[sds(s, F32) for s in shapes],
        compiler_params=pltpu.CompilerParams(vmem_limit_bytes=VMEM_LIMIT),
        cost_estimate=cost(1000000, 24000000),
        name="arrange",
    )(place, mine_gu, far_gu, mine_dn, far_dn, mine_in, far_in, mine_out, far_out)


def local_fast(
    stream_in,
    cotangent,
    doc_lengths,
    mixer_gain,
    input_weight,
    branch_weight,
    filter_taps,
    recall_gate,
    admit_gate,
    decay_param,
    output_weight,
    feed_gain,
    gate_weight,
    up_weight,
    down_weight,
):
    tokens = stream_in.shape[1]
    count = lax.axis_size("seq")
    part = stream_in.shape[2]
    seq = lax.axis_index("seq")
    row = lax.axis_index("row")
    col = lax.axis_index("col")
    y, core = col // 2, col % 2
    heads = recall_gate.shape[0] // 2
    rw = lax.dynamic_slice_in_dim(recall_gate, y * heads, heads, 0)
    aw = lax.dynamic_slice_in_dim(admit_gate, y * heads, heads, 0)
    soft_own = jax.nn.softplus(-decay_param)[None]
    small = jnp.concatenate(
        [filter_taps, soft_own, decay_param[None], jnp.zeros((2,) + decay_param.shape, F32)]
    )
    gains = jnp.concatenate([mixer_gain[None], feed_gain[None], jnp.zeros((6, part), F32)])

    lengths = lax.dynamic_index_in_dim(doc_lengths, core, 0, False)
    offset = doc_offset(lengths, seq * tokens, tokens)
    edge = jnp.full((8,), -1, jnp.int32)
    off = jnp.concatenate([edge, offset, edge])[:, None]

    (
        g_low, w_down, gains_all, small, s1, border, earlier, mid, mid_low,
        n1, conv, recall, admit, states, mixed, mx, my, md, far_w, sib_own, sib_far, w_in,
        x, g, w_out, u, v,
    ) = front(
        jnp.swapaxes(stream_in, 1, 2), jnp.swapaxes(cotangent, 1, 2), input_weight, branch_weight, output_weight, gate_weight, up_weight, down_weight,
        gains, small, recall_gate, admit_gate, off, count - 1,
    )
    taps, soft, decay = small[:KW], small[KW : KW + 1], small[KW + 1 : KW + 2]
    p0, p1, p2, p3, dx2, *dx_all, grad_feed, sum_down, sum_gu = feed(
        (mid_low, mx, my, md), g_low, mid, g, gains_all, w_down,
        (gate_weight, up_weight, sib_own, far_w, sib_far),
    )
    (
        euv, grad_chunk, grad_mixer, grad_small, mine_gu, far_gu, far_down, mine_out, far_out, gates
    ) = back(
        dx_all, w_out, states, v, recall, conv, admit, u, off, soft, taps, rw, aw, border, earlier,
        w_in, s1, x, dx2, gains_all, sum_gu, sum_down, mixed,
    )
    mine_in, far_in, tiny, out, grad = tail(
        n1, euv, grad_small, grad_mixer, grad_feed, (p0, p1, p2, p3), mid, grad_chunk
    )
    place = jnp.stack([row, y]).astype(jnp.int32)
    grad_gate, grad_up, grad_down, grad_input, grad_branch, grad_output = arrange(
        place, mine_gu, far_gu, sum_down, far_down, mine_in, far_in, mine_out, far_out
    )
    gates = gates.astype(F32).reshape((2,) + recall_gate.shape)
    own = taps.shape[1] // 2
    mine = lax.dynamic_slice_in_dim(tiny[:8], core * own, own, 1)
    gain_grads = lax.dynamic_slice_in_dim(tiny[8:10, : 2 * part], core * part, part, 1)
    return (
        jnp.swapaxes(out, 1, 2),
        jnp.swapaxes(grad, 1, 2),
        gain_grads[0],
        grad_input,
        grad_branch,
        mine[:KW],
        gates[0],
        gates[1],
        mine[KW] * 8.0 * jax.nn.sigmoid(-decay_param),
        grad_output,
        gain_grads[1],
        grad_gate,
        grad_up,
        grad_down,
    )


def solution(mesh):
    in_specs = (
        P(None, "seq", ("col", "row")),
        P(None, "seq", ("col", "row")),
        P(),
        P(("col", "row")),
        P("col", "row"),
        P("col", "row"),
        P(None, ("row", "col")),
        P("row", None, None),
        P("row", None, None),
        P(("row", "col")),
        P("row", "col"),
        P(("col", "row")),
        P("col", "row"),
        P("col", "row"),
        P("row", "col"),
    )
    out_specs = (
        P(None, "seq", ("col", "row")),
        P(None, "seq", ("col", "row")),
        P(("col", "row")),
        P("col", "row"),
        P("col", "row"),
        P(None, ("row", "col")),
        P("row", None, None),
        P("row", None, None),
        P(("row", "col")),
        P("row", "col"),
        P(("col", "row")),
        P("col", "row"),
        P("col", "row"),
        P("row", "col"),
    )
    plan = local_fast if dict(mesh.shape) == {"seq": 4, "row": 2, "col": 4} else local
    return jax.shard_map(plan, mesh=mesh, in_specs=in_specs, out_specs=out_specs, check_vma=False)
```
